32 devices in a mesh: dp: 4 (over y, x), wide: 2 (over core), narrow: 4 (over z).
Axes of the slice: x: 2, y: 2, z: 4, core: 2. Of those that a mesh axis runs over, the one named last changes fastest.
Arguments:
- patches: bfloat16 [48, 196, 768], P(('dp', 'wide')), may hold values from -6 to 6
- vis_index: int32 [48, 98], P(('dp', 'wide')), may hold values from 0 to 195, as said below
- keep_mask: int32 [48, 196], P(('dp', 'wide')), may hold values from 0 to 1, as said below
- counts: int32 [48], P(('dp', 'wide')), may hold values from 40 to 98, as said below
- step_count: int32 [1], replicated, may hold values from 1 to 20
- w_embed: float32 [768, 768], P(('dp', 'wide'), 'narrow'), may hold values from -0.21875 to 0.21875
- enc_qkv: float32 [768, 2304], P(('dp', 'wide'), 'narrow'), may hold values from -0.21875 to 0.21875
- enc_out: float32 [768, 768], P('narrow', ('dp', 'wide')), may hold values from -0.625 to 0.625
- enc_up: float32 [768, 3072], P(('dp', 'wide'), 'narrow'), may hold values from -0.21875 to 0.21875
- enc_down: float32 [3072, 768], P('narrow', ('dp', 'wide')), may hold values from -0.109375 to 0.109375
- w_bridge: float32 [768, 512], P(('dp', 'wide'), 'narrow'), may hold values from -0.21875 to 0.21875
- dec_qkv: float32 [512, 1536], P(('dp', 'wide'), 'narrow'), may hold values from -0.25 to 0.25
- dec_out: float32 [512, 512], P('narrow', ('dp', 'wide')), may hold values from -1 to 1
- dec_up: float32 [512, 2048], P(('dp', 'wide'), 'narrow'), may hold values from -0.25 to 0.25
- dec_down: float32 [2048, 512], P('narrow', ('dp', 'wide')), may hold values from -0.125 to 0.125
- w_head: float32 [512, 768], P(('dp', 'wide'), 'narrow'), may hold values from -0.25 to 0.25
- vectors: float32 [4, 2048], P('narrow')
- first_moment: float32 [4, 2048], P('narrow'), may hold values from -0.0024414062 to 0.0024414062
- second_moment: float32 [4, 2048], P('narrow'), may hold values from 1.0768376e-09 to 8.614701e-09
- enc_small: float32 [8, 4, 41, 96, 96], P(('dp', 'wide'), 'narrow'), as said below
- enc_big: float32 [8, 4, 41, 64, 64], P(('dp', 'wide'), 'narrow'), as said below
- dec_small: float32 [8, 4, 27, 64, 64], P(('dp', 'wide'), 'narrow'), as said below
- dec_big: float32 [8, 4, 27, 64, 64], P(('dp', 'wide'), 'narrow'), as said below
Outputs:
- new_embed: float32 [768, 768], P(('dp', 'wide'), 'narrow')
- new_enc_qkv: float32 [768, 2304], P(('dp', 'wide'), 'narrow')
- new_enc_out: float32 [768, 768], P('narrow', ('dp', 'wide'))
- new_enc_up: float32 [768, 3072], P(('dp', 'wide'), 'narrow')
- new_enc_down: float32 [3072, 768], P('narrow', ('dp', 'wide'))
- new_bridge: float32 [768, 512], P(('dp', 'wide'), 'narrow')
- new_dec_qkv: float32 [512, 1536], P(('dp', 'wide'), 'narrow')
- new_dec_out: float32 [512, 512], P('narrow', ('dp', 'wide'))
- new_dec_up: float32 [512, 2048], P(('dp', 'wide'), 'narrow')
- new_dec_down: float32 [2048, 512], P('narrow', ('dp', 'wide'))
- new_head: float32 [512, 768], P(('dp', 'wide'), 'narrow')
- new_enc_small: float32 [8, 4, 41, 96, 96], P(('dp', 'wide'), 'narrow')
- new_enc_big: float32 [8, 4, 41, 64, 64], P(('dp', 'wide'), 'narrow')
- new_dec_small: float32 [8, 4, 27, 64, 64], P(('dp', 'wide'), 'narrow')
- new_dec_big: float32 [8, 4, 27, 64, 64], P(('dp', 'wide'), 'narrow')
- new_vectors: float32 [4, 2048], P('narrow')
- new_first: float32 [4, 2048], P('narrow')
- new_second: float32 [4, 2048], P('narrow')
- norms: float32 [2], replicated
- loss_sum: float32 [], replicated
- weight_total: float32 [], replicated
The draws below stay inside these ranges and needn't reach their ends.
Inputs may be any that keep to these rules, and one draw needn't show every extreme that they name: `vis_index`: for each image the first counts entries are its kept patches in increasing order; the other entries are 0. `keep_mask`: 1 exactly at the patches that vis_index lists for the image. `counts`: among the images of one index of dp and wide, one keeps 98 patches; the images of the last index include one that keeps 40. `enc_small`: each block's statistic is symmetric and positive definite. `enc_big`: each block's statistic is symmetric and positive definite. `dec_small`: each block's statistic is symmetric and positive definite. `dec_big`: each block's statistic is symmetric and positive definite.
All inputs are finite; a program needn't handle non-finite values.
Results may differ from the reference program's by a relative error of at most 0.00085.
The reference program's roundings to bfloat16 on the way count: a program that leaves them out, or rounds other values in their place, can miss the bound.
Values may be sent and summed in bfloat16 or wider, within the bound.
A program may use at most 192 MiB of HBM per device.

```python
import math
import jax
import jax.numpy as jnp
from jax import lax

D = 768
DH = 64
FE = 3072
DD = 512
DHD = 32
FD = 2048
PIX = 768
NP = 196
IMG_DEV = 6
BLOCK = 64
NEWTON = 3
KEEP_MOST = 98
KEEP_LEAST = 40
IMAGES = 48
AE = 96
AD = 64
CE = 41
CD = 27
VW = 2048
PARAMS = 11608064
N_DP = 4
N_WIDE = 2
N_NARROW = 4


def visible_plan(key):
    base = jax.random.fold_in(key, 11)
    key_counts, key_places, key_perm = jax.random.split(base, 3)
    owners = IMAGES // IMG_DEV
    within = jnp.arange(IMAGES) % IMG_DEV
    owner_of = jnp.arange(IMAGES) // IMG_DEV
    upper = KEEP_LEAST + (KEEP_MOST - KEEP_LEAST) * (owner_of + 1) // owners
    counts = jax.random.randint(key_counts, (IMAGES,), KEEP_LEAST, upper + 1)
    first_pick = jax.random.randint(key_places, (owners,), 0, IMG_DEV)
    second_pick = (first_pick + 1) % IMG_DEV
    last_owner = owner_of == owners - 1
    counts = jnp.where(within == first_pick[owner_of], KEEP_MOST, jnp.where(last_owner & (within == second_pick[owner_of]), KEEP_LEAST, counts))
    perm_keys = jax.random.split(key_perm, IMAGES)

    def permute(single):
        return jax.random.permutation(single, NP)
    orders = jax.vmap(permute)(perm_keys)
    taken = jnp.arange(NP)[None, :] < counts[:, None]
    chosen = jnp.sort(jnp.where(taken, orders, NP), axis=1)[:, :KEEP_MOST]
    index = jnp.where(chosen < NP, chosen, 0).astype(jnp.int32)
    keep = jnp.sum((chosen[:, :, None] == jnp.arange(NP)[None, None, :]).astype(jnp.int32), axis=1)
    return (index, keep.astype(jnp.int32), counts.astype(jnp.int32))


def draw_vis_index(key, part):
    return visible_plan(key)[0]


def draw_keep_mask(key, part):
    return visible_plan(key)[1]


def draw_counts(key, part):
    return visible_plan(key)[2]


def draw_vectors(key, part):
    widths = [D] * 6 + [DD] * 7
    kinds = ['gain', 'bias', 'gain', 'bias', 'gain', 'bias', 'token', 'gain', 'bias', 'gain', 'bias', 'gain', 'bias']
    pieces = []
    for member, width_one in enumerate(widths):
        subkey = jax.random.fold_in(key, 100 + member)
        if kinds[member] == 'gain':
            piece = jax.random.uniform(subkey, (width_one,), jnp.float32, 0.6, 1.4)
        elif kinds[member] == 'bias':
            piece = 0.3 * jax.random.normal(subkey, (width_one,), jnp.float32)
        else:
            piece = jax.random.normal(subkey, (width_one,), jnp.float32)
        pieces.append(piece.reshape(N_NARROW, -1))
    return jnp.concatenate(pieces, axis=1)


def statistic(key, blocks, side, level):
    key_noise, key_diag = jax.random.split(key)
    shape = (N_DP * N_WIDE, N_NARROW, blocks, side, side)
    noise = jax.random.uniform(key_noise, shape, jnp.float32, -1.0, 1.0)
    noise = 0.5 * (noise + jnp.swapaxes(noise, -1, -2))
    spread = jax.random.uniform(key_diag, shape[:-1], jnp.float32, 1.0, 2.0)
    diagonal = 1.4 * side ** 0.5 * spread[..., None] * jnp.eye(side, dtype=jnp.float32)
    return level / (1.4 * side ** 0.5 * 1.5) * (noise + diagonal)


def draw_enc_small(key, part):
    return statistic(jax.random.fold_in(key, 21), CE, AE, BLOCK / PARAMS)


def draw_enc_big(key, part):
    return statistic(jax.random.fold_in(key, 22), CE, BLOCK, AE / PARAMS)


def draw_dec_small(key, part):
    return statistic(jax.random.fold_in(key, 23), CD, AD, BLOCK / PARAMS)


def draw_dec_big(key, part):
    return statistic(jax.random.fold_in(key, 24), CD, BLOCK, AD / PARAMS)


def shard_levels(key, dims, shards, least, high):
    def one(dim, parts):
        heights = jax.random.uniform(jax.random.fold_in(jax.random.fold_in(key, 6), dim), (parts,), jnp.float32, least / len(shards), high / len(shards))
        return jnp.repeat(jnp.exp(heights), dims[dim] // parts).reshape((-1,) + (1,) * (len(dims) - dim - 1))

    level = one(*shards[0])
    for cut in shards[1:]:
        level = level * one(*cut)
    return level


def scatter_about(own_key, shape, scale, reach, cuts=(), kind=jnp.bfloat16):
    drawn = scale * jax.random.normal(own_key, shape, jnp.float32)
    if cuts:
        drawn = drawn * shard_levels(own_key, shape, cuts, -0.22, 0.18)
    return jnp.clip(drawn, -reach, reach).astype(kind)


def setup_inputs(seed: int = 0) -> dict:
    arg_keys = jax.random.split(jax.random.key(seed), 24)
    patches = scatter_about(arg_keys[0], (IMAGES, NP, PIX), 1.0, 6.0, ((0, 8),))
    vis_index = draw_vis_index(jax.random.fold_in(arg_keys[23], 71), 0)
    keep_mask = draw_keep_mask(jax.random.fold_in(arg_keys[23], 71), 0)
    counts = draw_counts(jax.random.fold_in(arg_keys[23], 71), 0)
    step_count = jax.random.randint(arg_keys[4], (1,), 1, 21).astype(jnp.int32)
    w_embed = scatter_about(arg_keys[5], (PIX, D), PIX ** -0.5, 0.21875, ((0, 8), (1, 4)), jnp.float32)
    enc_qkv = scatter_about(arg_keys[6], (D, 3 * D), D ** -0.5, 0.21875, ((0, 8), (1, 4)), jnp.float32)
    enc_out = scatter_about(arg_keys[7], (D, D), (D // 10) ** -0.5, 0.625, ((0, 4), (1, 8)), jnp.float32)
    enc_up = scatter_about(arg_keys[8], (D, FE), D ** -0.5, 0.21875, ((0, 8), (1, 4)), jnp.float32)
    enc_down = scatter_about(arg_keys[9], (FE, D), FE ** -0.5, 0.109375, ((0, 4), (1, 8)), jnp.float32)
    w_bridge = scatter_about(arg_keys[10], (D, DD), D ** -0.5, 0.21875, ((0, 8), (1, 4)), jnp.float32)
    dec_qkv = scatter_about(arg_keys[11], (DD, 3 * DD), DD ** -0.5, 0.25, ((0, 8), (1, 4)), jnp.float32)
    dec_out = scatter_about(arg_keys[12], (DD, DD), (DD // 14) ** -0.5, 1.0, ((0, 4), (1, 8)), jnp.float32)
    dec_up = scatter_about(arg_keys[13], (DD, FD), DD ** -0.5, 0.25, ((0, 8), (1, 4)), jnp.float32)
    dec_down = scatter_about(arg_keys[14], (FD, DD), FD ** -0.5, 0.125, ((0, 4), (1, 8)), jnp.float32)
    w_head = scatter_about(arg_keys[15], (DD, PIX), DD ** -0.5, 0.25, ((0, 8), (1, 4)), jnp.float32)
    vectors = draw_vectors(jax.random.fold_in(arg_keys[23], 71), 0)
    first_moment = scatter_about(arg_keys[17], (N_NARROW, VW), (0.55 * PARAMS ** -0.5), 0.0024414062, ((0, 4),), jnp.float32)
    second_moment = jnp.clip(jnp.exp(math.log(8.614700952591647e-09) - 2.0794415 * jax.random.uniform(arg_keys[18], (N_NARROW, VW), jnp.float32) ** shard_levels(arg_keys[18], (N_NARROW, VW), ((0, 4),), -0.2, 0.2)), 1.076837619073956e-09, 8.614700952591647e-09)
    enc_small = draw_enc_small(jax.random.fold_in(arg_keys[23], 71), 0)
    enc_big = draw_enc_big(jax.random.fold_in(arg_keys[23], 71), 0)
    dec_small = draw_dec_small(jax.random.fold_in(arg_keys[23], 71), 0)
    dec_big = draw_dec_big(jax.random.fold_in(arg_keys[23], 71), 0)
    return dict(patches=patches, vis_index=vis_index, keep_mask=keep_mask, counts=counts, step_count=step_count, w_embed=w_embed, enc_qkv=enc_qkv, enc_out=enc_out, enc_up=enc_up, enc_down=enc_down, w_bridge=w_bridge, dec_qkv=dec_qkv, dec_out=dec_out, dec_up=dec_up, dec_down=dec_down, w_head=w_head, vectors=vectors, first_moment=first_moment, second_moment=second_moment, enc_small=enc_small, enc_big=enc_big, dec_small=dec_small, dec_big=dec_big)


HIGH = lax.Precision.HIGHEST
EPS_NORM = 1e-06
VISIBLE_WEIGHT = 0.1
STAT_DECAY = 0.5
LR_MATRIX = 0.2
LR_VECTOR = 0.2
LAYER_DECAY = 0.75
BETA_FIRST = 0.9
BETA_SECOND = 0.999
EPS_ADAM = 1e-08
CLIP_NORM = 1.0
ENC_KINDS = (True, True, False, True, False, True)
DEC_KINDS = (True, False, True, False, True)

@jax.custom_vjp
def low(v):
    return lax.optimization_barrier(v.astype(jnp.bfloat16)).astype(jnp.float32)

@jax.custom_vjp
def low_back(v):
    return v

def low_keep(v):
    return (low(v), None)

def low_pass(kept, grad):
    return (grad,)

def back_keep(v):
    return (v, None)

def back_low(kept, grad):
    return (low(grad),)
low.defvjp(low_keep, low_pass)
low_back.defvjp(back_keep, back_low)

def matmul_hi(left, right):
    return jnp.matmul(left, right, precision=HIGH)

def norm_rows(values, gain_vec, bias_vec):
    row_mean = lax.optimization_barrier(jnp.mean(values, -1, keepdims=True))
    row_var = lax.optimization_barrier(jnp.mean(jnp.square(values - row_mean), -1, keepdims=True))
    return (values - row_mean) * lax.rsqrt(row_var + EPS_NORM) * gain_vec + bias_vec

def sincos(position, offset, columns, width_all):
    column = offset + jnp.arange(columns, dtype=jnp.int32)
    freq_col = jnp.power(10000.0, -(2 * (column // 2)).astype(jnp.float32) / width_all)
    angle = position[:, None] * freq_col[None, :]
    return jnp.where(column % 2 == 0, jnp.sin(angle), jnp.cos(angle))

def placement(vis_index, counts):
    slot_ids = jnp.arange(KEEP_MOST, dtype=jnp.int32)
    hit_map = (vis_index[:, :, None] == jnp.arange(NP, dtype=jnp.int32)[None, None, :]) & (slot_ids[None, :, None] < counts[:, None, None])
    slot_of = lax.optimization_barrier(jnp.sum(jnp.where(hit_map, slot_ids[None, :, None], 0), axis=1)).astype(jnp.int32)
    return (slot_of, jnp.any(hit_map, axis=1))

def unpack(packed, enc_cols, dec_cols):
    widths = [enc_cols] * 6 + [dec_cols] * 7
    pieces, offset = ([], 0)
    for width_one in widths:
        pieces.append(packed[:, offset:offset + width_one].reshape(-1))
        offset += width_one
    return pieces

def attend(packed, key_count):
    queries = packed[:, :, :, 0]
    keys_all = packed[:, :, :, 1]
    values = packed[:, :, :, 2]
    score_scale = queries.shape[-1] ** (-0.5)
    scores = low_back(jnp.einsum('gqhe,gkhe->ghqk', queries, keys_all, precision=HIGH) * score_scale)
    key_valid = jnp.arange(queries.shape[1])[None, :] < key_count[:, None]
    scores = jnp.where(key_valid[:, None, None, :], scores, -1e+30)
    shifted = jnp.exp(scores - lax.optimization_barrier(jnp.max(scores, -1, keepdims=True)))
    soft_max = shifted / lax.optimization_barrier(jnp.sum(shifted, -1, keepdims=True))
    return jnp.einsum('ghqk,gkhe->gqhe', low(soft_max), values, precision=HIGH)

def block(values, matrices, gains, key_count, head_size, seq_len):
    w_qkv, w_out, w_up, w_down = matrices
    normed = low(norm_rows(values, gains[0], gains[1]))
    packed = low(low_back(matmul_hi(normed, w_qkv)))
    packed = packed.reshape(-1, seq_len, w_qkv.shape[1] // (3 * head_size), 3, head_size)
    attended = attend(packed, key_count)
    attended = low(low_back(attended.reshape(values.shape[0], -1)))
    values = values + low_back(matmul_hi(attended, w_out))
    normed = low(norm_rows(values, gains[2], gains[3]))
    hidden = low_back(matmul_hi(normed, w_up))
    return values + low_back(matmul_hi(low(jax.nn.gelu(hidden, approximate=False)), w_down))

def group_loss(weights, vectors_all, group):
    patch_bf, vis_index, keep_mask, counts = group
    pixels = patch_bf.astype(jnp.float32)
    pix_mean = lax.optimization_barrier(jnp.mean(pixels, -1, keepdims=True))
    pix_var = lax.optimization_barrier(jnp.mean(jnp.square(pixels - pix_mean), -1, keepdims=True))
    target = (pixels - pix_mean) * lax.rsqrt(pix_var + EPS_NORM)
    chosen = jnp.take_along_axis(pixels, vis_index[:, :, None], axis=1).reshape(-1, PIX)
    values = low_back(matmul_hi(chosen, weights[0])) + sincos(vis_index.reshape(-1).astype(jnp.float32), 0, D, D)
    values = block(values, weights[1:5], vectors_all[0:4], counts, DH, KEEP_MOST)
    encoded = low(norm_rows(values, vectors_all[4], vectors_all[5]))
    bridged = low_back(matmul_hi(encoded, weights[5])).reshape(-1, KEEP_MOST, DD)
    slot_of, seen = placement(vis_index, counts)
    placed = jnp.take_along_axis(bridged, slot_of[:, :, None], axis=1)
    grid = jnp.where(seen[:, :, None], placed, vectors_all[6]) + sincos(jnp.arange(NP).astype(jnp.float32), 0, DD, DD)[None]
    full_count = jnp.full(counts.shape, NP, jnp.int32)
    values = block(grid.reshape(-1, DD), weights[6:10], vectors_all[7:11], full_count, DHD, NP)
    decoded = low(norm_rows(values, vectors_all[11], vectors_all[12]))
    predicted = low_back(matmul_hi(decoded, weights[10])).reshape(-1, NP, PIX)
    loss_weight = jnp.where(keep_mask == 1, VISIBLE_WEIGHT, 1.0)
    return jnp.sum(loss_weight[:, :, None] * jnp.square(predicted - target))

def to_blocks(matrix, row_major, wide_owners, narrow_owners):
    rows_all, cols_all = matrix.shape
    if row_major:
        shaped = matrix.reshape(wide_owners, rows_all // wide_owners, narrow_owners, cols_all // narrow_owners // BLOCK, BLOCK)
        return shaped.transpose(0, 2, 3, 1, 4)
    shaped = matrix.reshape(narrow_owners, rows_all // narrow_owners // BLOCK, BLOCK, wide_owners, cols_all // wide_owners)
    return shaped.transpose(3, 0, 1, 4, 2)

def from_blocks(blocks, row_major, shape_all):
    if row_major:
        return blocks.transpose(0, 3, 1, 2, 4).reshape(shape_all)
    return blocks.transpose(1, 2, 4, 0, 3).reshape(shape_all)

def root_quarter(matrix):
    identity = jnp.eye(matrix.shape[-1], dtype=matrix.dtype)
    magnitude = jnp.sqrt(lax.optimization_barrier(jnp.sum(jnp.square(matrix), axis=(-2, -1), keepdims=True)))
    current = matrix / magnitude
    result = jnp.broadcast_to(identity, matrix.shape)
    for newton_step in range(NEWTON):
        factor = (5.0 * identity - current) * 0.25
        result = matmul_hi(result, factor)
        if newton_step + 1 < NEWTON:
            square = matmul_hi(factor, factor)
            current = matmul_hi(matmul_hi(square, square), current)
    return result * magnitude ** (-0.25)

def shampoo(gradients, weights, row_kinds, small_stat, large_stat, learn_rate, wide_owners, narrow_owners):
    pieces = [to_blocks(grad_one, kind_one, wide_owners, narrow_owners) for grad_one, kind_one in zip(gradients, row_kinds)]
    blocks = jnp.concatenate(pieces, axis=2)
    flipped = jnp.swapaxes(blocks, -1, -2)
    small_new = STAT_DECAY * small_stat + (1.0 - STAT_DECAY) * matmul_hi(blocks, flipped)
    large_new = STAT_DECAY * large_stat + (1.0 - STAT_DECAY) * matmul_hi(flipped, blocks)
    update = matmul_hi(matmul_hi(root_quarter(small_new), blocks), root_quarter(large_new))
    results, offset = ([], 0)
    for weight_one, kind_one, piece in zip(weights, row_kinds, pieces):
        width_one = piece.shape[2]
        results.append(weight_one - learn_rate * from_blocks(update[:, :, offset:offset + width_one], kind_one, weight_one.shape))
        offset += width_one
    return (results, small_new, large_new)

def adam(gradient, weight, first, second, step_count, enc_columns):
    moment_one = BETA_FIRST * first + (1.0 - BETA_FIRST) * gradient
    moment_two = BETA_SECOND * second + (1.0 - BETA_SECOND) * jnp.square(gradient)
    steps_done = step_count[0].astype(jnp.float32)
    corrected_one = moment_one / (1.0 - jnp.power(BETA_FIRST, steps_done))
    corrected_two = moment_two / (1.0 - jnp.power(BETA_SECOND, steps_done))
    column = jnp.arange(weight.shape[1])
    rates = jnp.where(column < enc_columns, LR_VECTOR * LAYER_DECAY, LR_VECTOR)
    return (weight - rates * corrected_one / (jnp.sqrt(corrected_two) + EPS_ADAM), moment_one, moment_two)

def reference(patches, vis_index, keep_mask, counts, step_count, w_embed, enc_qkv, enc_out, enc_up, enc_down, w_bridge, dec_qkv, dec_out, dec_up, dec_down, w_head, vectors, first_moment, second_moment, enc_small, enc_big, dec_small, dec_big):
    matrices = (w_embed, enc_qkv, enc_out, enc_up, enc_down, w_bridge, dec_qkv, dec_out, dec_up, dec_down, w_head)
    enc_cols = D // N_NARROW
    dec_cols = DD // N_NARROW
    divisor = jnp.sum(NP - (1.0 - VISIBLE_WEIGHT) * counts.astype(jnp.float32))
    groups = IMAGES // IMG_DEV
    batch = tuple((member.reshape((groups, IMG_DEV) + member.shape[1:]) for member in (patches, vis_index, keep_mask, counts)))

    def loss_of(params):
        weights = tuple((low(member) for member in params[:11]))
        vectors_all = unpack(params[11], enc_cols, dec_cols)

        def one_group(group):
            return group_loss(weights, vectors_all, group)
        total = jnp.sum(lax.map(jax.checkpoint(one_group), batch))
        return (total / divisor, total)
    loss_value, pull_back, loss_total = jax.vjp(loss_of, matrices + (vectors,), has_aux=True)
    gradients = pull_back(jnp.ones_like(loss_value))[0]
    vec_grad = gradients[11]
    enc_sq = sum((jnp.sum(jnp.square(member)) for member in gradients[0:6])) + jnp.sum(jnp.square(vec_grad[:, :6 * enc_cols]))
    dec_sq = sum((jnp.sum(jnp.square(member)) for member in gradients[6:11])) + jnp.sum(jnp.square(vec_grad[:, 6 * enc_cols:]))
    norms = jnp.sqrt(jnp.stack([enc_sq, dec_sq]))
    clip_factor = jnp.minimum(1.0, CLIP_NORM / jnp.sqrt(enc_sq + dec_sq))
    owners = N_DP * N_WIDE
    enc_new, enc_small_new, enc_big_new = shampoo([clip_factor * member for member in gradients[0:6]], matrices[0:6], ENC_KINDS, enc_small, enc_big, LR_MATRIX * LAYER_DECAY, owners, N_NARROW)
    dec_new, dec_small_new, dec_big_new = shampoo([clip_factor * member for member in gradients[6:11]], matrices[6:11], DEC_KINDS, dec_small, dec_big, LR_MATRIX, owners, N_NARROW)
    vectors_new, first_new, second_new = adam(clip_factor * vec_grad, vectors, first_moment, second_moment, step_count, 6 * enc_cols)
    return (enc_new[0], enc_new[1], enc_new[2], enc_new[3], enc_new[4], enc_new[5], dec_new[0], dec_new[1], dec_new[2], dec_new[3], dec_new[4], enc_small_new, enc_big_new, dec_small_new, dec_big_new, vectors_new, first_new, second_new, norms, loss_total, divisor)
```

```python
import functools

import jax
import jax.numpy as jnp
import numpy as np
from jax import lax
from jax.experimental import pallas as pl
from jax.experimental.pallas import tpu as pltpu
from jax.sharding import PartitionSpec as P

D = 768
DH = 64
DD = 512
DHD = 32
PIX = 768
NP = 196
BLOCK = 64
NEWTON = 3
KEEP_MOST = 98

HIGH = lax.Precision.HIGHEST
EPS_NORM = 1e-06
VISIBLE_WEIGHT = 0.1
STAT_DECAY = 0.5
LR_MATRIX = 0.2
LR_VECTOR = 0.2
LAYER_DECAY = 0.75
BETA_FIRST = 0.9
BETA_SECOND = 0.999
EPS_ADAM = 1e-08
CLIP_NORM = 1.0
ENC_KINDS = (True, True, False, True, False, True)
DEC_KINDS = (True, False, True, False, True)


MESHT = pl.DeviceIdType.MESH
FULL_CODE = 32767.0
FLOOR = 1e-30

def xors(n):
    return list(range(1, n))

def bits(n):
    r, b = [], 1
    while b < n:
        r.append(b)
        b *= 2
    return r

def extents(sizes):
    n_dp, n_wide, n_nar = sizes
    return {"n": n_nar, "h": n_dp // 2, "l": 2, "w": n_wide // 2}

def phases_of(order, ext):
    return [d for d in order if ext[d] > 1]

def messages(order, ext):
    out, left = [], 1
    for d in ext: left *= ext[d]
    for d in phases_of(order, ext):
        left //= ext[d]
        out.append((d, ext[d] - 1, left))
    return out

def plan(units, events, shapes, ext):
    flat = []
    for step in events:
        for u, p in step:
            if p <= len(phases_of(units[u][3], ext)) + 2: flat.append((u, p))
    at = {e: i for i, e in enumerate(flat)}
    heads = (ext["n"], ext["h"], ext["l"], ext["w"])
    wants = []
    for u, (m, lo, hi, order) in enumerate(units):
        a, c = shapes[m][0], hi - lo
        last = at[u, len(phases_of(order, ext)) + 2]
        wants.append((at[u, 0], last, ("acc", u), heads + (a, c), "f"))
        wants.append((at[u, 1], at[u, 2], ("stage", u), heads + (a, c), "f"))
        for p, (d, k, n) in enumerate(messages(order, ext)):
            wants.append((at[u, p + 2], last, ("q", u, p), (k, n, a, c), "q"))
    wants.sort(key=lambda w: w[0])
    bufs, where = [], {}
    for start, end, name, shape, kind in wants:
        for i, b in enumerate(bufs):
            if b[0] == (shape, kind) and b[1] < start:
                b[1] = end
                where[name] = i
                break
        else:
            bufs.append([(shape, kind), end])
            where[name] = len(bufs) - 1
    return [b[0] for b in bufs], where

def reduce_kernel(sizes, units, events, count, planned, is_enc, *refs):
    n_dp, n_wide, n_nar = sizes
    ext = extents(sizes)
    slots = ext["n"] * ext["h"] * ext["l"] * ext["w"]
    it = iter(refs)
    take = lambda k: [next(it) for _ in range(k)]
    grads = take(count); vec = next(it)
    outs = take(count); vec_out = next(it); sq_out = next(it); land = take(count)
    nu = len(units)
    kinds, where = planned
    pool = [take(1)[0] if kind == "f" else tuple(take(2)) for _, kind in kinds]
    acc = [pool[where["acc", u]] for u in range(nu)]
    stage_buf = [pool[where["stage", u]] for u in range(nu)]
    recv_q, recv_s = [], []
    for u in range(nu):
        k = len(messages(units[u][3], ext))
        recv_q.append(take(k)); recv_s.append(take(k))
    last_use = {}
    vec_land = next(it); sq_land = next(it)
    core_send, core_recv, local_sem, stage_sem, q_send, q_recv, s_send, s_recv, v_send, v_recv, t_send, t_recv = take(12)

    dp = lax.axis_index("dp"); wi = lax.axis_index("wide"); na = lax.axis_index("narrow")
    own = {"n": na, "h": dp // 2, "l": dp % 2, "w": wi // 2}
    core = wi % 2
    def peer(dim, k):
        if dim == "n": return {"narrow": na ^ k}
        if dim == "h": return {"dp": dp ^ (2 * k)}
        if dim == "l": return {"dp": dp ^ k}
        if dim == "w": return {"wide": wi ^ (2 * k)}
        return {"wide": wi ^ 1}
    partners = [peer(d, k) for d in "nhlw" for k in xors(ext[d])] + [peer("c", 1)]
    barrier = pltpu.get_barrier_semaphore()
    for p in partners:
        pl.semaphore_signal(barrier, inc=1, device_id=p, device_id_type=MESHT)
    pl.semaphore_wait(barrier, len(partners))

    def remote(src, dst, ss, rs, dev):
        return pltpu.make_async_remote_copy(src_ref=src, dst_ref=dst, send_sem=ss, recv_sem=rs, device_id=dev, device_id_type=MESHT)
    pending = []

    hops = [("c", 1)] + [(d, b) for d in "lhwn" for b in bits(ext[d])]
    def vec_hop(i, value_ref, land_ref, ss, rs):
        d, k = hops[i]
        c = remote(value_ref, land_ref.at[i], ss.at[i], rs.at[i], peer(d, k))
        c.start()
        return c
    vec_out[...] = vec[...]
    def vec_start(i):
        vec_flight[i] = vec_hop(i, vec_out, vec_land, v_send, v_recv)
    def vec_end(i):
        vec_flight[i].wait()
        vec_out[...] = vec_out[...] + vec_land[i]
    vec_flight = {}

    def cols(u):
        m, lo, hi, order = units[u]
        return m, lo, hi
    def shape(u):
        m, lo, hi = cols(u)
        return outs[m].shape[0], hi - lo
    def whole(u):
        m, lo, hi = cols(u)
        return (lo, hi) == (0, outs[m].shape[1])
    def view(u, ref, head):
        m, lo, hi = cols(u)
        return ref.at[head] if whole(u) else ref.at[head + (slice(None),) * (6 - len(head)) + (slice(lo, hi),)]
    def acc_view(u):
        a, c = shape(u)
        return acc[u]
    def slab(u, idx):
        a, c = shape(u)
        return acc[u].at[idx["n"], idx["h"], idx["l"], idx["w"]]
    def stage_view(u):
        a, c = shape(u)
        return stage_buf[u]
    flight = {}
    def split(s, dims):
        idx = {}
        for d in reversed(dims):
            if ext[d] == 1:
                idx[d] = 0
            else:
                idx[d] = s % ext[d]
                s = s // ext[d]
        return idx
    sums = [jnp.zeros((1, 1), jnp.float32), jnp.zeros((1, 1), jnp.float32)]

    def code_and_send(u, p):
        ph = phases_of(units[u][3], ext)
        msgs = messages(units[u][3], ext)
        d, peers, slabs = msgs[p]
        gone = ph[:p]
        free = [x for x in "nhlw" if x != d and x not in gone]
        sends = []
        b = where["q", u, p]
        for c in last_use.pop(b, []): c.wait_send()
        out_q, out_s = pool[b]
        for k in range(1, peers + 1):
            def body(s, _):
                idx = split(s, free)
                for x in gone: idx[x] = own[x]
                idx[d] = own[d] ^ k
                x = slab(u, idx)[...]
                top = jnp.maximum(jnp.max(jnp.abs(x), axis=0, keepdims=True), FLOOR)
                out_q[k - 1, s] = jnp.round(x * (FULL_CODE / top)).astype(jnp.int32).astype(jnp.int16)
                out_s[k - 1, s] = top * (1.0 / FULL_CODE)
                return 0
            lax.fori_loop(0, slabs, body, 0)
            a_ = remote(out_q.at[k - 1], recv_q[u][p].at[k - 1], q_send.at[u, p, k - 1], q_recv.at[u, p, k - 1], peer(d, k))
            b_ = remote(out_s.at[k - 1], recv_s[u][p].at[k - 1], s_send.at[u, p, k - 1], s_recv.at[u, p, k - 1], peer(d, k))
            a_.start(); b_.start()
            sends.append((a_, b_))
        last_use[b] = [c for pair in sends for c in pair]
        flight[u, p] = sends
    def take_in(u, p):
        ph = phases_of(units[u][3], ext)
        d, peers, slabs = messages(units[u][3], ext)[p]
        gone = ph[:p + 1]
        free = [x for x in "nhlw" if x not in gone]
        for a, b in flight[u, p]:
            a.wait_recv(); b.wait_recv()
        def body(s, _):
            idx = split(s, free)
            for x in gone: idx[x] = own[x]
            ref = slab(u, idx)
            v = ref[...]
            for k in range(peers):
                v = v + recv_q[u][p][k, s].astype(jnp.int32).astype(jnp.float32) * recv_s[u][p][k, s]
            ref[...] = v
            return 0
        lax.fori_loop(0, slabs, body, 0)

    def stage(u, p):
        m, lo, hi = cols(u)
        n_ph = len(phases_of(units[u][3], ext))
        if p == 0:
            full = (slice(None),) * 4
            c = remote(view(u, grads[m], full + (1 - core,)), land_view(u), core_send.at[u], core_recv.at[u], peer("c", 1))
            c.start()
            flight[u, "core"] = c
            pending.append(c)
            l = pltpu.make_async_copy(view(u, grads[m], full + (core,)), acc_view(u), local_sem.at[u])
            l.start()
            flight[u, "local"] = l
        elif p == 1:
            flight[u, "core"].wait_recv()
            c = pltpu.make_async_copy(land_view(u), stage_view(u), stage_sem.at[u])
            c.start()
            flight[u, "stage"] = c
        elif p == 2:
            flight[u, "local"].wait()
            flight[u, "stage"].wait()
            a, c = shape(u)
            def body(s, _):
                idx = split(s, list("nhlw"))
                ref = slab(u, idx)
                ref[...] = ref[...] + stage_buf[u][idx["n"], idx["h"], idx["l"], idx["w"]]
                return 0
            lax.fori_loop(0, slots, body, 0)
            code_and_send(u, 0)
        else:
            take_in(u, p - 3)
            if p - 2 < n_ph:
                code_and_send(u, p - 2)
            else:
                x = slab(u, own)[...]
                outs[m][:, pl.ds(lo, hi - lo)] = x
                w = 0 if is_enc[m] else 1
                sums[w] = sums[w] + jnp.sum(x * x, keepdims=True)
    def land_view(u):
        m, lo, hi = cols(u)
        return land[m] if whole(u) else land[m].at[:, :, :, :, :, slice(lo, hi)]

    hop = 0
    for step, group in enumerate(events):
        if hop < len(hops):
            if hop: vec_end(hop - 1)
            vec_start(hop)
            hop += 1
        for u, p in group:
            n_ph = len(phases_of(units[u][3], ext))
            if p <= n_ph + 2: stage(u, p)
    while hop < len(hops):
        vec_end(hop - 1); vec_start(hop); hop += 1
    vec_end(len(hops) - 1)
    row = lax.broadcasted_iota(jnp.int32, (8, 128), 0)
    sq_out[...] = jnp.where(row == 0, sums[0], jnp.where(row == 1, sums[1], 0.0))
    for i in range(len(hops)):
        c = vec_hop(i, sq_out, sq_land, t_send, t_recv)
        c.wait()
        sq_out[...] = sq_out[...] + sq_land[i]
    for c in pending + [c for cs in last_use.values() for c in cs]:
        c.wait_send()

def reduce_scatter(grads, vec, sizes, units, events, is_enc, cid=1):
    count = len(grads)
    ext = extents(sizes)
    heads = (ext["n"], ext["h"], ext["l"], ext["w"])
    planned = plan(units, events, [g.shape[-2:] for g in grads], ext)
    def coded(k, n, a, c):
        return [pltpu.VMEM((k, n, a, c), jnp.int16), pltpu.VMEM((k, n, 1, c), jnp.float32)]
    scratch = []
    for shape, kind in planned[0]:
        scratch += [pltpu.VMEM(shape, jnp.float32)] if kind == "f" else coded(*shape)
    for m, lo, hi, order in units:
        a = grads[m].shape[-2]
        ms = [coded(k, n, a, hi - lo) for d, k, n in messages(order, ext)]
        scratch += [x[0] for x in ms] + [x[1] for x in ms]
    hops = 1 + sum(len(bits(ext[d])) for d in ext)
    scratch += [pltpu.VMEM((hops,) + vec.shape, jnp.float32), pltpu.VMEM((hops, 8, 128), jnp.float32)]
    nu = len(units)
    kmax = max(ext.values())
    D = pltpu.SemaphoreType.DMA
    scratch += [D((nu,))] * 4 + [D((nu, 4, kmax))] * 4 + [D((hops,))] * 4
    vm = pl.BlockSpec(memory_space=pltpu.VMEM); an = pl.BlockSpec(memory_space=pl.ANY)
    f32 = jnp.float32
    res = pl.pallas_call(
        functools.partial(reduce_kernel, sizes, units, events, count, planned, is_enc),
        out_shape=[jax.ShapeDtypeStruct(g.shape[-2:], f32) for g in grads]
        + [jax.ShapeDtypeStruct(vec.shape, f32), jax.ShapeDtypeStruct((8, 128), f32)]
        + [jax.ShapeDtypeStruct(heads + g.shape[-2:], f32) for g in grads],
        in_specs=[an] * count + [vm],
        out_specs=[vm] * (count + 2) + [an] * count,
        scratch_shapes=scratch,
        compiler_params=pltpu.CompilerParams(collective_id=cid, has_side_effects=True, vmem_limit_bytes=62 << 20),
    )(*grads, vec)
    return res[:count], res[count], res[count + 1]


def gather_kernel(sizes, units, events, count, *refs):
    n_dp, n_wide, n_nar = sizes
    shards = refs[:count]
    vec, weight = refs[count:count + 2]
    outs = refs[count + 2:2 * count + 2]
    vec_all, weight_sum = refs[2 * count + 2:2 * count + 4]
    weight_land, send_sem, recv_sem, loc_sem, vec_send, vec_recv, sum_send, sum_recv = refs[2 * count + 4:]
    dp = lax.axis_index("dp"); wi = lax.axis_index("wide"); na = lax.axis_index("narrow")
    d_low = 2
    d_high = n_dp // 2
    w_high = n_wide // 2
    own = {"n": na, "h": dp // 2, "l": dp % 2, "w": wi // 2}
    core = wi % 2
    def peer(dim, k):
        if dim == "n": return {"narrow": na ^ k}
        if dim == "h": return {"dp": dp ^ (2 * k)}
        if dim == "l": return {"dp": dp ^ k}
        if dim == "w": return {"wide": wi ^ (2 * k)}
        return {"wide": wi ^ 1}
    extent = {"n": n_nar, "h": d_high, "l": d_low, "w": w_high}
    partners = [peer(d, k) for d in "nhlw" for k in xors(extent[d])] + [peer("c", 1)]
    barrier = pltpu.get_barrier_semaphore()
    for p in partners:
        pl.semaphore_signal(barrier, inc=1, device_id=p, device_id_type=MESHT)
    pl.semaphore_wait(barrier, len(partners))
    pending = []
    sib_recv = []
    vec_flight = []
    for k in xors(n_nar):
        c = pltpu.make_async_remote_copy(src_ref=vec, dst_ref=vec_all.at[na], send_sem=vec_send.at[k - 1], recv_sem=vec_recv.at[k - 1], device_id=peer("n", k), device_id_type=MESHT)
        c.start()
        vec_flight.append(c)
    vec_all[na] = vec[...]
    weight_sum[...] = weight[...]
    hops = [("c", 1)] + [(d, b) for d in "lhw" for b in bits(extent[d])]
    slot_of = [0] * len(units)
    def region(u, full, at, which_core):
        m, lo, hi, order = units[u]
        idx = []
        for d in "nhlw":
            if d in full: idx.append(slice(None))
            elif at and d == at[0]: idx.append(own[d] ^ at[1])
            else: idx.append(own[d])
        r = outs[m].at[tuple(idx) + (which_core,)]
        if (lo, hi) != (0, shards[m].shape[1]):
            r = outs[m].at[tuple(idx) + (which_core, slice(None), slice(lo, hi))]
        return r
    def remote(u, src, dst, dev, recv_view):
        s = slot_of[u]; slot_of[u] += 1
        c = pltpu.make_async_remote_copy(src_ref=src, dst_ref=dst, send_sem=send_sem.at[u, s], recv_sem=recv_sem.at[u, s], device_id=dev, device_id_type=MESHT)
        c.start()
        pending.append(c)
        return pltpu.make_async_remote_copy(src_ref=recv_view, dst_ref=recv_view, send_sem=send_sem.at[u, s], recv_sem=recv_sem.at[u, s], device_id=dev, device_id_type=MESHT)
    def shard(u):
        m, lo, hi, order = units[u]
        return shards[m] if (lo, hi) == (0, shards[m].shape[1]) else shards[m].at[:, slice(lo, hi)]
    state = {}
    def phases(u):
        return [d for d in units[u][3] if extent[d] > 1]
    def stage(u, p):
        ph = phases(u)
        if p == 0:
            lc = pltpu.make_async_copy(shard(u), region(u, (), None, core), loc_sem.at[u]); lc.start()
            sib_recv.append(remote(u, shard(u), region(u, (), None, core), peer("c", 1), region(u, (), None, 1 - core)))
            src = shard(u)
            state[u] = []
            state[u, "loc"] = lc
        else:
            done = ph[:p - 1]
            for k, w in state[u]:
                w.wait_recv()
            for k, w in state[u]:
                here = region(u, done, (ph[p - 1], k), core)
                there = region(u, done, (ph[p - 1], k), 1 - core)
                state[u, k] = (here, there)
            if p == 1: state[u, "loc"].wait()
            src = None
        old = state[u]
        state[u] = []
        if p < len(ph):
            full = ph[:p]
            for k in xors(extent[ph[p]]):
                mine = region(u, full, None, core) if src is None else src
                w = remote(u, mine, region(u, full, None, core), peer(ph[p], k), region(u, full, (ph[p], k), core))
                state[u].append((k, w))
        if p > 0:
            for k, _ in old:
                here, there = state[u, k]
                sib_recv.append(remote(u, here, here, peer("c", 1), there))
    for step in events:
        for u, p in step:
            if p <= len(phases(u)): stage(u, p)
    for i, (d, k) in enumerate(hops):
        c = pltpu.make_async_remote_copy(src_ref=weight_sum, dst_ref=weight_land.at[i], send_sem=sum_send.at[i], recv_sem=sum_recv.at[i], device_id=peer(d, k), device_id_type=MESHT)
        c.start()
        c.wait()
        weight_sum[...] = weight_sum[...] + weight_land[i]
    for c in vec_flight:
        c.wait()
    for c in pending:
        c.wait_send()
    for w in sib_recv:
        w.wait_recv()


def gather(shards, vec, weight, sizes, units, events, cid=0):
    n_dp, n_wide, n_nar = sizes
    count = len(shards)
    ext = extents(sizes)
    slots = 2 * sum(ext.values())
    nu = len(units)
    hops = 1 + sum(len(bits(ext[d])) for d in "lhw")
    DMA = pltpu.SemaphoreType.DMA
    an = pl.BlockSpec(memory_space=pl.ANY)
    vm = pl.BlockSpec(memory_space=pltpu.VMEM)
    heads = (ext["n"], ext["h"], ext["l"], ext["w"], 2)
    res = pl.pallas_call(
        functools.partial(gather_kernel, sizes, units, events, count),
        out_shape=[jax.ShapeDtypeStruct(heads + s.shape, s.dtype) for s in shards]
        + [jax.ShapeDtypeStruct((n_nar,) + vec.shape, vec.dtype), jax.ShapeDtypeStruct(weight.shape, weight.dtype)],
        in_specs=[an] * count + [vm, vm],
        out_specs=[an] * count + [vm, vm],
        scratch_shapes=[pltpu.VMEM((hops,) + weight.shape, jnp.float32), DMA((nu, slots)), DMA((nu, slots)), DMA((nu,)), DMA((n_nar,)), DMA((n_nar,)), DMA((hops,)), DMA((hops,))],
        compiler_params=pltpu.CompilerParams(collective_id=cid, has_side_effects=True),
    )(*shards, vec, weight)
    return res[:count], res[count], res[count + 1]


def gather_plan(ext, shapes):
    cols = [s[1] for s in shapes]
    if ext["w"] > 1:
        units = [(m, 0, c, "nlhw") for m, c in enumerate(cols)]
        return units, [[(u, p)] for u in range(len(units)) for p in range(5)]
    A, B, XA, XB = "nlhw", "nhlw", "lhnw", "hlnw"
    half = cols[3] // 2
    groups = [
        [(0, 0, cols[0], A), (2, 0, cols[2], B)],
        [(1, 0, 256, A), (1, 256, cols[1], B)],
        [(3, 0, half, A), (4, 0, half, B)],
        [(3, half, cols[3], A), (4, half, cols[4], B)],
        [(8, 0, cols[8], A), (9, 0, cols[9], B)],
        [(5, 0, cols[5], A)],
    ]
    extra = [(6, 0, cols[6], XA), (10, 0, cols[10], XB), (7, 0, cols[7], XB)]
    units, ids = [], []
    for g in groups:
        ids.append(list(range(len(units), len(units) + len(g))))
        units += g
    more = list(range(len(units), len(units) + len(extra)))
    units += extra
    events = []
    for t in range(len(groups) + 3):
        step = []
        for p in range(4):
            if 0 <= t - p < len(groups):
                step += [(u, p) for u in ids[t - p]]
        for p, when in enumerate((0, 1, 5, 8)):
            if t == when:
                step += [(u, p) for u in more]
        events.append(step)
    return units, events


def reduce_plan(ext, shapes):
    cols = [s[1] for s in shapes]
    if ext["w"] > 1:
        units = [(m, lo, min(lo + 256, c), "wlhn") for m, c in enumerate(cols) for lo in range(0, c, 256)]
        return units, [[(u, p)] for u in range(len(units)) for p in range(7)]
    A, B, XA, XB = "lhwn", "hlwn", "nlhw", "nhlw"
    h2, h7 = cols[2] // 2, cols[7] // 2
    groups = [
        [(7, 0, h7, A), (8, 0, h7, B)],
        [(7, h7, cols[7], A), (8, h7, cols[8], B)],
        [(2, 0, h2, A), (3, 0, h2, B)],
        [(2, h2, cols[2], A), (3, h2, cols[3], B)],
        [(1, 0, 256, A), (1, 256, cols[1], B)],
        [(0, 0, 256, A), (0, 256, cols[0], B)],
        [(4, 0, cols[4], A)],
    ]
    extra = [(5, 0, cols[5], XA), (9, 0, cols[9], XB), (6, 0, cols[6], XB)]
    units, ids = [], []
    for g in groups:
        ids.append(list(range(len(units), len(units) + len(g))))
        units += g
    more = list(range(len(units), len(units) + len(extra)))
    units += extra
    of = lambda t: ids[t] if 0 <= t < len(ids) else []
    events = []
    for t in range(-2, len(groups) + 4):
        step = [(u, 0) for u in of(t + 2)]
        now, nxt = of(t), of(t + 1)
        for i in range(max(len(now), len(nxt))):
            if i < len(now):
                step.append((now[i], 2))
            if i < len(nxt):
                step.append((nxt[i], 1))
        for p in (3, 4, 5):
            step += [(u, p) for u in of(t - (p - 2))]
        for p, when in enumerate((-2, -1, 0, 3, 4, 5)):
            if t == when:
                step += [(u, p) for u in more]
        events.append(step)
    return units, events


def matmul_hi(left, right):
    return jnp.matmul(left, right, precision=HIGH)


def dense(tokens, weight):
    return jnp.einsum("td,ndc->tnc", tokens, weight, preferred_element_type=jnp.float32)


def dense_back(hidden, weight):
    return jnp.einsum("tnc,ndc->td", hidden, weight, preferred_element_type=jnp.float32)


def weight_grad(tokens, hidden):
    return jnp.einsum("td,tnc->ndc", tokens, hidden, preferred_element_type=jnp.float32)


def gelu_exact(values):
    return jax.nn.gelu(values, approximate=False)


def sincos_table(rows, width):
    column = np.arange(width)
    freq = np.power(np.float32(10000.0), (-(2 * (column // 2)).astype(np.float32) / np.float32(width)).astype(np.float32))
    angle = (np.arange(rows, dtype=np.float32)[:, None] * freq[None, :]).astype(np.float32)
    return np.where(column % 2 == 0, np.sin(angle), np.cos(angle)).astype(np.float32)


def norm_forward(residual, gain_vec, bias_vec):
    row_mean = jnp.mean(residual, -1, keepdims=True)
    row_var = jnp.mean(jnp.square(residual - row_mean), -1, keepdims=True)
    inv_std = lax.rsqrt(row_var + EPS_NORM)
    centred = (residual - row_mean) * inv_std
    return (centred * gain_vec + bias_vec).astype(jnp.bfloat16), centred, inv_std


def norm_backward(norm_grad, centred, inv_std, gain_vec):
    scaled = norm_grad * gain_vec
    residual_grad = inv_std * (
        scaled
        - jnp.mean(scaled, -1, keepdims=True)
        - centred * jnp.mean(scaled * centred, -1, keepdims=True)
    )
    return residual_grad, jnp.sum(norm_grad * centred, 0), jnp.sum(norm_grad, 0)


def attention_scores(packed, key_count, head_size):
    queries = packed[:, :, :, 0]
    keys_all = packed[:, :, :, 1]
    scores = jnp.einsum(
        "bqhe,bkhe->bhqk", queries, keys_all, preferred_element_type=jnp.float32
    ) * head_size ** (-0.5)
    key_valid = jnp.arange(packed.shape[1])[None, :] < key_count[:, None]
    return jnp.where(key_valid[:, None, None, :], scores, -1e30)


def block_forward(residual, matrices, gains, key_count, head_size):
    w_qkv, w_out, w_up, w_down = matrices
    images = key_count.shape[0]
    tokens = residual.shape[0]
    normed_one, centred_one, inv_one = norm_forward(residual, gains[0], gains[1])
    packed = dense(normed_one, w_qkv).astype(jnp.bfloat16)
    packed = packed.reshape(images, tokens // images, -1, 3, head_size)
    scores = attention_scores(packed, key_count, head_size)
    shifted = jnp.exp(scores - jnp.max(scores, -1, keepdims=True))
    soft_max = shifted / jnp.sum(shifted, -1, keepdims=True)
    attended = jnp.einsum(
        "bhqk,bkhe->bqhe",
        soft_max.astype(jnp.bfloat16),
        packed[:, :, :, 2],
        preferred_element_type=jnp.float32,
    )
    attended = attended.astype(jnp.bfloat16).reshape(tokens, w_out.shape[0], -1)
    residual = residual + dense_back(attended, w_out)
    normed_two, centred_two, inv_two = norm_forward(residual, gains[2], gains[3])
    hidden = dense(normed_two, w_up)
    activated = gelu_exact(hidden).astype(jnp.bfloat16)
    residual = residual + dense_back(activated, w_down)
    kept = (normed_one, centred_one, inv_one, packed, soft_max, attended, normed_two, centred_two, inv_two, hidden, activated)
    return residual, kept


def block_backward(residual_grad, matrices, gains, kept, head_size):
    w_qkv, w_out, w_up, w_down = matrices
    normed_one, centred_one, inv_one, packed, soft_max, attended, normed_two, centred_two, inv_two, hidden, activated = kept
    tokens = residual_grad.shape[0]
    out_grad = residual_grad.astype(jnp.bfloat16)
    down_grad = weight_grad(out_grad, activated)
    act_grad = dense(out_grad, w_down)
    hidden_grad = jax.vjp(gelu_exact, hidden)[1](act_grad)[0].astype(jnp.bfloat16)
    up_grad = weight_grad(normed_two, hidden_grad)
    mlp_grad, gain_two, bias_two = norm_backward(dense_back(hidden_grad, w_up), centred_two, inv_two, gains[2])
    residual_grad = residual_grad + mlp_grad
    out_grad = residual_grad.astype(jnp.bfloat16)
    proj_grad = weight_grad(out_grad, attended)
    attn_grad = dense(out_grad, w_out).astype(jnp.bfloat16)
    attn_grad = attn_grad.reshape(packed.shape[0], packed.shape[1], packed.shape[2], head_size)
    queries = packed[:, :, :, 0]
    keys_all = packed[:, :, :, 1]
    values = packed[:, :, :, 2]
    f32 = dict(preferred_element_type=jnp.float32)
    prob_grad = jnp.einsum("bqhe,bkhe->bhqk", attn_grad, values, **f32)
    value_grad = jnp.einsum("bhqk,bqhe->bkhe", soft_max.astype(jnp.bfloat16), attn_grad, **f32)
    score_grad = soft_max * (prob_grad - jnp.sum(prob_grad * soft_max, -1, keepdims=True))
    score_grad = score_grad.astype(jnp.bfloat16)
    scale = head_size ** (-0.5)
    query_grad = jnp.einsum("bhqk,bkhe->bqhe", score_grad, keys_all, **f32) * scale
    key_grad = jnp.einsum("bhqk,bqhe->bkhe", score_grad, queries, **f32) * scale
    packed_grad = jnp.stack([query_grad, key_grad, value_grad], axis=3).astype(jnp.bfloat16)
    packed_grad = packed_grad.reshape(tokens, w_qkv.shape[0], -1)
    qkv_grad = weight_grad(normed_one, packed_grad)
    attn_in_grad, gain_one, bias_one = norm_backward(dense_back(packed_grad, w_qkv), centred_one, inv_one, gains[0])
    return (
        residual_grad + attn_in_grad,
        (qkv_grad, proj_grad, up_grad, down_grad),
        (gain_one, bias_one, gain_two, bias_two),
    )


def root_quarter(matrix):
    identity = jnp.eye(matrix.shape[-1], dtype=matrix.dtype)
    magnitude = jnp.sqrt(jnp.sum(jnp.square(matrix), axis=(-2, -1), keepdims=True))
    current = matrix / magnitude
    result = None
    for newton_step in range(NEWTON):
        factor = (5.0 * identity - current) * 0.25
        result = factor if result is None else matmul_hi(result, factor)
        if newton_step + 1 < NEWTON:
            square = matmul_hi(factor, factor)
            current = matmul_hi(matmul_hi(square, square), current)
    return result * magnitude ** (-0.25)


def shampoo(gradients, weights, kinds, small_stat, large_stat, learn_rate):
    pieces = [g.reshape(g.shape[0], -1, BLOCK).transpose(1, 0, 2) for g in gradients]
    blocks = jnp.concatenate(pieces, axis=0)[None, None]
    flipped = jnp.swapaxes(blocks, -1, -2)
    small_new = STAT_DECAY * small_stat + (1.0 - STAT_DECAY) * matmul_hi(blocks, flipped)
    large_new = STAT_DECAY * large_stat + (1.0 - STAT_DECAY) * matmul_hi(flipped, blocks)
    update = matmul_hi(matmul_hi(root_quarter(small_new), blocks), root_quarter(large_new))[0, 0]
    results, offset = [], 0
    for weight, kind, piece in zip(weights, kinds, pieces):
        step = update[offset : offset + piece.shape[0]]
        offset += piece.shape[0]
        if kind:
            step = step.transpose(1, 0, 2).reshape(weight.shape)
        else:
            step = step.transpose(0, 2, 1).reshape(weight.shape)
        results.append(weight - learn_rate * step)
    return results, small_new, large_new


def adam(gradient, weight, first, second, step_count, enc_columns):
    moment_one = BETA_FIRST * first + (1.0 - BETA_FIRST) * gradient
    moment_two = BETA_SECOND * second + (1.0 - BETA_SECOND) * jnp.square(gradient)
    steps_done = step_count[0].astype(jnp.float32)
    corrected_one = moment_one / (1.0 - jnp.power(BETA_FIRST, steps_done))
    corrected_two = moment_two / (1.0 - jnp.power(BETA_SECOND, steps_done))
    column = jnp.arange(weight.shape[1])
    rates = jnp.where(column < enc_columns, LR_VECTOR * LAYER_DECAY, LR_VECTOR)
    return (
        weight - rates * corrected_one / (jnp.sqrt(corrected_two) + EPS_ADAM),
        moment_one,
        moment_two,
    )


def unpack(packed, enc_cols, dec_cols):
    pieces, offset = [], 0
    for width in [enc_cols] * 6 + [dec_cols] * 7:
        pieces.append(packed[:, offset : offset + width].reshape(-1))
        offset += width
    return pieces


def pad_cols(matrix):
    short = -matrix.shape[-1] % 128
    return jnp.pad(matrix, ((0, 0), (0, 0), (0, short))) if short else matrix


def per_device(
    sizes,
    patches, vis_index, keep_mask, counts, step_count,
    w_embed, enc_qkv, enc_out, enc_up, enc_down, w_bridge,
    dec_qkv, dec_out, dec_up, dec_down, w_head,
    vectors, first_moment, second_moment, enc_small, enc_big, dec_small, dec_big,
):
    n_dp, n_wide, n_nar = sizes
    ext = extents(sizes)
    narrow_at = lax.axis_index("narrow")
    masters = (w_embed, enc_qkv, enc_out, enc_up, enc_down, w_bridge, dec_qkv, dec_out, dec_up, dec_down, w_head)
    kinds = ENC_KINDS + DEC_KINDS
    shards = [(w if kind else w.T).astype(jnp.bfloat16) for w, kind in zip(masters, kinds)]
    weight_part = jnp.sum(NP - (1.0 - VISIBLE_WEIGHT) * counts.astype(jnp.float32))
    units, events = gather_plan(ext, [s.shape for s in shards])
    gathered, vec_all, weight_sum = gather(
        shards, vectors.reshape(-1, 128), jnp.full((8, 128), weight_part, jnp.float32), sizes, units, events
    )
    divisor = weight_sum[0, 0]
    full = [g.reshape(n_nar, -1, g.shape[-1]) for g in gathered]
    f_embed, f_qkv, f_out, f_up, f_down, f_bridge, d_qkv, d_out, d_up, d_down, f_head = full
    enc_mats = (f_qkv, f_out, f_up, f_down)
    dec_mats = (d_qkv, d_out, d_up, d_down)
    enc_cols, dec_cols = w_embed.shape[1], w_bridge.shape[1]
    vecs = unpack(vec_all.reshape(n_nar, -1), enc_cols, dec_cols)

    all_images = counts.shape[0]
    per = -(-all_images // n_nar)
    first = narrow_at * per
    start = jnp.minimum(first, all_images - per)
    live = (start + jnp.arange(per) >= first).astype(jnp.float32)
    pick = lambda x: lax.dynamic_slice_in_dim(x, start, per, 0)
    patches, vis_index, keep_mask, counts = map(pick, (patches, vis_index, keep_mask, counts))

    at_patch = vis_index[:, :, None] == jnp.arange(NP)[None, None, :]
    slot_live = jnp.arange(KEEP_MOST)[None, :] < counts[:, None]
    hit = (at_patch & slot_live[:, :, None]).astype(jnp.float32)
    seen = jnp.sum(hit, axis=1)
    chosen = jnp.einsum("isp,ipx->isx", at_patch.astype(jnp.bfloat16), patches, preferred_element_type=jnp.float32)
    chosen = chosen.astype(jnp.bfloat16).reshape(-1, PIX)
    table = jnp.asarray(sincos_table(NP, D))
    place = jnp.matmul(at_patch.astype(jnp.float32), table, precision=HIGH).reshape(-1, D)
    residual = dense(chosen, f_embed).reshape(-1, D) + place
    residual, enc_kept = block_forward(residual, enc_mats, vecs[0:4], counts, DH)
    encoded, enc_hat, enc_inv = norm_forward(residual, vecs[4], vecs[5])
    bridged = dense(encoded, f_bridge).reshape(per, KEEP_MOST, DD)
    placed = jnp.einsum("isp,isd->ipd", hit, bridged, precision=HIGH)
    grid = jnp.where(seen[:, :, None] > 0, placed, vecs[6]) + jnp.asarray(sincos_table(NP, DD))[None]
    full_count = jnp.full((per,), NP, jnp.int32)
    residual, dec_kept = block_forward(grid.reshape(-1, DD), dec_mats, vecs[7:11], full_count, DHD)
    decoded, dec_hat, dec_inv = norm_forward(residual, vecs[11], vecs[12])
    predicted = dense(decoded, f_head).reshape(per, NP, PIX)
    pixels = patches.astype(jnp.float32)
    pix_mean = jnp.mean(pixels, -1, keepdims=True)
    pix_var = jnp.mean(jnp.square(pixels - pix_mean), -1, keepdims=True)
    target = (pixels - pix_mean) * lax.rsqrt(pix_var + EPS_NORM)
    loss_weight = (jnp.where(keep_mask == 1, VISIBLE_WEIGHT, 1.0) * live[:, None])[:, :, None]
    error = predicted - target
    loss_part = jnp.sum(loss_weight * error * error)
    pred_grad = (2.0 * loss_weight * error / divisor).astype(jnp.bfloat16).reshape(-1, n_nar, w_head.shape[1])
    head_grad = weight_grad(decoded, pred_grad)
    residual_grad, dec_final_gain, dec_final_bias = norm_backward(dense_back(pred_grad, f_head), dec_hat, dec_inv, vecs[11])
    residual_grad, dec_grads, dec_vec = block_backward(residual_grad, dec_mats, vecs[7:11], dec_kept, DHD)
    grid_grad = residual_grad.reshape(per, NP, DD)
    mask_grad = jnp.sum(jnp.where(seen[:, :, None] > 0, 0.0, grid_grad), axis=(0, 1))
    bridge_in = jnp.einsum("isp,ipd->isd", hit, grid_grad, precision=HIGH).astype(jnp.bfloat16)
    bridge_in = bridge_in.reshape(-1, n_nar, dec_cols)
    bridge_grad = weight_grad(encoded, bridge_in)
    residual_grad, enc_final_gain, enc_final_bias = norm_backward(dense_back(bridge_in, f_bridge), enc_hat, enc_inv, vecs[4])
    residual_grad, enc_grads, enc_vec = block_backward(residual_grad, enc_mats, vecs[0:4], enc_kept, DH)
    embed_grad = weight_grad(chosen, residual_grad.astype(jnp.bfloat16).reshape(-1, n_nar, enc_cols))
    vec_local = jnp.concatenate(
        [
            v.reshape(n_nar, -1)
            for v in (*enc_vec, enc_final_gain, enc_final_bias, mask_grad, *dec_vec, dec_final_gain, dec_final_bias)
        ],
        axis=1,
    )
    vec_rows = jnp.concatenate([vec_local.reshape(-1, 128), jnp.full((8, 128), loss_part, jnp.float32)])
    parts = [
        jnp.concatenate([embed_grad, enc_grads[1]], axis=2),
        enc_grads[0], enc_grads[2], enc_grads[3], bridge_grad,
        dec_grads[0], dec_grads[1], dec_grads[2], dec_grads[3], head_grad,
    ]
    heads = (ext["n"], ext["h"], ext["l"], ext["w"], 2)
    blocked = []
    for i, g in enumerate(parts):
        g = pad_cols(g)
        blocked.append(g.reshape(heads + (-1, g.shape[-1])))
    units, events = reduce_plan(ext, [g.shape[-2:] for g in blocked])
    owned, vec_sum, squares = reduce_scatter(blocked, vec_rows, sizes, units, events, [True] * 5 + [False] * 5)
    loss_total = vec_sum[-1, 0]
    vec_sum = vec_sum[:-8].reshape(n_nar, -1)
    both, qkv_own, up_own, down_own, bridge_own, dqkv_own, dout_own, dup_own, ddown_own, head_own = owned
    enc_owned = [both[:, :enc_cols], qkv_own[:, : enc_qkv.shape[1]], both[:, enc_cols:], up_own, down_own, bridge_own]
    dec_owned = [dqkv_own, dout_own, dup_own, ddown_own, head_own[:, : w_head.shape[1]]]
    vec_square = jnp.square(vec_sum)
    enc_sq = squares[0, 0] + jnp.sum(vec_square[:, : 6 * enc_cols])
    dec_sq = squares[1, 0] + jnp.sum(vec_square[:, 6 * enc_cols :])
    norms = jnp.sqrt(jnp.stack([enc_sq, dec_sq]))
    clip_factor = jnp.minimum(1.0, CLIP_NORM / jnp.sqrt(enc_sq + dec_sq))
    enc_new, enc_small_new, enc_big_new = shampoo(
        [clip_factor * g for g in enc_owned], masters[:6], ENC_KINDS, enc_small, enc_big, LR_MATRIX * LAYER_DECAY
    )
    dec_new, dec_small_new, dec_big_new = shampoo(
        [clip_factor * g for g in dec_owned], masters[6:], DEC_KINDS, dec_small, dec_big, LR_MATRIX
    )
    own_vec = lax.dynamic_slice_in_dim(vec_sum, narrow_at, 1, 0)
    vectors_new, first_new, second_new = adam(
        clip_factor * own_vec, vectors, first_moment, second_moment, step_count, 6 * enc_cols
    )
    return (
        *enc_new, *dec_new, enc_small_new, enc_big_new, dec_small_new, dec_big_new,
        vectors_new, first_new, second_new, norms, loss_total, divisor,
    )


def solution(mesh):
    sizes = (mesh.shape["dp"], mesh.shape["wide"], mesh.shape["narrow"])
    rows = P(("dp", "wide"))
    matrix = P(("dp", "wide"), "narrow")
    turned = P("narrow", ("dp", "wide"))
    matrices = tuple(matrix if kind else turned for kind in ENC_KINDS + DEC_KINDS)
    stats = (P(("dp", "wide"), "narrow"),) * 4
    packed = (P("narrow"),) * 3
    in_specs = (rows, rows, rows, rows, P()) + matrices + packed + stats
    out_specs = matrices + stats + packed + (P(), P(), P())
    return jax.shard_map(
        functools.partial(per_device, sizes), mesh=mesh, in_specs=in_specs, out_specs=out_specs, check_vma=False
    )
```

```python
import functools

import jax
import jax.numpy as jnp
import numpy as np
from jax import lax
from jax.experimental import pallas as pl
from jax.experimental.pallas import tpu as pltpu
from jax.sharding import PartitionSpec as P

D = 768
DH = 64
DD = 512
DHD = 32
PIX = 768
NP = 196
BLOCK = 64
NEWTON = 3
KEEP_MOST = 98

HIGH = lax.Precision.HIGHEST
EPS_NORM = 1e-06
VISIBLE_WEIGHT = 0.1
STAT_DECAY = 0.5
LR_MATRIX = 0.2
LR_VECTOR = 0.2
LAYER_DECAY = 0.75
BETA_FIRST = 0.9
BETA_SECOND = 0.999
EPS_ADAM = 1e-08
CLIP_NORM = 1.0
ENC_KINDS = (True, True, False, True, False, True)
DEC_KINDS = (True, False, True, False, True)


MESHT = pl.DeviceIdType.MESH
FULL_CODE = 32767.0
FLOOR = 1e-30

def xors(n):
    return list(range(1, n))

def bits(n):
    r, b = [], 1
    while b < n:
        r.append(b)
        b *= 2
    return r

def extents(sizes):
    n_dp, n_wide, n_nar = sizes
    return {"n": n_nar, "h": n_dp // 2, "l": 2, "w": n_wide // 2}

def phases_of(order, ext):
    return [d for d in order if ext[d] > 1]

def messages(order, ext):
    out, left = [], 1
    for d in ext: left *= ext[d]
    for d in phases_of(order, ext):
        left //= ext[d]
        out.append((d, ext[d] - 1, left))
    return out

def plan(units, events, shapes, ext):
    flat = []
    for step in events:
        for u, p in step:
            if p <= len(phases_of(units[u][3], ext)) + 2: flat.append((u, p))
    at = {e: i for i, e in enumerate(flat)}
    heads = (ext["n"], ext["h"], ext["l"], ext["w"])
    wants = []
    for u, (m, lo, hi, order) in enumerate(units):
        a, c = shapes[m][0], hi - lo
        last = at[u, len(phases_of(order, ext)) + 2]
        wants.append((at[u, 0], last, ("acc", u), heads + (a, c), "f"))
        wants.append((at[u, 1], at[u, 2], ("stage", u), heads + (a, c), "f"))
        for p, (d, k, n) in enumerate(messages(order, ext)):
            wants.append((at[u, p + 2], last, ("q", u, p), (k, n, a, c), "q"))
    wants.sort(key=lambda w: w[0])
    bufs, where = [], {}
    for start, end, name, shape, kind in wants:
        for i, b in enumerate(bufs):
            if b[0] == (shape, kind) and b[1] < start:
                b[1] = end
                where[name] = i
                break
        else:
            bufs.append([(shape, kind), end])
            where[name] = len(bufs) - 1
    return [b[0] for b in bufs], where

def reduce_kernel(sizes, units, events, count, planned, is_enc, *refs):
    n_dp, n_wide, n_nar = sizes
    ext = extents(sizes)
    slots = ext["n"] * ext["h"] * ext["l"] * ext["w"]
    it = iter(refs)
    take = lambda k: [next(it) for _ in range(k)]
    grads = take(count); vec = next(it)
    outs = take(count); vec_out = next(it); sq_out = next(it); land = take(count)
    nu = len(units)
    kinds, where = planned
    pool = [take(1)[0] if kind == "f" else tuple(take(2)) for _, kind in kinds]
    acc = [pool[where["acc", u]] for u in range(nu)]
    stage_buf = [pool[where["stage", u]] for u in range(nu)]
    recv_q, recv_s = [], []
    for u in range(nu):
        k = len(messages(units[u][3], ext))
        recv_q.append(take(k)); recv_s.append(take(k))
    last_use = {}
    vec_land = next(it); sq_land = next(it)
    core_send, core_recv, local_sem, stage_sem, q_send, q_recv, s_send, s_recv, v_send, v_recv, t_send, t_recv = take(12)

    dp = lax.axis_index("dp"); wi = lax.axis_index("wide"); na = lax.axis_index("narrow")
    own = {"n": na, "h": dp // 2, "l": dp % 2, "w": wi // 2}
    core = wi % 2
    def peer(dim, k):
        if dim == "n": return {"narrow": na ^ k}
        if dim == "h": return {"dp": dp ^ (2 * k)}
        if dim == "l": return {"dp": dp ^ k}
        if dim == "w": return {"wide": wi ^ (2 * k)}
        return {"wide": wi ^ 1}
    partners = [peer(d, k) for d in "nhlw" for k in xors(ext[d])] + [peer("c", 1)]
    barrier = pltpu.get_barrier_semaphore()
    for p in partners:
        pl.semaphore_signal(barrier, inc=1, device_id=p, device_id_type=MESHT)
    pl.semaphore_wait(barrier, len(partners))

    def remote(src, dst, ss, rs, dev):
        return pltpu.make_async_remote_copy(src_ref=src, dst_ref=dst, send_sem=ss, recv_sem=rs, device_id=dev, device_id_type=MESHT)
    pending = []

    hops = [("c", 1)] + [(d, b) for d in "lhwn" for b in bits(ext[d])]
    def vec_hop(i, value_ref, land_ref, ss, rs):
        d, k = hops[i]
        c = remote(value_ref, land_ref.at[i], ss.at[i], rs.at[i], peer(d, k))
        c.start()
        return c
    vec_out[...] = vec[...]
    def vec_start(i):
        vec_flight[i] = vec_hop(i, vec_out, vec_land, v_send, v_recv)
    def vec_end(i):
        vec_flight[i].wait()
        vec_out[...] = vec_out[...] + vec_land[i]
    vec_flight = {}

    def cols(u):
        m, lo, hi, order = units[u]
        return m, lo, hi
    def shape(u):
        m, lo, hi = cols(u)
        return outs[m].shape[0], hi - lo
    def whole(u):
        m, lo, hi = cols(u)
        return (lo, hi) == (0, outs[m].shape[1])
    def view(u, ref, head):
        m, lo, hi = cols(u)
        return ref.at[head] if whole(u) else ref.at[head + (slice(None),) * (6 - len(head)) + (slice(lo, hi),)]
    def acc_view(u):
        a, c = shape(u)
        return acc[u]
    def slab(u, idx):
        a, c = shape(u)
        return acc[u].at[idx["n"], idx["h"], idx["l"], idx["w"]]
    def stage_view(u):
        a, c = shape(u)
        return stage_buf[u]
    flight = {}
    def split(s, dims):
        idx = {}
        for d in reversed(dims):
            if ext[d] == 1:
                idx[d] = 0
            else:
                idx[d] = s % ext[d]
                s = s // ext[d]
        return idx
    sums = [jnp.zeros((1, 1), jnp.float32), jnp.zeros((1, 1), jnp.float32)]

    def code_and_send(u, p):
        ph = phases_of(units[u][3], ext)
        msgs = messages(units[u][3], ext)
        d, peers, slabs = msgs[p]
        gone = ph[:p]
        free = [x for x in "nhlw" if x != d and x not in gone]
        sends = []
        b = where["q", u, p]
        for c in last_use.pop(b, []): c.wait_send()
        out_q, out_s = pool[b]
        for k in range(1, peers + 1):
            def body(s, _):
                idx = split(s, free)
                for x in gone: idx[x] = own[x]
                idx[d] = own[d] ^ k
                x = slab(u, idx)[...]
                top = jnp.maximum(jnp.max(jnp.abs(x), axis=0, keepdims=True), FLOOR)
                out_q[k - 1, s] = jnp.round(x * (FULL_CODE / top)).astype(jnp.int32).astype(jnp.int16)
                out_s[k - 1, s] = top * (1.0 / FULL_CODE)
                return 0
            lax.fori_loop(0, slabs, body, 0)
            a_ = remote(out_q.at[k - 1], recv_q[u][p].at[k - 1], q_send.at[u, p, k - 1], q_recv.at[u, p, k - 1], peer(d, k))
            b_ = remote(out_s.at[k - 1], recv_s[u][p].at[k - 1], s_send.at[u, p, k - 1], s_recv.at[u, p, k - 1], peer(d, k))
            a_.start(); b_.start()
            sends.append((a_, b_))
        last_use[b] = [c for pair in sends for c in pair]
        flight[u, p] = sends
    def take_in(u, p):
        ph = phases_of(units[u][3], ext)
        d, peers, slabs = messages(units[u][3], ext)[p]
        gone = ph[:p + 1]
        free = [x for x in "nhlw" if x not in gone]
        for a, b in flight[u, p]:
            a.wait_recv(); b.wait_recv()
        def body(s, _):
            idx = split(s, free)
            for x in gone: idx[x] = own[x]
            ref = slab(u, idx)
            v = ref[...]
            for k in range(peers):
                v = v + recv_q[u][p][k, s].astype(jnp.int32).astype(jnp.float32) * recv_s[u][p][k, s]
            ref[...] = v
            return 0
        lax.fori_loop(0, slabs, body, 0)

    def stage(u, p):
        m, lo, hi = cols(u)
        n_ph = len(phases_of(units[u][3], ext))
        if p == 0:
            full = (slice(None),) * 4
            c = remote(view(u, grads[m], full + (1 - core,)), land_view(u), core_send.at[u], core_recv.at[u], peer("c", 1))
            c.start()
            flight[u, "core"] = c
            pending.append(c)
            l = pltpu.make_async_copy(view(u, grads[m], full + (core,)), acc_view(u), local_sem.at[u])
            l.start()
            flight[u, "local"] = l
        elif p == 1:
            flight[u, "core"].wait_recv()
            c = pltpu.make_async_copy(land_view(u), stage_view(u), stage_sem.at[u])
            c.start()
            flight[u, "stage"] = c
        elif p == 2:
            flight[u, "local"].wait()
            flight[u, "stage"].wait()
            a, c = shape(u)
            def body(s, _):
                idx = split(s, list("nhlw"))
                ref = slab(u, idx)
                ref[...] = ref[...] + stage_buf[u][idx["n"], idx["h"], idx["l"], idx["w"]]
                return 0
            lax.fori_loop(0, slots, body, 0)
            code_and_send(u, 0)
        else:
            take_in(u, p - 3)
            if p - 2 < n_ph:
                code_and_send(u, p - 2)
            else:
                x = slab(u, own)[...]
                outs[m][:, pl.ds(lo, hi - lo)] = x
                w = 0 if is_enc[m] else 1
                sums[w] = sums[w] + jnp.sum(x * x, keepdims=True)
    def land_view(u):
        m, lo, hi = cols(u)
        return land[m] if whole(u) else land[m].at[:, :, :, :, :, slice(lo, hi)]

    hop = 0
    for step, group in enumerate(events):
        if hop < len(hops):
            if hop: vec_end(hop - 1)
            vec_start(hop)
            hop += 1
        for u, p in group:
            n_ph = len(phases_of(units[u][3], ext))
            if p <= n_ph + 2: stage(u, p)
    while hop < len(hops):
        vec_end(hop - 1); vec_start(hop); hop += 1
    vec_end(len(hops) - 1)
    row = lax.broadcasted_iota(jnp.int32, (8, 128), 0)
    sq_out[...] = jnp.where(row == 0, sums[0], jnp.where(row == 1, sums[1], 0.0))
    for i in range(len(hops)):
        c = vec_hop(i, sq_out, sq_land, t_send, t_recv)
        c.wait()
        sq_out[...] = sq_out[...] + sq_land[i]
    for c in pending + [c for cs in last_use.values() for c in cs]:
        c.wait_send()

def reduce_scatter(grads, vec, sizes, units, events, is_enc, cid=1):
    count = len(grads)
    ext = extents(sizes)
    heads = (ext["n"], ext["h"], ext["l"], ext["w"])
    planned = plan(units, events, [g.shape[-2:] for g in grads], ext)
    def coded(k, n, a, c):
        return [pltpu.VMEM((k, n, a, c), jnp.int16), pltpu.VMEM((k, n, 1, c), jnp.float32)]
    scratch = []
    for shape, kind in planned[0]:
        scratch += [pltpu.VMEM(shape, jnp.float32)] if kind == "f" else coded(*shape)
    for m, lo, hi, order in units:
        a = grads[m].shape[-2]
        ms = [coded(k, n, a, hi - lo) for d, k, n in messages(order, ext)]
        scratch += [x[0] for x in ms] + [x[1] for x in ms]
    hops = 1 + sum(len(bits(ext[d])) for d in ext)
    scratch += [pltpu.VMEM((hops,) + vec.shape, jnp.float32), pltpu.VMEM((hops, 8, 128), jnp.float32)]
    nu = len(units)
    kmax = max(ext.values())
    D = pltpu.SemaphoreType.DMA
    scratch += [D((nu,))] * 4 + [D((nu, 4, kmax))] * 4 + [D((hops,))] * 4
    vm = pl.BlockSpec(memory_space=pltpu.VMEM); an = pl.BlockSpec(memory_space=pl.ANY)
    f32 = jnp.float32
    res = pl.pallas_call(
        functools.partial(reduce_kernel, sizes, units, events, count, planned, is_enc),
        out_shape=[jax.ShapeDtypeStruct(g.shape[-2:], f32) for g in grads]
        + [jax.ShapeDtypeStruct(vec.shape, f32), jax.ShapeDtypeStruct((8, 128), f32)]
        + [jax.ShapeDtypeStruct(heads + g.shape[-2:], f32) for g in grads],
        in_specs=[an] * count + [vm],
        out_specs=[vm] * (count + 2) + [an] * count,
        scratch_shapes=scratch,
        compiler_params=pltpu.CompilerParams(collective_id=cid, has_side_effects=True, vmem_limit_bytes=62 << 20),
    )(*grads, vec)
    return res[:count], res[count], res[count + 1]


def gather_kernel(sizes, units, events, count, *refs):
    n_dp, n_wide, n_nar = sizes
    shards = refs[:count]
    vec, weight = refs[count:count + 2]
    outs = refs[count + 2:2 * count + 2]
    vec_all, weight_sum = refs[2 * count + 2:2 * count + 4]
    weight_land, send_sem, recv_sem, loc_sem, vec_send, vec_recv, sum_send, sum_recv = refs[2 * count + 4:]
    dp = lax.axis_index("dp"); wi = lax.axis_index("wide"); na = lax.axis_index("narrow")
    d_low = 2
    d_high = n_dp // 2
    w_high = n_wide // 2
    own = {"n": na, "h": dp // 2, "l": dp % 2, "w": wi // 2}
    core = wi % 2
    def peer(dim, k):
        if dim == "n": return {"narrow": na ^ k}
        if dim == "h": return {"dp": dp ^ (2 * k)}
        if dim == "l": return {"dp": dp ^ k}
        if dim == "w": return {"wide": wi ^ (2 * k)}
        return {"wide": wi ^ 1}
    extent = {"n": n_nar, "h": d_high, "l": d_low, "w": w_high}
    partners = [peer(d, k) for d in "nhlw" for k in xors(extent[d])] + [peer("c", 1)]
    barrier = pltpu.get_barrier_semaphore()
    for p in partners:
        pl.semaphore_signal(barrier, inc=1, device_id=p, device_id_type=MESHT)
    pl.semaphore_wait(barrier, len(partners))
    pending = []
    sib_recv = []
    vec_flight = []
    for k in xors(n_nar):
        c = pltpu.make_async_remote_copy(src_ref=vec, dst_ref=vec_all.at[na], send_sem=vec_send.at[k - 1], recv_sem=vec_recv.at[k - 1], device_id=peer("n", k), device_id_type=MESHT)
        c.start()
        vec_flight.append(c)
    vec_all[na] = vec[...]
    weight_sum[...] = weight[...]
    hops = [("c", 1)] + [(d, b) for d in "lhw" for b in bits(extent[d])]
    slot_of = [0] * len(units)
    def region(u, full, at, which_core):
        m, lo, hi, order = units[u]
        idx = []
        for d in "nhlw":
            if d in full: idx.append(slice(None))
            elif at and d == at[0]: idx.append(own[d] ^ at[1])
            else: idx.append(own[d])
        r = outs[m].at[tuple(idx) + (which_core,)]
        if (lo, hi) != (0, shards[m].shape[1]):
            r = outs[m].at[tuple(idx) + (which_core, slice(None), slice(lo, hi))]
        return r
    def remote(u, src, dst, dev, recv_view):
        s = slot_of[u]; slot_of[u] += 1
        c = pltpu.make_async_remote_copy(src_ref=src, dst_ref=dst, send_sem=send_sem.at[u, s], recv_sem=recv_sem.at[u, s], device_id=dev, device_id_type=MESHT)
        c.start()
        pending.append(c)
        return pltpu.make_async_remote_copy(src_ref=recv_view, dst_ref=recv_view, send_sem=send_sem.at[u, s], recv_sem=recv_sem.at[u, s], device_id=dev, device_id_type=MESHT)
    def shard(u):
        m, lo, hi, order = units[u]
        return shards[m] if (lo, hi) == (0, shards[m].shape[1]) else shards[m].at[:, slice(lo, hi)]
    state = {}
    def phases(u):
        return [d for d in units[u][3] if extent[d] > 1]
    def stage(u, p):
        ph = phases(u)
        if p == 0:
            lc = pltpu.make_async_copy(shard(u), region(u, (), None, core), loc_sem.at[u]); lc.start()
            sib_recv.append(remote(u, shard(u), region(u, (), None, core), peer("c", 1), region(u, (), None, 1 - core)))
            src = shard(u)
            state[u] = []
            state[u, "loc"] = lc
        else:
            done = ph[:p - 1]
            for k, w in state[u]:
                w.wait_recv()
            for k, w in state[u]:
                here = region(u, done, (ph[p - 1], k), core)
                there = region(u, done, (ph[p - 1], k), 1 - core)
                state[u, k] = (here, there)
            if p == 1: state[u, "loc"].wait()
            src = None
        old = state[u]
        state[u] = []
        if p < len(ph):
            full = ph[:p]
            for k in xors(extent[ph[p]]):
                mine = region(u, full, None, core) if src is None else src
                w = remote(u, mine, region(u, full, None, core), peer(ph[p], k), region(u, full, (ph[p], k), core))
                state[u].append((k, w))
        if p > 0:
            for k, _ in old:
                here, there = state[u, k]
                sib_recv.append(remote(u, here, here, peer("c", 1), there))
    for step in events:
        for u, p in step:
            if p <= len(phases(u)): stage(u, p)
    for i, (d, k) in enumerate(hops):
        c = pltpu.make_async_remote_copy(src_ref=weight_sum, dst_ref=weight_land.at[i], send_sem=sum_send.at[i], recv_sem=sum_recv.at[i], device_id=peer(d, k), device_id_type=MESHT)
        c.start()
        c.wait()
        weight_sum[...] = weight_sum[...] + weight_land[i]
    for c in vec_flight:
        c.wait()
    for c in pending:
        c.wait_send()
    for w in sib_recv:
        w.wait_recv()


def gather(shards, vec, weight, sizes, units, events, cid=0):
    n_dp, n_wide, n_nar = sizes
    count = len(shards)
    ext = extents(sizes)
    slots = 2 * sum(ext.values())
    nu = len(units)
    hops = 1 + sum(len(bits(ext[d])) for d in "lhw")
    DMA = pltpu.SemaphoreType.DMA
    an = pl.BlockSpec(memory_space=pl.ANY)
    vm = pl.BlockSpec(memory_space=pltpu.VMEM)
    heads = (ext["n"], ext["h"], ext["l"], ext["w"], 2)
    res = pl.pallas_call(
        functools.partial(gather_kernel, sizes, units, events, count),
        out_shape=[jax.ShapeDtypeStruct(heads + s.shape, s.dtype) for s in shards]
        + [jax.ShapeDtypeStruct((n_nar,) + vec.shape, vec.dtype), jax.ShapeDtypeStruct(weight.shape, weight.dtype)],
        in_specs=[an] * count + [vm, vm],
        out_specs=[an] * count + [vm, vm],
        scratch_shapes=[pltpu.VMEM((hops,) + weight.shape, jnp.float32), DMA((nu, slots)), DMA((nu, slots)), DMA((nu,)), DMA((n_nar,)), DMA((n_nar,)), DMA((hops,)), DMA((hops,))],
        compiler_params=pltpu.CompilerParams(collective_id=cid, has_side_effects=True),
    )(*shards, vec, weight)
    return res[:count], res[count], res[count + 1]


def gather_plan(ext, shapes):
    cols = [s[1] for s in shapes]
    if ext["w"] > 1:
        units = [(m, 0, c, "nlhw") for m, c in enumerate(cols)]
        return units, [[(u, p)] for u in range(len(units)) for p in range(5)]
    A, B, XA, XB = "nlhw", "nhlw", "lhnw", "hlnw"
    half = cols[2] // 2
    groups = [
        [(1, 0, cols[1], A), (0, 0, 256, B)],
        [(0, 256, 512, A), (0, 512, cols[0], B)],
        [(2, 0, half, A), (3, 0, half, B)],
        [(2, half, cols[2], A), (3, half, cols[3], B)],
        [(7, 0, cols[7], A), (8, 0, cols[8], B)],
        [(4, 0, cols[4], A)],
    ]
    extra = [(5, 0, cols[5], XA), (9, 0, cols[9], XB), (6, 0, cols[6], XB)]
    units, ids = [], []
    for g in groups:
        ids.append(list(range(len(units), len(units) + len(g))))
        units += g
    more = list(range(len(units), len(units) + len(extra)))
    units += extra
    events = []
    for t in range(len(groups) + 3):
        step = []
        for p in range(4):
            if 0 <= t - p < len(groups):
                step += [(u, p) for u in ids[t - p]]
        for p, when in enumerate((0, 1, 5, 8)):
            if t == when:
                step += [(u, p) for u in more]
        events.append(step)
    return units, events


def reduce_plan(ext, shapes):
    cols = [s[1] for s in shapes]
    if ext["w"] > 1:
        units = [(m, lo, min(lo + 256, c), "wlhn") for m, c in enumerate(cols) for lo in range(0, c, 256)]
        return units, [[(u, p)] for u in range(len(units)) for p in range(7)]
    A, B, XA, XB = "lhwn", "hlwn", "nlhw", "nhlw"
    h2, h7 = cols[2] // 2, cols[7] // 2
    groups = [
        [(7, 0, h7, A), (8, 0, h7, B)],
        [(7, h7, cols[7], A), (8, h7, cols[8], B)],
        [(2, 0, h2, A), (3, 0, h2, B)],
        [(2, h2, cols[2], A), (3, h2, cols[3], B)],
        [(0, 0, 256, A), (0, 256, 512, B)],
        [(0, 512, cols[0], A), (1, 0, cols[1], B)],
        [(4, 0, cols[4], A)],
    ]
    extra = [(5, 0, cols[5], XA), (9, 0, cols[9], XB), (6, 0, cols[6], XB)]
    units, ids = [], []
    for g in groups:
        ids.append(list(range(len(units), len(units) + len(g))))
        units += g
    more = list(range(len(units), len(units) + len(extra)))
    units += extra
    of = lambda t: ids[t] if 0 <= t < len(ids) else []
    events = []
    for t in range(-2, len(groups) + 4):
        step = [(u, 0) for u in of(t + 2)]
        now, nxt = of(t), of(t + 1)
        for i in range(max(len(now), len(nxt))):
            if i < len(now):
                step.append((now[i], 2))
            if i < len(nxt):
                step.append((nxt[i], 1))
        for p in (3, 4, 5):
            step += [(u, p) for u in of(t - (p - 2))]
        for p, when in enumerate((-2, -1, 0, 3, 4, 5)):
            if t == when:
                step += [(u, p) for u in more]
        events.append(step)
    return units, events


def matmul_hi(left, right):
    return jnp.matmul(left, right, precision=HIGH)


def sincos_table(rows, width):
    column = np.arange(width)
    freq = np.power(np.float32(10000.0), (-(2 * (column // 2)).astype(np.float32) / np.float32(width)).astype(np.float32))
    angle = (np.arange(rows, dtype=np.float32)[:, None] * freq[None, :]).astype(np.float32)
    return np.where(column % 2 == 0, np.sin(angle), np.cos(angle)).astype(np.float32)


def dot_nn(a, b):
    return lax.dot_general(a, b, (((1,), (0,)), ((), ())), preferred_element_type=jnp.float32)


def dot_nt(a, b):
    return lax.dot_general(a, b, (((1,), (1,)), ((), ())), preferred_element_type=jnp.float32)


def dot_tn(a, b):
    return lax.dot_general(a, b, (((0,), (0,)), ((), ())), preferred_element_type=jnp.float32)


def dot_exact(a, b):
    return lax.dot_general(a, b, (((1,), (0,)), ((), ())), precision=HIGH, preferred_element_type=jnp.float32)


class Side:
    def __init__(self, width, head, heads, rows, images, slabs):
        self.width, self.head, self.heads, self.rows = width, head, heads, rows
        self.slabs = slabs
        self.tokens = rows * images
        self.lane = head * heads
        self.packed = -(-3 * self.lane // 128) * 128

    def scratch(self, hidden):
        t, n, w = self.tokens, self.slabs, self.width
        lane_pad = self.lane
        bf, f = jnp.bfloat16, jnp.float32
        return {
            "x": ((t, w), f),
            "hat1": ((t, w), f), "hat2": ((t, w), f), "hat3": ((t, w), f),
            "inv": ((t, 128), f),
            "n1": ((t, w), bf), "n2": ((t, w), bf), "n3": ((t, w), bf),
            "qkv": ((n, t, self.packed), bf),
            "lse": ((t, 128), f),
            "att": ((n, t, lane_pad), bf),
            "slope": ((n, t, hidden), f),
            "act": ((n, t, hidden), bf),
            "dn": ((t, w), f),
            "og": ((t, w), bf),
            "turn": ((w, t), bf),
        }


def compute_kernel(per, slabs, names, count, *refs):
    it = iter(refs)
    take = lambda k: [next(it) for _ in range(k)]
    hbm = take(count)
    patches, vis_col, vis_row, loss_w, vec_parts, weight_sum, table_e, table_d, counts = take(9)
    grads = take(count)
    vec_out = next(it)
    w = take(count)
    load_sem, store_sem = take(2)
    stage = next(it)
    buf = dict(zip(names, it))
    w_eq, w_out, w_up, w_down, w_bridge, w_dqkv, w_dout, w_dup, w_ddown, w_head = w
    f32, bf16 = jnp.float32, jnp.bfloat16
    loads = []
    for m in range(count):
        c = pltpu.make_async_copy(hbm[m], w[m], load_sem.at[m])
        c.start()
        loads.append(c)
    waited = set()

    def need(m):
        if m not in waited:
            waited.add(m)
            loads[m].wait()


    enc_rows, dec_rows = vis_col.shape[1], patches.shape[1]
    enc_w, dec_w = table_e.shape[1], table_d.shape[1]
    enc = Side(enc_w, DH, w_out.shape[2] // DH, enc_rows, per, slabs)
    dec = Side(dec_w, DHD, w_dout.shape[2] // DHD, dec_rows, per, slabs)
    for s, tag in ((enc, "e_"), (dec, "d_")):
        s.b = {k[2:]: v for k, v in buf.items() if k.startswith(tag)}
    enc.w, dec.w = (w_eq, w_out, w_up, w_down), (w_dqkv, w_dout, w_dup, w_ddown)
    enc.ids, dec.ids = (0, 1, 2, 3), (5, 6, 7, 8)
    enc.base, dec.base = 0, 7
    vec_full = buf["vec_full"]
    enc_c, dec_c = enc_w // slabs, dec_w // slabs
    for n in range(slabs):
        vec_full[0:6, pl.ds(n * enc_c, enc_c)] = vec_parts[n, 0:6, 0:enc_c]
        vec_full[6:13, pl.ds(n * dec_c, dec_c)] = vec_parts[n, 6:13, 0:dec_c]
    vec_out[...] = jnp.zeros_like(vec_out)

    def vector(k, width):
        return vec_full[k : k + 1, 0:width]

    CH = 32

    def chunks(total, body):
        def step(i, carry):
            body(pl.ds(pl.multiple_of(i * CH, CH), CH))
            return carry
        lax.fori_loop(0, total // CH, step, 0)

    def norm_fwd(s, k, out, hat, inv):
        gain, bias = vector(s.base + k, s.width), vector(s.base + k + 1, s.width)
        x = s.b["x"]
        def body(r):
            v = x[r, :]
            mean = jnp.mean(v, axis=1, keepdims=True)
            d = v - mean
            i = lax.rsqrt(jnp.mean(d * d, axis=1, keepdims=True) + EPS_NORM)
            h = d * i
            s.b[hat][r, :] = h
            s.b["inv"][r, inv : inv + 1] = i
            s.b[out][r, :] = (h * gain + bias).astype(bf16)
        chunks(s.tokens, body)

    def norm_bwd(s, k, hat, inv, add):
        gain = vector(s.base + k, s.width)
        def body(r):
            dn = s.b["dn"][r, :]
            h = s.b[hat][r, :]
            vec_out[s.base + k : s.base + k + 1, 0 : s.width] += jnp.sum(dn * h, axis=0, keepdims=True)
            vec_out[s.base + k + 1 : s.base + k + 2, 0 : s.width] += jnp.sum(dn, axis=0, keepdims=True)
            g = dn * gain
            d = s.b["inv"][r, inv : inv + 1] * (
                g - jnp.mean(g, axis=1, keepdims=True) - h * jnp.mean(g * h, axis=1, keepdims=True)
            )
            s.b["x"][r, :] = s.b["x"][r, :] + d if add else d
        chunks(s.tokens, body)

    def slab_loop(body):
        def step(n, carry):
            body(n)
            return carry
        lax.fori_loop(0, slabs, step, 0)

    def head_mask(s, h):
        lane = lax.broadcasted_iota(jnp.int32, (1, s.lane), 1)
        return (lane >= h * s.head) & (lane < (h + 1) * s.head)

    def scores(s, q, k, mask, limit):
        v = dot_nt(jnp.where(mask, q, jnp.zeros_like(q)), k) * (s.head ** -0.5)
        key = lax.broadcasted_iota(jnp.int32, (s.rows, s.rows), 1)
        return jnp.where(key < limit, v, -1e30)

    def attention_loop(body):
        def step(i, carry):
            image, n = i // slabs, i % slabs
            body(image, n)
            return carry
        lax.fori_loop(0, per * slabs, step, 0)

    def image_rows(s, image):
        return pl.ds(pl.multiple_of(image * s.rows, 16), s.rows)

    def block_fwd(s, limit):
        b = s.b
        b["lse"][...] = jnp.zeros_like(b["lse"])
        qkv_w, out_w, up_w, down_w = s.w
        need(s.ids[0])
        norm_fwd(s, 0, "n1", "hat1", 1)
        def qkv(n):
            b["qkv"][n] = dot_nn(b["n1"][...], qkv_w[n, :, 0 : s.packed]).astype(bf16)
        slab_loop(qkv)
        def attend(image, n):
            r = image_rows(s, image)
            q = b["qkv"][n, r, 0 : s.lane]
            k = b["qkv"][n, r, s.lane : 2 * s.lane]
            v = b["qkv"][n, r, 2 * s.lane : 3 * s.lane]
            lane = lax.broadcasted_iota(jnp.int32, (s.rows, 128), 1)
            total = jnp.zeros((s.rows, s.lane), f32)
            lse = b["lse"][r, :]
            for h in range(s.heads):
                mask = head_mask(s, h)
                sc = scores(s, q, k, mask, limit(image))
                top = jnp.max(sc, axis=1, keepdims=True)
                e = jnp.exp(sc - top)
                z = jnp.sum(e, axis=1, keepdims=True)
                p = (e / z).astype(bf16)
                total = jnp.where(mask, dot_nn(p, v), total)
                lse = jnp.where(lane == n * s.heads + h, top + jnp.log(z), lse)
            b["att"][n, r, :] = total.astype(bf16)
            b["lse"][r, :] = lse
        attention_loop(attend)
        need(s.ids[1])
        def project(n):
            b["x"][...] += dot_nt(b["att"][n], out_w[n])
        slab_loop(project)
        norm_fwd(s, 2, "n2", "hat2", 2)
        need(s.ids[2])
        need(s.ids[3])
        hid = buf["hid"]
        c = up_w.shape[2]
        def mlp(n):
            hid[0 : s.tokens, 0:c] = dot_nn(b["n2"][...], up_w[n])
            def body(r):
                v = hid[r, 0:c]
                cdf = 0.5 * (1.0 + lax.erf(v * 0.7071067811865476))
                b["act"][n, r, :] = (v * cdf).astype(bf16)
                b["slope"][n, r, :] = cdf + v * (0.3989422804014327 * jnp.exp(-0.5 * v * v))
            chunks(s.tokens, body)
            b["x"][...] += dot_nt(b["act"][n], down_w[n])
        slab_loop(mlp)
        norm_fwd(s, 4, "n3", "hat3", 3)

    prior = []

    def pieces(m):
        cols = grads[m].shape[2]
        return (2, cols // 2) if cols > 384 else (1, cols)

    def leave(m, n, p, slot):
        rows, (_, cols) = grads[m].shape[1], pieces(m)
        return pltpu.make_async_copy(
            stage.at[slot, pl.ds(0, rows), pl.ds(0, cols)], grads[m].at[n, :, pl.ds(p * cols, cols)], store_sem.at[slot]
        )

    def weight_out(m, value):
        rows, (parts, cols) = grads[m].shape[1], pieces(m)
        before = prior[-1] if prior else None
        prior.append(m)
        def emit(n):
            for p in range(parts):
                slot = p if parts == 2 else n % 2
                early = n < 1 if parts == 2 else n < 2
                if before is not None:
                    @pl.when(early)
                    def _(): leave(before, 0, 0, slot).wait()
                @pl.when(jnp.logical_not(early))
                def _(): leave(m, n, p, slot).wait()
                stage[slot, 0:rows, 0:cols] = value(n, p * cols, (p + 1) * cols)
                leave(m, n, p, slot).start()
        return emit

    def turned(s, name):
        s.b["turn"][...] = s.b[name][...].T

    def block_bwd(s, limit):
        b = s.b
        qkv_w, out_w, up_w, down_w = s.w
        b["og"][...] = b["x"][...].astype(bf16)
        turned(s, "og")
        b["dn"][...] = jnp.zeros_like(b["dn"])
        emit_down = weight_out(s.ids[3], lambda n, lo, hi: dot_nn(b["turn"][...], b["act"][n, :, lo:hi]))
        def down(n):
            emit_down(n)
            b["act"][n] = (dot_nn(b["og"][...], down_w[n]) * b["slope"][n]).astype(bf16)
            b["dn"][...] += dot_nt(b["act"][n], up_w[n])
        slab_loop(down)
        turned(s, "n2")
        slab_loop(weight_out(s.ids[2], lambda n, lo, hi: dot_nn(b["turn"][...], b["act"][n, :, lo:hi])))
        norm_bwd(s, 2, "hat2", 2, True)
        b["og"][...] = b["x"][...].astype(bf16)
        turned(s, "og")
        width = grads[s.ids[1]].shape[2]
        def out_grad(n, lo, hi):
            v = dot_nn(b["turn"][...], b["att"][n])
            if width != s.lane:
                v = jnp.concatenate([v, jnp.zeros((s.width, width - s.lane), f32)], axis=1)
            return v
        emit_proj = weight_out(s.ids[1], out_grad)
        def proj(n):
            emit_proj(n)
            b["att"][n] = dot_nn(b["og"][...], out_w[n]).astype(bf16)
        slab_loop(proj)
        def attend(image, n):
            r = image_rows(s, image)
            q = b["qkv"][n, r, 0 : s.lane]
            k = b["qkv"][n, r, s.lane : 2 * s.lane]
            v = b["qkv"][n, r, 2 * s.lane : 3 * s.lane]
            g = b["att"][n, r, :]
            lane = lax.broadcasted_iota(jnp.int32, (s.rows, 128), 1)
            lse = b["lse"][r, :]
            dq = jnp.zeros((s.rows, s.lane), f32)
            dk = dq
            dv = dq
            for h in range(s.heads):
                mask = head_mask(s, h)
                level = jnp.sum(jnp.where(lane == n * s.heads + h, lse, 0.0), axis=1, keepdims=True)
                p = jnp.exp(scores(s, q, k, mask, limit(image)) - level)
                dp = dot_nt(jnp.where(mask, g, jnp.zeros_like(g)), v)
                dv = jnp.where(mask, dot_tn(p.astype(bf16), g), dv)
                ds = (p * (dp - jnp.sum(dp * p, axis=1, keepdims=True))).astype(bf16)
                dq = jnp.where(mask, dot_nn(ds, k), dq)
                dk = jnp.where(mask, dot_tn(ds, q), dk)
            scale = s.head ** -0.5
            if s.packed != 3 * s.lane:
                b["qkv"][n, r, 2 * s.lane : s.packed] = jnp.zeros((s.rows, s.packed - 2 * s.lane), bf16)
            b["qkv"][n, r, 0 : s.lane] = (dq * scale).astype(bf16)
            b["qkv"][n, r, s.lane : 2 * s.lane] = (dk * scale).astype(bf16)
            b["qkv"][n, r, 2 * s.lane : 3 * s.lane] = dv.astype(bf16)
        attention_loop(attend)
        b["dn"][...] = jnp.zeros_like(b["dn"])
        def qkv(n):
            b["dn"][...] += dot_nt(b["qkv"][n], qkv_w[n, :, 0 : s.packed])
        slab_loop(qkv)
        norm_bwd(s, 0, "hat1", 1, True)

    chosen = buf["chosen"]
    need(0)
    for i in range(per):
        r = pl.ds(i * enc_rows, enc_rows)
        patch = lax.broadcasted_iota(jnp.int32, (enc_rows, dec_rows), 1)
        one = patch == vis_col[i]
        chosen[r, :] = dot_nn(one.astype(f32).astype(bf16), patches[i]).astype(bf16)
        enc.b["x"][r, :] = dot_exact(one.astype(f32), table_e[...])
    for n in range(slabs):
        lead = w_eq.shape[2] - 256
        part = dot_nn(chosen[...], w_eq[n, :, lead : lead + 256])
        enc.b["x"][:, n * enc_c : (n + 1) * enc_c] += part[:, 256 - enc_c : 256]
    block_fwd(enc, lambda image: counts[image])
    need(4)
    bridged = buf["hid"]
    for n in range(slabs):
        bridged[0 : enc.tokens, n * dec_c : (n + 1) * dec_c] = dot_nn(enc.b["n3"][...], w_bridge[n])

    def hits(i, turned_way):
        if turned_way:
            patch = lax.broadcasted_iota(jnp.int32, (dec_rows, enc_rows), 0)
            slot = lax.broadcasted_iota(jnp.int32, (dec_rows, enc_rows), 1)
            return ((patch == vis_row[i]) & (slot < counts[i])).astype(f32)
        patch = lax.broadcasted_iota(jnp.int32, (enc_rows, dec_rows), 1)
        slot = lax.broadcasted_iota(jnp.int32, (enc_rows, dec_rows), 0)
        return ((patch == vis_col[i]) & (slot < counts[i])).astype(f32)

    for i in range(per):
        r = pl.ds(i * dec_rows, dec_rows)
        hit = hits(i, True)
        placed = dot_exact(hit, bridged[pl.ds(i * enc_rows, enc_rows), 0:dec_w])
        seen = jnp.sum(hit, axis=1, keepdims=True) > 0
        dec.b["x"][r, :] = jnp.where(seen, placed, vector(6, dec_w)) + table_d[...]
    block_fwd(dec, lambda image: NP)
    need(9)
    pred = buf["hid"]
    pix_c = w_head.shape[2]
    pix = patches.shape[2]
    for n in range(slabs):
        pred[0 : dec.tokens, n * pix_c : (n + 1) * pix_c] = dot_nn(dec.b["n3"][...], w_head[n])

    pgrad = buf["pgrad"]
    divisor = weight_sum[0:1, 0:1]
    loss = jnp.zeros((1, 1), f32)
    LC = 16
    for i in range(per):
        def lossy(j, total):
            r = pl.ds(pl.multiple_of(j * LC, LC), LC)
            px = patches[i, r, :].astype(f32)
            d = px - jnp.mean(px, axis=1, keepdims=True)
            target = d * lax.rsqrt(jnp.mean(d * d, axis=1, keepdims=True) + EPS_NORM)
            rr = pl.ds(pl.multiple_of(i * dec_rows + j * LC, LC), LC)
            error = pred[rr, 0:pix] - target
            weight = loss_w[i, r, :]
            pgrad[rr, :] = (2.0 * weight * error / divisor).astype(bf16)
            return total + jnp.sum(weight * error * error, keepdims=True)
        loss = lax.fori_loop(0, dec_rows // LC, lossy, loss)
    turned(dec, "n3")
    head_pad = grads[9].shape[2]
    part9 = buf["part9"]
    part9[...] = jnp.zeros_like(part9)
    for n in range(slabs):
        part9[n, :, 0:pix_c] = pgrad[:, n * pix_c : (n + 1) * pix_c]
    dec.b["dn"][...] = jnp.zeros_like(dec.b["dn"])
    emit_head = weight_out(9, lambda n, lo, hi: dot_nn(dec.b["turn"][...], part9[n]))
    def head_bwd(n):
        emit_head(n)
        dec.b["dn"][...] += dot_nt(part9[n, :, 0:pix_c], w_head[n])
    slab_loop(head_bwd)
    norm_bwd(dec, 4, "hat3", 3, False)
    block_bwd(dec, lambda image: NP)
    turned(dec, "n1")
    slab_loop(weight_out(5, lambda n, lo, hi: dot_nn(dec.b["turn"][...], dec.b["qkv"][n, :, lo:hi])))

    part4 = buf["part4"]
    for i in range(per):
        r = pl.ds(i * dec_rows, dec_rows)
        seen = jnp.sum(hits(i, True), axis=1, keepdims=True) > 0
        grad = dec.b["x"][r, :]
        vec_out[6:7, 0:dec_w] += jnp.sum(jnp.where(seen, 0.0, grad), axis=0, keepdims=True)
        back = dot_exact(hits(i, False), grad).astype(bf16)
        for n in range(slabs):
            part4[n, pl.ds(i * enc_rows, enc_rows), :] = back[:, n * dec_c : (n + 1) * dec_c]
    turned(enc, "n3")
    enc.b["dn"][...] = jnp.zeros_like(enc.b["dn"])
    emit_bridge = weight_out(4, lambda n, lo, hi: dot_nn(enc.b["turn"][...], part4[n]))
    def bridge_bwd(n):
        emit_bridge(n)
        enc.b["dn"][...] += dot_nt(part4[n], w_bridge[n])
    slab_loop(bridge_bwd)
    norm_bwd(enc, 4, "hat3", 3, False)
    block_bwd(enc, lambda image: counts[image])

    turned(enc, "n1")
    turn2 = buf["turn2"]
    turn2[...] = chosen[...].T
    part0 = buf["part0"]
    part0[...] = jnp.zeros_like(part0)
    late = 3 * enc.lane
    for n in range(slabs):
        part0[n, :, 384 - enc_c : 384] = enc.b["x"][:, n * enc_c : (n + 1) * enc_c].astype(bf16)
    def eq_grad(n, lo, hi):
        have = min(hi, enc.packed)
        v = dot_nn(enc.b["turn"][...], enc.b["qkv"][n, :, lo:have])
        if have < hi:
            v = jnp.concatenate([v, jnp.zeros((enc.width, hi - have), f32)], axis=1)
        if hi > late:
            v = v + dot_nn(turn2[...], part0[n])
        return v
    slab_loop(weight_out(0, eq_grad))
    row = lax.broadcasted_iota(jnp.int32, (1, vec_out.shape[1]), 1)
    vec_out[13:14, :] = jnp.where(row >= 0, loss, 0.0)
    for slot in range(2):
        leave(0, 0, 0, slot).wait()


def compute(weights, patches, vis_col, vis_row, loss_w, vec_parts, weight_sum, counts):
    per, dec_rows, pix = patches.shape
    slabs = weights[0].shape[0]
    enc_rows = vis_col.shape[1]
    enc_w, dec_w = weights[0].shape[1], weights[5].shape[1]
    enc = Side(enc_w, DH, weights[1].shape[2] // DH, enc_rows, per, slabs)
    dec = Side(dec_w, DHD, weights[6].shape[2] // DHD, dec_rows, per, slabs)
    named = {}
    for s, tag, up in ((enc, "e_", weights[2]), (dec, "d_", weights[7])):
        for k, v in s.scratch(up.shape[2]).items():
            named[tag + k] = v
    f32, bf16 = jnp.float32, jnp.bfloat16
    top = max(enc.tokens, dec.tokens)
    named["hid"] = ((top, max(pix, weights[2].shape[2], weights[7].shape[2])), f32)
    named["vec_full"] = ((16, enc_w), f32)
    named["chosen"] = ((enc.tokens, pix), bf16)
    named["pgrad"] = ((dec.tokens, pix), bf16)
    up128 = lambda c: -(-c // 128) * 128
    named["part9"] = ((slabs, dec.tokens, up128(weights[9].shape[2])), bf16)
    named["part4"] = ((slabs, enc.tokens, weights[4].shape[2]), bf16)
    named["part0"] = ((slabs, enc.tokens, 384), bf16)
    named["turn2"] = ((pix, enc.tokens), bf16)
    grad_shapes = [jax.ShapeDtypeStruct(g.shape[:2] + (up128(g.shape[2]),), f32) for g in weights]
    an = pl.BlockSpec(memory_space=pl.ANY)
    vm = pl.BlockSpec(memory_space=pltpu.VMEM)
    sm = pl.BlockSpec(memory_space=pltpu.SMEM)
    DMA = pltpu.SemaphoreType.DMA
    count = len(weights)
    rows = max(g.shape[1] for g in grad_shapes)
    cols = max(384, *(g.shape[2] // 2 for g in grad_shapes))
    pad_rows = lambda t: jnp.pad(t, ((0, dec_rows - NP), (0, 0)))
    table_e = jnp.asarray(np.pad(sincos_table(NP, enc_w), ((0, dec_rows - NP), (0, 0))))
    table_d = jnp.asarray(np.pad(sincos_table(NP, dec_w), ((0, dec_rows - NP), (0, 0))))
    res = pl.pallas_call(
        functools.partial(compute_kernel, per, slabs, list(named), count),
        out_shape=grad_shapes + [jax.ShapeDtypeStruct((16, enc_w), f32)],
        in_specs=[an] * count + [vm] * 8 + [sm],
        out_specs=[an] * count + [vm],
        scratch_shapes=[pltpu.VMEM(g.shape, bf16) for g in weights]
        + [DMA((count,)), DMA((2,)), pltpu.VMEM((2, rows, cols), f32)]
        + [pltpu.VMEM(s, d) for s, d in named.values()],
        compiler_params=pltpu.CompilerParams(vmem_limit_bytes=60 << 20),
    )(*weights, patches, vis_col, vis_row, loss_w, vec_parts, weight_sum, table_e, table_d, counts)
    return res[:count], res[count]


def root_quarter(matrix):
    identity = jnp.eye(matrix.shape[-1], dtype=matrix.dtype)
    magnitude = jnp.sqrt(jnp.sum(jnp.square(matrix), axis=(-2, -1), keepdims=True))
    current = matrix / magnitude
    result = None
    for newton_step in range(NEWTON):
        factor = (5.0 * identity - current) * 0.25
        result = factor if result is None else matmul_hi(result, factor)
        if newton_step + 1 < NEWTON:
            square = matmul_hi(factor, factor)
            current = matmul_hi(matmul_hi(square, square), current)
    return result * magnitude ** (-0.25)


def shampoo(gradients, weights, kinds, small_stat, large_stat, learn_rate):
    pieces = [g.reshape(g.shape[0], -1, BLOCK).transpose(1, 0, 2) for g in gradients]
    blocks = jnp.concatenate(pieces, axis=0)[None, None]
    flipped = jnp.swapaxes(blocks, -1, -2)
    small_new = STAT_DECAY * small_stat + (1.0 - STAT_DECAY) * matmul_hi(blocks, flipped)
    large_new = STAT_DECAY * large_stat + (1.0 - STAT_DECAY) * matmul_hi(flipped, blocks)
    update = matmul_hi(matmul_hi(root_quarter(small_new), blocks), root_quarter(large_new))[0, 0]
    results, offset = [], 0
    for weight, kind, piece in zip(weights, kinds, pieces):
        step = update[offset : offset + piece.shape[0]]
        offset += piece.shape[0]
        if kind:
            step = step.transpose(1, 0, 2).reshape(weight.shape)
        else:
            step = step.transpose(0, 2, 1).reshape(weight.shape)
        results.append(weight - learn_rate * step)
    return results, small_new, large_new


def adam(gradient, weight, first, second, step_count, enc_columns):
    moment_one = BETA_FIRST * first + (1.0 - BETA_FIRST) * gradient
    moment_two = BETA_SECOND * second + (1.0 - BETA_SECOND) * jnp.square(gradient)
    steps_done = step_count[0].astype(jnp.float32)
    corrected_one = moment_one / (1.0 - jnp.power(BETA_FIRST, steps_done))
    corrected_two = moment_two / (1.0 - jnp.power(BETA_SECOND, steps_done))
    column = jnp.arange(weight.shape[1])
    rates = jnp.where(column < enc_columns, LR_VECTOR * LAYER_DECAY, LR_VECTOR)
    return (
        weight - rates * corrected_one / (jnp.sqrt(corrected_two) + EPS_ADAM),
        moment_one,
        moment_two,
    )


def heads_apart(shard, head):
    return shard.reshape(shard.shape[0], -1, 3, head).transpose(0, 2, 1, 3).reshape(shard.shape)


def heads_together(shard, head):
    return shard.reshape(shard.shape[0], 3, -1, head).transpose(0, 2, 1, 3).reshape(shard.shape)


def per_device(
    sizes,
    patches, vis_index, keep_mask, counts, step_count,
    w_embed, enc_qkv, enc_out, enc_up, enc_down, w_bridge,
    dec_qkv, dec_out, dec_up, dec_down, w_head,
    vectors, first_moment, second_moment, enc_small, enc_big, dec_small, dec_big,
):
    n_dp, n_wide, n_nar = sizes
    ext = extents(sizes)
    narrow_at = lax.axis_index("narrow")
    masters = (w_embed, enc_qkv, enc_out, enc_up, enc_down, w_bridge, dec_qkv, dec_out, dec_up, dec_down, w_head)
    low = lambda w: w.astype(jnp.bfloat16)
    shards = [
        jnp.concatenate([heads_apart(low(enc_qkv), DH), low(w_embed)], axis=1),
        low(enc_out).T, low(enc_up), low(enc_down).T, low(w_bridge),
        heads_apart(low(dec_qkv), DHD), low(dec_out).T, low(dec_up), low(dec_down).T, low(w_head),
    ]
    enc_cols, dec_cols = w_embed.shape[1], w_bridge.shape[1]
    weight_part = jnp.sum(NP - (1.0 - VISIBLE_WEIGHT) * counts.astype(jnp.float32))
    vec_part = jnp.concatenate(
        [
            vectors[:, : 6 * enc_cols].reshape(6, enc_cols),
            jnp.pad(vectors[:, 6 * enc_cols :].reshape(7, dec_cols), ((0, 3), (0, enc_cols - dec_cols))),
        ]
    )
    units, events = gather_plan(ext, [s.shape for s in shards])
    gathered, vec_parts, weight_sum = gather(
        shards, vec_part, jnp.full((8, 128), weight_part, jnp.float32), sizes, units, events
    )

    all_images = counts.shape[0]
    per = -(-all_images // n_nar)
    first = narrow_at * per
    start = jnp.minimum(first, all_images - per)
    live = (start + jnp.arange(per) >= first).astype(jnp.float32)
    pick = lambda x: lax.dynamic_slice_in_dim(x, start, per, 0)
    patches, vis_index, keep_mask, counts = map(pick, (patches, vis_index, keep_mask, counts))
    dec_rows, enc_rows = -(-NP // 16) * 16, -(-KEEP_MOST // 16) * 16
    patches = jnp.pad(patches, ((0, 0), (0, dec_rows - NP), (0, 0)))
    vis = jnp.pad(vis_index, ((0, 0), (0, enc_rows - KEEP_MOST)), constant_values=-1)
    loss_w = jnp.where(keep_mask == 1, VISIBLE_WEIGHT, 1.0) * live[:, None]
    loss_w = jnp.pad(loss_w, ((0, 0), (0, dec_rows - NP)))
    grads, vec_grad = compute(
        [g.reshape(n_nar, -1, g.shape[-1]) for g in gathered],
        patches, vis[:, :, None], vis[:, None, :], loss_w[:, :, None], vec_parts, weight_sum, counts,
    )
    heads = (ext["n"], ext["h"], ext["l"], ext["w"], 2)
    blocked = [g.reshape(heads + (-1, g.shape[-1])) for g in grads]
    units, events = reduce_plan(ext, [g.shape[-2:] for g in blocked])
    owned, vec_sum, squares = reduce_scatter(blocked, vec_grad, sizes, units, events, [True] * 5 + [False] * 5)
    loss_total = vec_sum[13, 0]
    enc_vec, dec_vec = vec_sum[0:6], vec_sum[6:13, : n_nar * dec_cols]
    eq, out, up, down, bridge, dqkv, dout, dup, ddown, head = owned
    enc_owned = [
        eq[:, enc_qkv.shape[1] :], heads_together(eq[:, : enc_qkv.shape[1]], DH),
        out[:, : enc_out.shape[0]], up, down, bridge,
    ]
    dec_owned = [heads_together(dqkv, DHD), dout, dup, ddown, head[:, : w_head.shape[1]]]
    enc_sq = squares[0, 0] + jnp.sum(jnp.square(enc_vec))
    dec_sq = squares[1, 0] + jnp.sum(jnp.square(dec_vec))
    norms = jnp.sqrt(jnp.stack([enc_sq, dec_sq]))
    clip_factor = jnp.minimum(1.0, CLIP_NORM / jnp.sqrt(enc_sq + dec_sq))
    enc_new, enc_small_new, enc_big_new = shampoo(
        [clip_factor * g for g in enc_owned], masters[:6], ENC_KINDS, enc_small, enc_big, LR_MATRIX * LAYER_DECAY
    )
    dec_new, dec_small_new, dec_big_new = shampoo(
        [clip_factor * g for g in dec_owned], masters[6:], DEC_KINDS, dec_small, dec_big, LR_MATRIX
    )
    own_vec = jnp.concatenate(
        [
            lax.dynamic_slice_in_dim(enc_vec, narrow_at * enc_cols, enc_cols, 1).reshape(1, -1),
            lax.dynamic_slice_in_dim(dec_vec, narrow_at * dec_cols, dec_cols, 1).reshape(1, -1),
        ],
        axis=1,
    )
    vectors_new, first_new, second_new = adam(
        clip_factor * own_vec, vectors, first_moment, second_moment, step_count, 6 * enc_cols
    )
    return (
        *enc_new, *dec_new, enc_small_new, enc_big_new, dec_small_new, dec_big_new,
        vectors_new, first_new, second_new, norms, loss_total, weight_sum[0, 0],
    )


def solution(mesh):
    sizes = (mesh.shape["dp"], mesh.shape["wide"], mesh.shape["narrow"])
    rows = P(("dp", "wide"))
    matrix = P(("dp", "wide"), "narrow")
    turned = P("narrow", ("dp", "wide"))
    matrices = tuple(matrix if kind else turned for kind in ENC_KINDS + DEC_KINDS)
    stats = (P(("dp", "wide"), "narrow"),) * 4
    packed = (P("narrow"),) * 3
    in_specs = (rows, rows, rows, rows, P()) + matrices + packed + stats
    out_specs = matrices + stats + packed + (P(), P(), P())
    return jax.shard_map(
        functools.partial(per_device, sizes), mesh=mesh, in_specs=in_specs, out_specs=out_specs, check_vma=False
    )
```

```python
import functools

import jax
import jax.numpy as jnp
import numpy as np
from jax import lax
from jax.experimental import pallas as pl
from jax.experimental.pallas import tpu as pltpu
from jax.sharding import PartitionSpec as P

D = 768
DH = 64
DD = 512
DHD = 32
PIX = 768
NP = 196
BLOCK = 64
NEWTON = 3
KEEP_MOST = 98

HIGH = lax.Precision.HIGHEST
EPS_NORM = 1e-06
VISIBLE_WEIGHT = 0.1
STAT_DECAY = 0.5
LR_MATRIX = 0.2
LR_VECTOR = 0.2
LAYER_DECAY = 0.75
BETA_FIRST = 0.9
BETA_SECOND = 0.999
EPS_ADAM = 1e-08
CLIP_NORM = 1.0
ENC_KINDS = (True, True, False, True, False, True)
DEC_KINDS = (True, False, True, False, True)


MESHT = pl.DeviceIdType.MESH
FULL_CODE = 32767.0
FLOOR = 1e-30


def xors(n):
    return list(range(1, n))


def extents(sizes):
    n_dp, n_wide, n_nar = sizes
    return {"n": n_nar, "h": n_dp // 2, "l": 2, "w": n_wide // 2}


def phases_of(order, ext):
    return [d for d in order if ext[d] > 1]


def messages(order, ext):
    out, left = [], 1
    for d in ext:
        left *= ext[d]
    for d in phases_of(order, ext):
        left //= ext[d]
        out.append((d, ext[d] - 1, left))
    return out


class Place:
    def __init__(self, sizes):
        self.sizes = sizes
        self.ext = extents(sizes)
        self.dp, self.wi, self.na = (lax.axis_index(x) for x in ("dp", "wide", "narrow"))
        self.own = {"n": self.na, "h": self.dp // 2, "l": self.dp % 2, "w": self.wi // 2}
        self.core = self.wi % 2

    def peer(self, dim, k):
        if dim == "n":
            return {"narrow": self.na ^ k}
        if dim == "h":
            return {"dp": self.dp ^ (2 * k)}
        if dim in "ld":
            return {"dp": self.dp ^ k}
        if dim == "w":
            return {"wide": self.wi ^ (2 * k)}
        return {"wide": self.wi ^ 1}

    def greet(self):
        ext = self.ext
        partners = [self.peer(d, k) for d in "nw" for k in xors(ext[d])]
        partners += [self.peer("d", k) for k in xors(self.sizes[0])] + [self.peer("c", 1)]
        barrier = pltpu.get_barrier_semaphore()
        for p in partners:
            pl.semaphore_signal(barrier, inc=1, device_id=p, device_id_type=MESHT)
        pl.semaphore_wait(barrier, len(partners))

    def hops(self, narrow):
        out = [("c", 2, self.core), ("d", self.sizes[0], self.dp)]
        if self.ext["w"] > 1:
            out.append(("w", self.ext["w"], self.wi // 2))
        if narrow and self.ext["n"] > 1:
            out.append(("n", self.ext["n"], self.na))
        return out


def remote(src, dst, ss, rs, dev):
    return pltpu.make_async_remote_copy(
        src_ref=src, dst_ref=dst, send_sem=ss, recv_sem=rs, device_id=dev, device_id_type=MESHT
    )


class SmallSum:
    def __init__(self, place, value, lands, send, recv, narrow):
        self.place, self.value, self.lands, self.send, self.recv = place, value, lands, send, recv
        self.axes = place.hops(narrow)
        self.flight = None

    def start(self, i):
        d, members, at = self.axes[i]
        land = self.lands[i]
        land[at] = self.value[...]
        self.flight = []
        for k in xors(members):
            c = remote(self.value, land.at[at], self.send.at[i, k - 1], self.recv.at[i, k - 1], self.place.peer(d, k))
            c.start()
            self.flight.append(c)

    def finish(self, i):
        d, members, at = self.axes[i]
        for c in self.flight:
            c.wait()
        total = self.lands[i][0]
        for j in range(1, members):
            total = total + self.lands[i][j]
        self.value[...] = total

    @staticmethod
    def scratch(sizes, shape, narrow):
        members = [2, sizes[0]] + ([sizes[1] // 2] if sizes[1] > 2 else []) + ([sizes[2]] if narrow and sizes[2] > 1 else [])
        return [pltpu.VMEM((m,) + shape, jnp.float32) for m in members]

    @staticmethod
    def sems(sizes):
        return [pltpu.SemaphoreType.DMA((4, max(*sizes, 2)))] * 2


def plan(units, events, mats, ext, tokens):
    flat = []
    for step in events:
        for u, p in step:
            if p <= len(phases_of(units[u][3], ext)) + 3:
                flat.append((u, p))
    at = {e: i for i, e in enumerate(flat)}
    blocks = ext["h"] * ext["l"] * ext["w"]
    wants = []
    big = max((mats[m][0] for m, *_ in units)), max(hi - lo for m, lo, hi, o in units)
    first_use, last_need = {}, {}
    for u, (m, lo, hi, order) in enumerate(units):
        a, c = mats[m][0], hi - lo
        for x, g, *_ in terms_of(mats, m, lo, hi):
            first_use[x] = min(first_use.get(x, (len(flat),)), (at[u, 0], at[u, 1], tokens[g], a))
            last_need[x] = max(last_need.get(x, 0), at[u, 3])
        last = at[u, len(phases_of(order, ext)) + 3]
        full = (ext["n"], blocks) + (big if a * c * 5 > 2 * big[0] * big[1] else (a, c))
        for j, (x, g, c_lo, c_hi, g_lo) in enumerate(terms_of(mats, m, lo, hi)):
            wants.append((at[u, 0], at[u, 3], ("g", u, j), (ext["n"], tokens[g], c_hi - c_lo), "b"))
        wants.append((at[u, 1], at[u, 3], ("out", u), full, "f"))
        wants.append((at[u, 2], at[u, 3], ("stage", u), full, "f"))
        wants.append((at[u, 3], at[u, 3], ("acc", u), full, "f"))
        wants.append((at[u, 3], last, ("kept", u), (messages(order, ext)[0][2], a, c), "f"))
        for p, (d, k, n) in enumerate(messages(order, ext)):
            wants.append((at[u, p + 3], last, ("q", u, p), (k, n, a, c), "q"))
    for x, (start, turn, rows, a) in first_use.items():
        turn = min(at[u, 1] for u, (m, lo, hi, o) in enumerate(units) if any(x == t[0] for t in terms_of(mats, m, lo, hi)))
        wants.append((start, turn, ("plain", x), (rows, 2 * blocks * a), "b"))
        wants.append((start, last_need[x], ("turned", x), (blocks, 2, a, rows), "b"))
    wants.sort(key=lambda w: w[0])
    bufs, where = [], {}
    for start, end, name, shape, kind in wants:
        for i, b in enumerate(bufs):
            if b[0] == (shape, kind) and b[1] < start:
                b[1] = end
                where[name] = i
                break
        else:
            bufs.append([(shape, kind), end])
            where[name] = len(bufs) - 1
    return [b[0] for b in bufs], where


def terms_of(mats, m, lo, hi):
    out = []
    for x, g, first, width in mats[m][2]:
        a, b = max(lo, first), min(hi, first + width)
        if a < b:
            out.append((x, g, a - lo, b - lo, a - first))
    out.sort(key=lambda t: t[2] - t[3])
    return out


def reduce_kernel(sizes, units, events, mats, n_left, n_right, planned, is_enc, *refs):
    place = Place(sizes)
    ext, own, core = place.ext, place.own, place.core
    count, nu = len(mats), len(units)
    blocks = ext["h"] * ext["l"] * ext["w"]
    f32 = jnp.float32
    it = iter(refs)
    take = lambda k: [next(it) for _ in range(k)]
    lefts, rights = take(n_left), take(n_right)
    vec = next(it)
    outs = take(count)
    vec_out, sq_out = take(2)
    land = take(nu)
    kinds, where = planned
    pool = [tuple(take(2)) if kind == "q" else take(1)[0] for _, kind in kinds]
    recv_q, recv_s = [], []
    for u in range(nu):
        k = len(messages(units[u][3], ext))
        recv_q.append(take(k))
        recv_s.append(take(k))
    plain = [pool[where["plain", x]] for x in range(n_left)]
    turned = [pool[where["turned", x]] for x in range(n_left)]
    n_axes = len(place.hops(True))
    vec_land, sq_land = take(n_axes), take(n_axes)
    (core_send, core_recv, stage_sem, g_sem, x_sem, q_send, q_recv, s_send, s_recv, v_send, v_recv, t_send, t_recv) = take(13)
    left_copies = {}
    place.greet()
    small = SmallSum(place, vec_out, vec_land, v_send, v_recv, True)
    vec_out[...] = vec[...]
    squares = SmallSum(place, sq_out, sq_land, t_send, t_recv, True)

    pending = []
    last_use = {}
    flight = {}
    sums = [jnp.zeros((1, 1), f32), jnp.zeros((1, 1), f32)]
    ready = set()

    def turn(k):
        if k in ready:
            return
        ready.add(k)
        left_copies[k].wait()
        t = plain[k][...].T
        a = turned[k].shape[2]
        if a % 16 == 0:
            turned[k][...] = t.reshape(turned[k].shape)
        else:
            for i in range(2 * blocks):
                turned[k][i // 2, i % 2] = t[i * a : (i + 1) * a]

    def product(u, n, which, ref_of):
        m, lo, hi, order = units[u]
        a, c = mats[m][0], hi - lo
        for j, (x, g, c_lo, c_hi, g_lo) in enumerate(terms_of(mats, m, lo, hi)):
            right = pool[where["g", u, j]][n]
            if a % 16 == 0:
                rows = turned[x][:, which].reshape(blocks * a, turned[x].shape[3])
                v = lax.dot_general(rows, right, (((1,), (0,)), ((), ())), preferred_element_type=f32)
                v = v.reshape(blocks, a, c_hi - c_lo)
                if j == 0:
                    ref_of[n] = v
                else:
                    ref_of[n, :, :, c_lo:c_hi] += v
            else:
                for b in range(blocks):
                    v = lax.dot_general(turned[x][b, which], right, (((1,), (0,)), ((), ())), preferred_element_type=f32)
                    if j == 0:
                        ref_of[n, b] = v
                    else:
                        ref_of[n, b, :, c_lo:c_hi] += v

    def whole(kind, u):
        m, lo, hi, order = units[u]
        ref = pool[where[kind, u]]
        a, c = mats[m][0], hi - lo
        return ref if ref.shape[2:] == (a, c) else ref.at[:, :, pl.ds(0, a), pl.ds(0, c)]

    def block_of(idx):
        return (idx["h"] * ext["l"] + idx["l"]) * ext["w"] + idx["w"]

    def slab(u, idx):
        at = 0
        for d in "nhlw":
            if d != phases_of(units[u][3], ext)[0]:
                at = at * ext[d] + idx[d]
        return pool[where["kept", u]].at[at]

    def split(s, dims):
        idx = {}
        for d in reversed(dims):
            if ext[d] == 1:
                idx[d] = 0
            else:
                idx[d] = s % ext[d]
                s = s // ext[d]
        return idx

    def loop(total, body):
        def step(s, carry):
            body(s)
            return carry
        lax.fori_loop(0, total, step, 0)

    def reuse(b):
        for c in last_use.pop(b, []):
            c.wait_send()

    def code_and_send(u, p):
        ph = phases_of(units[u][3], ext)
        d, peers, slabs = messages(units[u][3], ext)[p]
        gone = ph[:p]
        free = [x for x in "nhlw" if x != d and x not in gone]
        b = where["q", u, p]
        reuse(b)
        out_q, out_s = pool[b]
        sends = []
        for k in range(1, peers + 1):
            def body(s):
                idx = split(s, free)
                for x in gone:
                    idx[x] = own[x]
                idx[d] = own[d] ^ k
                x = (whole("acc", u).at[idx["n"], block_of(idx)] if p == 0 else slab(u, idx))[...]
                top = jnp.maximum(jnp.max(jnp.abs(x), axis=0, keepdims=True), FLOOR)
                out_q[k - 1, s] = jnp.round(x * (FULL_CODE / top)).astype(jnp.int32).astype(jnp.int16)
                out_s[k - 1, s] = top * (1.0 / FULL_CODE)
            loop(slabs, body)
            dev = place.peer(d, k)
            first = remote(out_q.at[k - 1], recv_q[u][p].at[k - 1], q_send.at[u, p, k - 1], q_recv.at[u, p, k - 1], dev)
            second = remote(out_s.at[k - 1], recv_s[u][p].at[k - 1], s_send.at[u, p, k - 1], s_recv.at[u, p, k - 1], dev)
            first.start()
            second.start()
            sends += [first, second]
        flight[u, p] = sends
        last_use[b] = sends

    def take_in(u, p):
        ph = phases_of(units[u][3], ext)
        d, peers, slabs = messages(units[u][3], ext)[p]
        gone = ph[: p + 1]
        free = [x for x in "nhlw" if x not in gone]
        for c in flight[u, p]:
            c.wait_recv()
        def body(s):
            idx = split(s, free)
            for x in gone:
                idx[x] = own[x]
            ref = slab(u, idx)
            v = ref[...]
            for k in range(peers):
                v = v + recv_q[u][p][k, s].astype(jnp.int32).astype(f32) * recv_s[u][p][k, s]
            ref[...] = v
        loop(slabs, body)

    def stage(u, p):
        m, lo, hi, order = units[u]
        n_ph = len(phases_of(order, ext))
        if p == 0:
            copies = []
            for j, (x, g, c_lo, c_hi, g_lo) in enumerate(terms_of(mats, m, lo, hi)):
                if x not in left_copies:
                    left_copies[x] = pltpu.make_async_copy(lefts[x], plain[x], x_sem.at[x])
                    left_copies[x].start()
                src = rights[g]
                if c_hi - c_lo != src.shape[2]:
                    src = src.at[:, :, slice(g_lo, g_lo + c_hi - c_lo)]
                c = pltpu.make_async_copy(src, pool[where["g", u, j]], g_sem.at[u, j])
                c.start()
                copies.append(c)
            flight[u, "g"] = copies
        elif p == 1:
            for c in flight[u, "g"]:
                c.wait()
            for x, *_ in terms_of(mats, m, lo, hi):
                turn(x)
            b = where["out", u]
            reuse(b)
            loop(ext["n"], lambda n: product(u, n, 1 - core, whole("out", u)))
            c = remote(whole("out", u), land[u], core_send.at[u], core_recv.at[u], place.peer("c", 1))
            c.start()
            flight[u, "core"] = c
            last_use[b] = [c]
        elif p == 2:
            flight[u, "core"].wait_recv()
            reuse(where["stage", u])
            c = pltpu.make_async_copy(land[u], whole("stage", u), stage_sem.at[u])
            c.start()
            flight[u, "stage"] = c
        elif p == 3:
            acc, more = whole("acc", u), whole("stage", u)
            reuse(where["acc", u])
            flight[u, "stage"].wait()
            def body(n):
                product(u, n, core, acc)
                acc[n] = acc[n] + more[n]
            loop(ext["n"], body)
            code_and_send(u, 0)
            d, peers, slabs = messages(order, ext)[0]
            def keep(i):
                idx = split(i, [x for x in "nhlw" if x != d])
                idx[d] = own[d]
                slab(u, idx)[...] = acc.at[idx["n"], block_of(idx)][...]
            loop(slabs, keep)
        else:
            take_in(u, p - 4)
            if p - 3 < n_ph:
                code_and_send(u, p - 3)
            else:
                x = slab(u, own)[...]
                outs[m][:, pl.ds(lo, hi - lo)] = x
                w = 0 if is_enc[m] else 1
                sums[w] = sums[w] + jnp.sum(x * x, keepdims=True)

    hop = 0
    for step in events:
        for u, p in step:
            if p <= len(phases_of(units[u][3], ext)) + 3:
                stage(u, p)
                if p == 3 and hop <= n_axes:
                    if hop:
                        small.finish(hop - 1)
                    if hop < n_axes:
                        small.start(hop)
                    hop += 1
    while hop <= n_axes:
        if hop:
            small.finish(hop - 1)
        if hop < n_axes:
            small.start(hop)
        hop += 1
    row = lax.broadcasted_iota(jnp.int32, (8, 128), 0)
    sq_out[...] = jnp.where(row == 0, sums[0], jnp.where(row == 1, sums[1], 0.0))
    for i in range(n_axes):
        squares.start(i)
        squares.finish(i)
    for c in [c for cs in last_use.values() for c in cs]:
        c.wait_send()


def reduce_scatter(lefts, rights, mats, vec, sizes, units, events, is_enc, cid=1):
    ext = extents(sizes)
    blocks = ext["h"] * ext["l"] * ext["w"]
    f32, bf16 = jnp.float32, jnp.bfloat16
    tokens = [r.shape[1] for r in rights]
    planned = plan(units, events, mats, ext, tokens)
    coded = lambda k, n, a, c: [pltpu.VMEM((k, n, a, c), jnp.int16), pltpu.VMEM((k, n, 1, c), f32)]
    scratch = []
    for shape, kind in planned[0]:
        scratch += coded(*shape) if kind == "q" else [pltpu.VMEM(shape, f32 if kind == "f" else bf16)]
    for m, lo, hi, order in units:
        ms = [coded(k, n, mats[m][0], hi - lo) for d, k, n in messages(order, ext)]
        scratch += [x[0] for x in ms] + [x[1] for x in ms]
    scratch += SmallSum.scratch(sizes, vec.shape, True) + SmallSum.scratch(sizes, (8, 128), True)
    nu, kmax = len(units), max(ext.values())
    D_ = pltpu.SemaphoreType.DMA
    scratch += [D_((nu,))] * 3 + [D_((nu, 2)), D_((len(lefts),))] + [D_((nu, 4, kmax))] * 4 + SmallSum.sems(sizes) * 2
    vm = pl.BlockSpec(memory_space=pltpu.VMEM)
    an = pl.BlockSpec(memory_space=pl.ANY)
    res = pl.pallas_call(
        functools.partial(reduce_kernel, sizes, units, events, mats, len(lefts), len(rights), planned, is_enc),
        out_shape=[jax.ShapeDtypeStruct(m[:2], f32) for m in mats]
        + [jax.ShapeDtypeStruct(vec.shape, f32), jax.ShapeDtypeStruct((8, 128), f32)]
        + [jax.ShapeDtypeStruct((ext["n"], blocks, mats[m][0], hi - lo), f32) for m, lo, hi, o in units],
        in_specs=[an] * (len(lefts) + len(rights)) + [vm],
        out_specs=[vm] * (len(mats) + 2) + [an] * nu,
        scratch_shapes=scratch,
        compiler_params=pltpu.CompilerParams(collective_id=cid, has_side_effects=True, vmem_limit_bytes=60 << 20),
    )(*lefts, *rights, vec)
    return res[: len(mats)], res[len(mats)], res[len(mats) + 1]


def gather_kernel(sizes, units, events, count, *refs):
    place = Place(sizes)
    extent, own, core, na, peer = place.ext, place.own, place.core, place.na, place.peer
    n_axes = len(place.hops(False))
    it = iter(refs)
    take = lambda k: [next(it) for _ in range(k)]
    shards = take(count)
    vec, weight = take(2)
    outs = take(count)
    vec_all, weight_sum = take(2)
    weight_land = take(n_axes)
    send_sem, recv_sem, loc_sem, vec_send, vec_recv, sum_send, sum_recv = take(7)
    place.greet()
    pending = []
    sib_recv = []
    vec_flight = []
    for k in xors(extent["n"]):
        c = remote(vec, vec_all.at[na], vec_send.at[k - 1], vec_recv.at[k - 1], peer("n", k))
        c.start()
        vec_flight.append(c)
    vec_all[na] = vec[...]
    weight_sum[...] = weight[...]
    small = SmallSum(place, weight_sum, weight_land, sum_send, sum_recv, False)
    slot_of = [0] * len(units)
    def region(u, full, at, which_core):
        m, lo, hi, order = units[u]
        idx = []
        for d in "nhlw":
            if d in full: idx.append(slice(None))
            elif at and d == at[0]: idx.append(own[d] ^ at[1])
            else: idx.append(own[d])
        r = outs[m].at[tuple(idx) + (which_core,)]
        if (lo, hi) != (0, shards[m].shape[1]):
            r = outs[m].at[tuple(idx) + (which_core, slice(None), slice(lo, hi))]
        return r
    def send(u, src, dst, dev, recv_view):
        s = slot_of[u]; slot_of[u] += 1
        c = remote(src, dst, send_sem.at[u, s], recv_sem.at[u, s], dev)
        c.start()
        pending.append(c)
        return remote(recv_view, recv_view, send_sem.at[u, s], recv_sem.at[u, s], dev)
    def shard(u):
        m, lo, hi, order = units[u]
        return shards[m] if (lo, hi) == (0, shards[m].shape[1]) else shards[m].at[:, slice(lo, hi)]
    state = {}
    def phases(u):
        return [d for d in units[u][3] if extent[d] > 1]
    def stage(u, p):
        ph = phases(u)
        if p == 0:
            lc = pltpu.make_async_copy(shard(u), region(u, (), None, core), loc_sem.at[u]); lc.start()
            sib_recv.append(send(u, shard(u), region(u, (), None, core), peer("c", 1), region(u, (), None, 1 - core)))
            src = shard(u)
            state[u] = []
            state[u, "loc"] = lc
        else:
            done = ph[:p - 1]
            for k, w in state[u]:
                w.wait_recv()
            for k, w in state[u]:
                here = region(u, done, (ph[p - 1], k), core)
                there = region(u, done, (ph[p - 1], k), 1 - core)
                state[u, k] = (here, there)
            if p == 1: state[u, "loc"].wait()
            src = None
        old = state[u]
        state[u] = []
        if p < len(ph):
            full = ph[:p]
            for k in xors(extent[ph[p]]):
                mine = region(u, full, None, core) if src is None else src
                w = send(u, mine, region(u, full, None, core), peer(ph[p], k), region(u, full, (ph[p], k), core))
                state[u].append((k, w))
        if p > 0:
            for k, _ in old:
                here, there = state[u, k]
                sib_recv.append(send(u, here, here, peer("c", 1), there))
    for t, step in enumerate(events):
        for u, p in step:
            if p <= len(phases(u)):
                stage(u, p)
        if 0 < t <= n_axes:
            small.finish(t - 1)
        if t < n_axes:
            small.start(t)
    for c in vec_flight:
        c.wait()
    for c in pending:
        c.wait_send()
    for w in sib_recv:
        w.wait_recv()


def gather(shards, vec, weight, sizes, units, events, cid=0):
    n_dp, n_wide, n_nar = sizes
    count = len(shards)
    ext = extents(sizes)
    slots = 2 * sum(ext.values())
    nu = len(units)
    DMA = pltpu.SemaphoreType.DMA
    an = pl.BlockSpec(memory_space=pl.ANY)
    vm = pl.BlockSpec(memory_space=pltpu.VMEM)
    heads = (ext["n"], ext["h"], ext["l"], ext["w"], 2)
    res = pl.pallas_call(
        functools.partial(gather_kernel, sizes, units, events, count),
        out_shape=[jax.ShapeDtypeStruct(heads + s.shape, s.dtype) for s in shards]
        + [jax.ShapeDtypeStruct((n_nar,) + vec.shape, vec.dtype), jax.ShapeDtypeStruct(weight.shape, weight.dtype)],
        in_specs=[an] * count + [vm, vm],
        out_specs=[an] * count + [vm, vm],
        scratch_shapes=SmallSum.scratch(sizes, weight.shape, False)
        + [DMA((nu, slots)), DMA((nu, slots)), DMA((nu,)), DMA((n_nar,)), DMA((n_nar,))]
        + SmallSum.sems(sizes),
        compiler_params=pltpu.CompilerParams(collective_id=cid, has_side_effects=True),
    )(*shards, vec, weight)
    return res[:count], res[count], res[count + 1]


def gather_plan(ext, shapes):
    cols = [s[1] for s in shapes]
    if ext["w"] > 1:
        units = [(m, 0, c, "nlhw") for m, c in enumerate(cols)]
        return units, [[(u, p)] for u in range(len(units)) for p in range(5)]
    A, B, XA, XB = "nlhw", "nhlw", "lhnw", "hlnw"
    half = cols[2] // 2
    groups = [
        [(1, 0, cols[1], A), (0, 0, 256, B)],
        [(0, 256, 512, A), (0, 512, cols[0], B)],
        [(2, 0, half, A), (3, 0, half, B)],
        [(2, half, cols[2], A), (3, half, cols[3], B)],
        [(7, 0, cols[7], A), (8, 0, cols[8], B)],
        [(4, 0, cols[4], A)],
    ]
    extra = [(5, 0, cols[5], XA), (9, 0, cols[9], XB), (6, 0, cols[6], XB)]
    units, ids = [], []
    for g in groups:
        ids.append(list(range(len(units), len(units) + len(g))))
        units += g
    more = list(range(len(units), len(units) + len(extra)))
    units += extra
    events = []
    for t in range(len(groups) + 3):
        step = []
        for p in range(4):
            if 0 <= t - p < len(groups):
                step += [(u, p) for u in ids[t - p]]
        for p, when in enumerate((0, 1, 5, 8)):
            if t == when:
                step += [(u, p) for u in more]
        events.append(step)
    return units, events


REDUCE_UNITS = (
    (0, 0, 256, "hlwn"), (0, 256, 512, "lhwn"), (0, 512, 768, "lhwn"), (1, 0, 256, "hlwn"), (2, 0, 384, "hlwn"),
    (2, 384, 768, "nlhw"), (3, 0, 384, "hnlw"), (3, 384, 768, "lhwn"), (4, 0, 128, "lnhw"), (5, 0, 384, "hlwn"),
    (6, 0, 128, "hlwn"), (7, 0, 256, "hlwn"), (7, 256, 512, "hlwn"), (8, 0, 256, "nlhw"), (8, 256, 512, "lhwn"),
    (9, 0, 256, "nlhw"),
)
REDUCE_ORDER = (
    (8, 0), (9, 0), (8, 1), (9, 1), (8, 2), (8, 3), (9, 2), (10, 0), (10, 1), (9, 3), (10, 2), (13, 0), (8, 4),
    (10, 3), (13, 1), (6, 0), (6, 1), (13, 2), (8, 5), (13, 3), (9, 4), (6, 2), (5, 0), (10, 4), (8, 6), (5, 1),
    (6, 3), (9, 5), (10, 5), (4, 0), (5, 2), (4, 1), (5, 3), (13, 4), (9, 6), (4, 2), (7, 0), (10, 6), (7, 1), (4,
    3), (13, 5), (6, 4), (7, 2), (0, 0), (0, 1), (7, 3), (1, 0), (0, 2), (1, 1), (0, 3), (3, 0), (4, 4), (13, 6),
    (1, 2), (3, 1), (1, 3), (5, 4), (3, 2), (15, 0), (7, 4), (0, 4), (3, 3), (15, 1), (4, 5), (6, 5), (2, 0), (15,
    2), (7, 5), (2, 1), (15, 3), (1, 4), (11, 0), (4, 6), (2, 2), (11, 1), (5, 5), (3, 4), (2, 3), (7, 6), (0, 5),
    (6, 6), (5, 6), (1, 5), (11, 2), (14, 0), (14, 1), (3, 5), (11, 3), (12, 0), (14, 2), (12, 1), (14, 3), (15,
    4), (2, 4), (12, 2), (0, 6), (11, 4), (12, 3), (1, 6), (14, 4), (2, 5), (15, 5), (3, 6), (11, 5), (12, 4), (2,
    6), (14, 5), (15, 6), (11, 6), (12, 5), (14, 6), (12, 6),
)


def reduce_plan(ext, mats):
    if ext["w"] > 1:
        units = [(m, lo, min(lo + 256, x[1]), "wlhn") for m, x in enumerate(mats) for lo in range(0, x[1], 256)]
        return units, [[(u, p)] for u in range(len(units)) for p in range(8)]
    return list(REDUCE_UNITS), [list(REDUCE_ORDER)]


def matmul_hi(left, right):
    return jnp.matmul(left, right, precision=lax.Precision.HIGH)


def sincos_table(rows, width):
    column = np.arange(width)
    freq = np.power(np.float32(10000.0), (-(2 * (column // 2)).astype(np.float32) / np.float32(width)).astype(np.float32))
    angle = (np.arange(rows, dtype=np.float32)[:, None] * freq[None, :]).astype(np.float32)
    return np.where(column % 2 == 0, np.sin(angle), np.cos(angle)).astype(np.float32)


def dot_nn(a, b):
    return lax.dot_general(a, b, (((1,), (0,)), ((), ())), preferred_element_type=jnp.float32)


def dot_nt(a, b):
    return lax.dot_general(a, b, (((1,), (1,)), ((), ())), preferred_element_type=jnp.float32)


def dot_tn(a, b):
    return lax.dot_general(a, b, (((0,), (0,)), ((), ())), preferred_element_type=jnp.float32)


def dot_exact(a, b):
    return lax.dot_general(a, b, (((1,), (0,)), ((), ())), precision=HIGH, preferred_element_type=jnp.float32)


class Side:
    def __init__(self, width, head, heads, rows, images, slabs):
        self.width, self.head, self.heads, self.rows = width, head, heads, rows
        self.slabs = slabs
        self.tokens = rows * images
        self.lane = head * heads
        self.packed = -(-3 * self.lane // 128) * 128

    def scratch(self, hidden):
        t, n, w = self.tokens, self.slabs, self.width
        bf, f = jnp.bfloat16, jnp.float32
        return {
            "x": ((t, w), f),
            "hat1": ((t, w), f), "hat2": ((t, w), f), "hat3": ((t, w), f),
            "inv": ((t, 128), f),
            "n1": ((t, w), bf), "n2": ((t, w), bf), "n3": ((t, w), bf),
            "qkv": ((n, t, self.packed), bf),
            "lse": ((t, 128), f),
            "att": ((n, t, -(-self.lane // 128) * 128), bf),
            "slope": ((n, t, hidden), f),
            "act": ((n, t, hidden), bf),
            "dn": ((t, w), f),
            "og1": ((t, w), bf),
            "og2": ((t, w), bf),
        }


LEFTS = ("e_n1", "chosen", "e_og1", "e_n2", "e_og2", "e_n3", "d_n1", "d_og1", "d_n2", "d_og2", "d_n3")
RIGHTS = ("e_qkv", "part0", "e_att", "e_dh", "e_act", "part4", "d_qkv", "d_att", "d_dh", "d_act", "part9")
SHIPPED = LEFTS + RIGHTS
BUFFER_OF = {"e_dh": "e_act", "d_dh": "d_act"}


def compute_kernel(per, slabs, names, count, *refs):
    it = iter(refs)
    take = lambda k: [next(it) for _ in range(k)]
    hbm = take(count)
    patches, vis_col, vis_row, loss_w, vec_parts, weight_sum, table_e, table_d, counts = take(9)
    shipped = take(len(SHIPPED))
    vec_out = next(it)
    w = take(count)
    load_sem, store_sem = take(2)
    buf = dict(zip(names, it))
    w_eq, w_out, w_up, w_down, w_bridge, w_dqkv, w_dout, w_dup, w_ddown, w_head = w
    f32, bf16 = jnp.float32, jnp.bfloat16
    loads = []
    for m in range(count):
        c = pltpu.make_async_copy(hbm[m], w[m], load_sem.at[m])
        c.start()
        loads.append(c)
    waited = set()

    def need(m):
        if m not in waited:
            waited.add(m)
            loads[m].wait()


    enc_rows, dec_rows = vis_col.shape[1], patches.shape[1]
    enc_w, dec_w = table_e.shape[1], table_d.shape[1]
    enc = Side(enc_w, DH, w_out.shape[2] // DH, enc_rows, per, slabs)
    dec = Side(dec_w, DHD, w_dout.shape[2] // DHD, dec_rows, per, slabs)
    for s, tag in ((enc, "e_"), (dec, "d_")):
        s.tag = tag
        s.b = {k[2:]: v for k, v in buf.items() if k.startswith(tag)}
    enc.w, dec.w = (w_eq, w_out, w_up, w_down), (w_dqkv, w_dout, w_dup, w_ddown)
    enc.ids, dec.ids = (0, 1, 2, 3), (5, 6, 7, 8)
    enc.base, dec.base = 0, 7
    vec_full = buf["vec_full"]
    enc_c, dec_c = enc_w // slabs, dec_w // slabs
    for n in range(slabs):
        vec_full[0:6, pl.ds(n * enc_c, enc_c)] = vec_parts[n, 0:6, 0:enc_c]
        vec_full[6:13, pl.ds(n * dec_c, dec_c)] = vec_parts[n, 6:13, 0:dec_c]
    vec_out[...] = jnp.zeros_like(vec_out)

    def vector(k, width):
        return vec_full[k : k + 1, 0:width]

    CH = 32

    def chunks(total, body):
        def step(i, carry):
            body(pl.ds(pl.multiple_of(i * CH, CH), CH))
            return carry
        lax.fori_loop(0, total // CH, step, 0)

    def norm_fwd(s, k, out, hat, inv):
        gain, bias = vector(s.base + k, s.width), vector(s.base + k + 1, s.width)
        x = s.b["x"]
        def body(r):
            v = x[r, :]
            mean = jnp.mean(v, axis=1, keepdims=True)
            d = v - mean
            i = lax.rsqrt(jnp.mean(d * d, axis=1, keepdims=True) + EPS_NORM)
            h = d * i
            s.b[hat][r, :] = h
            s.b["inv"][r, inv : inv + 1] = i
            s.b[out][r, :] = (h * gain + bias).astype(bf16)
        chunks(s.tokens, body)

    def norm_bwd(s, k, hat, inv, add):
        gain = vector(s.base + k, s.width)
        def body(r):
            dn = s.b["dn"][r, :]
            h = s.b[hat][r, :]
            vec_out[s.base + k : s.base + k + 1, 0 : s.width] += jnp.sum(dn * h, axis=0, keepdims=True)
            vec_out[s.base + k + 1 : s.base + k + 2, 0 : s.width] += jnp.sum(dn, axis=0, keepdims=True)
            g = dn * gain
            d = s.b["inv"][r, inv : inv + 1] * (
                g - jnp.mean(g, axis=1, keepdims=True) - h * jnp.mean(g * h, axis=1, keepdims=True)
            )
            s.b["x"][r, :] = s.b["x"][r, :] + d if add else d
        chunks(s.tokens, body)

    def slab_loop(body):
        def step(n, carry):
            body(n)
            return carry
        lax.fori_loop(0, slabs, step, 0)

    def head_mask(s, h):
        lane = lax.broadcasted_iota(jnp.int32, (1, s.lane), 1)
        return (lane >= h * s.head) & (lane < (h + 1) * s.head)

    def scores(s, q, k, mask, limit):
        v = dot_nt(jnp.where(mask, q, jnp.zeros_like(q)), k) * (s.head ** -0.5)
        key = lax.broadcasted_iota(jnp.int32, (s.rows, s.rows), 1)
        return jnp.where(key < limit, v, -1e30)

    def attention_loop(body):
        def step(i, carry):
            image, n = i // slabs, i % slabs
            body(image, n)
            return carry
        lax.fori_loop(0, per * slabs, step, 0)

    def image_rows(s, image):
        return pl.ds(pl.multiple_of(image * s.rows, 16), s.rows)

    def block_fwd(s, limit):
        b = s.b
        b["lse"][...] = jnp.zeros_like(b["lse"])
        if b["att"].shape[2] != s.lane:
            b["att"][...] = jnp.zeros_like(b["att"])
        qkv_w, out_w, up_w, down_w = s.w
        need(s.ids[0])
        norm_fwd(s, 0, "n1", "hat1", 1)
        def qkv(n):
            b["qkv"][n] = dot_nn(b["n1"][...], qkv_w[n, :, 0 : s.packed]).astype(bf16)
        slab_loop(qkv)
        def attend(image, n):
            r = image_rows(s, image)
            q = b["qkv"][n, r, 0 : s.lane]
            k = b["qkv"][n, r, s.lane : 2 * s.lane]
            v = b["qkv"][n, r, 2 * s.lane : 3 * s.lane]
            lane = lax.broadcasted_iota(jnp.int32, (s.rows, 128), 1)
            total = jnp.zeros((s.rows, s.lane), f32)
            lse = b["lse"][r, :]
            for h in range(s.heads):
                mask = head_mask(s, h)
                sc = scores(s, q, k, mask, limit(image))
                top = jnp.max(sc, axis=1, keepdims=True)
                e = jnp.exp(sc - top)
                z = jnp.sum(e, axis=1, keepdims=True)
                p = (e / z).astype(bf16)
                total = jnp.where(mask, dot_nn(p, v), total)
                lse = jnp.where(lane == n * s.heads + h, top + jnp.log(z), lse)
            b["att"][n, r, 0 : s.lane] = total.astype(bf16)
            b["lse"][r, :] = lse
        attention_loop(attend)
        need(s.ids[1])
        ship(s.tag + "att")
        def project(n):
            b["x"][...] += dot_nt(b["att"][n, :, 0 : s.lane], out_w[n])
        slab_loop(project)
        norm_fwd(s, 2, "n2", "hat2", 2)
        need(s.ids[2])
        need(s.ids[3])
        hid = buf["hid"]
        c = up_w.shape[2]
        def mlp(n):
            hid[0 : s.tokens, 0:c] = dot_nn(b["n2"][...], up_w[n])
            def body(r):
                v = hid[r, 0:c]
                cdf = 0.5 * (1.0 + lax.erf(v * 0.7071067811865476))
                b["act"][n, r, :] = (v * cdf).astype(bf16)
                b["slope"][n, r, :] = cdf + v * (0.3989422804014327 * jnp.exp(-0.5 * v * v))
            chunks(s.tokens, body)
            b["x"][...] += dot_nt(b["act"][n], down_w[n])
        slab_loop(mlp)
        ship(s.tag + "act")
        norm_fwd(s, 4, "n3", "hat3", 3)
        for name in ("n1", "n2", "n3"):
            ship(s.tag + name)

    on_way = {}

    def ship(name):
        at = SHIPPED.index(name)
        c = pltpu.make_async_copy(buf[BUFFER_OF.get(name, name)], shipped[at], store_sem.at[at])
        c.start()
        on_way[name] = c

    def arrived(name):
        on_way.pop(name).wait()

    def block_bwd(s, limit):
        b = s.b
        qkv_w, out_w, up_w, down_w = s.w
        b["og2"][...] = b["x"][...].astype(bf16)
        ship(s.tag + "og2")
        b["dn"][...] = jnp.zeros_like(b["dn"])
        arrived(s.tag + "act")
        def down(n):
            b["act"][n] = (dot_nn(b["og2"][...], down_w[n]) * b["slope"][n]).astype(bf16)
            b["dn"][...] += dot_nt(b["act"][n], up_w[n])
        slab_loop(down)
        ship(s.tag + "dh")
        norm_bwd(s, 2, "hat2", 2, True)
        b["og1"][...] = b["x"][...].astype(bf16)
        ship(s.tag + "og1")
        arrived(s.tag + "att")
        def proj(n):
            b["att"][n, :, 0 : s.lane] = dot_nn(b["og1"][...], out_w[n]).astype(bf16)
        slab_loop(proj)
        def attend(image, n):
            r = image_rows(s, image)
            q = b["qkv"][n, r, 0 : s.lane]
            k = b["qkv"][n, r, s.lane : 2 * s.lane]
            v = b["qkv"][n, r, 2 * s.lane : 3 * s.lane]
            g = b["att"][n, r, 0 : s.lane]
            lane = lax.broadcasted_iota(jnp.int32, (s.rows, 128), 1)
            lse = b["lse"][r, :]
            dq = jnp.zeros((s.rows, s.lane), f32)
            dk = dq
            dv = dq
            for h in range(s.heads):
                mask = head_mask(s, h)
                level = jnp.sum(jnp.where(lane == n * s.heads + h, lse, 0.0), axis=1, keepdims=True)
                p = jnp.exp(scores(s, q, k, mask, limit(image)) - level)
                dp = dot_nt(jnp.where(mask, g, jnp.zeros_like(g)), v)
                dv = jnp.where(mask, dot_tn(p.astype(bf16), g), dv)
                ds = (p * (dp - jnp.sum(dp * p, axis=1, keepdims=True))).astype(bf16)
                dq = jnp.where(mask, dot_nn(ds, k), dq)
                dk = jnp.where(mask, dot_tn(ds, q), dk)
            scale = s.head ** -0.5
            if s.packed != 3 * s.lane:
                b["qkv"][n, r, 2 * s.lane : s.packed] = jnp.zeros((s.rows, s.packed - 2 * s.lane), bf16)
            b["qkv"][n, r, 0 : s.lane] = (dq * scale).astype(bf16)
            b["qkv"][n, r, s.lane : 2 * s.lane] = (dk * scale).astype(bf16)
            b["qkv"][n, r, 2 * s.lane : 3 * s.lane] = dv.astype(bf16)
        attention_loop(attend)
        ship(s.tag + "qkv")
        b["dn"][...] = jnp.zeros_like(b["dn"])
        def qkv(n):
            b["dn"][...] += dot_nt(b["qkv"][n], qkv_w[n, :, 0 : s.packed])
        slab_loop(qkv)
        norm_bwd(s, 0, "hat1", 1, True)

    chosen = buf["chosen"]
    need(0)
    for i in range(per):
        r = pl.ds(i * enc_rows, enc_rows)
        patch = lax.broadcasted_iota(jnp.int32, (enc_rows, dec_rows), 1)
        one = patch == vis_col[i]
        chosen[r, :] = dot_nn(one.astype(f32).astype(bf16), patches[i]).astype(bf16)
        enc.b["x"][r, :] = dot_exact(one.astype(f32), table_e[...])
    for n in range(slabs):
        lead = w_eq.shape[2] - 256
        part = dot_nn(chosen[...], w_eq[n, :, lead : lead + 256])
        enc.b["x"][:, n * enc_c : (n + 1) * enc_c] += part[:, 256 - enc_c : 256]
    ship("chosen")
    block_fwd(enc, lambda image: counts[image])
    need(4)
    bridged = buf["hid"]
    for n in range(slabs):
        bridged[0 : enc.tokens, n * dec_c : (n + 1) * dec_c] = dot_nn(enc.b["n3"][...], w_bridge[n])

    def hits(i, turned_way):
        if turned_way:
            patch = lax.broadcasted_iota(jnp.int32, (dec_rows, enc_rows), 0)
            slot = lax.broadcasted_iota(jnp.int32, (dec_rows, enc_rows), 1)
            return ((patch == vis_row[i]) & (slot < counts[i])).astype(f32)
        patch = lax.broadcasted_iota(jnp.int32, (enc_rows, dec_rows), 1)
        slot = lax.broadcasted_iota(jnp.int32, (enc_rows, dec_rows), 0)
        return ((patch == vis_col[i]) & (slot < counts[i])).astype(f32)

    for i in range(per):
        r = pl.ds(i * dec_rows, dec_rows)
        hit = hits(i, True)
        placed = dot_exact(hit, bridged[pl.ds(i * enc_rows, enc_rows), 0:dec_w])
        seen = jnp.sum(hit, axis=1, keepdims=True) > 0
        dec.b["x"][r, :] = jnp.where(seen, placed, vector(6, dec_w)) + table_d[...]
    block_fwd(dec, lambda image: NP)
    need(9)
    pred = buf["hid"]
    pix_c = w_head.shape[2]
    pix = patches.shape[2]
    for n in range(slabs):
        pred[0 : dec.tokens, n * pix_c : (n + 1) * pix_c] = dot_nn(dec.b["n3"][...], w_head[n])

    pgrad = buf["pgrad"]
    divisor = weight_sum[0:1, 0:1]
    loss = jnp.zeros((1, 1), f32)
    LC = 16
    for i in range(per):
        def lossy(j, total):
            r = pl.ds(pl.multiple_of(j * LC, LC), LC)
            px = patches[i, r, :].astype(f32)
            d = px - jnp.mean(px, axis=1, keepdims=True)
            target = d * lax.rsqrt(jnp.mean(d * d, axis=1, keepdims=True) + EPS_NORM)
            rr = pl.ds(pl.multiple_of(i * dec_rows + j * LC, LC), LC)
            error = pred[rr, 0:pix] - target
            weight = loss_w[i, r, :]
            pgrad[rr, :] = (2.0 * weight * error / divisor).astype(bf16)
            return total + jnp.sum(weight * error * error, keepdims=True)
        loss = lax.fori_loop(0, dec_rows // LC, lossy, loss)
    part9 = buf["part9"]
    part9[...] = jnp.zeros_like(part9)
    for n in range(slabs):
        part9[n, :, 0:pix_c] = pgrad[:, n * pix_c : (n + 1) * pix_c]
    dec.b["dn"][...] = jnp.zeros_like(dec.b["dn"])
    ship("part9")
    def head_bwd(n):
        dec.b["dn"][...] += dot_nt(part9[n, :, 0:pix_c], w_head[n])
    slab_loop(head_bwd)
    norm_bwd(dec, 4, "hat3", 3, False)
    block_bwd(dec, lambda image: NP)
    part4 = buf["part4"]
    for i in range(per):
        r = pl.ds(i * dec_rows, dec_rows)
        seen = jnp.sum(hits(i, True), axis=1, keepdims=True) > 0
        grad = dec.b["x"][r, :]
        vec_out[6:7, 0:dec_w] += jnp.sum(jnp.where(seen, 0.0, grad), axis=0, keepdims=True)
        back = dot_exact(hits(i, False), grad).astype(bf16)
        for n in range(slabs):
            part4[n, pl.ds(i * enc_rows, enc_rows), :] = back[:, n * dec_c : (n + 1) * dec_c]
    ship("part4")
    enc.b["dn"][...] = jnp.zeros_like(enc.b["dn"])
    def bridge_bwd(n):
        enc.b["dn"][...] += dot_nt(part4[n], w_bridge[n])
    slab_loop(bridge_bwd)
    norm_bwd(enc, 4, "hat3", 3, False)
    block_bwd(enc, lambda image: counts[image])

    part0 = buf["part0"]
    part0[...] = jnp.zeros_like(part0)
    for n in range(slabs):
        part0[n, :, 256 - enc_c : 256] = enc.b["x"][:, n * enc_c : (n + 1) * enc_c].astype(bf16)
    ship("part0")
    row = lax.broadcasted_iota(jnp.int32, (1, vec_out.shape[1]), 1)
    vec_out[13:14, :] = jnp.where(row >= 0, loss, 0.0)
    for name in list(on_way):
        arrived(name)


def compute(weights, patches, vis_col, vis_row, loss_w, vec_parts, weight_sum, counts):
    per, dec_rows, pix = patches.shape
    slabs = weights[0].shape[0]
    enc_rows = vis_col.shape[1]
    enc_w, dec_w = weights[0].shape[1], weights[5].shape[1]
    enc = Side(enc_w, DH, weights[1].shape[2] // DH, enc_rows, per, slabs)
    dec = Side(dec_w, DHD, weights[6].shape[2] // DHD, dec_rows, per, slabs)
    named = {}
    for s, tag, up in ((enc, "e_", weights[2]), (dec, "d_", weights[7])):
        for k, v in s.scratch(up.shape[2]).items():
            named[tag + k] = v
    f32, bf16 = jnp.float32, jnp.bfloat16
    top = max(enc.tokens, dec.tokens)
    named["hid"] = ((top, max(pix, weights[2].shape[2], weights[7].shape[2])), f32)
    named["vec_full"] = ((16, enc_w), f32)
    named["chosen"] = ((enc.tokens, pix), bf16)
    named["pgrad"] = ((dec.tokens, pix), bf16)
    up128 = lambda c: -(-c // 128) * 128
    named["part9"] = ((slabs, dec.tokens, up128(weights[9].shape[2])), bf16)
    named["part4"] = ((slabs, enc.tokens, weights[4].shape[2]), bf16)
    named["part0"] = ((slabs, enc.tokens, 256), bf16)
    ship_shapes = [jax.ShapeDtypeStruct(named[BUFFER_OF.get(k, k)][0], bf16) for k in SHIPPED]
    an = pl.BlockSpec(memory_space=pl.ANY)
    vm = pl.BlockSpec(memory_space=pltpu.VMEM)
    sm = pl.BlockSpec(memory_space=pltpu.SMEM)
    DMA = pltpu.SemaphoreType.DMA
    count = len(weights)
    pad_rows = lambda t: jnp.pad(t, ((0, dec_rows - NP), (0, 0)))
    table_e = jnp.asarray(np.pad(sincos_table(NP, enc_w), ((0, dec_rows - NP), (0, 0))))
    table_d = jnp.asarray(np.pad(sincos_table(NP, dec_w), ((0, dec_rows - NP), (0, 0))))
    res = pl.pallas_call(
        functools.partial(compute_kernel, per, slabs, list(named), count),
        out_shape=ship_shapes + [jax.ShapeDtypeStruct((16, enc_w), f32)],
        in_specs=[an] * count + [vm] * 8 + [sm],
        out_specs=[an] * len(SHIPPED) + [vm],
        scratch_shapes=[pltpu.VMEM(g.shape, bf16) for g in weights]
        + [DMA((count,)), DMA((len(SHIPPED),))]
        + [pltpu.VMEM(s, d) for s, d in named.values()],
        compiler_params=pltpu.CompilerParams(vmem_limit_bytes=60 << 20),
    )(*weights, patches, vis_col, vis_row, loss_w, vec_parts, weight_sum, table_e, table_d, counts)
    return res[: len(SHIPPED)], res[len(SHIPPED)]


def root_quarter(matrix):
    identity = jnp.eye(matrix.shape[-1], dtype=matrix.dtype)
    magnitude = jnp.sqrt(jnp.sum(jnp.square(matrix), axis=(-2, -1), keepdims=True))
    current = matrix / magnitude
    result = None
    for newton_step in range(NEWTON):
        factor = (5.0 * identity - current) * 0.25
        result = factor if result is None else matmul_hi(result, factor)
        if newton_step + 1 < NEWTON:
            square = matmul_hi(factor, factor)
            current = matmul_hi(matmul_hi(square, square), current)
    return result * magnitude ** (-0.25)


def shampoo(gradients, weights, kinds, small_stat, large_stat, learn_rate):
    pieces = [g.reshape(g.shape[0], -1, BLOCK).transpose(1, 0, 2) for g in gradients]
    blocks = jnp.concatenate(pieces, axis=0)[None, None]
    flipped = jnp.swapaxes(blocks, -1, -2)
    small_new = STAT_DECAY * small_stat + (1.0 - STAT_DECAY) * matmul_hi(blocks, flipped)
    large_new = STAT_DECAY * large_stat + (1.0 - STAT_DECAY) * matmul_hi(flipped, blocks)
    update = matmul_hi(matmul_hi(root_quarter(small_new), blocks), root_quarter(large_new))[0, 0]
    results, offset = [], 0
    for weight, kind, piece in zip(weights, kinds, pieces):
        step = update[offset : offset + piece.shape[0]]
        offset += piece.shape[0]
        if kind:
            step = step.transpose(1, 0, 2).reshape(weight.shape)
        else:
            step = step.transpose(0, 2, 1).reshape(weight.shape)
        results.append(weight - learn_rate * step)
    return results, small_new, large_new


def adam(gradient, weight, first, second, step_count, enc_columns):
    moment_one = BETA_FIRST * first + (1.0 - BETA_FIRST) * gradient
    moment_two = BETA_SECOND * second + (1.0 - BETA_SECOND) * jnp.square(gradient)
    steps_done = step_count[0].astype(jnp.float32)
    corrected_one = moment_one / (1.0 - jnp.power(BETA_FIRST, steps_done))
    corrected_two = moment_two / (1.0 - jnp.power(BETA_SECOND, steps_done))
    column = jnp.arange(weight.shape[1])
    rates = jnp.where(column < enc_columns, LR_VECTOR * LAYER_DECAY, LR_VECTOR)
    return (
        weight - rates * corrected_one / (jnp.sqrt(corrected_two) + EPS_ADAM),
        moment_one,
        moment_two,
    )


def heads_apart(shard, head):
    return shard.reshape(shard.shape[0], -1, 3, head).transpose(0, 2, 1, 3).reshape(shard.shape)


def heads_together(shard, head):
    return shard.reshape(shard.shape[0], 3, -1, head).transpose(0, 2, 1, 3).reshape(shard.shape)


def per_device(
    sizes,
    patches, vis_index, keep_mask, counts, step_count,
    w_embed, enc_qkv, enc_out, enc_up, enc_down, w_bridge,
    dec_qkv, dec_out, dec_up, dec_down, w_head,
    vectors, first_moment, second_moment, enc_small, enc_big, dec_small, dec_big,
):
    n_dp, n_wide, n_nar = sizes
    ext = extents(sizes)
    narrow_at = lax.axis_index("narrow")
    masters = (w_embed, enc_qkv, enc_out, enc_up, enc_down, w_bridge, dec_qkv, dec_out, dec_up, dec_down, w_head)
    low = lambda w: w.astype(jnp.bfloat16)
    shards = [
        jnp.concatenate([heads_apart(low(enc_qkv), DH), low(w_embed)], axis=1),
        low(enc_out).T, low(enc_up), low(enc_down).T, low(w_bridge),
        heads_apart(low(dec_qkv), DHD), low(dec_out).T, low(dec_up), low(dec_down).T, low(w_head),
    ]
    enc_cols, dec_cols = w_embed.shape[1], w_bridge.shape[1]
    weight_part = jnp.sum(NP - (1.0 - VISIBLE_WEIGHT) * counts.astype(jnp.float32))
    vec_part = jnp.concatenate(
        [
            vectors[:, : 6 * enc_cols].reshape(6, enc_cols),
            jnp.pad(vectors[:, 6 * enc_cols :].reshape(7, dec_cols), ((0, 3), (0, enc_cols - dec_cols))),
        ]
    )
    units, events = gather_plan(ext, [s.shape for s in shards])
    gathered, vec_parts, weight_sum = gather(
        shards, vec_part, jnp.full((8, 128), weight_part, jnp.float32), sizes, units, events
    )

    all_images = counts.shape[0]
    per = -(-all_images // n_nar)
    first = narrow_at * per
    start = jnp.minimum(first, all_images - per)
    live = (start + jnp.arange(per) >= first).astype(jnp.float32)
    pick = lambda x: lax.dynamic_slice_in_dim(x, start, per, 0)
    patches, vis_index, keep_mask, counts = map(pick, (patches, vis_index, keep_mask, counts))
    dec_rows, enc_rows = -(-NP // 16) * 16, -(-KEEP_MOST // 16) * 16
    patches = jnp.pad(patches, ((0, 0), (0, dec_rows - NP), (0, 0)))
    vis = jnp.pad(vis_index, ((0, 0), (0, enc_rows - KEEP_MOST)), constant_values=-1)
    loss_w = jnp.where(keep_mask == 1, VISIBLE_WEIGHT, 1.0) * live[:, None]
    loss_w = jnp.pad(loss_w, ((0, 0), (0, dec_rows - NP)))
    shipped, vec_grad = compute(
        [g.reshape(n_nar, -1, g.shape[-1]) for g in gathered],
        patches, vis[:, :, None], vis[:, None, :], loss_w[:, :, None], vec_parts, weight_sum, counts,
    )
    lefts, rights = shipped[: len(LEFTS)], shipped[len(LEFTS) :]
    pairs = ([(0, 0), (1, 1)], [(2, 2)], [(3, 3)], [(4, 4)], [(5, 5)], [(6, 6)], [(7, 7)], [(8, 8)], [(9, 9)], [(10, 10)])
    mats = []
    for terms, shard in zip(pairs, shards):
        cols = -(-shard.shape[1] // 128) * 128
        wide = [rights[g].shape[2] for _, g in terms]
        mats.append((shard.shape[0], cols, [(x, g, 0 if i == 0 else cols - wide[i], wide[i]) for i, (x, g) in enumerate(terms)]))
    units, events = reduce_plan(ext, mats)
    owned, vec_sum, squares = reduce_scatter(
        lefts, rights, mats, vec_grad, sizes, units, events, [True] * 5 + [False] * 5
    )
    loss_total = vec_sum[13, 0]
    enc_vec, dec_vec = vec_sum[0:6], vec_sum[6:13, : n_nar * dec_cols]
    eq, out, up, down, bridge, dqkv, dout, dup, ddown, head = owned
    enc_owned = [
        eq[:, enc_qkv.shape[1] :], heads_together(eq[:, : enc_qkv.shape[1]], DH),
        out[:, : enc_out.shape[0]], up, down, bridge,
    ]
    dec_owned = [heads_together(dqkv, DHD), dout, dup, ddown, head[:, : w_head.shape[1]]]
    enc_sq = squares[0, 0] + jnp.sum(jnp.square(enc_vec))
    dec_sq = squares[1, 0] + jnp.sum(jnp.square(dec_vec))
    norms = jnp.sqrt(jnp.stack([enc_sq, dec_sq]))
    clip_factor = jnp.minimum(1.0, CLIP_NORM / jnp.sqrt(enc_sq + dec_sq))
    enc_new, enc_small_new, enc_big_new = shampoo(
        [clip_factor * g for g in enc_owned], masters[:6], ENC_KINDS, enc_small, enc_big, LR_MATRIX * LAYER_DECAY
    )
    dec_new, dec_small_new, dec_big_new = shampoo(
        [clip_factor * g for g in dec_owned], masters[6:], DEC_KINDS, dec_small, dec_big, LR_MATRIX
    )
    own_vec = jnp.concatenate(
        [
            lax.dynamic_slice_in_dim(enc_vec, narrow_at * enc_cols, enc_cols, 1).reshape(1, -1),
            lax.dynamic_slice_in_dim(dec_vec, narrow_at * dec_cols, dec_cols, 1).reshape(1, -1),
        ],
        axis=1,
    )
    vectors_new, first_new, second_new = adam(
        clip_factor * own_vec, vectors, first_moment, second_moment, step_count, 6 * enc_cols
    )
    return (
        *enc_new, *dec_new, enc_small_new, enc_big_new, dec_small_new, dec_big_new,
        vectors_new, first_new, second_new, norms, loss_total, weight_sum[0, 0],
    )


def solution(mesh):
    sizes = (mesh.shape["dp"], mesh.shape["wide"], mesh.shape["narrow"])
    rows = P(("dp", "wide"))
    matrix = P(("dp", "wide"), "narrow")
    turned = P("narrow", ("dp", "wide"))
    matrices = tuple(matrix if kind else turned for kind in ENC_KINDS + DEC_KINDS)
    stats = (P(("dp", "wide"), "narrow"),) * 4
    packed = (P("narrow"),) * 3
    in_specs = (rows, rows, rows, rows, P()) + matrices + packed + stats
    out_specs = matrices + stats + packed + (P(), P(), P())
    return jax.shard_map(
        functools.partial(per_device, sizes), mesh=mesh, in_specs=in_specs, out_specs=out_specs, check_vma=False
    )
```

```python
import functools
import math

import jax
import jax.numpy as jnp
import numpy as np
from jax import lax
from jax.experimental import pallas as pl
from jax.experimental.pallas import tpu as pltpu
from jax.sharding import PartitionSpec as P

D = 768
DH = 64
DD = 512
DHD = 32
PIX = 768
NP = 196
BLOCK = 64
NEWTON = 3
KEEP_MOST = 98

HIGH = lax.Precision.HIGHEST
EPS_NORM = 1e-06
VISIBLE_WEIGHT = 0.1
STAT_DECAY = 0.5
LR_MATRIX = 0.2
LR_VECTOR = 0.2
LAYER_DECAY = 0.75
BETA_FIRST = 0.9
BETA_SECOND = 0.999
EPS_ADAM = 1e-08
CLIP_NORM = 1.0
ENC_KINDS = (True, True, False, True, False, True)
DEC_KINDS = (True, False, True, False, True)


MESHT = pl.DeviceIdType.MESH
FULL_CODE = 32767.0
FLOOR = 1e-30


def xors(n):
    return list(range(1, n))


def extents(sizes):
    n_dp, n_wide, n_nar = sizes
    return {"n": n_nar, "h": n_dp // 2, "l": 2, "w": n_wide // 2}


def phases_of(order, ext):
    return [d for d in order if ext[d] > 1]


def messages(order, ext):
    out, left = [], 1
    for d in ext:
        left *= ext[d]
    for d in phases_of(order, ext):
        left //= ext[d]
        out.append((d, ext[d] - 1, left))
    return out


class Place:
    def __init__(self, sizes):
        self.sizes = sizes
        self.ext = extents(sizes)
        self.dp, self.wi, self.na = (lax.axis_index(x) for x in ("dp", "wide", "narrow"))
        self.own = {"n": self.na, "h": self.dp // 2, "l": self.dp % 2, "w": self.wi // 2}
        self.core = self.wi % 2

    def peer(self, dim, k):
        if dim == "n":
            return {"narrow": self.na ^ k}
        if dim == "h":
            return {"dp": self.dp ^ (2 * k)}
        if dim in "ld":
            return {"dp": self.dp ^ k}
        if dim == "w":
            return {"wide": self.wi ^ (2 * k)}
        return {"wide": self.wi ^ 1}

    def greet(self):
        ext = self.ext
        partners = [self.peer(d, k) for d in "nw" for k in xors(ext[d])]
        partners += [self.peer("d", k) for k in xors(self.sizes[0])] + [self.peer("c", 1)]
        barrier = pltpu.get_barrier_semaphore()
        for p in partners:
            pl.semaphore_signal(barrier, inc=1, device_id=p, device_id_type=MESHT)
        pl.semaphore_wait(barrier, len(partners))

    def hops(self, narrow):
        out = [("c", 2, self.core), ("d", self.sizes[0], self.dp)]
        if self.ext["w"] > 1:
            out.append(("w", self.ext["w"], self.wi // 2))
        if narrow and self.ext["n"] > 1:
            out.append(("n", self.ext["n"], self.na))
        return out


def remote(src, dst, ss, rs, dev):
    return pltpu.make_async_remote_copy(
        src_ref=src, dst_ref=dst, send_sem=ss, recv_sem=rs, device_id=dev, device_id_type=MESHT
    )


class SmallSum:
    def __init__(self, place, value, lands, send, recv, narrow):
        self.place, self.value, self.lands, self.send, self.recv = place, value, lands, send, recv
        self.axes = place.hops(narrow)
        self.flight = None

    def start(self, i):
        d, members, at = self.axes[i]
        land = self.lands[i]
        land[at] = self.value[...]
        self.flight = []
        for k in xors(members):
            c = remote(self.value, land.at[at], self.send.at[i, k - 1], self.recv.at[i, k - 1], self.place.peer(d, k))
            c.start()
            self.flight.append(c)

    def finish(self, i):
        d, members, at = self.axes[i]
        for c in self.flight:
            c.wait()
        total = self.lands[i][0]
        for j in range(1, members):
            total = total + self.lands[i][j]
        self.value[...] = total

    @staticmethod
    def scratch(sizes, shape, narrow):
        members = [2, sizes[0]] + ([sizes[1] // 2] if sizes[1] > 2 else []) + ([sizes[2]] if narrow and sizes[2] > 1 else [])
        return [pltpu.VMEM((m,) + shape, jnp.float32) for m in members]

    @staticmethod
    def sems(sizes):
        return [pltpu.SemaphoreType.DMA((4, max(*sizes, 2)))] * 2


def plan(units, events, mats, ext, tokens):
    flat = []
    for step in events:
        for u, p in step:
            if p <= len(phases_of(units[u][3], ext)) + 3:
                flat.append((u, p))
    at = {e: i for i, e in enumerate(flat)}
    blocks = ext["h"] * ext["l"] * ext["w"]
    wants = []
    big = max((mats[m][0] for m, *_ in units)), max(hi - lo for m, lo, hi, o in units)
    first_use, last_need = {}, {}
    for u, (m, lo, hi, order) in enumerate(units):
        a, c = mats[m][0], hi - lo
        for x, g, *_ in terms_of(mats, m, lo, hi):
            first_use[x] = min(first_use.get(x, (len(flat),)), (at[u, 0], at[u, 1], tokens[g], a))
            last_need[x] = max(last_need.get(x, 0), at[u, 3])
        last = at[u, len(phases_of(order, ext)) + 3]
        full = (ext["n"], blocks) + (big if a * c * 5 > 2 * big[0] * big[1] else (a, c))
        for j, (x, g, c_lo, c_hi, g_lo) in enumerate(terms_of(mats, m, lo, hi)):
            wants.append((at[u, 0], at[u, 3], ("g", u, j), (ext["n"], tokens[g], c_hi - c_lo), "b"))
        wants.append((at[u, 1], at[u, 3], ("out", u), full, "f"))
        wants.append((at[u, 2], at[u, 3], ("stage", u), full, "f"))
        wants.append((at[u, 3], at[u, 3], ("acc", u), full, "f"))
        wants.append((at[u, 3], last, ("kept", u), (messages(order, ext)[0][2], a, c), "f"))
        for p, (d, k, n) in enumerate(messages(order, ext)):
            wants.append((at[u, p + 3], last, ("q", u, p), (k, n, a, c), "q"))
    for x, (start, turn, rows, a) in first_use.items():
        turn = min(at[u, 1] for u, (m, lo, hi, o) in enumerate(units) if any(x == t[0] for t in terms_of(mats, m, lo, hi)))
        wants.append((start, turn, ("plain", x), (rows, 2 * blocks * a), "b"))
        wants.append((start, last_need[x], ("turned", x), (blocks, 2, a, rows), "b"))
    wants.sort(key=lambda w: w[0])
    bufs, where = [], {}
    for start, end, name, shape, kind in wants:
        for i, b in enumerate(bufs):
            if b[0] == (shape, kind) and b[1] < start:
                b[1] = end
                where[name] = i
                break
        else:
            bufs.append([(shape, kind), end])
            where[name] = len(bufs) - 1
    return [b[0] for b in bufs], where


def terms_of(mats, m, lo, hi):
    out = []
    for x, g, first, width in mats[m][2]:
        a, b = max(lo, first), min(hi, first + width)
        if a < b:
            out.append((x, g, a - lo, b - lo, a - first))
    out.sort(key=lambda t: t[2] - t[3])
    return out


def reduce_kernel(sizes, units, events, mats, n_left, n_right, planned, is_enc, *refs):
    place = Place(sizes)
    ext, own, core = place.ext, place.own, place.core
    count, nu = len(mats), len(units)
    blocks = ext["h"] * ext["l"] * ext["w"]
    f32 = jnp.float32
    it = iter(refs)
    take = lambda k: [next(it) for _ in range(k)]
    lefts, rights = take(n_left), take(n_right)
    vec = next(it)
    outs = take(count)
    vec_out, sq_out = take(2)
    land = take(nu)
    kinds, where = planned
    pool = [tuple(take(2)) if kind == "q" else take(1)[0] for _, kind in kinds]
    recv_q, recv_s = [], []
    for u in range(nu):
        k = len(messages(units[u][3], ext))
        recv_q.append(take(k))
        recv_s.append(take(k))
    plain = [pool[where["plain", x]] for x in range(n_left)]
    turned = [pool[where["turned", x]] for x in range(n_left)]
    n_axes = len(place.hops(True))
    vec_land, sq_land = take(n_axes), take(n_axes)
    (core_send, core_recv, stage_sem, g_sem, x_sem, q_send, q_recv, s_send, s_recv, v_send, v_recv, t_send, t_recv) = take(13)
    left_copies = {}
    place.greet()
    small = SmallSum(place, vec_out, vec_land, v_send, v_recv, True)
    vec_out[...] = vec[...]
    squares = SmallSum(place, sq_out, sq_land, t_send, t_recv, True)

    pending = []
    last_use = {}
    flight = {}
    sums = [jnp.zeros((1, 1), f32), jnp.zeros((1, 1), f32)]
    ready = set()

    def turn(k):
        if k in ready:
            return
        ready.add(k)
        left_copies[k].wait()
        t = plain[k][...].T
        a = turned[k].shape[2]
        if a % 16 == 0:
            turned[k][...] = t.reshape(turned[k].shape)
        else:
            for i in range(2 * blocks):
                turned[k][i // 2, i % 2] = t[i * a : (i + 1) * a]

    def product(u, n, which, ref_of):
        m, lo, hi, order = units[u]
        a, c = mats[m][0], hi - lo
        for j, (x, g, c_lo, c_hi, g_lo) in enumerate(terms_of(mats, m, lo, hi)):
            right = pool[where["g", u, j]][n]
            if a % 16 == 0:
                rows = turned[x][:, which].reshape(blocks * a, turned[x].shape[3])
                v = lax.dot_general(rows, right, (((1,), (0,)), ((), ())), preferred_element_type=f32)
                v = v.reshape(blocks, a, c_hi - c_lo)
                if j == 0:
                    ref_of[n] = v
                else:
                    ref_of[n, :, :, c_lo:c_hi] += v
            else:
                for b in range(blocks):
                    v = lax.dot_general(turned[x][b, which], right, (((1,), (0,)), ((), ())), preferred_element_type=f32)
                    if j == 0:
                        ref_of[n, b] = v
                    else:
                        ref_of[n, b, :, c_lo:c_hi] += v

    def whole(kind, u):
        m, lo, hi, order = units[u]
        ref = pool[where[kind, u]]
        a, c = mats[m][0], hi - lo
        return ref if ref.shape[2:] == (a, c) else ref.at[:, :, pl.ds(0, a), pl.ds(0, c)]

    def block_of(idx):
        return (idx["h"] * ext["l"] + idx["l"]) * ext["w"] + idx["w"]

    def slab(u, idx):
        at = 0
        for d in "nhlw":
            if d != phases_of(units[u][3], ext)[0]:
                at = at * ext[d] + idx[d]
        return pool[where["kept", u]].at[at]

    def split(s, dims):
        idx = {}
        for d in reversed(dims):
            if ext[d] == 1:
                idx[d] = 0
            else:
                idx[d] = s % ext[d]
                s = s // ext[d]
        return idx

    def loop(total, body):
        def step(s, carry):
            body(s)
            return carry
        lax.fori_loop(0, total, step, 0)

    def reuse(b):
        for c in last_use.pop(b, []):
            c.wait_send()

    def code_and_send(u, p):
        ph = phases_of(units[u][3], ext)
        d, peers, slabs = messages(units[u][3], ext)[p]
        gone = ph[:p]
        free = [x for x in "nhlw" if x != d and x not in gone]
        b = where["q", u, p]
        reuse(b)
        out_q, out_s = pool[b]
        sends = []
        for k in range(1, peers + 1):
            def body(s):
                idx = split(s, free)
                for x in gone:
                    idx[x] = own[x]
                idx[d] = own[d] ^ k
                x = (whole("acc", u).at[idx["n"], block_of(idx)] if p == 0 else slab(u, idx))[...]
                top = jnp.maximum(jnp.max(jnp.abs(x), axis=0, keepdims=True), FLOOR)
                out_q[k - 1, s] = jnp.round(x * (FULL_CODE / top)).astype(jnp.int32).astype(jnp.int16)
                out_s[k - 1, s] = top * (1.0 / FULL_CODE)
            loop(slabs, body)
            dev = place.peer(d, k)
            first = remote(out_q.at[k - 1], recv_q[u][p].at[k - 1], q_send.at[u, p, k - 1], q_recv.at[u, p, k - 1], dev)
            second = remote(out_s.at[k - 1], recv_s[u][p].at[k - 1], s_send.at[u, p, k - 1], s_recv.at[u, p, k - 1], dev)
            first.start()
            second.start()
            sends += [first, second]
        flight[u, p] = sends
        last_use[b] = sends

    def take_in(u, p):
        ph = phases_of(units[u][3], ext)
        d, peers, slabs = messages(units[u][3], ext)[p]
        gone = ph[: p + 1]
        free = [x for x in "nhlw" if x not in gone]
        for c in flight[u, p]:
            c.wait_recv()
        def body(s):
            idx = split(s, free)
            for x in gone:
                idx[x] = own[x]
            ref = slab(u, idx)
            v = ref[...]
            for k in range(peers):
                v = v + recv_q[u][p][k, s].astype(jnp.int32).astype(f32) * recv_s[u][p][k, s]
            ref[...] = v
        loop(slabs, body)

    def stage(u, p):
        m, lo, hi, order = units[u]
        n_ph = len(phases_of(order, ext))
        if p == 0:
            copies = []
            for j, (x, g, c_lo, c_hi, g_lo) in enumerate(terms_of(mats, m, lo, hi)):
                if x not in left_copies:
                    left_copies[x] = pltpu.make_async_copy(lefts[x], plain[x], x_sem.at[x])
                    left_copies[x].start()
                src = rights[g]
                if c_hi - c_lo != src.shape[2]:
                    src = src.at[:, :, slice(g_lo, g_lo + c_hi - c_lo)]
                c = pltpu.make_async_copy(src, pool[where["g", u, j]], g_sem.at[u, j])
                c.start()
                copies.append(c)
            flight[u, "g"] = copies
        elif p == 1:
            for c in flight[u, "g"]:
                c.wait()
            for x, *_ in terms_of(mats, m, lo, hi):
                turn(x)
            b = where["out", u]
            reuse(b)
            loop(ext["n"], lambda n: product(u, n, 1 - core, whole("out", u)))
            c = remote(whole("out", u), land[u], core_send.at[u], core_recv.at[u], place.peer("c", 1))
            c.start()
            flight[u, "core"] = c
            last_use[b] = [c]
        elif p == 2:
            flight[u, "core"].wait_recv()
            reuse(where["stage", u])
            c = pltpu.make_async_copy(land[u], whole("stage", u), stage_sem.at[u])
            c.start()
            flight[u, "stage"] = c
        elif p == 3:
            acc, more = whole("acc", u), whole("stage", u)
            reuse(where["acc", u])
            flight[u, "stage"].wait()
            def body(n):
                product(u, n, core, acc)
                acc[n] = acc[n] + more[n]
            loop(ext["n"], body)
            code_and_send(u, 0)
            d, peers, slabs = messages(order, ext)[0]
            def keep(i):
                idx = split(i, [x for x in "nhlw" if x != d])
                idx[d] = own[d]
                slab(u, idx)[...] = acc.at[idx["n"], block_of(idx)][...]
            loop(slabs, keep)
        else:
            take_in(u, p - 4)
            if p - 3 < n_ph:
                code_and_send(u, p - 3)
            else:
                x = slab(u, own)[...]
                outs[m][:, pl.ds(lo, hi - lo)] = x
                w = 0 if is_enc[m] else 1
                sums[w] = sums[w] + jnp.sum(x * x, keepdims=True)

    hop = 0
    for step in events:
        for u, p in step:
            if p <= len(phases_of(units[u][3], ext)) + 3:
                stage(u, p)
                if p == 3 and hop <= n_axes:
                    if hop:
                        small.finish(hop - 1)
                    if hop < n_axes:
                        small.start(hop)
                    hop += 1
    while hop <= n_axes:
        if hop:
            small.finish(hop - 1)
        if hop < n_axes:
            small.start(hop)
        hop += 1
    row = lax.broadcasted_iota(jnp.int32, (8, 128), 0)
    sq_out[...] = jnp.where(row == 0, sums[0], jnp.where(row == 1, sums[1], 0.0))
    for i in range(n_axes):
        squares.start(i)
        squares.finish(i)
    for c in [c for cs in last_use.values() for c in cs]:
        c.wait_send()


def reduce_scatter(lefts, rights, mats, vec, sizes, units, events, is_enc, cid=1):
    ext = extents(sizes)
    blocks = ext["h"] * ext["l"] * ext["w"]
    f32, bf16 = jnp.float32, jnp.bfloat16
    tokens = [r.shape[1] for r in rights]
    planned = plan(units, events, mats, ext, tokens)
    coded = lambda k, n, a, c: [pltpu.VMEM((k, n, a, c), jnp.int16), pltpu.VMEM((k, n, 1, c), f32)]
    scratch = []
    for shape, kind in planned[0]:
        scratch += coded(*shape) if kind == "q" else [pltpu.VMEM(shape, f32 if kind == "f" else bf16)]
    for m, lo, hi, order in units:
        ms = [coded(k, n, mats[m][0], hi - lo) for d, k, n in messages(order, ext)]
        scratch += [x[0] for x in ms] + [x[1] for x in ms]
    scratch += SmallSum.scratch(sizes, vec.shape, True) + SmallSum.scratch(sizes, (8, 128), True)
    nu, kmax = len(units), max(ext.values())
    D_ = pltpu.SemaphoreType.DMA
    scratch += [D_((nu,))] * 3 + [D_((nu, 2)), D_((len(lefts),))] + [D_((nu, 4, kmax))] * 4 + SmallSum.sems(sizes) * 2
    vm = pl.BlockSpec(memory_space=pltpu.VMEM)
    an = pl.BlockSpec(memory_space=pl.ANY)
    res = pl.pallas_call(
        functools.partial(reduce_kernel, sizes, units, events, mats, len(lefts), len(rights), planned, is_enc),
        out_shape=[jax.ShapeDtypeStruct(m[:2], f32) for m in mats]
        + [jax.ShapeDtypeStruct(vec.shape, f32), jax.ShapeDtypeStruct((8, 128), f32)]
        + [jax.ShapeDtypeStruct((ext["n"], blocks, mats[m][0], hi - lo), f32) for m, lo, hi, o in units],
        in_specs=[an] * (len(lefts) + len(rights)) + [vm],
        out_specs=[vm] * (len(mats) + 2) + [an] * nu,
        scratch_shapes=scratch,
        compiler_params=pltpu.CompilerParams(collective_id=cid, has_side_effects=True, vmem_limit_bytes=60 << 20),
    )(*lefts, *rights, vec)
    return res[: len(mats)], res[len(mats)], res[len(mats) + 1]


def gather_kernel(sizes, units, events, count, *refs):
    place = Place(sizes)
    extent, own, core, na, peer = place.ext, place.own, place.core, place.na, place.peer
    n_axes = len(place.hops(False))
    it = iter(refs)
    take = lambda k: [next(it) for _ in range(k)]
    shards = take(count)
    vec, weight = take(2)
    outs = take(count)
    vec_all, weight_sum = take(2)
    weight_land = take(n_axes)
    send_sem, recv_sem, loc_sem, vec_send, vec_recv, sum_send, sum_recv = take(7)
    place.greet()
    pending = []
    sib_recv = []
    vec_flight = []
    for k in xors(extent["n"]):
        c = remote(vec, vec_all.at[na], vec_send.at[k - 1], vec_recv.at[k - 1], peer("n", k))
        c.start()
        vec_flight.append(c)
    vec_all[na] = vec[...]
    weight_sum[...] = weight[...]
    small = SmallSum(place, weight_sum, weight_land, sum_send, sum_recv, False)
    slot_of = [0] * len(units)
    def region(u, full, at, which_core):
        m, lo, hi, order = units[u]
        idx = []
        for d in "nhlw":
            if d in full: idx.append(slice(None))
            elif at and d == at[0]: idx.append(own[d] ^ at[1])
            else: idx.append(own[d])
        r = outs[m].at[tuple(idx) + (which_core,)]
        if (lo, hi) != (0, shards[m].shape[1]):
            r = outs[m].at[tuple(idx) + (which_core, slice(None), slice(lo, hi))]
        return r
    def send(u, src, dst, dev, recv_view):
        s = slot_of[u]; slot_of[u] += 1
        c = remote(src, dst, send_sem.at[u, s], recv_sem.at[u, s], dev)
        c.start()
        pending.append(c)
        return remote(recv_view, recv_view, send_sem.at[u, s], recv_sem.at[u, s], dev)
    def shard(u):
        m, lo, hi, order = units[u]
        return shards[m] if (lo, hi) == (0, shards[m].shape[1]) else shards[m].at[:, slice(lo, hi)]
    state = {}
    def phases(u):
        return [d for d in units[u][3] if extent[d] > 1]
    def stage(u, p):
        ph = phases(u)
        if p == 0:
            lc = pltpu.make_async_copy(shard(u), region(u, (), None, core), loc_sem.at[u]); lc.start()
            sib_recv.append(send(u, shard(u), region(u, (), None, core), peer("c", 1), region(u, (), None, 1 - core)))
            src = shard(u)
            state[u] = []
            state[u, "loc"] = lc
        else:
            done = ph[:p - 1]
            for k, w in state[u]:
                w.wait_recv()
            for k, w in state[u]:
                here = region(u, done, (ph[p - 1], k), core)
                there = region(u, done, (ph[p - 1], k), 1 - core)
                state[u, k] = (here, there)
            if p == 1: state[u, "loc"].wait()
            src = None
        old = state[u]
        state[u] = []
        if p < len(ph):
            full = ph[:p]
            for k in xors(extent[ph[p]]):
                mine = region(u, full, None, core) if src is None else src
                w = send(u, mine, region(u, full, None, core), peer(ph[p], k), region(u, full, (ph[p], k), core))
                state[u].append((k, w))
        if p > 0:
            for k, _ in old:
                here, there = state[u, k]
                sib_recv.append(send(u, here, here, peer("c", 1), there))
    for t, step in enumerate(events):
        for u, p in step:
            if p <= len(phases(u)):
                stage(u, p)
        if 0 < t <= n_axes:
            small.finish(t - 1)
        if t < n_axes:
            small.start(t)
    for c in vec_flight:
        c.wait()
    for c in pending:
        c.wait_send()
    for w in sib_recv:
        w.wait_recv()


def gather(shards, vec, weight, sizes, units, events, cid=0):
    n_dp, n_wide, n_nar = sizes
    count = len(shards)
    ext = extents(sizes)
    slots = 2 * sum(ext.values())
    nu = len(units)
    DMA = pltpu.SemaphoreType.DMA
    an = pl.BlockSpec(memory_space=pl.ANY)
    vm = pl.BlockSpec(memory_space=pltpu.VMEM)
    heads = (ext["n"], ext["h"], ext["l"], ext["w"], 2)
    res = pl.pallas_call(
        functools.partial(gather_kernel, sizes, units, events, count),
        out_shape=[jax.ShapeDtypeStruct(heads + s.shape, s.dtype) for s in shards]
        + [jax.ShapeDtypeStruct((n_nar,) + vec.shape, vec.dtype), jax.ShapeDtypeStruct(weight.shape, weight.dtype)],
        in_specs=[an] * count + [vm, vm],
        out_specs=[an] * count + [vm, vm],
        scratch_shapes=SmallSum.scratch(sizes, weight.shape, False)
        + [DMA((nu, slots)), DMA((nu, slots)), DMA((nu,)), DMA((n_nar,)), DMA((n_nar,))]
        + SmallSum.sems(sizes),
        compiler_params=pltpu.CompilerParams(collective_id=cid, has_side_effects=True),
    )(*shards, vec, weight)
    return res[:count], res[count], res[count + 1]


GATHER_UNITS = (
    (0, 0, 256, "nlhw"), (0, 256, 512, "hnlw"), (0, 512, 768, "hnlw"), (1, 0, 256, "nlhw"), (2, 0, 256, "nhlw"),
    (2, 256, 512, "nhlw"), (2, 512, 768, "lnhw"), (3, 0, 256, "nlhw"), (3, 256, 512, "nhlw"), (3, 512, 768,
    "nlhw"), (4, 0, 128, "nhlw"), (5, 0, 256, "nlhw"), (5, 256, 384, "hnlw"), (6, 0, 128, "nhlw"), (7, 0, 256,
    "nlhw"), (7, 256, 512, "hnlw"), (8, 0, 256, "nlhw"), (8, 256, 512, "lnhw"), (9, 0, 256, "hlwn"),
)
GATHER_ORDER = (
    (13, 0), (14, 0), (10, 0), (16, 0), (13, 1), (5, 0), (14, 1), (12, 0), (13, 2), (10, 1), (11, 0), (12, 1), (4,
    0), (16, 1), (14, 2), (8, 0), (10, 2), (13, 3), (5, 1), (9, 0), (16, 2), (11, 1), (7, 0), (14, 3), (12, 2),
    (10, 3), (5, 2), (11, 2), (4, 1), (17, 0), (12, 3), (16, 3), (8, 1), (2, 0), (9, 1), (3, 0), (11, 3), (5, 3),
    (17, 1), (18, 0), (7, 1), (1, 0), (4, 2), (9, 2), (3, 1), (0, 0), (8, 2), (2, 1), (7, 2), (6, 0), (18, 1),
    (15, 0), (1, 1), (17, 2), (0, 1), (4, 3), (9, 3), (3, 2), (2, 2), (7, 3), (15, 1), (8, 3), (6, 1), (18, 2),
    (1, 2), (17, 3), (0, 2), (15, 2), (3, 3), (2, 3), (6, 2), (0, 3), (1, 3), (18, 3), (6, 3), (15, 3),
)


def gather_plan(ext, shapes):
    cols = [s[1] for s in shapes]
    if ext["w"] > 1:
        units = [(m, 0, c, "nlhw") for m, c in enumerate(cols)]
        return units, [[(u, p)] for u in range(len(units)) for p in range(5)]
    units = [(m, lo, min(hi, cols[m]), order) for m, lo, hi, order in GATHER_UNITS]
    return units, [list(GATHER_ORDER[i : i + 12]) for i in range(0, len(GATHER_ORDER), 12)]


REDUCE_UNITS = (
    (0, 0, 256, "lnhw"), (0, 256, 512, "lhwn"), (0, 512, 768, "hlwn"), (1, 0, 256, "lhwn"), (2, 0, 256, "hlwn"),
    (2, 256, 512, "nhlw"), (2, 512, 768, "lhwn"), (3, 0, 256, "hnlw"), (3, 256, 512, "lhwn"), (3, 512, 768,
    "lhwn"), (4, 0, 128, "lnhw"), (5, 0, 256, "lhwn"), (5, 256, 384, "hlwn"), (6, 0, 128, "hnlw"), (7, 0, 256,
    "hnlw"), (7, 256, 512, "lhwn"), (8, 0, 256, "hlwn"), (8, 256, 512, "hlwn"), (9, 0, 256, "hlwn"),
)
REDUCE_ORDER = (
    (13, 0), (10, 0), (14, 0), (15, 0), (13, 1), (10, 1), (14, 1), (15, 1), (13, 2), (10, 2), (13, 3), (2, 0),
    (10, 3), (14, 2), (2, 1), (0, 0), (15, 2), (14, 3), (0, 1), (5, 0), (13, 4), (15, 3), (5, 1), (8, 0), (2, 2),
    (8, 1), (10, 4), (2, 3), (0, 2), (12, 0), (13, 5), (12, 1), (0, 3), (14, 4), (5, 2), (4, 0), (15, 4), (13, 6),
    (4, 1), (8, 2), (10, 5), (5, 3), (12, 2), (3, 0), (8, 3), (12, 3), (3, 1), (16, 0), (9, 0), (4, 2), (16, 1),
    (9, 1), (2, 4), (14, 5), (4, 3), (7, 0), (3, 2), (0, 4), (15, 5), (7, 1), (10, 6), (16, 2), (3, 3), (18, 0),
    (16, 3), (12, 4), (9, 2), (18, 1), (17, 0), (17, 1), (9, 3), (7, 2), (11, 0), (8, 4), (18, 2), (11, 1), (7,
    3), (1, 0), (17, 2), (18, 3), (6, 0), (1, 1), (4, 4), (2, 5), (17, 3), (14, 6), (11, 2), (6, 1), (5, 4), (11,
    3), (1, 2), (16, 4), (1, 3), (6, 2), (6, 3), (8, 5), (3, 4), (0, 5), (12, 5), (15, 6), (2, 6), (7, 4), (9, 4),
    (8, 6), (12, 6), (4, 5), (18, 4), (11, 4), (17, 4), (5, 5), (7, 5), (16, 5), (3, 5), (4, 6), (0, 6), (16, 6),
    (1, 4), (9, 5), (3, 6), (11, 5), (9, 6), (1, 5), (6, 4), (11, 6), (18, 5), (17, 5), (1, 6), (5, 6), (6, 5),
    (7, 6), (18, 6), (17, 6), (6, 6),
)


def reduce_plan(ext, mats):
    if ext["w"] > 1:
        units = [(m, lo, min(lo + 256, x[1]), "wlhn") for m, x in enumerate(mats) for lo in range(0, x[1], 256)]
        return units, [[(u, p)] for u in range(len(units)) for p in range(8)]
    return list(REDUCE_UNITS), [list(REDUCE_ORDER)]


def sincos_table(rows, width):
    column = np.arange(width)
    freq = np.power(np.float32(10000.0), (-(2 * (column // 2)).astype(np.float32) / np.float32(width)).astype(np.float32))
    angle = (np.arange(rows, dtype=np.float32)[:, None] * freq[None, :]).astype(np.float32)
    return np.where(column % 2 == 0, np.sin(angle), np.cos(angle)).astype(np.float32)


def dot_nn(a, b):
    return lax.dot_general(a, b, (((1,), (0,)), ((), ())), preferred_element_type=jnp.float32)


def dot_nt(a, b):
    return lax.dot_general(a, b, (((1,), (1,)), ((), ())), preferred_element_type=jnp.float32)


def dot_tn(a, b):
    return lax.dot_general(a, b, (((0,), (0,)), ((), ())), preferred_element_type=jnp.float32)


def dot_exact(a, b):
    return lax.dot_general(a, b, (((1,), (0,)), ((), ())), precision=HIGH, preferred_element_type=jnp.float32)


class Side:
    def __init__(self, width, head, heads, rows, images, slabs):
        self.width, self.head, self.heads, self.rows = width, head, heads, rows
        self.slabs = slabs
        self.tokens = rows * images
        self.lane = head * heads
        self.packed = -(-3 * self.lane // 128) * 128

    def scratch(self, hidden):
        t, n, w = self.tokens, self.slabs, self.width
        bf, f = jnp.bfloat16, jnp.float32
        return {
            "x": ((t, w), f),
            "hat1": ((t, w), f), "hat2": ((t, w), f), "hat3": ((t, w), f),
            "inv": ((t, 128), f),
            "n1": ((t, w), bf), "n2": ((t, w), bf), "n3": ((t, w), bf),
            "qkv": ((n, t, self.packed), bf),
            "lse": ((t, 128), f),
            "att": ((n, t, -(-self.lane // 128) * 128), bf),
            "slope": ((n, t, hidden), f),
            "act": ((n, t, hidden), bf),
            "dn": ((t, w), f),
            "og1": ((t, w), bf),
            "og2": ((t, w), bf),
        }


LEFTS = ("e_n1", "chosen", "e_og1", "e_n2", "e_og2", "e_n3", "d_n1", "d_og1", "d_n2", "d_og2", "d_n3")
RIGHTS = ("e_qkv", "part0", "e_att", "e_dh", "e_act", "part4", "d_qkv", "d_att", "d_dh", "d_act", "part9")
SHIPPED = LEFTS + RIGHTS
BUFFER_OF = {"e_dh": "e_act", "d_dh": "d_act"}


def compute_kernel(per, slabs, names, count, *refs):
    it = iter(refs)
    take = lambda k: [next(it) for _ in range(k)]
    hbm = take(count)
    patches, vis_col, vis_row, loss_w, vec_parts, weight_sum, table_e, table_d, counts = take(9)
    shipped = take(len(SHIPPED))
    vec_out = next(it)
    w = take(count)
    load_sem, store_sem = take(2)
    buf = dict(zip(names, it))
    w_eq, w_out, w_up, w_down, w_bridge, w_dqkv, w_dout, w_dup, w_ddown, w_head = w
    f32, bf16 = jnp.float32, jnp.bfloat16
    loads = []
    for m in range(count):
        c = pltpu.make_async_copy(hbm[m], w[m], load_sem.at[m])
        c.start()
        loads.append(c)
    waited = set()

    def need(m):
        if m not in waited:
            waited.add(m)
            loads[m].wait()


    enc_rows, dec_rows = vis_col.shape[1], patches.shape[1]
    enc_w, dec_w = table_e.shape[1], table_d.shape[1]
    enc = Side(enc_w, DH, w_out.shape[2] // DH, enc_rows, per, slabs)
    dec = Side(dec_w, DHD, w_dout.shape[2] // DHD, dec_rows, per, slabs)
    for s, tag in ((enc, "e_"), (dec, "d_")):
        s.tag = tag
        s.b = {k[2:]: v for k, v in buf.items() if k.startswith(tag)}
    enc.w, dec.w = (w_eq, w_out, w_up, w_down), (w_dqkv, w_dout, w_dup, w_ddown)
    enc.ids, dec.ids = (0, 1, 2, 3), (5, 6, 7, 8)
    enc.base, dec.base = 0, 7
    vec_full = buf["vec_full"]
    enc_c, dec_c = enc_w // slabs, dec_w // slabs
    for n in range(slabs):
        vec_full[0:6, pl.ds(n * enc_c, enc_c)] = vec_parts[n, 0:6, 0:enc_c]
        vec_full[6:13, pl.ds(n * dec_c, dec_c)] = vec_parts[n, 6:13, 0:dec_c]
    vec_out[...] = jnp.zeros_like(vec_out)

    def vector(k, width):
        return vec_full[k : k + 1, 0:width]

    CH = 32

    def chunks(total, body):
        def step(i, carry):
            body(pl.ds(pl.multiple_of(i * CH, CH), CH))
            return carry
        lax.fori_loop(0, total // CH, step, 0)

    def norm_fwd(s, k, out, hat, inv):
        gain, bias = vector(s.base + k, s.width), vector(s.base + k + 1, s.width)
        x = s.b["x"]
        def body(r):
            v = x[r, :]
            mean = jnp.mean(v, axis=1, keepdims=True)
            d = v - mean
            i = lax.rsqrt(jnp.mean(d * d, axis=1, keepdims=True) + EPS_NORM)
            h = d * i
            s.b[hat][r, :] = h
            s.b["inv"][r, inv : inv + 1] = i
            s.b[out][r, :] = (h * gain + bias).astype(bf16)
        chunks(s.tokens, body)

    def norm_bwd(s, k, hat, inv, add):
        gain = vector(s.base + k, s.width)
        def body(r):
            dn = s.b["dn"][r, :]
            h = s.b[hat][r, :]
            vec_out[s.base + k : s.base + k + 1, 0 : s.width] += jnp.sum(dn * h, axis=0, keepdims=True)
            vec_out[s.base + k + 1 : s.base + k + 2, 0 : s.width] += jnp.sum(dn, axis=0, keepdims=True)
            g = dn * gain
            d = s.b["inv"][r, inv : inv + 1] * (
                g - jnp.mean(g, axis=1, keepdims=True) - h * jnp.mean(g * h, axis=1, keepdims=True)
            )
            s.b["x"][r, :] = s.b["x"][r, :] + d if add else d
        chunks(s.tokens, body)

    def slab_loop(body):
        def step(n, carry):
            body(n)
            return carry
        lax.fori_loop(0, slabs, step, 0)

    def head_mask(s, h):
        lane = lax.broadcasted_iota(jnp.int32, (1, s.lane), 1)
        return (lane >= h * s.head) & (lane < (h + 1) * s.head)

    def scores(s, q, k, mask, limit):
        v = dot_nt(jnp.where(mask, q, jnp.zeros_like(q)), k) * (s.head ** -0.5)
        key = lax.broadcasted_iota(jnp.int32, (s.rows, s.rows), 1)
        return jnp.where(key < limit, v, -1e30)

    def attention_loop(body):
        def step(i, carry):
            image, n = i // slabs, i % slabs
            body(image, n)
            return carry
        lax.fori_loop(0, per * slabs, step, 0)

    def image_rows(s, image):
        return pl.ds(pl.multiple_of(image * s.rows, 16), s.rows)

    def block_fwd(s, limit):
        b = s.b
        b["lse"][...] = jnp.zeros_like(b["lse"])
        if b["att"].shape[2] != s.lane:
            b["att"][...] = jnp.zeros_like(b["att"])
        qkv_w, out_w, up_w, down_w = s.w
        need(s.ids[0])
        norm_fwd(s, 0, "n1", "hat1", 1)
        def qkv(n):
            b["qkv"][n] = dot_nn(b["n1"][...], qkv_w[n, :, 0 : s.packed]).astype(bf16)
        slab_loop(qkv)
        def attend(image, n):
            r = image_rows(s, image)
            q = b["qkv"][n, r, 0 : s.lane]
            k = b["qkv"][n, r, s.lane : 2 * s.lane]
            v = b["qkv"][n, r, 2 * s.lane : 3 * s.lane]
            lane = lax.broadcasted_iota(jnp.int32, (s.rows, 128), 1)
            total = jnp.zeros((s.rows, s.lane), f32)
            lse = b["lse"][r, :]
            for h in range(s.heads):
                mask = head_mask(s, h)
                sc = scores(s, q, k, mask, limit(image))
                top = jnp.max(sc, axis=1, keepdims=True)
                e = jnp.exp(sc - top)
                z = jnp.sum(e, axis=1, keepdims=True)
                p = (e * (1.0 / z)).astype(bf16)
                total = jnp.where(mask, dot_nn(p, v), total)
                lse = jnp.where(lane == n * s.heads + h, top + jnp.log(z), lse)
            b["att"][n, r, 0 : s.lane] = total.astype(bf16)
            b["lse"][r, :] = lse
        attention_loop(attend)
        need(s.ids[1])
        ship(s.tag + "att")
        def project(n):
            b["x"][...] += dot_nt(b["att"][n, :, 0 : s.lane], out_w[n])
        slab_loop(project)
        norm_fwd(s, 2, "n2", "hat2", 2)
        need(s.ids[2])
        need(s.ids[3])
        hid = buf["hid"]
        c = up_w.shape[2]
        def mlp(n):
            hid[0 : s.tokens, 0:c] = dot_nn(b["n2"][...], up_w[n])
            def body(r):
                v = hid[r, 0:c]
                cdf = 0.5 * (1.0 + lax.erf(v * 0.7071067811865476))
                b["act"][n, r, :] = (v * cdf).astype(bf16)
                b["slope"][n, r, :] = cdf + v * (0.3989422804014327 * jnp.exp(-0.5 * v * v))
            chunks(s.tokens, body)
            b["x"][...] += dot_nt(b["act"][n], down_w[n])
        slab_loop(mlp)
        ship(s.tag + "act")
        norm_fwd(s, 4, "n3", "hat3", 3)
        for name in ("n1", "n2", "n3"):
            ship(s.tag + name)

    on_way = {}

    def ship(name):
        at = SHIPPED.index(name)
        c = pltpu.make_async_copy(buf[BUFFER_OF.get(name, name)], shipped[at], store_sem.at[at])
        c.start()
        on_way[name] = c

    def arrived(name):
        on_way.pop(name).wait()

    def block_bwd(s, limit):
        b = s.b
        qkv_w, out_w, up_w, down_w = s.w
        b["og2"][...] = b["x"][...].astype(bf16)
        ship(s.tag + "og2")
        b["dn"][...] = jnp.zeros_like(b["dn"])
        arrived(s.tag + "act")
        def down(n):
            b["act"][n] = (dot_nn(b["og2"][...], down_w[n]) * b["slope"][n]).astype(bf16)
            b["dn"][...] += dot_nt(b["act"][n], up_w[n])
        slab_loop(down)
        ship(s.tag + "dh")
        norm_bwd(s, 2, "hat2", 2, True)
        b["og1"][...] = b["x"][...].astype(bf16)
        ship(s.tag + "og1")
        arrived(s.tag + "att")
        def proj(n):
            b["att"][n, :, 0 : s.lane] = dot_nn(b["og1"][...], out_w[n]).astype(bf16)
        slab_loop(proj)
        def attend(image, n):
            r = image_rows(s, image)
            q = b["qkv"][n, r, 0 : s.lane]
            k = b["qkv"][n, r, s.lane : 2 * s.lane]
            v = b["qkv"][n, r, 2 * s.lane : 3 * s.lane]
            g = b["att"][n, r, 0 : s.lane]
            lane = lax.broadcasted_iota(jnp.int32, (s.rows, 128), 1)
            lse = b["lse"][r, :]
            dq = jnp.zeros((s.rows, s.lane), f32)
            dk = dq
            dv = dq
            for h in range(s.heads):
                mask = head_mask(s, h)
                level = jnp.sum(jnp.where(lane == n * s.heads + h, lse, 0.0), axis=1, keepdims=True)
                p = jnp.exp(scores(s, q, k, mask, limit(image)) - level)
                dp = dot_nt(jnp.where(mask, g, jnp.zeros_like(g)), v)
                dv = jnp.where(mask, dot_tn(p.astype(bf16), g), dv)
                ds = (p * (dp - jnp.sum(dp * p, axis=1, keepdims=True))).astype(bf16)
                dq = jnp.where(mask, dot_nn(ds, k), dq)
                dk = jnp.where(mask, dot_tn(ds, q), dk)
            scale = s.head ** -0.5
            if s.packed != 3 * s.lane:
                b["qkv"][n, r, 2 * s.lane : s.packed] = jnp.zeros((s.rows, s.packed - 2 * s.lane), bf16)
            b["qkv"][n, r, 0 : s.lane] = (dq * scale).astype(bf16)
            b["qkv"][n, r, s.lane : 2 * s.lane] = (dk * scale).astype(bf16)
            b["qkv"][n, r, 2 * s.lane : 3 * s.lane] = dv.astype(bf16)
        attention_loop(attend)
        ship(s.tag + "qkv")
        b["dn"][...] = jnp.zeros_like(b["dn"])
        def qkv(n):
            b["dn"][...] += dot_nt(b["qkv"][n], qkv_w[n, :, 0 : s.packed])
        slab_loop(qkv)
        norm_bwd(s, 0, "hat1", 1, True)

    chosen = buf["chosen"]
    need(0)
    for i in range(per):
        r = pl.ds(i * enc_rows, enc_rows)
        patch = lax.broadcasted_iota(jnp.int32, (enc_rows, dec_rows), 1)
        one = patch == vis_col[i]
        chosen[r, :] = dot_nn(one.astype(f32).astype(bf16), patches[i]).astype(bf16)
        enc.b["x"][r, :] = dot_exact(one.astype(f32), table_e[...])
    for n in range(slabs):
        lead = w_eq.shape[2] - 256
        part = dot_nn(chosen[...], w_eq[n, :, lead : lead + 256])
        enc.b["x"][:, n * enc_c : (n + 1) * enc_c] += part[:, 256 - enc_c : 256]
    ship("chosen")
    block_fwd(enc, lambda image: counts[image])
    need(4)
    bridged = buf["hid"]
    for n in range(slabs):
        bridged[0 : enc.tokens, n * dec_c : (n + 1) * dec_c] = dot_nn(enc.b["n3"][...], w_bridge[n])

    def hits(i, turned_way):
        if turned_way:
            patch = lax.broadcasted_iota(jnp.int32, (dec_rows, enc_rows), 0)
            slot = lax.broadcasted_iota(jnp.int32, (dec_rows, enc_rows), 1)
            return ((patch == vis_row[i]) & (slot < counts[i])).astype(f32)
        patch = lax.broadcasted_iota(jnp.int32, (enc_rows, dec_rows), 1)
        slot = lax.broadcasted_iota(jnp.int32, (enc_rows, dec_rows), 0)
        return ((patch == vis_col[i]) & (slot < counts[i])).astype(f32)

    for i in range(per):
        r = pl.ds(i * dec_rows, dec_rows)
        hit = hits(i, True)
        placed = dot_exact(hit, bridged[pl.ds(i * enc_rows, enc_rows), 0:dec_w])
        seen = jnp.sum(hit, axis=1, keepdims=True) > 0
        dec.b["x"][r, :] = jnp.where(seen, placed, vector(6, dec_w)) + table_d[...]
    block_fwd(dec, lambda image: NP)
    need(9)
    pred = buf["hid"]
    pix_c = w_head.shape[2]
    pix = patches.shape[2]
    for n in range(slabs):
        pred[0 : dec.tokens, n * pix_c : (n + 1) * pix_c] = dot_nn(dec.b["n3"][...], w_head[n])

    pgrad = buf["pgrad"]
    divisor = weight_sum[0:1, 0:1]
    loss = jnp.zeros((1, 1), f32)
    LC = 16
    for i in range(per):
        def lossy(j, total):
            r = pl.ds(pl.multiple_of(j * LC, LC), LC)
            px = patches[i, r, :].astype(f32)
            d = px - jnp.mean(px, axis=1, keepdims=True)
            target = d * lax.rsqrt(jnp.mean(d * d, axis=1, keepdims=True) + EPS_NORM)
            rr = pl.ds(pl.multiple_of(i * dec_rows + j * LC, LC), LC)
            error = pred[rr, 0:pix] - target
            weight = loss_w[i, r, :]
            pgrad[rr, :] = (2.0 * weight * error / divisor).astype(bf16)
            return total + jnp.sum(weight * error * error, keepdims=True)
        loss = lax.fori_loop(0, dec_rows // LC, lossy, loss)
    part9 = buf["part9"]
    part9[...] = jnp.zeros_like(part9)
    for n in range(slabs):
        part9[n, :, 0:pix_c] = pgrad[:, n * pix_c : (n + 1) * pix_c]
    dec.b["dn"][...] = jnp.zeros_like(dec.b["dn"])
    ship("part9")
    def head_bwd(n):
        dec.b["dn"][...] += dot_nt(part9[n, :, 0:pix_c], w_head[n])
    slab_loop(head_bwd)
    norm_bwd(dec, 4, "hat3", 3, False)
    block_bwd(dec, lambda image: NP)
    part4 = buf["part4"]
    for i in range(per):
        r = pl.ds(i * dec_rows, dec_rows)
        seen = jnp.sum(hits(i, True), axis=1, keepdims=True) > 0
        grad = dec.b["x"][r, :]
        vec_out[6:7, 0:dec_w] += jnp.sum(jnp.where(seen, 0.0, grad), axis=0, keepdims=True)
        back = dot_exact(hits(i, False), grad).astype(bf16)
        for n in range(slabs):
            part4[n, pl.ds(i * enc_rows, enc_rows), :] = back[:, n * dec_c : (n + 1) * dec_c]
    ship("part4")
    enc.b["dn"][...] = jnp.zeros_like(enc.b["dn"])
    def bridge_bwd(n):
        enc.b["dn"][...] += dot_nt(part4[n], w_bridge[n])
    slab_loop(bridge_bwd)
    norm_bwd(enc, 4, "hat3", 3, False)
    block_bwd(enc, lambda image: counts[image])

    part0 = buf["part0"]
    part0[...] = jnp.zeros_like(part0)
    for n in range(slabs):
        part0[n, :, 256 - enc_c : 256] = enc.b["x"][:, n * enc_c : (n + 1) * enc_c].astype(bf16)
    ship("part0")
    row = lax.broadcasted_iota(jnp.int32, (1, vec_out.shape[1]), 1)
    vec_out[13:14, :] = jnp.where(row >= 0, loss, 0.0)
    for name in list(on_way):
        arrived(name)


def compute(weights, patches, vis_col, vis_row, loss_w, vec_parts, weight_sum, counts):
    per, dec_rows, pix = patches.shape
    slabs = weights[0].shape[0]
    enc_rows = vis_col.shape[1]
    enc_w, dec_w = weights[0].shape[1], weights[5].shape[1]
    enc = Side(enc_w, DH, weights[1].shape[2] // DH, enc_rows, per, slabs)
    dec = Side(dec_w, DHD, weights[6].shape[2] // DHD, dec_rows, per, slabs)
    named = {}
    for s, tag, up in ((enc, "e_", weights[2]), (dec, "d_", weights[7])):
        for k, v in s.scratch(up.shape[2]).items():
            named[tag + k] = v
    f32, bf16 = jnp.float32, jnp.bfloat16
    top = max(enc.tokens, dec.tokens)
    named["hid"] = ((top, max(pix, weights[2].shape[2], weights[7].shape[2])), f32)
    named["vec_full"] = ((16, enc_w), f32)
    named["chosen"] = ((enc.tokens, pix), bf16)
    named["pgrad"] = ((dec.tokens, pix), bf16)
    up128 = lambda c: -(-c // 128) * 128
    named["part9"] = ((slabs, dec.tokens, up128(weights[9].shape[2])), bf16)
    named["part4"] = ((slabs, enc.tokens, weights[4].shape[2]), bf16)
    named["part0"] = ((slabs, enc.tokens, 256), bf16)
    ship_shapes = [jax.ShapeDtypeStruct(named[BUFFER_OF.get(k, k)][0], bf16) for k in SHIPPED]
    an = pl.BlockSpec(memory_space=pl.ANY)
    vm = pl.BlockSpec(memory_space=pltpu.VMEM)
    sm = pl.BlockSpec(memory_space=pltpu.SMEM)
    DMA = pltpu.SemaphoreType.DMA
    count = len(weights)
    pad_rows = lambda t: jnp.pad(t, ((0, dec_rows - NP), (0, 0)))
    table_e = jnp.asarray(np.pad(sincos_table(NP, enc_w), ((0, dec_rows - NP), (0, 0))))
    table_d = jnp.asarray(np.pad(sincos_table(NP, dec_w), ((0, dec_rows - NP), (0, 0))))
    res = pl.pallas_call(
        functools.partial(compute_kernel, per, slabs, list(named), count),
        out_shape=ship_shapes + [jax.ShapeDtypeStruct((16, enc_w), f32)],
        in_specs=[an] * count + [vm] * 8 + [sm],
        out_specs=[an] * len(SHIPPED) + [vm],
        scratch_shapes=[pltpu.VMEM(g.shape, bf16) for g in weights]
        + [DMA((count,)), DMA((len(SHIPPED),))]
        + [pltpu.VMEM(s, d) for s, d in named.values()],
        compiler_params=pltpu.CompilerParams(vmem_limit_bytes=60 << 20),
    )(*weights, patches, vis_col, vis_row, loss_w, vec_parts, weight_sum, table_e, table_d, counts)
    return res[: len(SHIPPED)], res[len(SHIPPED)]


def split_low(x):
    high = x.astype(jnp.bfloat16)
    return high, (x - high.astype(jnp.float32)).astype(jnp.bfloat16)


def dot_three(a, b, kind=dot_nn):
    (ah, al), (bh, bl) = a, b
    return kind(ah, bh) + (kind(ah, bl) + kind(al, bh))


def roots(mats):
    side = mats[0].shape[0]
    eye = lax.broadcasted_iota(jnp.int32, (side, side), 0) == lax.broadcasted_iota(jnp.int32, (side, side), 1)
    five = jnp.where(eye, 5.0, 0.0)
    size = [jnp.sqrt(jnp.sum(m * m, keepdims=True)) for m in mats]
    current = [m * (1.0 / s) for m, s in zip(mats, size)]
    result = None
    for step in range(NEWTON):
        factor = [split_low((five - c) * 0.25) for c in current]
        if result is None:
            result = [(five - c) * 0.25 for c in current]
        else:
            result = [dot_three(split_low(r), f) for r, f in zip(result, factor)]
        if step + 1 < NEWTON:
            square = [split_low(dot_three(f, f)) for f in factor]
            fourth = [split_low(dot_three(q, q)) for q in square]
            current = [dot_three(q, split_low(c)) for q, c in zip(fourth, current)]
    return [r * lax.rsqrt(jnp.sqrt(s)) for r, s in zip(result, size)]


GROUPS = (21, 14)


def optimizer_kernel(pieces, upright, sides, enc_cols, dec_cols, *refs):
    it = iter(refs)
    take = lambda k: [next(it) for _ in range(k)]
    n_mats = len(pieces)
    owned = take(max(p[0] for blocks in pieces for parts in blocks for p in parts) + 1)
    masters = take(n_mats)
    stats = take(4)
    squares, vec_sum, weight_sum, vectors, first, second, step_count = take(7)
    new = take(n_mats)
    new_stats = take(4)
    new_vectors, new_first, new_second, norms, loss_out, weight_out = take(6)
    g_enc, g_dec, u_enc, u_dec = take(4)
    old = take(4)
    fresh = take(4)
    in_sem, out_sem = take(2)
    f32 = jnp.float32
    loads = []
    for i in (2, 3, 0, 1):
        c = pltpu.make_async_copy(stats[i], old[i], in_sem.at[i])
        c.start()
        loads.append((i, c))
    loads = dict(loads)

    enc_vec, dec_vec = vec_sum[0:6, :], vec_sum[6:13, 0 : dec_cols * (vec_sum.shape[1] // enc_cols)]
    enc_sq = squares[0:1, 0:1] + jnp.sum(enc_vec * enc_vec, keepdims=True)
    dec_sq = squares[1:2, 0:1] + jnp.sum(dec_vec * dec_vec, keepdims=True)
    norms[0] = jnp.sqrt(enc_sq)[0, 0]
    norms[1] = jnp.sqrt(dec_sq)[0, 0]
    loss_out[0] = vec_sum[13:14, 0:1][0, 0]
    weight_out[0] = weight_sum[0:1, 0:1][0, 0]
    clip = jnp.minimum(1.0, CLIP_NORM / jnp.sqrt(enc_sq + dec_sq))

    sections = ((1, g_dec, u_dec, 2, LR_MATRIX), (0, g_enc, u_enc, 0, LR_MATRIX * LAYER_DECAY))
    for which, grad, update, base, rate in sections:
        at = 0
        for i in range(n_mats):
            if sides[i] != which:
                continue
            for parts in pieces[i]:
                col = 0
                for src, lo, width in parts:
                    grad[at, :, col : col + width] = owned[src][:, lo : lo + width] * clip
                    col += width
                at += 1
        total = at
        loads[base].wait()
        loads[base + 1].wait()
        group = min(GROUPS[which], total)
        def body(i, carry):
            start = jnp.minimum(i * group, total - group)
            g = [grad[start + j] for j in range(group)]
            low = [split_low(x) for x in g]
            turned = [split_low(x.T) for x in g]
            small = [STAT_DECAY * old[base][start + j] + (1.0 - STAT_DECAY) * dot_three(low[j], low[j], dot_nt) for j in range(group)]
            large = [STAT_DECAY * old[base + 1][start + j] + (1.0 - STAT_DECAY) * dot_three(turned[j], turned[j], dot_nt) for j in range(group)]
            for j in range(group):
                fresh[base][start + j] = small[j]
                fresh[base + 1][start + j] = large[j]
            left = roots(small)
            right = roots(large)
            for j in range(group):
                half = dot_three(split_low(left[j]), low[j])
                update[start + j] = rate * dot_three(split_low(half), split_low(right[j]))
            return carry
        lax.fori_loop(0, -(-total // group), body, 0)
        for k in (base, base + 1):
            pltpu.make_async_copy(fresh[k], new_stats[k], out_sem.at[k]).start()
        at = 0
        for i in range(n_mats):
            if sides[i] != which:
                continue
            for k in range(len(pieces[i])):
                lo = k * BLOCK
                if upright[i]:
                    new[i][:, lo : lo + BLOCK] = masters[i][:, lo : lo + BLOCK] - update[at]
                else:
                    new[i][lo : lo + BLOCK, :] = masters[i][lo : lo + BLOCK, :] - update[at].T
                at += 1

    na = lax.axis_index("narrow")
    steps = jnp.full((1, 128), step_count[0], jnp.int32).astype(f32)[0:1, 0:1]
    scale_one = 1.0 / (1.0 - jnp.exp(steps * math.log(BETA_FIRST)))
    scale_two = 1.0 / (1.0 - jnp.exp(steps * math.log(BETA_SECOND)))
    slabs = vec_sum.shape[1] // enc_cols
    at = 0
    for k in range(13):
        width = enc_cols if k < 6 else dec_cols
        rate = LR_VECTOR * LAYER_DECAY if k < 6 else LR_VECTOR
        g = vec_sum[k : k + 1, 0:width]
        for n in range(1, slabs):
            g = jnp.where(na == n, vec_sum[k : k + 1, n * width : (n + 1) * width], g)
        g = g * clip
        cols = slice(at, at + width)
        one = BETA_FIRST * first[:, cols] + (1.0 - BETA_FIRST) * g
        two = BETA_SECOND * second[:, cols] + (1.0 - BETA_SECOND) * g * g
        new_first[:, cols] = one
        new_second[:, cols] = two
        new_vectors[:, cols] = vectors[:, cols] - rate * (one * scale_one) / (jnp.sqrt(two * scale_two) + EPS_ADAM)
        at += width
    for k in range(4):
        pltpu.make_async_copy(fresh[k], new_stats[k], out_sem.at[k]).wait()


def optimizer(owned, masters, stats, squares, vec_sum, weight_sum, vectors, first, second, step_count, enc_cols, dec_cols):
    kinds = ENC_KINDS + DEC_KINDS
    sides = (0,) * len(ENC_KINDS) + (1,) * len(DEC_KINDS)
    width = [m.shape[1] if kind else m.shape[0] for m, kind in zip(masters, kinds)]
    def plain(src, first_col, cols):
        return [[(src, first_col + k * BLOCK, BLOCK)] for k in range(cols // BLOCK)]
    def by_head(src, cols, head):
        heads = cols // (3 * head)
        per = BLOCK // head
        order = [(t * heads + h) * head for h in range(heads) for t in range(3)]
        return [[(src, order[k * per + j], head) for j in range(per)] for k in range(cols // BLOCK)]
    pieces = [
        plain(0, width[1], width[0]), by_head(0, width[1], DH), plain(1, 0, width[2]), plain(2, 0, width[3]),
        plain(3, 0, width[4]), plain(4, 0, width[5]), by_head(5, width[6], DHD), plain(6, 0, width[7]),
        plain(7, 0, width[8]), plain(8, 0, width[9]), plain(9, 0, width[10]),
    ]
    flat = [s.reshape(s.shape[2:]) for s in stats]
    upright = [kind or i != 2 for i, kind in enumerate(kinds)]
    masters = [m if kind or not up else m.T for m, kind, up in zip(masters, kinds, upright)]
    f32 = jnp.float32
    like = lambda x: jax.ShapeDtypeStruct(x.shape, f32)
    an = pl.BlockSpec(memory_space=pl.ANY)
    vm = pl.BlockSpec(memory_space=pltpu.VMEM)
    sm = pl.BlockSpec(memory_space=pltpu.SMEM)
    block = [pltpu.VMEM((flat[i].shape[0], flat[i].shape[1], BLOCK), f32) for i in (0, 2)]
    whole = [pltpu.VMEM(s.shape, f32) for s in flat]
    DMA = pltpu.SemaphoreType.DMA
    n = len(masters)
    res = pl.pallas_call(
        functools.partial(optimizer_kernel, pieces, upright, sides, enc_cols, dec_cols),
        out_shape=[like(m) for m in masters] + [like(s) for s in flat]
        + [like(vectors)] * 3 + [jax.ShapeDtypeStruct((k,), f32) for k in (2, 1, 1)],
        in_specs=[vm] * (len(owned) + n) + [an] * 4 + [vm] * 6 + [sm],
        out_specs=[vm] * n + [an] * 4 + [vm] * 3 + [sm] * 3,
        scratch_shapes=block + block + whole + whole + [DMA((4,)), DMA((4,))],
        compiler_params=pltpu.CompilerParams(vmem_limit_bytes=56 << 20),
    )(*owned, *masters, *flat, squares, vec_sum, weight_sum, vectors, first, second, step_count)
    new_stats = [r.reshape(s.shape) for r, s in zip(res[n : n + 4], stats)]
    new = [r if kind or not up else r.T for r, kind, up in zip(res[:n], kinds, upright)]
    return new, new_stats, res[n + 4 : n + 7], res[n + 7], res[n + 8].reshape(()), res[n + 9].reshape(())


def heads_apart(shard, head):
    return shard.reshape(shard.shape[0], -1, 3, head).transpose(0, 2, 1, 3).reshape(shard.shape)


def per_device(
    sizes,
    patches, vis_index, keep_mask, counts, step_count,
    w_embed, enc_qkv, enc_out, enc_up, enc_down, w_bridge,
    dec_qkv, dec_out, dec_up, dec_down, w_head,
    vectors, first_moment, second_moment, enc_small, enc_big, dec_small, dec_big,
):
    n_dp, n_wide, n_nar = sizes
    ext = extents(sizes)
    narrow_at = lax.axis_index("narrow")
    masters = (w_embed, enc_qkv, enc_out, enc_up, enc_down, w_bridge, dec_qkv, dec_out, dec_up, dec_down, w_head)
    low = lambda w: w.astype(jnp.bfloat16)
    shards = [
        jnp.concatenate([heads_apart(low(enc_qkv), DH), low(w_embed)], axis=1),
        low(enc_out).T, low(enc_up), low(enc_down).T, low(w_bridge),
        heads_apart(low(dec_qkv), DHD), low(dec_out).T, low(dec_up), low(dec_down).T, low(w_head),
    ]
    enc_cols, dec_cols = w_embed.shape[1], w_bridge.shape[1]
    weight_part = jnp.sum(NP - (1.0 - VISIBLE_WEIGHT) * counts.astype(jnp.float32))
    vec_part = jnp.concatenate(
        [
            vectors[:, : 6 * enc_cols].reshape(6, enc_cols),
            jnp.pad(vectors[:, 6 * enc_cols :].reshape(7, dec_cols), ((0, 3), (0, enc_cols - dec_cols))),
        ]
    )
    units, events = gather_plan(ext, [s.shape for s in shards])
    gathered, vec_parts, weight_sum = gather(
        shards, vec_part, jnp.full((8, 128), weight_part, jnp.float32), sizes, units, events
    )

    all_images = counts.shape[0]
    per = -(-all_images // n_nar)
    first = narrow_at * per
    start = jnp.minimum(first, all_images - per)
    live = (start + jnp.arange(per) >= first).astype(jnp.float32)
    pick = lambda x: lax.dynamic_slice_in_dim(x, start, per, 0)
    patches, vis_index, keep_mask, counts = map(pick, (patches, vis_index, keep_mask, counts))
    dec_rows, enc_rows = -(-NP // 16) * 16, -(-KEEP_MOST // 16) * 16
    patches = jnp.pad(patches, ((0, 0), (0, dec_rows - NP), (0, 0)))
    vis = jnp.pad(vis_index, ((0, 0), (0, enc_rows - KEEP_MOST)), constant_values=-1)
    loss_w = jnp.where(keep_mask == 1, VISIBLE_WEIGHT, 1.0) * live[:, None]
    loss_w = jnp.pad(loss_w, ((0, 0), (0, dec_rows - NP)))
    shipped, vec_grad = compute(
        [g.reshape(n_nar, -1, g.shape[-1]) for g in gathered],
        patches, vis[:, :, None], vis[:, None, :], loss_w[:, :, None], vec_parts, weight_sum, counts,
    )
    lefts, rights = shipped[: len(LEFTS)], shipped[len(LEFTS) :]
    pairs = ([(0, 0), (1, 1)], [(2, 2)], [(3, 3)], [(4, 4)], [(5, 5)], [(6, 6)], [(7, 7)], [(8, 8)], [(9, 9)], [(10, 10)])
    mats = []
    for terms, shard in zip(pairs, shards):
        cols = -(-shard.shape[1] // 128) * 128
        wide = [rights[g].shape[2] for _, g in terms]
        mats.append((shard.shape[0], cols, [(x, g, 0 if i == 0 else cols - wide[i], wide[i]) for i, (x, g) in enumerate(terms)]))
    units, events = reduce_plan(ext, mats)
    owned, vec_sum, squares = reduce_scatter(
        lefts, rights, mats, vec_grad, sizes, units, events, [True] * 5 + [False] * 5
    )
    new, new_stats, new_vecs, norms, loss_total, weight_total = optimizer(
        owned, masters, (enc_small, enc_big, dec_small, dec_big), squares, vec_sum,
        weight_sum, vectors, first_moment, second_moment, step_count, enc_cols, dec_cols,
    )
    return (*new, *new_stats, *new_vecs, norms, loss_total, weight_total)


def solution(mesh):
    sizes = (mesh.shape["dp"], mesh.shape["wide"], mesh.shape["narrow"])
    rows = P(("dp", "wide"))
    matrix = P(("dp", "wide"), "narrow")
    turned = P("narrow", ("dp", "wide"))
    matrices = tuple(matrix if kind else turned for kind in ENC_KINDS + DEC_KINDS)
    stats = (P(("dp", "wide"), "narrow"),) * 4
    packed = (P("narrow"),) * 3
    in_specs = (rows, rows, rows, rows, P()) + matrices + packed + stats
    out_specs = matrices + stats + packed + (P(), P(), P())
    return jax.shard_map(
        functools.partial(per_device, sizes), mesh=mesh, in_specs=in_specs, out_specs=out_specs, check_vma=False
    )
```

```python
import functools
import math

import jax
import jax.numpy as jnp
import numpy as np
from jax import lax
from jax.experimental import pallas as pl
from jax.experimental.pallas import tpu as pltpu
from jax.sharding import PartitionSpec as P

D = 768
DH = 64
DD = 512
DHD = 32
PIX = 768
NP = 196
BLOCK = 64
NEWTON = 3
KEEP_MOST = 98

HIGH = lax.Precision.HIGHEST
EPS_NORM = 1e-06
VISIBLE_WEIGHT = 0.1
STAT_DECAY = 0.5
LR_MATRIX = 0.2
LR_VECTOR = 0.2
LAYER_DECAY = 0.75
BETA_FIRST = 0.9
BETA_SECOND = 0.999
EPS_ADAM = 1e-08
CLIP_NORM = 1.0
ENC_KINDS = (True, True, False, True, False, True)
DEC_KINDS = (True, False, True, False, True)


MESHT = pl.DeviceIdType.MESH
FULL_CODE = 32767.0
FLOOR = 1e-30


def xors(n):
    return list(range(1, n))


def extents(sizes):
    n_dp, n_wide, n_nar = sizes
    return {"n": n_nar, "h": n_dp // 2, "l": 2, "w": n_wide // 2}


def phases_of(order, ext):
    return [d for d in order if ext[d] > 1]


def messages(order, ext):
    out, left = [], 1
    for d in ext:
        left *= ext[d]
    for d in phases_of(order, ext):
        left //= ext[d]
        out.append((d, ext[d] - 1, left))
    return out


class Place:
    def __init__(self, sizes):
        self.sizes = sizes
        self.ext = extents(sizes)
        self.dp, self.wi, self.na = (lax.axis_index(x) for x in ("dp", "wide", "narrow"))
        self.own = {"n": self.na, "h": self.dp // 2, "l": self.dp % 2, "w": self.wi // 2}
        self.core = self.wi % 2

    def peer(self, dim, k):
        if dim == "n":
            return {"narrow": self.na ^ k}
        if dim == "h":
            return {"dp": self.dp ^ (2 * k)}
        if dim in "ld":
            return {"dp": self.dp ^ k}
        if dim == "w":
            return {"wide": self.wi ^ (2 * k)}
        return {"wide": self.wi ^ 1}

    def greet(self):
        ext = self.ext
        partners = [self.peer(d, k) for d in "nw" for k in xors(ext[d])]
        partners += [self.peer("d", k) for k in xors(self.sizes[0])] + [self.peer("c", 1)]
        barrier = pltpu.get_barrier_semaphore()
        for p in partners:
            pl.semaphore_signal(barrier, inc=1, device_id=p, device_id_type=MESHT)
        pl.semaphore_wait(barrier, len(partners))

    def hops(self, narrow):
        out = [("c", 2, self.core), ("d", self.sizes[0], self.dp)]
        if self.ext["w"] > 1:
            out.append(("w", self.ext["w"], self.wi // 2))
        if narrow and self.ext["n"] > 1:
            out.append(("n", self.ext["n"], self.na))
        return out


def remote(src, dst, ss, rs, dev):
    return pltpu.make_async_remote_copy(
        src_ref=src, dst_ref=dst, send_sem=ss, recv_sem=rs, device_id=dev, device_id_type=MESHT
    )


class SmallSum:
    def __init__(self, place, value, lands, send, recv, narrow):
        self.place, self.value, self.lands, self.send, self.recv = place, value, lands, send, recv
        self.axes = place.hops(narrow)
        self.flight = None

    def start(self, i):
        d, members, at = self.axes[i]
        land = self.lands[i]
        land[at] = self.value[...]
        self.flight = []
        for k in xors(members):
            c = remote(self.value, land.at[at], self.send.at[i, k - 1], self.recv.at[i, k - 1], self.place.peer(d, k))
            c.start()
            self.flight.append(c)

    def finish(self, i):
        d, members, at = self.axes[i]
        for c in self.flight:
            c.wait()
        total = self.lands[i][0]
        for j in range(1, members):
            total = total + self.lands[i][j]
        self.value[...] = total

    @staticmethod
    def scratch(sizes, shape, narrow):
        members = [2, sizes[0]] + ([sizes[1] // 2] if sizes[1] > 2 else []) + ([sizes[2]] if narrow and sizes[2] > 1 else [])
        return [pltpu.VMEM((m,) + shape, jnp.float32) for m in members]

    @staticmethod
    def sems(sizes):
        return [pltpu.SemaphoreType.DMA((4, max(*sizes, 2)))] * 2


def plan(units, events, mats, ext, tokens):
    flat = []
    for step in events:
        for u, p in step:
            if p <= len(phases_of(units[u][3], ext)) + 3:
                flat.append((u, p))
    at = {e: i for i, e in enumerate(flat)}
    blocks = ext["h"] * ext["l"] * ext["w"]
    wants = []
    big = max((mats[m][0] for m, *_ in units)), max(hi - lo for m, lo, hi, o in units)
    first_use, last_need = {}, {}
    for u, (m, lo, hi, order) in enumerate(units):
        a, c = mats[m][0], hi - lo
        for x, g, *_ in terms_of(mats, m, lo, hi):
            first_use[x] = min(first_use.get(x, (len(flat),)), (at[u, 0], at[u, 1], tokens[g], a))
            last_need[x] = max(last_need.get(x, 0), at[u, 3])
        last = at[u, len(phases_of(order, ext)) + 3]
        full = (ext["n"], blocks) + (big if a * c * 5 > 2 * big[0] * big[1] else (a, c))
        for j, (x, g, c_lo, c_hi, g_lo) in enumerate(terms_of(mats, m, lo, hi)):
            wants.append((at[u, 0], at[u, 3], ("g", u, j), (ext["n"], tokens[g], c_hi - c_lo), "b"))
        wants.append((at[u, 1], at[u, 3], ("out", u), full, "f"))
        wants.append((at[u, 2], at[u, 3], ("stage", u), full, "f"))
        wants.append((at[u, 3], at[u, 3], ("acc", u), full, "f"))
        wants.append((at[u, 3], last, ("kept", u), (messages(order, ext)[0][2], a, c), "f"))
        for p, (d, k, n) in enumerate(messages(order, ext)):
            wants.append((at[u, p + 3], last, ("q", u, p), (k, n, a, c), "q"))
    for x, (start, turn, rows, a) in first_use.items():
        turn = min(at[u, 1] for u, (m, lo, hi, o) in enumerate(units) if any(x == t[0] for t in terms_of(mats, m, lo, hi)))
        wants.append((start, turn, ("plain", x), (rows, 2 * blocks * a), "b"))
        wants.append((start, last_need[x], ("turned", x), (blocks, 2, a, rows), "b"))
    wants.sort(key=lambda w: w[0])
    bufs, where = [], {}
    for start, end, name, shape, kind in wants:
        for i, b in enumerate(bufs):
            if b[0] == (shape, kind) and b[1] < start:
                b[1] = end
                where[name] = i
                break
        else:
            bufs.append([(shape, kind), end])
            where[name] = len(bufs) - 1
    return [b[0] for b in bufs], where


def terms_of(mats, m, lo, hi):
    out = []
    for x, g, first, width in mats[m][2]:
        a, b = max(lo, first), min(hi, first + width)
        if a < b:
            out.append((x, g, a - lo, b - lo, a - first))
    out.sort(key=lambda t: t[2] - t[3])
    return out


def reduce_kernel(sizes, units, events, mats, n_left, n_right, planned, is_enc, *refs):
    place = Place(sizes)
    ext, own, core = place.ext, place.own, place.core
    count, nu = len(mats), len(units)
    blocks = ext["h"] * ext["l"] * ext["w"]
    f32 = jnp.float32
    it = iter(refs)
    take = lambda k: [next(it) for _ in range(k)]
    lefts, rights = take(n_left), take(n_right)
    vec = next(it)
    outs = take(count)
    vec_out, sq_out = take(2)
    land = take(nu)
    kinds, where = planned
    pool = [tuple(take(2)) if kind == "q" else take(1)[0] for _, kind in kinds]
    recv_q, recv_s = [], []
    for u in range(nu):
        k = len(messages(units[u][3], ext))
        recv_q.append(take(k))
        recv_s.append(take(k))
    plain = [pool[where["plain", x]] for x in range(n_left)]
    turned = [pool[where["turned", x]] for x in range(n_left)]
    n_axes = len(place.hops(True))
    vec_land, sq_land = take(n_axes), take(n_axes)
    (core_send, core_recv, stage_sem, g_sem, x_sem, q_send, q_recv, s_send, s_recv, v_send, v_recv, t_send, t_recv) = take(13)
    left_copies = {}
    place.greet()
    small = SmallSum(place, vec_out, vec_land, v_send, v_recv, True)
    vec_out[...] = vec[...]
    squares = SmallSum(place, sq_out, sq_land, t_send, t_recv, True)

    pending = []
    last_use = {}
    flight = {}
    sums = [jnp.zeros((1, 1), f32), jnp.zeros((1, 1), f32)]
    ready = set()

    def turn(k):
        if k in ready:
            return
        ready.add(k)
        left_copies[k].wait()
        t = plain[k][...].T
        a = turned[k].shape[2]
        if a % 16 == 0:
            turned[k][...] = t.reshape(turned[k].shape)
        else:
            for i in range(2 * blocks):
                turned[k][i // 2, i % 2] = t[i * a : (i + 1) * a]

    def product(u, n, which, ref_of):
        m, lo, hi, order = units[u]
        a, c = mats[m][0], hi - lo
        for j, (x, g, c_lo, c_hi, g_lo) in enumerate(terms_of(mats, m, lo, hi)):
            right = pool[where["g", u, j]][n]
            if a % 16 == 0:
                rows = turned[x][:, which].reshape(blocks * a, turned[x].shape[3])
                v = lax.dot_general(rows, right, (((1,), (0,)), ((), ())), preferred_element_type=f32)
                v = v.reshape(blocks, a, c_hi - c_lo)
                if j == 0:
                    ref_of[n] = v
                else:
                    ref_of[n, :, :, c_lo:c_hi] += v
            else:
                for b in range(blocks):
                    v = lax.dot_general(turned[x][b, which], right, (((1,), (0,)), ((), ())), preferred_element_type=f32)
                    if j == 0:
                        ref_of[n, b] = v
                    else:
                        ref_of[n, b, :, c_lo:c_hi] += v

    def whole(kind, u):
        m, lo, hi, order = units[u]
        ref = pool[where[kind, u]]
        a, c = mats[m][0], hi - lo
        return ref if ref.shape[2:] == (a, c) else ref.at[:, :, pl.ds(0, a), pl.ds(0, c)]

    def block_of(idx):
        return (idx["h"] * ext["l"] + idx["l"]) * ext["w"] + idx["w"]

    def slab(u, idx):
        at = 0
        for d in "nhlw":
            if d != phases_of(units[u][3], ext)[0]:
                at = at * ext[d] + idx[d]
        return pool[where["kept", u]].at[at]

    def split(s, dims):
        idx = {}
        for d in reversed(dims):
            if ext[d] == 1:
                idx[d] = 0
            else:
                idx[d] = s % ext[d]
                s = s // ext[d]
        return idx

    def loop(total, body):
        def step(s, carry):
            body(s)
            return carry
        lax.fori_loop(0, total, step, 0)

    def reuse(b):
        for c in last_use.pop(b, []):
            c.wait_send()

    def code_and_send(u, p):
        ph = phases_of(units[u][3], ext)
        d, peers, slabs = messages(units[u][3], ext)[p]
        gone = ph[:p]
        free = [x for x in "nhlw" if x != d and x not in gone]
        b = where["q", u, p]
        reuse(b)
        out_q, out_s = pool[b]
        sends = []
        for k in range(1, peers + 1):
            def body(s):
                idx = split(s, free)
                for x in gone:
                    idx[x] = own[x]
                idx[d] = own[d] ^ k
                x = (whole("acc", u).at[idx["n"], block_of(idx)] if p == 0 else slab(u, idx))[...]
                top = jnp.maximum(jnp.max(jnp.abs(x), axis=0, keepdims=True), FLOOR)
                out_q[k - 1, s] = jnp.round(x * (FULL_CODE / top)).astype(jnp.int32).astype(jnp.int16)
                out_s[k - 1, s] = top * (1.0 / FULL_CODE)
            loop(slabs, body)
            dev = place.peer(d, k)
            first = remote(out_q.at[k - 1], recv_q[u][p].at[k - 1], q_send.at[u, p, k - 1], q_recv.at[u, p, k - 1], dev)
            second = remote(out_s.at[k - 1], recv_s[u][p].at[k - 1], s_send.at[u, p, k - 1], s_recv.at[u, p, k - 1], dev)
            first.start()
            second.start()
            sends += [first, second]
        flight[u, p] = sends
        last_use[b] = sends

    def take_in(u, p):
        ph = phases_of(units[u][3], ext)
        d, peers, slabs = messages(units[u][3], ext)[p]
        gone = ph[: p + 1]
        free = [x for x in "nhlw" if x not in gone]
        for c in flight[u, p]:
            c.wait_recv()
        def body(s):
            idx = split(s, free)
            for x in gone:
                idx[x] = own[x]
            ref = slab(u, idx)
            v = ref[...]
            for k in range(peers):
                v = v + recv_q[u][p][k, s].astype(jnp.int32).astype(f32) * recv_s[u][p][k, s]
            ref[...] = v
        loop(slabs, body)

    def stage(u, p):
        m, lo, hi, order = units[u]
        n_ph = len(phases_of(order, ext))
        if p == 0:
            copies = []
            for j, (x, g, c_lo, c_hi, g_lo) in enumerate(terms_of(mats, m, lo, hi)):
                if x not in left_copies:
                    left_copies[x] = pltpu.make_async_copy(lefts[x], plain[x], x_sem.at[x])
                    left_copies[x].start()
                src = rights[g]
                if c_hi - c_lo != src.shape[2]:
                    src = src.at[:, :, slice(g_lo, g_lo + c_hi - c_lo)]
                c = pltpu.make_async_copy(src, pool[where["g", u, j]], g_sem.at[u, j])
                c.start()
                copies.append(c)
            flight[u, "g"] = copies
        elif p == 1:
            for c in flight[u, "g"]:
                c.wait()
            for x, *_ in terms_of(mats, m, lo, hi):
                turn(x)
            b = where["out", u]
            reuse(b)
            loop(ext["n"], lambda n: product(u, n, 1 - core, whole("out", u)))
            c = remote(whole("out", u), land[u], core_send.at[u], core_recv.at[u], place.peer("c", 1))
            c.start()
            flight[u, "core"] = c
            last_use[b] = [c]
        elif p == 2:
            flight[u, "core"].wait_recv()
            reuse(where["stage", u])
            c = pltpu.make_async_copy(land[u], whole("stage", u), stage_sem.at[u])
            c.start()
            flight[u, "stage"] = c
        elif p == 3:
            acc, more = whole("acc", u), whole("stage", u)
            reuse(where["acc", u])
            flight[u, "stage"].wait()
            def body(n):
                product(u, n, core, acc)
                acc[n] = acc[n] + more[n]
            loop(ext["n"], body)
            code_and_send(u, 0)
            d, peers, slabs = messages(order, ext)[0]
            def keep(i):
                idx = split(i, [x for x in "nhlw" if x != d])
                idx[d] = own[d]
                slab(u, idx)[...] = acc.at[idx["n"], block_of(idx)][...]
            loop(slabs, keep)
        else:
            take_in(u, p - 4)
            if p - 3 < n_ph:
                code_and_send(u, p - 3)
            else:
                x = slab(u, own)[...]
                outs[m][:, pl.ds(lo, hi - lo)] = x
                w = 0 if is_enc[m] else 1
                sums[w] = sums[w] + jnp.sum(x * x, keepdims=True)

    hop = 0
    for step in events:
        for u, p in step:
            if p <= len(phases_of(units[u][3], ext)) + 3:
                stage(u, p)
                if p == 3 and hop <= n_axes:
                    if hop:
                        small.finish(hop - 1)
                    if hop < n_axes:
                        small.start(hop)
                    hop += 1
    while hop <= n_axes:
        if hop:
            small.finish(hop - 1)
        if hop < n_axes:
            small.start(hop)
        hop += 1
    row = lax.broadcasted_iota(jnp.int32, (8, 128), 0)
    sq_out[...] = jnp.where(row == 0, sums[0], jnp.where(row == 1, sums[1], 0.0))
    for i in range(n_axes):
        squares.start(i)
        squares.finish(i)
    for c in [c for cs in last_use.values() for c in cs]:
        c.wait_send()


def reduce_scatter(lefts, rights, mats, vec, sizes, units, events, is_enc, cid=1):
    ext = extents(sizes)
    blocks = ext["h"] * ext["l"] * ext["w"]
    f32, bf16 = jnp.float32, jnp.bfloat16
    tokens = [r.shape[1] for r in rights]
    planned = plan(units, events, mats, ext, tokens)
    coded = lambda k, n, a, c: [pltpu.VMEM((k, n, a, c), jnp.int16), pltpu.VMEM((k, n, 1, c), f32)]
    scratch = []
    for shape, kind in planned[0]:
        scratch += coded(*shape) if kind == "q" else [pltpu.VMEM(shape, f32 if kind == "f" else bf16)]
    for m, lo, hi, order in units:
        ms = [coded(k, n, mats[m][0], hi - lo) for d, k, n in messages(order, ext)]
        scratch += [x[0] for x in ms] + [x[1] for x in ms]
    scratch += SmallSum.scratch(sizes, vec.shape, True) + SmallSum.scratch(sizes, (8, 128), True)
    nu, kmax = len(units), max(ext.values())
    D_ = pltpu.SemaphoreType.DMA
    scratch += [D_((nu,))] * 3 + [D_((nu, 2)), D_((len(lefts),))] + [D_((nu, 4, kmax))] * 4 + SmallSum.sems(sizes) * 2
    vm = pl.BlockSpec(memory_space=pltpu.VMEM)
    an = pl.BlockSpec(memory_space=pl.ANY)
    res = pl.pallas_call(
        functools.partial(reduce_kernel, sizes, units, events, mats, len(lefts), len(rights), planned, is_enc),
        out_shape=[jax.ShapeDtypeStruct(m[:2], f32) for m in mats]
        + [jax.ShapeDtypeStruct(vec.shape, f32), jax.ShapeDtypeStruct((8, 128), f32)]
        + [jax.ShapeDtypeStruct((ext["n"], blocks, mats[m][0], hi - lo), f32) for m, lo, hi, o in units],
        in_specs=[an] * (len(lefts) + len(rights)) + [vm],
        out_specs=[vm] * (len(mats) + 2) + [an] * nu,
        scratch_shapes=scratch,
        compiler_params=pltpu.CompilerParams(collective_id=cid, has_side_effects=True, vmem_limit_bytes=60 << 20),
    )(*lefts, *rights, vec)
    return res[: len(mats)], res[len(mats)], res[len(mats) + 1]


class Gather:
    def __init__(self, place, units, events, shards, outs, sems):
        self.place, self.units, self.shards, self.outs = place, units, shards, outs
        self.send_sem, self.recv_sem, self.loc_sem = sems
        self.events = [(u, p) for step in events for u, p in step if p <= len(self.phases(u, units))]
        self.next = 0
        self.pending, self.from_sibling = [], []
        self.slots = [0] * len(units)
        self.flight, self.local = {}, {}
        self.complete = set()

    def phases(self, u, units=None):
        return [d for d in (units or self.units)[u][3] if self.place.ext[d] > 1]

    def region(self, u, full, at, which_core):
        m, lo, hi, order = self.units[u]
        own = self.place.own
        idx = [slice(None) if d in full else own[d] ^ at[1] if at and d == at[0] else own[d] for d in "nhlw"]
        if (lo, hi) == (0, self.shards[m].shape[1]):
            return self.outs[m].at[tuple(idx) + (which_core,)]
        return self.outs[m].at[tuple(idx) + (which_core, slice(None), slice(lo, hi))]

    def shard(self, u):
        m, lo, hi, order = self.units[u]
        return self.shards[m] if (lo, hi) == (0, self.shards[m].shape[1]) else self.shards[m].at[:, slice(lo, hi)]

    def send(self, u, src, dst, dev, landing):
        k = self.slots[u]
        self.slots[u] += 1
        c = remote(src, dst, self.send_sem.at[u, k], self.recv_sem.at[u, k], dev)
        c.start()
        self.pending.append(c)
        return remote(landing, landing, self.send_sem.at[u, k], self.recv_sem.at[u, k], dev)

    def stage(self, u, p):
        place, core = self.place, self.place.core
        m, ph = self.units[u][0], self.phases(u)
        sibling = place.peer("c", 1)
        came = self.flight.pop(u, [])
        if p == 0:
            c = pltpu.make_async_copy(self.shard(u), self.region(u, (), None, core), self.loc_sem.at[u])
            c.start()
            self.local[u] = c
            src = self.shard(u)
            self.from_sibling.append((m, self.send(u, src, self.region(u, (), None, core), sibling, self.region(u, (), None, 1 - core))))
        else:
            for k, w in came:
                w.wait_recv()
            if p == 1:
                self.local[u].wait()
            src = None
        if p < len(ph):
            mine = src if src is not None else self.region(u, ph[:p], None, core)
            self.flight[u] = [
                (k, self.send(u, mine, self.region(u, ph[:p], None, core), place.peer(ph[p], k), self.region(u, ph[:p], (ph[p], k), core)))
                for k in xors(place.ext[ph[p]])
            ]
        for k, _ in came:
            here = self.region(u, ph[: p - 1], (ph[p - 1], k), core)
            there = self.region(u, ph[: p - 1], (ph[p - 1], k), 1 - core)
            self.from_sibling.append((m, self.send(u, here, here, sibling, there)))

    def tick(self, steps):
        for u, p in self.events[self.next : self.next + steps]:
            self.stage(u, p)
        self.next += steps

    def need(self, m):
        if m in self.complete:
            return
        self.complete.add(m)
        last = max(i for i, (u, p) in enumerate(self.events) if self.units[u][0] == m)
        self.tick(max(0, last + 1 - self.next))
        for which, c in self.from_sibling:
            if which == m:
                c.wait_recv()

    def finish(self):
        for m in range(len(self.shards)):
            self.need(m)
        for c in self.pending:
            c.wait_send()


def cast_shards(masters, shards):
    embed, eqkv, eout, eup, edown, bridge, dqkv, dout, dup, ddown, head = masters
    low = jnp.bfloat16
    def by_kind(src, dst, size):
        heads = src.shape[1] // (3 * size)
        for t in range(3):
            for h in range(heads):
                to, at = (t * heads + h) * size, (h * 3 + t) * size
                dst[:, to : to + size] = src[:, at : at + size].astype(low)
    by_kind(eqkv, shards[0], DH)
    shards[0][:, eqkv.shape[1] :] = embed[...].astype(low)
    shards[1][...] = eout[...].T.astype(low)
    by_kind(dqkv, shards[5], DHD)
    for m, src in ((2, eup), (3, edown), (4, bridge), (6, dout), (7, dup), (8, ddown), (9, head)):
        shards[m][...] = src[...].astype(low)


def shard_shapes(masters):
    a, d = masters[0].shape[0], masters[6].shape[0]
    enc = (masters[0].shape[1] + masters[1].shape[1], masters[2].shape[0], *(m.shape[1] for m in masters[3:6]))
    return [(a, c) for c in enc] + [(d, m.shape[1]) for m in masters[6:]]


class Start:
    def __init__(self, sizes, masters, shards, vec, counts, vec_all, weight_sum, lands, sems):
        self.place = place = Place(sizes)
        vec_send, vec_recv, sum_send, sum_recv = sems
        cast_shards(masters, shards)
        total = jnp.float32(0.0)
        for i in range(counts.shape[0]):
            total = total + (NP - (1.0 - VISIBLE_WEIGHT) * counts[i].astype(jnp.float32))
        weight_sum[...] = jnp.zeros(weight_sum.shape, jnp.float32) + total
        place.greet()
        self.flight = []
        for k in xors(place.ext["n"]):
            c = remote(vec, vec_all.at[place.na], vec_send.at[k - 1], vec_recv.at[k - 1], place.peer("n", k))
            c.start()
            self.flight.append(c)
        vec_all[place.na] = vec[...]
        self.small = SmallSum(place, weight_sum, lands, sum_send, sum_recv, False)

    def sum_hops(self):
        return len(self.small.axes)

    def vectors_here(self):
        for c in self.flight:
            c.wait()

    @staticmethod
    def scratch(sizes, shapes):
        n = sizes[2]
        return (
            [pltpu.VMEM(s, jnp.bfloat16) for s in shapes]
            + SmallSum.scratch(sizes, (8, 128), False)
            + [pltpu.SemaphoreType.DMA((n,))] * 2
            + SmallSum.sems(sizes)
        )


def gather_sems(sizes, units):
    slots = 2 * sum(extents(sizes).values())
    DMA = pltpu.SemaphoreType.DMA
    return [DMA((len(units), slots)), DMA((len(units), slots)), DMA((len(units),))]


def gather_kernel(sizes, units, events, *refs):
    it = iter(refs)
    take = lambda k: [next(it) for _ in range(k)]
    masters = take(11)
    vec, counts = take(2)
    outs = take(10)
    vec_all, weight_sum = take(2)
    shards = take(10)
    lands = take(len(SmallSum.scratch(sizes, (8, 128), False)))
    small_sems, sems = take(4), take(3)
    start = Start(sizes, masters, shards, vec, counts, vec_all, weight_sum, lands, small_sems)
    g = Gather(start.place, units, events, shards, outs, sems)
    for i in range(start.sum_hops()):
        start.small.start(i)
        start.small.finish(i)
    g.finish()
    start.vectors_here()


def gather(masters, vec, counts, sizes, units, events, cid=0):
    ext = extents(sizes)
    an = pl.BlockSpec(memory_space=pl.ANY)
    vm = pl.BlockSpec(memory_space=pltpu.VMEM)
    sm = pl.BlockSpec(memory_space=pltpu.SMEM)
    shapes = shard_shapes(masters)
    heads = (ext["n"], ext["h"], ext["l"], ext["w"], 2)
    res = pl.pallas_call(
        functools.partial(gather_kernel, sizes, units, events),
        out_shape=[jax.ShapeDtypeStruct(heads + s, jnp.bfloat16) for s in shapes]
        + [jax.ShapeDtypeStruct((sizes[2],) + vec.shape, vec.dtype), jax.ShapeDtypeStruct((8, 128), jnp.float32)],
        in_specs=[vm] * 12 + [sm],
        out_specs=[an] * 10 + [vm, vm],
        scratch_shapes=Start.scratch(sizes, shapes) + gather_sems(sizes, units),
        compiler_params=pltpu.CompilerParams(collective_id=cid, has_side_effects=True),
    )(*masters, vec, counts)
    return res[:10], res[10], res[11]


GATHER_UNITS = (
    (0, 0, 256, "lhwn"), (0, 256, 512, "nlhw"), (0, 512, 768, "nhlw"), (1, 0, 256, "nlhw"), (2, 0, 384, "nhlw"),
    (2, 384, 768, "nlhw"), (3, 0, 384, "nlhw"), (3, 384, 768, "nhlw"), (4, 0, 128, "nhlw"), (5, 0, 384, "hlwn"),
    (6, 0, 128, "lnhw"), (7, 0, 256, "nhlw"), (7, 256, 512, "nlhw"), (8, 0, 256, "nlhw"), (8, 256, 512, "nhlw"),
    (9, 0, 256, "hnlw"),
)
GATHER_ORDER = (
    (8, 0), (3, 0), (2, 0), (1, 0), (0, 0), (7, 0), (8, 1), (0, 1), (5, 0), (4, 0), (3, 1), (8, 2), (6, 0), (0,
    2), (2, 1), (15, 0), (3, 2), (1, 1), (10, 0), (8, 3), (2, 2), (15, 1), (12, 0), (7, 1), (1, 2), (10, 1), (9,
    0), (13, 0), (3, 3), (5, 1), (14, 0), (2, 3), (7, 2), (4, 1), (11, 0), (5, 2), (6, 1), (1, 3), (9, 1), (4, 2),
    (7, 3), (6, 2), (0, 3), (9, 2), (5, 3), (15, 2), (12, 1), (10, 2), (4, 3), (13, 1), (6, 3), (14, 1), (15, 3),
    (10, 3), (11, 1), (12, 2), (14, 2), (13, 2), (11, 2), (14, 3), (12, 3), (11, 3), (13, 3), (9, 3),
)


def gather_plan(ext, shapes):
    cols = [s[1] for s in shapes]
    if ext["w"] > 1:
        units = [(m, 0, c, "nlhw") for m, c in enumerate(cols)]
        return units, [[(u, p)] for u in range(len(units)) for p in range(5)]
    units = [(m, lo, min(hi, cols[m]), order) for m, lo, hi, order in GATHER_UNITS]
    return units, [list(GATHER_ORDER[i : i + 12]) for i in range(0, len(GATHER_ORDER), 12)]


REDUCE_UNITS = (
    (0, 0, 256, "lnhw"), (0, 256, 512, "lhwn"), (0, 512, 768, "hlwn"), (1, 0, 256, "lhwn"), (2, 0, 256, "hlwn"),
    (2, 256, 512, "nhlw"), (2, 512, 768, "lhwn"), (3, 0, 256, "hnlw"), (3, 256, 512, "lhwn"), (3, 512, 768,
    "lhwn"), (4, 0, 128, "lnhw"), (5, 0, 256, "lhwn"), (5, 256, 384, "hlwn"), (6, 0, 128, "hnlw"), (7, 0, 256,
    "hnlw"), (7, 256, 512, "lhwn"), (8, 0, 256, "hlwn"), (8, 256, 512, "hlwn"), (9, 0, 256, "hlwn"),
)
REDUCE_ORDER = (
    (13, 0), (10, 0), (14, 0), (15, 0), (13, 1), (10, 1), (14, 1), (15, 1), (13, 2), (10, 2), (13, 3), (2, 0),
    (10, 3), (14, 2), (2, 1), (0, 0), (15, 2), (14, 3), (0, 1), (5, 0), (13, 4), (15, 3), (5, 1), (8, 0), (2, 2),
    (8, 1), (10, 4), (2, 3), (0, 2), (12, 0), (13, 5), (12, 1), (0, 3), (14, 4), (5, 2), (4, 0), (15, 4), (13, 6),
    (4, 1), (8, 2), (10, 5), (5, 3), (12, 2), (3, 0), (8, 3), (12, 3), (3, 1), (16, 0), (9, 0), (4, 2), (16, 1),
    (9, 1), (2, 4), (14, 5), (4, 3), (7, 0), (3, 2), (0, 4), (15, 5), (7, 1), (10, 6), (16, 2), (3, 3), (18, 0),
    (16, 3), (12, 4), (9, 2), (18, 1), (17, 0), (17, 1), (9, 3), (7, 2), (11, 0), (8, 4), (18, 2), (11, 1), (7,
    3), (1, 0), (17, 2), (18, 3), (6, 0), (1, 1), (4, 4), (2, 5), (17, 3), (14, 6), (11, 2), (6, 1), (5, 4), (11,
    3), (1, 2), (16, 4), (1, 3), (6, 2), (6, 3), (8, 5), (3, 4), (0, 5), (12, 5), (15, 6), (2, 6), (7, 4), (9, 4),
    (8, 6), (12, 6), (4, 5), (18, 4), (11, 4), (17, 4), (5, 5), (7, 5), (16, 5), (3, 5), (4, 6), (0, 6), (16, 6),
    (1, 4), (9, 5), (3, 6), (11, 5), (9, 6), (1, 5), (6, 4), (11, 6), (18, 5), (17, 5), (1, 6), (5, 6), (6, 5),
    (7, 6), (18, 6), (17, 6), (6, 6),
)


def reduce_plan(ext, mats):
    if ext["w"] > 1:
        units = [(m, lo, min(lo + 256, x[1]), "wlhn") for m, x in enumerate(mats) for lo in range(0, x[1], 256)]
        return units, [[(u, p)] for u in range(len(units)) for p in range(8)]
    return list(REDUCE_UNITS), [list(REDUCE_ORDER)]


def sincos_table(rows, width):
    column = np.arange(width)
    freq = np.power(np.float32(10000.0), (-(2 * (column // 2)).astype(np.float32) / np.float32(width)).astype(np.float32))
    angle = (np.arange(rows, dtype=np.float32)[:, None] * freq[None, :]).astype(np.float32)
    return np.where(column % 2 == 0, np.sin(angle), np.cos(angle)).astype(np.float32)


def dot_nn(a, b):
    return lax.dot_general(a, b, (((1,), (0,)), ((), ())), preferred_element_type=jnp.float32)


def dot_nt(a, b):
    return lax.dot_general(a, b, (((1,), (1,)), ((), ())), preferred_element_type=jnp.float32)


def dot_tn(a, b):
    return lax.dot_general(a, b, (((0,), (0,)), ((), ())), preferred_element_type=jnp.float32)


def dot_exact(a, b):
    return lax.dot_general(a, b, (((1,), (0,)), ((), ())), precision=HIGH, preferred_element_type=jnp.float32)


class Side:
    def __init__(self, width, head, heads, rows, images, slabs):
        self.width, self.head, self.heads, self.rows = width, head, heads, rows
        self.slabs = slabs
        self.tokens = rows * images
        self.lane = head * heads
        self.packed = -(-3 * self.lane // 128) * 128

    def scratch(self, hidden):
        t, n, w = self.tokens, self.slabs, self.width
        bf, f = jnp.bfloat16, jnp.float32
        return {
            "x": ((t, w), f),
            "hat1": ((t, w), f), "hat2": ((t, w), f), "hat3": ((t, w), f),
            "inv": ((t, 128), f),
            "n1": ((t, w), bf), "n2": ((t, w), bf), "n3": ((t, w), bf),
            "qkv": ((n, t, self.packed), bf),
            "lse": ((t, 128), f),
            "att": ((n, t, -(-self.lane // 128) * 128), bf),
            "slope": ((n, t, hidden), f),
            "act": ((n, t, hidden), bf),
            "dn": ((t, w), f),
            "og1": ((t, w), bf),
            "og2": ((t, w), bf),
        }


LEFTS = ("e_n1", "chosen", "e_og1", "e_n2", "e_og2", "e_n3", "d_n1", "d_og1", "d_n2", "d_og2", "d_n3")
RIGHTS = ("e_qkv", "part0", "e_att", "e_dh", "e_act", "part4", "d_qkv", "d_att", "d_dh", "d_act", "part9")
SHIPPED = LEFTS + RIGHTS
BUFFER_OF = {"e_dh": "e_act", "d_dh": "d_act"}


def compute_kernel(sizes, merged, per, slabs, names, units, events, *refs):
    it = iter(refs)
    take = lambda k: [next(it) for _ in range(k)]
    f32, bf16 = jnp.float32, jnp.bfloat16
    count = 10
    sources = take(11 if merged else 10)
    vec_parts, weight_in = (take(1)[0], None) if merged else take(2)
    patches_all, vis_all, keep_all, table_e, table_d, counts_all = take(6)
    shipped = take(len(SHIPPED))
    vec_out, weight_out = take(2)
    store = take(count)
    load_sem, store_sem = take(2)
    if merged:
        vec_all = take(1)[0]
        shards = take(count)
        lands = take(len(SmallSum.scratch(sizes, (8, 128), False)))
        small_sems, sems = take(4), take(3)
    buf = dict(zip(names, it))

    all_images = counts_all.shape[0]
    first_image = lax.axis_index("narrow") * per
    start_image = jnp.minimum(first_image, all_images - per)
    patch_copies = []
    for i in range(per):
        c = pltpu.make_async_copy(patches_all.at[start_image + i], buf["raw"].at[i], load_sem.at[count + i])
        c.start()
        patch_copies.append(c)

    ticks = [0]
    if merged:
        begin = Start(sizes, sources, shards, vec_parts, counts_all, vec_all, weight_out, lands, small_sems)
        g = Gather(begin.place, units, events, shards, store, sems)
        g.tick(12)
        for i in range(begin.sum_hops()):
            begin.small.start(i)
            g.tick(12)
            begin.small.finish(i)
        begin.vectors_here()
        need = g.need
    else:
        vec_all = vec_parts
        weight_out[...] = weight_in[...]
        loads = []
        for m in range(count):
            c = pltpu.make_async_copy(sources[m], store[m], load_sem.at[m])
            c.start()
            loads.append(c)
        waited = set()

        def need(m):
            if m not in waited:
                waited.add(m)
                loads[m].wait()

    def tick():
        if merged:
            g.tick(TICK)

    class Weight:
        def __init__(self, ref):
            self.ref = ref
            self.shape = (slabs, math.prod(ref.shape[1:-1]), ref.shape[-1])

        def __getitem__(self, at):
            n, lo, hi = at if isinstance(at, tuple) else (at, 0, self.shape[2])
            v = self.ref[n] if (lo, hi) == (0, self.shape[2]) else self.ref.at[..., lo:hi][n]
            return v.reshape(self.shape[1], hi - lo)

    w_eq, w_out, w_up, w_down, w_bridge, w_dqkv, w_dout, w_dup, w_ddown, w_head = [Weight(r) for r in store]
    enc_w, dec_w = table_e.shape[1], table_d.shape[1]
    dec_rows, enc_rows = table_e.shape[0], -(-KEEP_MOST // 16) * 16
    patches, loss_w, vis_rows = buf["patches"], buf["loss_w"], []
    patches[...] = jnp.zeros_like(patches)
    loss_w[...] = jnp.zeros_like(loss_w)
    counts = []
    for i in range(per):
        patch_copies[i].wait()
        patches[i, 0:NP, :] = buf["raw"][i]
        vis_rows.append(vis_all[pl.ds(start_image + i, 1), :])
        counts.append(counts_all[start_image + i])
        live = jnp.where(start_image + i >= first_image, 1.0, 0.0)
        row = jnp.where(keep_all[pl.ds(start_image + i, 1), :] == 1, VISIBLE_WEIGHT, 1.0) * live
        loss_w[i, 0:NP, :] = jnp.broadcast_to(row, (8, NP)).T[:, 0:1]
    enc = Side(enc_w, DH, w_out.shape[2] // DH, enc_rows, per, slabs)
    dec = Side(dec_w, DHD, w_dout.shape[2] // DHD, dec_rows, per, slabs)
    for s, tag in ((enc, "e_"), (dec, "d_")):
        s.tag = tag
        s.b = {k[2:]: v for k, v in buf.items() if k.startswith(tag)}
    enc.w, dec.w = (w_eq, w_out, w_up, w_down), (w_dqkv, w_dout, w_dup, w_ddown)
    enc.ids, dec.ids = (0, 1, 2, 3), (5, 6, 7, 8)
    enc.base, dec.base = 0, 7
    vec_full = buf["vec_full"]
    enc_c, dec_c = enc_w // slabs, dec_w // slabs
    at = 0
    for k in range(13):
        width = enc_c if k < 6 else dec_c
        for n in range(slabs):
            vec_full[k : k + 1, n * width : (n + 1) * width] = vec_all[n, :, at : at + width]
        at += width
    vec_out[...] = jnp.zeros_like(vec_out)

    def vector(k, width):
        return vec_full[k : k + 1, 0:width]

    CH = 32

    def chunks(total, body):
        def step(i, carry):
            body(pl.ds(pl.multiple_of(i * CH, CH), CH))
            return carry
        lax.fori_loop(0, total // CH, step, 0)

    def norm_fwd(s, k, out, hat, inv):
        gain, bias = vector(s.base + k, s.width), vector(s.base + k + 1, s.width)
        x = s.b["x"]
        def body(r):
            v = x[r, :]
            mean = jnp.mean(v, axis=1, keepdims=True)
            d = v - mean
            i = lax.rsqrt(jnp.mean(d * d, axis=1, keepdims=True) + EPS_NORM)
            h = d * i
            s.b[hat][r, :] = h
            s.b["inv"][r, inv : inv + 1] = i
            s.b[out][r, :] = (h * gain + bias).astype(bf16)
        chunks(s.tokens, body)

    def norm_bwd(s, k, hat, inv, add):
        gain = vector(s.base + k, s.width)
        def body(r):
            dn = s.b["dn"][r, :]
            h = s.b[hat][r, :]
            vec_out[s.base + k : s.base + k + 1, 0 : s.width] += jnp.sum(dn * h, axis=0, keepdims=True)
            vec_out[s.base + k + 1 : s.base + k + 2, 0 : s.width] += jnp.sum(dn, axis=0, keepdims=True)
            g = dn * gain
            d = s.b["inv"][r, inv : inv + 1] * (
                g - jnp.mean(g, axis=1, keepdims=True) - h * jnp.mean(g * h, axis=1, keepdims=True)
            )
            s.b["x"][r, :] = s.b["x"][r, :] + d if add else d
        chunks(s.tokens, body)

    def slab_loop(body):
        def step(n, carry):
            body(n)
            return carry
        lax.fori_loop(0, slabs, step, 0)

    def head_mask(s, h):
        lane = lax.broadcasted_iota(jnp.int32, (1, s.lane), 1)
        return (lane >= h * s.head) & (lane < (h + 1) * s.head)

    def scores(s, q, k, mask, limit):
        v = dot_nt(jnp.where(mask, q, jnp.zeros_like(q)), k) * (s.head ** -0.5)
        key = lax.broadcasted_iota(jnp.int32, (s.rows, s.rows), 1)
        return jnp.where(key < limit, v, -1e30)

    def attention_loop(body, between=None):
        def step(i, carry):
            body(i // slabs, i % slabs)
            return carry
        if between is None or not merged:
            lax.fori_loop(0, per * slabs, step, 0)
            return
        for image in range(per):
            lax.fori_loop(image * slabs, (image + 1) * slabs, step, 0)
            between()

    def image_rows(s, image):
        return pl.ds(pl.multiple_of(image * s.rows, 16), s.rows)

    def block_fwd(s, limit):
        b = s.b
        b["lse"][...] = jnp.zeros_like(b["lse"])
        if b["att"].shape[2] != s.lane:
            b["att"][...] = jnp.zeros_like(b["att"])
        qkv_w, out_w, up_w, down_w = s.w
        need(s.ids[0])
        norm_fwd(s, 0, "n1", "hat1", 1)
        tick()
        def qkv(n):
            b["qkv"][n] = dot_nn(b["n1"][...], qkv_w[n, 0, s.packed]).astype(bf16)
        slab_loop(qkv)
        tick()
        def attend(image, n):
            r = image_rows(s, image)
            q = b["qkv"][n, r, 0 : s.lane]
            k = b["qkv"][n, r, s.lane : 2 * s.lane]
            v = b["qkv"][n, r, 2 * s.lane : 3 * s.lane]
            lane = lax.broadcasted_iota(jnp.int32, (s.rows, 128), 1)
            total = jnp.zeros((s.rows, s.lane), f32)
            lse = b["lse"][r, :]
            for h in range(s.heads):
                mask = head_mask(s, h)
                sc = scores(s, q, k, mask, limit(image))
                top = jnp.max(sc, axis=1, keepdims=True)
                e = jnp.exp(sc - top)
                z = jnp.sum(e, axis=1, keepdims=True)
                p = (e * (1.0 / z)).astype(bf16)
                total = jnp.where(mask, dot_nn(p, v), total)
                lse = jnp.where(lane == n * s.heads + h, top + jnp.log(z), lse)
            b["att"][n, r, 0 : s.lane] = total.astype(bf16)
            b["lse"][r, :] = lse
        attention_loop(attend, tick)
        need(s.ids[1])
        ship(s.tag + "att")
        def project(n):
            b["x"][...] += dot_nt(b["att"][n, :, 0 : s.lane], out_w[n])
        slab_loop(project)
        norm_fwd(s, 2, "n2", "hat2", 2)
        need(s.ids[2])
        need(s.ids[3])
        hid = buf["hid"]
        c = up_w.shape[2]
        def mlp(n):
            hid[0 : s.tokens, 0:c] = dot_nn(b["n2"][...], up_w[n])
            def body(r):
                v = hid[r, 0:c]
                cdf = 0.5 * (1.0 + lax.erf(v * 0.7071067811865476))
                b["act"][n, r, :] = (v * cdf).astype(bf16)
                b["slope"][n, r, :] = cdf + v * (0.3989422804014327 * jnp.exp(-0.5 * v * v))
            chunks(s.tokens, body)
            b["x"][...] += dot_nt(b["act"][n], down_w[n])
        if merged and s is enc:
            for n in range(slabs):
                mlp(n)
                tick()
        else:
            slab_loop(mlp)
        ship(s.tag + "act")
        norm_fwd(s, 4, "n3", "hat3", 3)
        for name in ("n1", "n2", "n3"):
            ship(s.tag + name)

    on_way = {}

    def ship(name):
        at = SHIPPED.index(name)
        c = pltpu.make_async_copy(buf[BUFFER_OF.get(name, name)], shipped[at], store_sem.at[at])
        c.start()
        on_way[name] = c

    def arrived(name):
        on_way.pop(name).wait()

    def block_bwd(s, limit):
        b = s.b
        qkv_w, out_w, up_w, down_w = s.w
        b["og2"][...] = b["x"][...].astype(bf16)
        ship(s.tag + "og2")
        b["dn"][...] = jnp.zeros_like(b["dn"])
        arrived(s.tag + "act")
        def down(n):
            b["act"][n] = (dot_nn(b["og2"][...], down_w[n]) * b["slope"][n]).astype(bf16)
            b["dn"][...] += dot_nt(b["act"][n], up_w[n])
        slab_loop(down)
        ship(s.tag + "dh")
        norm_bwd(s, 2, "hat2", 2, True)
        b["og1"][...] = b["x"][...].astype(bf16)
        ship(s.tag + "og1")
        arrived(s.tag + "att")
        def proj(n):
            b["att"][n, :, 0 : s.lane] = dot_nn(b["og1"][...], out_w[n]).astype(bf16)
        slab_loop(proj)
        def attend(image, n):
            r = image_rows(s, image)
            q = b["qkv"][n, r, 0 : s.lane]
            k = b["qkv"][n, r, s.lane : 2 * s.lane]
            v = b["qkv"][n, r, 2 * s.lane : 3 * s.lane]
            g = b["att"][n, r, 0 : s.lane]
            lane = lax.broadcasted_iota(jnp.int32, (s.rows, 128), 1)
            lse = b["lse"][r, :]
            dq = jnp.zeros((s.rows, s.lane), f32)
            dk = dq
            dv = dq
            for h in range(s.heads):
                mask = head_mask(s, h)
                level = jnp.sum(jnp.where(lane == n * s.heads + h, lse, 0.0), axis=1, keepdims=True)
                p = jnp.exp(scores(s, q, k, mask, limit(image)) - level)
                dp = dot_nt(jnp.where(mask, g, jnp.zeros_like(g)), v)
                dv = jnp.where(mask, dot_tn(p.astype(bf16), g), dv)
                ds = (p * (dp - jnp.sum(dp * p, axis=1, keepdims=True))).astype(bf16)
                dq = jnp.where(mask, dot_nn(ds, k), dq)
                dk = jnp.where(mask, dot_tn(ds, q), dk)
            scale = s.head ** -0.5
            if s.packed != 3 * s.lane:
                b["qkv"][n, r, 2 * s.lane : s.packed] = jnp.zeros((s.rows, s.packed - 2 * s.lane), bf16)
            b["qkv"][n, r, 0 : s.lane] = (dq * scale).astype(bf16)
            b["qkv"][n, r, s.lane : 2 * s.lane] = (dk * scale).astype(bf16)
            b["qkv"][n, r, 2 * s.lane : 3 * s.lane] = dv.astype(bf16)
        attention_loop(attend)
        ship(s.tag + "qkv")
        b["dn"][...] = jnp.zeros_like(b["dn"])
        def qkv(n):
            b["dn"][...] += dot_nt(b["qkv"][n], qkv_w[n, 0, s.packed])
        slab_loop(qkv)
        norm_bwd(s, 0, "hat1", 1, True)

    chosen = buf["chosen"]
    slots = KEEP_MOST
    chosen[...] = jnp.zeros_like(chosen)
    enc.b["x"][...] = jnp.zeros_like(enc.b["x"])
    for i in range(per):
        r = pl.ds(i * enc_rows, slots)
        patch = lax.broadcasted_iota(jnp.int32, (dec_rows, slots), 0)
        one = (patch == vis_rows[i]).astype(f32).T
        chosen[r, :] = dot_nn(one.astype(bf16), patches[i]).astype(bf16)
        enc.b["x"][r, :] = dot_exact(one, table_e[...])
    need(0)
    for n in range(slabs):
        lead = w_eq.shape[2] - 256
        part = dot_nn(chosen[...], w_eq[n, lead, lead + 256])
        enc.b["x"][:, n * enc_c : (n + 1) * enc_c] += part[:, 256 - enc_c : 256]
    ship("chosen")
    block_fwd(enc, lambda image: counts_all[start_image + image])
    need(4)
    bridged = buf["hid"]
    for n in range(slabs):
        bridged[0 : enc.tokens, n * dec_c : (n + 1) * dec_c] = dot_nn(enc.b["n3"][...], w_bridge[n])

    def hits(i, turned_way):
        patch = lax.broadcasted_iota(jnp.int32, (dec_rows, slots), 0)
        slot = lax.broadcasted_iota(jnp.int32, (dec_rows, slots), 1)
        hit = ((patch == vis_rows[i]) & (slot < counts[i])).astype(f32)
        return hit if turned_way else hit.T

    for i in range(per):
        r = pl.ds(i * dec_rows, dec_rows)
        hit = hits(i, True)
        placed = dot_exact(hit, bridged[pl.ds(i * enc_rows, slots), 0:dec_w])
        seen = jnp.sum(hit, axis=1, keepdims=True) > 0
        dec.b["x"][r, :] = jnp.where(seen, placed, vector(6, dec_w)) + table_d[...]
    block_fwd(dec, lambda image: NP)
    need(9)
    pred = buf["hid"]
    pix_c = w_head.shape[2]
    pix = patches.shape[2]
    for n in range(slabs):
        pred[0 : dec.tokens, n * pix_c : (n + 1) * pix_c] = dot_nn(dec.b["n3"][...], w_head[n])

    pgrad = buf["pgrad"]
    divisor = weight_out[0:1, 0:1]
    loss = jnp.zeros((1, 1), f32)
    LC = 16
    for i in range(per):
        def lossy(j, total):
            r = pl.ds(pl.multiple_of(j * LC, LC), LC)
            px = patches[i, r, :].astype(f32)
            d = px - jnp.mean(px, axis=1, keepdims=True)
            target = d * lax.rsqrt(jnp.mean(d * d, axis=1, keepdims=True) + EPS_NORM)
            rr = pl.ds(pl.multiple_of(i * dec_rows + j * LC, LC), LC)
            error = pred[rr, 0:pix] - target
            weight = loss_w[i, r, :]
            pgrad[rr, :] = (2.0 * weight * error / divisor).astype(bf16)
            return total + jnp.sum(weight * error * error, keepdims=True)
        loss = lax.fori_loop(0, dec_rows // LC, lossy, loss)
    part9 = buf["part9"]
    part9[...] = jnp.zeros_like(part9)
    for n in range(slabs):
        part9[n, :, 0:pix_c] = pgrad[:, n * pix_c : (n + 1) * pix_c]
    dec.b["dn"][...] = jnp.zeros_like(dec.b["dn"])
    ship("part9")
    def head_bwd(n):
        dec.b["dn"][...] += dot_nt(part9[n, :, 0:pix_c], w_head[n])
    slab_loop(head_bwd)
    norm_bwd(dec, 4, "hat3", 3, False)
    block_bwd(dec, lambda image: NP)
    part4 = buf["part4"]
    part4[...] = jnp.zeros_like(part4)
    for i in range(per):
        r = pl.ds(i * dec_rows, dec_rows)
        seen = jnp.sum(hits(i, True), axis=1, keepdims=True) > 0
        grad = dec.b["x"][r, :]
        vec_out[6:7, 0:dec_w] += jnp.sum(jnp.where(seen, 0.0, grad), axis=0, keepdims=True)
        back = dot_exact(hits(i, False), grad).astype(bf16)
        for n in range(slabs):
            part4[n, pl.ds(i * enc_rows, slots), :] = back[:, n * dec_c : (n + 1) * dec_c]
    ship("part4")
    enc.b["dn"][...] = jnp.zeros_like(enc.b["dn"])
    def bridge_bwd(n):
        enc.b["dn"][...] += dot_nt(part4[n], w_bridge[n])
    slab_loop(bridge_bwd)
    norm_bwd(enc, 4, "hat3", 3, False)
    block_bwd(enc, lambda image: counts_all[start_image + image])

    part0 = buf["part0"]
    part0[...] = jnp.zeros_like(part0)
    for n in range(slabs):
        part0[n, :, 256 - enc_c : 256] = enc.b["x"][:, n * enc_c : (n + 1) * enc_c].astype(bf16)
    ship("part0")
    row = lax.broadcasted_iota(jnp.int32, (1, vec_out.shape[1]), 1)
    vec_out[13:14, :] = jnp.where(row >= 0, loss, 0.0)
    for name in list(on_way):
        arrived(name)
    if merged:
        g.finish()


TICK = 3
MERGED = True


def compute(sources, shapes, vec_parts, weight_sum, patches, vis_index, keep_mask, counts, sizes, units, events, merged):
    slabs = sizes[2]
    ext = extents(sizes)
    heads = (slabs, ext["h"], ext["l"], ext["w"], 2)
    owners = math.prod(heads[1:])
    weights = [jax.ShapeDtypeStruct((slabs, owners * a, c), jnp.bfloat16) for a, c in shapes]
    per, pix = -(-counts.shape[0] // slabs), patches.shape[2]
    dec_rows, enc_rows = -(-NP // 16) * 16, -(-KEEP_MOST // 16) * 16
    enc_w, dec_w = weights[0].shape[1], weights[5].shape[1]
    enc = Side(enc_w, DH, weights[1].shape[2] // DH, enc_rows, per, slabs)
    dec = Side(dec_w, DHD, weights[6].shape[2] // DHD, dec_rows, per, slabs)
    named = {}
    for s, tag, up in ((enc, "e_", weights[2]), (dec, "d_", weights[7])):
        for k, v in s.scratch(up.shape[2]).items():
            named[tag + k] = v
    f32, bf16 = jnp.float32, jnp.bfloat16
    top = max(enc.tokens, dec.tokens)
    named["hid"] = ((top, max(pix, weights[2].shape[2], weights[7].shape[2])), f32)
    named["vec_full"] = ((16, enc_w), f32)
    named["chosen"] = ((enc.tokens, pix), bf16)
    named["pgrad"] = ((dec.tokens, pix), bf16)
    up128 = lambda c: -(-c // 128) * 128
    named["part9"] = ((slabs, dec.tokens, up128(weights[9].shape[2])), bf16)
    named["part4"] = ((slabs, enc.tokens, weights[4].shape[2]), bf16)
    named["part0"] = ((slabs, enc.tokens, 256), bf16)
    named["raw"] = ((per, NP, pix), bf16)
    named["patches"] = ((per, dec_rows, pix), bf16)
    named["loss_w"] = ((per, dec_rows, 1), f32)
    ship_shapes = [jax.ShapeDtypeStruct(named[BUFFER_OF.get(k, k)][0], bf16) for k in SHIPPED]
    an = pl.BlockSpec(memory_space=pl.ANY)
    vm = pl.BlockSpec(memory_space=pltpu.VMEM)
    sm = pl.BlockSpec(memory_space=pltpu.SMEM)
    DMA = pltpu.SemaphoreType.DMA
    table_e = jnp.asarray(np.pad(sincos_table(NP, enc_w), ((0, dec_rows - NP), (0, 0))))
    table_d = jnp.asarray(np.pad(sincos_table(NP, dec_w), ((0, dec_rows - NP), (0, 0))))
    store = [pltpu.VMEM(heads + s if merged else w.shape, bf16) for s, w in zip(shapes, weights)]
    scratch = store + [DMA((10 + per,)), DMA((len(SHIPPED),))]
    small = [vec_parts] if merged else [vec_parts, weight_sum]
    if merged:
        scratch += [pltpu.VMEM((slabs,) + vec_parts.shape, f32)] + Start.scratch(sizes, shapes) + gather_sems(sizes, units)
    params = dict(vmem_limit_bytes=61 << 20)
    if merged:
        params.update(collective_id=0, has_side_effects=True)
    res = pl.pallas_call(
        functools.partial(compute_kernel, sizes, merged, per, slabs, list(named), units, events),
        out_shape=ship_shapes + [jax.ShapeDtypeStruct((16, enc_w), f32), jax.ShapeDtypeStruct((8, 128), f32)],
        in_specs=[vm if merged else an] * len(sources) + [vm] * len(small) + [an] + [vm] * 4 + [sm],
        out_specs=[an] * len(SHIPPED) + [vm, vm],
        scratch_shapes=scratch + [pltpu.VMEM(s, d) for s, d in named.values()],
        compiler_params=pltpu.CompilerParams(**params),
    )(*sources, *small, patches, vis_index, keep_mask, table_e, table_d, counts)
    return res[: len(SHIPPED)], res[len(SHIPPED)], res[len(SHIPPED) + 1]


def split_low(x):
    high = x.astype(jnp.bfloat16)
    return high, (x - high.astype(jnp.float32)).astype(jnp.bfloat16)


def dot_three(a, b, kind=dot_nn):
    (ah, al), (bh, bl) = a, b
    return kind(ah, bh) + (kind(ah, bl) + kind(al, bh))


def roots(mats):
    side = mats[0].shape[0]
    eye = lax.broadcasted_iota(jnp.int32, (side, side), 0) == lax.broadcasted_iota(jnp.int32, (side, side), 1)
    five = jnp.where(eye, 5.0, 0.0)
    size = [jnp.sqrt(jnp.sum(m * m, keepdims=True)) for m in mats]
    current = [m * (1.0 / s) for m, s in zip(mats, size)]
    result = None
    for step in range(NEWTON):
        factor = [split_low((five - c) * 0.25) for c in current]
        if result is None:
            result = [(five - c) * 0.25 for c in current]
        else:
            result = [dot_three(split_low(r), f) for r, f in zip(result, factor)]
        if step + 1 < NEWTON:
            square = [split_low(dot_three(f, f)) for f in factor]
            fourth = [split_low(dot_three(q, q)) for q in square]
            current = [dot_three(q, split_low(c)) for q, c in zip(fourth, current)]
    return [r * lax.rsqrt(jnp.sqrt(s)) for r, s in zip(result, size)]


GROUPS = (21, 14)


def optimizer_kernel(pieces, upright, sides, enc_cols, dec_cols, *refs):
    it = iter(refs)
    take = lambda k: [next(it) for _ in range(k)]
    n_mats = len(pieces)
    owned = take(max(p[0] for blocks in pieces for parts in blocks for p in parts) + 1)
    masters = take(n_mats)
    stats = take(4)
    squares, vec_sum, weight_sum, vectors, first, second, step_count = take(7)
    new = take(n_mats)
    new_stats = take(4)
    new_vectors, new_first, new_second, norms, loss_out, weight_out = take(6)
    g_enc, g_dec, u_enc, u_dec = take(4)
    old = take(4)
    fresh = take(4)
    in_sem, out_sem = take(2)
    f32 = jnp.float32
    loads = []
    for i in (2, 3, 0, 1):
        c = pltpu.make_async_copy(stats[i], old[i], in_sem.at[i])
        c.start()
        loads.append((i, c))
    loads = dict(loads)

    enc_vec, dec_vec = vec_sum[0:6, :], vec_sum[6:13, 0 : dec_cols * (vec_sum.shape[1] // enc_cols)]
    enc_sq = squares[0:1, 0:1] + jnp.sum(enc_vec * enc_vec, keepdims=True)
    dec_sq = squares[1:2, 0:1] + jnp.sum(dec_vec * dec_vec, keepdims=True)
    norms[0] = jnp.sqrt(enc_sq)[0, 0]
    norms[1] = jnp.sqrt(dec_sq)[0, 0]
    loss_out[0] = vec_sum[13:14, 0:1][0, 0]
    weight_out[0] = weight_sum[0:1, 0:1][0, 0]
    clip = jnp.minimum(1.0, CLIP_NORM / jnp.sqrt(enc_sq + dec_sq))

    sections = ((1, g_dec, u_dec, 2, LR_MATRIX), (0, g_enc, u_enc, 0, LR_MATRIX * LAYER_DECAY))
    for which, grad, update, base, rate in sections:
        at = 0
        for i in range(n_mats):
            if sides[i] != which:
                continue
            for parts in pieces[i]:
                col = 0
                for src, lo, width in parts:
                    grad[at, :, col : col + width] = owned[src][:, lo : lo + width] * clip
                    col += width
                at += 1
        total = at
        loads[base].wait()
        loads[base + 1].wait()
        group = min(GROUPS[which], total)
        def body(i, carry):
            start = jnp.minimum(i * group, total - group)
            g = [grad[start + j] for j in range(group)]
            low = [split_low(x) for x in g]
            turned = [split_low(x.T) for x in g]
            small = [STAT_DECAY * old[base][start + j] + (1.0 - STAT_DECAY) * dot_three(low[j], low[j], dot_nt) for j in range(group)]
            large = [STAT_DECAY * old[base + 1][start + j] + (1.0 - STAT_DECAY) * dot_three(turned[j], turned[j], dot_nt) for j in range(group)]
            for j in range(group):
                fresh[base][start + j] = small[j]
                fresh[base + 1][start + j] = large[j]
            left = roots(small)
            right = roots(large)
            for j in range(group):
                half = dot_three(split_low(left[j]), low[j])
                update[start + j] = rate * dot_three(split_low(half), split_low(right[j]))
            return carry
        lax.fori_loop(0, -(-total // group), body, 0)
        for k in (base, base + 1):
            pltpu.make_async_copy(fresh[k], new_stats[k], out_sem.at[k]).start()
        at = 0
        for i in range(n_mats):
            if sides[i] != which:
                continue
            for k in range(len(pieces[i])):
                lo = k * BLOCK
                if upright[i]:
                    new[i][:, lo : lo + BLOCK] = masters[i][:, lo : lo + BLOCK] - update[at]
                else:
                    new[i][lo : lo + BLOCK, :] = masters[i][lo : lo + BLOCK, :] - update[at].T
                at += 1

    na = lax.axis_index("narrow")
    steps = jnp.full((1, 128), step_count[0], jnp.int32).astype(f32)[0:1, 0:1]
    scale_one = 1.0 / (1.0 - jnp.exp(steps * math.log(BETA_FIRST)))
    scale_two = 1.0 / (1.0 - jnp.exp(steps * math.log(BETA_SECOND)))
    slabs = vec_sum.shape[1] // enc_cols
    at = 0
    for k in range(13):
        width = enc_cols if k < 6 else dec_cols
        rate = LR_VECTOR * LAYER_DECAY if k < 6 else LR_VECTOR
        g = vec_sum[k : k + 1, 0:width]
        for n in range(1, slabs):
            g = jnp.where(na == n, vec_sum[k : k + 1, n * width : (n + 1) * width], g)
        g = g * clip
        cols = slice(at, at + width)
        one = BETA_FIRST * first[:, cols] + (1.0 - BETA_FIRST) * g
        two = BETA_SECOND * second[:, cols] + (1.0 - BETA_SECOND) * g * g
        new_first[:, cols] = one
        new_second[:, cols] = two
        new_vectors[:, cols] = vectors[:, cols] - rate * (one * scale_one) / (jnp.sqrt(two * scale_two) + EPS_ADAM)
        at += width
    for k in range(4):
        pltpu.make_async_copy(fresh[k], new_stats[k], out_sem.at[k]).wait()


def optimizer(owned, masters, stats, squares, vec_sum, weight_sum, vectors, first, second, step_count, enc_cols, dec_cols):
    kinds = ENC_KINDS + DEC_KINDS
    sides = (0,) * len(ENC_KINDS) + (1,) * len(DEC_KINDS)
    width = [m.shape[1] if kind else m.shape[0] for m, kind in zip(masters, kinds)]
    def plain(src, first_col, cols):
        return [[(src, first_col + k * BLOCK, BLOCK)] for k in range(cols // BLOCK)]
    def by_head(src, cols, head):
        heads = cols // (3 * head)
        per = BLOCK // head
        order = [(t * heads + h) * head for h in range(heads) for t in range(3)]
        return [[(src, order[k * per + j], head) for j in range(per)] for k in range(cols // BLOCK)]
    pieces = [
        plain(0, width[1], width[0]), by_head(0, width[1], DH), plain(1, 0, width[2]), plain(2, 0, width[3]),
        plain(3, 0, width[4]), plain(4, 0, width[5]), by_head(5, width[6], DHD), plain(6, 0, width[7]),
        plain(7, 0, width[8]), plain(8, 0, width[9]), plain(9, 0, width[10]),
    ]
    flat = [s.reshape(s.shape[2:]) for s in stats]
    upright = [kind or i != 2 for i, kind in enumerate(kinds)]
    masters = [m if kind or not up else m.T for m, kind, up in zip(masters, kinds, upright)]
    f32 = jnp.float32
    like = lambda x: jax.ShapeDtypeStruct(x.shape, f32)
    an = pl.BlockSpec(memory_space=pl.ANY)
    vm = pl.BlockSpec(memory_space=pltpu.VMEM)
    sm = pl.BlockSpec(memory_space=pltpu.SMEM)
    block = [pltpu.VMEM((flat[i].shape[0], flat[i].shape[1], BLOCK), f32) for i in (0, 2)]
    whole = [pltpu.VMEM(s.shape, f32) for s in flat]
    DMA = pltpu.SemaphoreType.DMA
    n = len(masters)
    res = pl.pallas_call(
        functools.partial(optimizer_kernel, pieces, upright, sides, enc_cols, dec_cols),
        out_shape=[like(m) for m in masters] + [like(s) for s in flat]
        + [like(vectors)] * 3 + [jax.ShapeDtypeStruct((k,), f32) for k in (2, 1, 1)],
        in_specs=[vm] * (len(owned) + n) + [an] * 4 + [vm] * 6 + [sm],
        out_specs=[vm] * n + [an] * 4 + [vm] * 3 + [sm] * 3,
        scratch_shapes=block + block + whole + whole + [DMA((4,)), DMA((4,))],
        compiler_params=pltpu.CompilerParams(vmem_limit_bytes=56 << 20),
    )(*owned, *masters, *flat, squares, vec_sum, weight_sum, vectors, first, second, step_count)
    new_stats = [r.reshape(s.shape) for r, s in zip(res[n : n + 4], stats)]
    new = [r if kind or not up else r.T for r, kind, up in zip(res[:n], kinds, upright)]
    return new, new_stats, res[n + 4 : n + 7], res[n + 7], res[n + 8].reshape(()), res[n + 9].reshape(())


def per_device(
    sizes,
    patches, vis_index, keep_mask, counts, step_count,
    w_embed, enc_qkv, enc_out, enc_up, enc_down, w_bridge,
    dec_qkv, dec_out, dec_up, dec_down, w_head,
    vectors, first_moment, second_moment, enc_small, enc_big, dec_small, dec_big,
):
    n_dp, n_wide, n_nar = sizes
    ext = extents(sizes)
    masters = (w_embed, enc_qkv, enc_out, enc_up, enc_down, w_bridge, dec_qkv, dec_out, dec_up, dec_down, w_head)
    sources = [m if kind or i == 2 else m.T for i, (m, kind) in enumerate(zip(masters, ENC_KINDS + DEC_KINDS))]
    enc_cols, dec_cols = w_embed.shape[1], w_bridge.shape[1]
    shapes = shard_shapes(sources)
    units, events = gather_plan(ext, shapes)
    merged = MERGED and all(a % 16 == 0 for a, _ in shapes)
    if merged:
        weights, vec_all, weight_sum = sources, vectors, None
    else:
        gathered, vec_all, weight_sum = gather(sources, vectors, counts, sizes, units, events)
        weights = [g.reshape(n_nar, -1, g.shape[-1]) for g in gathered]
    shipped, vec_grad, weight_sum = compute(
        weights, shapes, vec_all, weight_sum, patches, vis_index, keep_mask, counts, sizes, units, events, merged
    )
    lefts, rights = shipped[: len(LEFTS)], shipped[len(LEFTS) :]
    pairs = ([(0, 0), (1, 1)], [(2, 2)], [(3, 3)], [(4, 4)], [(5, 5)], [(6, 6)], [(7, 7)], [(8, 8)], [(9, 9)], [(10, 10)])
    mats = []
    for terms, shape in zip(pairs, shapes):
        cols = -(-shape[1] // 128) * 128
        wide = [rights[g].shape[2] for _, g in terms]
        mats.append((shape[0], cols, [(x, g, 0 if i == 0 else cols - wide[i], wide[i]) for i, (x, g) in enumerate(terms)]))
    units, events = reduce_plan(ext, mats)
    owned, vec_sum, squares = reduce_scatter(
        lefts, rights, mats, vec_grad, sizes, units, events, [True] * 5 + [False] * 5
    )
    new, new_stats, new_vecs, norms, loss_total, weight_total = optimizer(
        owned, masters, (enc_small, enc_big, dec_small, dec_big), squares, vec_sum,
        weight_sum, vectors, first_moment, second_moment, step_count, enc_cols, dec_cols,
    )
    return (*new, *new_stats, *new_vecs, norms, loss_total, weight_total)


def solution(mesh):
    sizes = (mesh.shape["dp"], mesh.shape["wide"], mesh.shape["narrow"])
    rows = P(("dp", "wide"))
    matrix = P(("dp", "wide"), "narrow")
    turned = P("narrow", ("dp", "wide"))
    matrices = tuple(matrix if kind else turned for kind in ENC_KINDS + DEC_KINDS)
    stats = (P(("dp", "wide"), "narrow"),) * 4
    packed = (P("narrow"),) * 3
    in_specs = (rows, rows, rows, rows, P()) + matrices + packed + stats
    out_specs = matrices + stats + packed + (P(), P(), P())
    return jax.shard_map(
        functools.partial(per_device, sizes), mesh=mesh, in_specs=in_specs, out_specs=out_specs, check_vma=False
    )
```

```python
import functools
import math

import jax
import jax.numpy as jnp
import numpy as np
from jax import lax
from jax.experimental import pallas as pl
from jax.experimental.pallas import tpu as pltpu
from jax.sharding import PartitionSpec as P

D = 768
DH = 64
DD = 512
DHD = 32
PIX = 768
NP = 196
BLOCK = 64
NEWTON = 3
KEEP_MOST = 98

HIGH = lax.Precision.HIGHEST
EPS_NORM = 1e-06
VISIBLE_WEIGHT = 0.1
STAT_DECAY = 0.5
LR_MATRIX = 0.2
LR_VECTOR = 0.2
LAYER_DECAY = 0.75
BETA_FIRST = 0.9
BETA_SECOND = 0.999
EPS_ADAM = 1e-08
CLIP_NORM = 1.0
ENC_KINDS = (True, True, False, True, False, True)
DEC_KINDS = (True, False, True, False, True)


MESHT = pl.DeviceIdType.MESH
FULL_CODE = 32767.0
FLOOR = 1e-30


def xors(n):
    return list(range(1, n))


def extents(sizes):
    n_dp, n_wide, n_nar = sizes
    return {"n": n_nar, "h": n_dp // 2, "l": 2, "w": n_wide // 2}


def phases_of(order, ext):
    return [d for d in order if ext[d] > 1]


def messages(order, ext):
    out, left = [], 1
    for d in ext:
        left *= ext[d]
    for d in phases_of(order, ext):
        left //= ext[d]
        out.append((d, ext[d] - 1, left))
    return out


class Place:
    def __init__(self, sizes):
        self.sizes = sizes
        self.ext = extents(sizes)
        self.dp, self.wi, self.na = (lax.axis_index(x) for x in ("dp", "wide", "narrow"))
        self.own = {"n": self.na, "h": self.dp // 2, "l": self.dp % 2, "w": self.wi // 2}
        self.core = self.wi % 2

    def peer(self, dim, k):
        if dim == "n":
            return {"narrow": self.na ^ k}
        if dim == "h":
            return {"dp": self.dp ^ (2 * k)}
        if dim in "ld":
            return {"dp": self.dp ^ k}
        if dim == "w":
            return {"wide": self.wi ^ (2 * k)}
        if dim == "g":
            return {"dp": self.dp ^ (k // 2), "wide": self.wi ^ (k % 2)}
        return {"wide": self.wi ^ 1}

    def greet(self):
        ext = self.ext
        partners = [self.peer(d, k) for d in "nw" for k in xors(ext[d])]
        partners += [self.peer("g", k) for k in xors(2 * self.sizes[0])]
        barrier = pltpu.get_barrier_semaphore()
        for p in partners:
            pl.semaphore_signal(barrier, inc=1, device_id=p, device_id_type=MESHT)
        pl.semaphore_wait(barrier, len(partners))

    def hops(self, narrow, joint):
        out = [("c", 2, self.core), ("d", self.sizes[0], self.dp)]
        if joint:
            out = [("g", 2 * self.sizes[0], self.dp * 2 + self.core)]
        if self.ext["w"] > 1:
            out.append(("w", self.ext["w"], self.wi // 2))
        if narrow and self.ext["n"] > 1:
            out.append(("n", self.ext["n"], self.na))
        return out


def remote(src, dst, ss, rs, dev):
    return pltpu.make_async_remote_copy(
        src_ref=src, dst_ref=dst, send_sem=ss, recv_sem=rs, device_id=dev, device_id_type=MESHT
    )


class SmallSum:
    def __init__(self, place, value, lands, send, recv, narrow, joint):
        self.place, self.value, self.lands, self.send, self.recv = place, value, lands, send, recv
        self.axes = place.hops(narrow, joint)
        self.flight = None

    def start(self, i):
        d, members, at = self.axes[i]
        land = self.lands[i]
        land[at] = self.value[...]
        self.flight = []
        for k in xors(members):
            c = remote(self.value, land.at[at], self.send.at[i, k - 1], self.recv.at[i, k - 1], self.place.peer(d, k))
            c.start()
            self.flight.append(c)

    def finish(self, i):
        d, members, at = self.axes[i]
        for c in self.flight:
            c.wait()
        total = self.lands[i][0]
        for j in range(1, members):
            total = total + self.lands[i][j]
        self.value[...] = total

    @staticmethod
    def scratch(sizes, shape, narrow, joint):
        members = ([2 * sizes[0]] if joint else [2, sizes[0]]) + ([sizes[1] // 2] if sizes[1] > 2 else []) + ([sizes[2]] if narrow and sizes[2] > 1 else [])
        return [pltpu.VMEM((m,) + shape, jnp.float32) for m in members]

    @staticmethod
    def sems(sizes):
        return [pltpu.SemaphoreType.DMA((4, max(*sizes, 2 * sizes[0])))] * 2


def plan(units, events, mats, ext, tokens):
    flat = []
    for step in events:
        for u, p in step:
            if p <= len(phases_of(units[u][3], ext)) + 3:
                flat.append((u, p))
    at = {e: i for i, e in enumerate(flat)}
    blocks = ext["h"] * ext["l"] * ext["w"]
    wants = []
    big = max((mats[m][0] for m, *_ in units)), max(hi - lo for m, lo, hi, o in units)
    first_use, last_need = {}, {}
    for u, (m, lo, hi, order) in enumerate(units):
        a, c = mats[m][0], hi - lo
        for x, g, *_ in terms_of(mats, m, lo, hi):
            first_use[x] = min(first_use.get(x, (len(flat),)), (at[u, 0], at[u, 1], tokens[g], a))
            last_need[x] = max(last_need.get(x, 0), at[u, 3])
        last = at[u, len(phases_of(order, ext)) + 3]
        full = (ext["n"], blocks) + (big if a * c * 5 > 2 * big[0] * big[1] else (a, c))
        for j, (x, g, c_lo, c_hi, g_lo) in enumerate(terms_of(mats, m, lo, hi)):
            wants.append((at[u, 0], at[u, 3], ("g", u, j), (ext["n"], tokens[g], c_hi - c_lo), "b"))
        wants.append((at[u, 1], at[u, 3], ("out", u), full, "f"))
        wants.append((at[u, 2], at[u, 3], ("stage", u), full, "f"))
        wants.append((at[u, 3], at[u, 3], ("acc", u), full, "f"))
        wants.append((at[u, 3], last, ("kept", u), (messages(order, ext)[0][2], a, c), "f"))
        for p, (d, k, n) in enumerate(messages(order, ext)):
            wants.append((at[u, p + 3], last, ("q", u, p), (k, n, a, c), "q"))
    for x, (start, turn, rows, a) in first_use.items():
        turn = min(at[u, 1] for u, (m, lo, hi, o) in enumerate(units) if any(x == t[0] for t in terms_of(mats, m, lo, hi)))
        wants.append((start, turn, ("plain", x), (rows, 2 * blocks * a), "b"))
        wants.append((start, last_need[x], ("turned", x), (blocks, 2, a, rows), "b"))
    wants.sort(key=lambda w: w[0])
    bufs, where = [], {}
    for start, end, name, shape, kind in wants:
        for i, b in enumerate(bufs):
            if b[0] == (shape, kind) and b[1] < start:
                b[1] = end
                where[name] = i
                break
        else:
            bufs.append([(shape, kind), end])
            where[name] = len(bufs) - 1
    return [b[0] for b in bufs], where


def terms_of(mats, m, lo, hi):
    out = []
    for x, g, first, width in mats[m][2]:
        a, b = max(lo, first), min(hi, first + width)
        if a < b:
            out.append((x, g, a - lo, b - lo, a - first))
    out.sort(key=lambda t: t[2] - t[3])
    return out


def reduce_kernel(sizes, units, events, mats, n_left, n_right, planned, is_enc, *refs):
    place = Place(sizes)
    ext, own, core = place.ext, place.own, place.core
    count, nu = len(mats), len(units)
    blocks = ext["h"] * ext["l"] * ext["w"]
    f32 = jnp.float32
    it = iter(refs)
    take = lambda k: [next(it) for _ in range(k)]
    lefts, rights = take(n_left), take(n_right)
    vec = next(it)
    outs = take(count)
    vec_out, sq_out = take(2)
    land = take(nu)
    kinds, where = planned
    pool = [tuple(take(2)) if kind == "q" else take(1)[0] for _, kind in kinds]
    recv_q, recv_s = [], []
    for u in range(nu):
        k = len(messages(units[u][3], ext))
        recv_q.append(take(k))
        recv_s.append(take(k))
    plain = [pool[where["plain", x]] for x in range(n_left)]
    turned = [pool[where["turned", x]] for x in range(n_left)]
    n_axes, n_square = len(place.hops(True, False)), len(place.hops(True, True))
    vec_land, sq_land = take(n_axes), take(n_square)
    (core_send, core_recv, stage_sem, g_sem, x_sem, q_send, q_recv, s_send, s_recv, v_send, v_recv, t_send, t_recv) = take(13)
    left_copies = {}
    place.greet()
    small = SmallSum(place, vec_out, vec_land, v_send, v_recv, True, False)
    vec_out[...] = vec[...]
    squares = SmallSum(place, sq_out, sq_land, t_send, t_recv, True, True)

    pending = []
    last_use = {}
    flight = {}
    sums = [jnp.zeros((1, 1), f32), jnp.zeros((1, 1), f32)]
    ready = set()

    def turn(k):
        if k in ready:
            return
        ready.add(k)
        left_copies[k].wait()
        t = plain[k][...].T
        a = turned[k].shape[2]
        if a % 16 == 0:
            turned[k][...] = t.reshape(turned[k].shape)
        else:
            for i in range(2 * blocks):
                turned[k][i // 2, i % 2] = t[i * a : (i + 1) * a]

    def product(u, n, which, ref_of):
        m, lo, hi, order = units[u]
        a, c = mats[m][0], hi - lo
        for j, (x, g, c_lo, c_hi, g_lo) in enumerate(terms_of(mats, m, lo, hi)):
            right = pool[where["g", u, j]][n]
            if a % 16 == 0:
                rows = turned[x][:, which].reshape(blocks * a, turned[x].shape[3])
                v = lax.dot_general(rows, right, (((1,), (0,)), ((), ())), preferred_element_type=f32)
                v = v.reshape(blocks, a, c_hi - c_lo)
                if j == 0:
                    ref_of[n] = v
                else:
                    ref_of[n, :, :, c_lo:c_hi] += v
            else:
                for b in range(blocks):
                    v = lax.dot_general(turned[x][b, which], right, (((1,), (0,)), ((), ())), preferred_element_type=f32)
                    if j == 0:
                        ref_of[n, b] = v
                    else:
                        ref_of[n, b, :, c_lo:c_hi] += v

    def whole(kind, u):
        m, lo, hi, order = units[u]
        ref = pool[where[kind, u]]
        a, c = mats[m][0], hi - lo
        return ref if ref.shape[2:] == (a, c) else ref.at[:, :, pl.ds(0, a), pl.ds(0, c)]

    def block_of(idx):
        return (idx["h"] * ext["l"] + idx["l"]) * ext["w"] + idx["w"]

    def slab(u, idx):
        at = 0
        for d in "nhlw":
            if d != phases_of(units[u][3], ext)[0]:
                at = at * ext[d] + idx[d]
        return pool[where["kept", u]].at[at]

    def split(s, dims):
        idx = {}
        for d in reversed(dims):
            if ext[d] == 1:
                idx[d] = 0
            else:
                idx[d] = s % ext[d]
                s = s // ext[d]
        return idx

    def loop(total, body):
        def step(s, carry):
            body(s)
            return carry
        lax.fori_loop(0, total, step, 0)

    def reuse(b):
        for c in last_use.pop(b, []):
            c.wait_send()

    def code_and_send(u, p):
        ph = phases_of(units[u][3], ext)
        d, peers, slabs = messages(units[u][3], ext)[p]
        gone = ph[:p]
        free = [x for x in "nhlw" if x != d and x not in gone]
        b = where["q", u, p]
        reuse(b)
        out_q, out_s = pool[b]
        sends = []
        for k in range(1, peers + 1):
            def body(s):
                idx = split(s, free)
                for x in gone:
                    idx[x] = own[x]
                idx[d] = own[d] ^ k
                x = (whole("acc", u).at[idx["n"], block_of(idx)] if p == 0 else slab(u, idx))[...]
                top = jnp.maximum(jnp.max(jnp.abs(x), axis=0, keepdims=True), FLOOR)
                out_q[k - 1, s] = jnp.round(x * (FULL_CODE / top)).astype(jnp.int32).astype(jnp.int16)
                out_s[k - 1, s] = top * (1.0 / FULL_CODE)
            loop(slabs, body)
            dev = place.peer(d, k)
            first = remote(out_q.at[k - 1], recv_q[u][p].at[k - 1], q_send.at[u, p, k - 1], q_recv.at[u, p, k - 1], dev)
            second = remote(out_s.at[k - 1], recv_s[u][p].at[k - 1], s_send.at[u, p, k - 1], s_recv.at[u, p, k - 1], dev)
            first.start()
            second.start()
            sends += [first, second]
        flight[u, p] = sends
        last_use[b] = sends

    def take_in(u, p):
        ph = phases_of(units[u][3], ext)
        d, peers, slabs = messages(units[u][3], ext)[p]
        gone = ph[: p + 1]
        free = [x for x in "nhlw" if x not in gone]
        for c in flight[u, p]:
            c.wait_recv()
        def body(s):
            idx = split(s, free)
            for x in gone:
                idx[x] = own[x]
            ref = slab(u, idx)
            v = ref[...]
            for k in range(peers):
                v = v + recv_q[u][p][k, s].astype(jnp.int32).astype(f32) * recv_s[u][p][k, s]
            ref[...] = v
        loop(slabs, body)

    def stage(u, p):
        m, lo, hi, order = units[u]
        n_ph = len(phases_of(order, ext))
        if p == 0:
            copies = []
            for j, (x, g, c_lo, c_hi, g_lo) in enumerate(terms_of(mats, m, lo, hi)):
                if x not in left_copies:
                    left_copies[x] = pltpu.make_async_copy(lefts[x], plain[x], x_sem.at[x])
                    left_copies[x].start()
                src = rights[g]
                if c_hi - c_lo != src.shape[2]:
                    src = src.at[:, :, slice(g_lo, g_lo + c_hi - c_lo)]
                c = pltpu.make_async_copy(src, pool[where["g", u, j]], g_sem.at[u, j])
                c.start()
                copies.append(c)
            flight[u, "g"] = copies
        elif p == 1:
            for c in flight[u, "g"]:
                c.wait()
            for x, *_ in terms_of(mats, m, lo, hi):
                turn(x)
            b = where["out", u]
            reuse(b)
            loop(ext["n"], lambda n: product(u, n, 1 - core, whole("out", u)))
            c = remote(whole("out", u), land[u], core_send.at[u], core_recv.at[u], place.peer("c", 1))
            c.start()
            flight[u, "core"] = c
            last_use[b] = [c]
        elif p == 2:
            flight[u, "core"].wait_recv()
            reuse(where["stage", u])
            c = pltpu.make_async_copy(land[u], whole("stage", u), stage_sem.at[u])
            c.start()
            flight[u, "stage"] = c
        elif p == 3:
            acc, more = whole("acc", u), whole("stage", u)
            reuse(where["acc", u])
            flight[u, "stage"].wait()
            def body(n):
                product(u, n, core, acc)
                acc[n] = acc[n] + more[n]
            loop(ext["n"], body)
            code_and_send(u, 0)
            d, peers, slabs = messages(order, ext)[0]
            def keep(i):
                idx = split(i, [x for x in "nhlw" if x != d])
                idx[d] = own[d]
                slab(u, idx)[...] = acc.at[idx["n"], block_of(idx)][...]
            loop(slabs, keep)
        else:
            take_in(u, p - 4)
            if p - 3 < n_ph:
                code_and_send(u, p - 3)
            else:
                x = slab(u, own)[...]
                outs[m][:, pl.ds(lo, hi - lo)] = x
                w = 0 if is_enc[m] else 1
                sums[w] = sums[w] + jnp.sum(x * x, keepdims=True)

    flat = [(u, p) for step in events for u, p in step if p <= len(phases_of(units[u][3], ext)) + 3]
    turns = [(i + 1) * len(flat) // (n_axes + 2) for i in range(n_axes + 1)]
    small.start(0)
    for i, (u, p) in enumerate(flat):
        stage(u, p)
        if i in turns[1:]:
            hop = turns.index(i)
            small.finish(hop - 1)
            if hop < n_axes:
                small.start(hop)
    row = lax.broadcasted_iota(jnp.int32, (8, 128), 0)
    sq_out[...] = jnp.where(row == 0, sums[0], jnp.where(row == 1, sums[1], 0.0))
    for i in range(n_square):
        squares.start(i)
        squares.finish(i)
    for c in [c for cs in last_use.values() for c in cs]:
        c.wait_send()


def reduce_scatter(lefts, rights, mats, vec, sizes, units, events, is_enc, cid=1):
    ext = extents(sizes)
    blocks = ext["h"] * ext["l"] * ext["w"]
    f32, bf16 = jnp.float32, jnp.bfloat16
    tokens = [r.shape[1] for r in rights]
    planned = plan(units, events, mats, ext, tokens)
    coded = lambda k, n, a, c: [pltpu.VMEM((k, n, a, c), jnp.int16), pltpu.VMEM((k, n, 1, c), f32)]
    scratch = []
    for shape, kind in planned[0]:
        scratch += coded(*shape) if kind == "q" else [pltpu.VMEM(shape, f32 if kind == "f" else bf16)]
    for m, lo, hi, order in units:
        ms = [coded(k, n, mats[m][0], hi - lo) for d, k, n in messages(order, ext)]
        scratch += [x[0] for x in ms] + [x[1] for x in ms]
    scratch += SmallSum.scratch(sizes, vec.shape, True, False) + SmallSum.scratch(sizes, (8, 128), True, True)
    nu, kmax = len(units), max(ext.values())
    D_ = pltpu.SemaphoreType.DMA
    scratch += [D_((nu,))] * 3 + [D_((nu, 2)), D_((len(lefts),))] + [D_((nu, 4, kmax))] * 4 + SmallSum.sems(sizes) * 2
    vm = pl.BlockSpec(memory_space=pltpu.VMEM)
    an = pl.BlockSpec(memory_space=pl.ANY)
    res = pl.pallas_call(
        functools.partial(reduce_kernel, sizes, units, events, mats, len(lefts), len(rights), planned, is_enc),
        out_shape=[jax.ShapeDtypeStruct(m[:2], f32) for m in mats]
        + [jax.ShapeDtypeStruct(vec.shape, f32), jax.ShapeDtypeStruct((8, 128), f32)]
        + [jax.ShapeDtypeStruct((ext["n"], blocks, mats[m][0], hi - lo), f32) for m, lo, hi, o in units],
        in_specs=[an] * (len(lefts) + len(rights)) + [vm],
        out_specs=[vm] * (len(mats) + 2) + [an] * nu,
        scratch_shapes=scratch,
        compiler_params=pltpu.CompilerParams(collective_id=cid, has_side_effects=True, vmem_limit_bytes=60 << 20),
    )(*lefts, *rights, vec)
    return res[: len(mats)], res[len(mats)], res[len(mats) + 1]


class Gather:
    def __init__(self, place, units, events, shards, outs, sems):
        self.place, self.units, self.shards, self.outs = place, units, shards, outs
        self.send_sem, self.recv_sem, self.loc_sem = sems
        self.events = [(u, p) for step in events for u, p in step if p <= len(self.phases(u, units))]
        self.next = 0
        self.pending, self.from_sibling = [], []
        self.slots = [0] * len(units)
        self.flight, self.local = {}, {}
        self.complete = set()

    def phases(self, u, units=None):
        return [d for d in (units or self.units)[u][3] if self.place.ext[d] > 1]

    def region(self, u, full, at, which_core):
        m, lo, hi, order = self.units[u]
        own = self.place.own
        idx = [slice(None) if d in full else own[d] ^ at[1] if at and d == at[0] else own[d] for d in "nhlw"]
        if (lo, hi) == (0, self.shards[m].shape[1]):
            return self.outs[m].at[tuple(idx) + (which_core,)]
        return self.outs[m].at[tuple(idx) + (which_core, slice(None), slice(lo, hi))]

    def shard(self, u):
        m, lo, hi, order = self.units[u]
        return self.shards[m] if (lo, hi) == (0, self.shards[m].shape[1]) else self.shards[m].at[:, slice(lo, hi)]

    def send(self, u, src, dst, dev, landing):
        k = self.slots[u]
        self.slots[u] += 1
        c = remote(src, dst, self.send_sem.at[u, k], self.recv_sem.at[u, k], dev)
        c.start()
        self.pending.append(c)
        return remote(landing, landing, self.send_sem.at[u, k], self.recv_sem.at[u, k], dev)

    def stage(self, u, p):
        place, core = self.place, self.place.core
        m, ph = self.units[u][0], self.phases(u)
        sibling = place.peer("c", 1)
        came = self.flight.pop(u, [])
        if p == 0:
            c = pltpu.make_async_copy(self.shard(u), self.region(u, (), None, core), self.loc_sem.at[u])
            c.start()
            self.local[u] = c
            src = self.shard(u)
            self.from_sibling.append((m, self.send(u, src, self.region(u, (), None, core), sibling, self.region(u, (), None, 1 - core))))
        else:
            for k, w in came:
                w.wait_recv()
            if p == 1:
                self.local[u].wait()
            src = None
        if p < len(ph):
            mine = src if src is not None else self.region(u, ph[:p], None, core)
            self.flight[u] = [
                (k, self.send(u, mine, self.region(u, ph[:p], None, core), place.peer(ph[p], k), self.region(u, ph[:p], (ph[p], k), core)))
                for k in xors(place.ext[ph[p]])
            ]
        for k, _ in came:
            here = self.region(u, ph[: p - 1], (ph[p - 1], k), core)
            there = self.region(u, ph[: p - 1], (ph[p - 1], k), 1 - core)
            self.from_sibling.append((m, self.send(u, here, here, sibling, there)))

    def tick(self, steps):
        for u, p in self.events[self.next : self.next + steps]:
            self.stage(u, p)
        self.next += steps

    def need(self, m):
        if m in self.complete:
            return
        self.complete.add(m)
        last = max(i for i, (u, p) in enumerate(self.events) if self.units[u][0] == m)
        self.tick(max(0, last + 1 - self.next))
        for which, c in self.from_sibling:
            if which == m:
                c.wait_recv()

    def finish(self):
        for m in range(len(self.shards)):
            self.need(m)
        for c in self.pending:
            c.wait_send()


def cast_shards(masters, shards):
    embed, eqkv, eout, eup, edown, bridge, dqkv, dout, dup, ddown, head = masters
    low = jnp.bfloat16
    def by_kind(src, dst, size):
        heads = src.shape[1] // (3 * size)
        for t in range(3):
            for h in range(heads):
                to, at = (t * heads + h) * size, (h * 3 + t) * size
                dst[:, to : to + size] = src[:, at : at + size].astype(low)
    by_kind(eqkv, shards[0], DH)
    shards[0][:, eqkv.shape[1] :] = embed[...].astype(low)
    shards[1][...] = eout[...].T.astype(low)
    by_kind(dqkv, shards[5], DHD)
    for m, src in ((2, eup), (3, edown), (4, bridge), (6, dout), (7, dup), (8, ddown), (9, head)):
        shards[m][...] = src[...].astype(low)


def shard_shapes(masters):
    a, d = masters[0].shape[0], masters[6].shape[0]
    enc = (masters[0].shape[1] + masters[1].shape[1], masters[2].shape[0], *(m.shape[1] for m in masters[3:6]))
    return [(a, c) for c in enc] + [(d, m.shape[1]) for m in masters[6:]]


class Start:
    def __init__(self, sizes, masters, shards, vec, counts, vec_all, weight_sum, lands, sems):
        self.place = place = Place(sizes)
        vec_send, vec_recv, sum_send, sum_recv = sems
        cast_shards(masters, shards)
        total = jnp.float32(0.0)
        for i in range(counts.shape[0]):
            total = total + (NP - (1.0 - VISIBLE_WEIGHT) * counts[i].astype(jnp.float32))
        weight_sum[...] = jnp.zeros(weight_sum.shape, jnp.float32) + total
        place.greet()
        self.flight = []
        for k in xors(place.ext["n"]):
            c = remote(vec, vec_all.at[place.na], vec_send.at[k - 1], vec_recv.at[k - 1], place.peer("n", k))
            c.start()
            self.flight.append(c)
        vec_all[place.na] = vec[...]
        self.small = SmallSum(place, weight_sum, lands, sum_send, sum_recv, False, True)

    def sum_hops(self):
        return len(self.small.axes)

    def vectors_here(self):
        for c in self.flight:
            c.wait()

    @staticmethod
    def scratch(sizes, shapes):
        n = sizes[2]
        return (
            [pltpu.VMEM(s, jnp.bfloat16) for s in shapes]
            + SmallSum.scratch(sizes, (8, 128), False, True)
            + [pltpu.SemaphoreType.DMA((n,))] * 2
            + SmallSum.sems(sizes)
        )


def gather_sems(sizes, units):
    slots = 2 * sum(extents(sizes).values())
    DMA = pltpu.SemaphoreType.DMA
    return [DMA((len(units), slots)), DMA((len(units), slots)), DMA((len(units),))]


def gather_kernel(sizes, units, events, *refs):
    it = iter(refs)
    take = lambda k: [next(it) for _ in range(k)]
    masters = take(11)
    vec, counts = take(2)
    outs = take(10)
    vec_all, weight_sum = take(2)
    shards = take(10)
    lands = take(len(SmallSum.scratch(sizes, (8, 128), False, True)))
    small_sems, sems = take(4), take(3)
    start = Start(sizes, masters, shards, vec, counts, vec_all, weight_sum, lands, small_sems)
    g = Gather(start.place, units, events, shards, outs, sems)
    for i in range(start.sum_hops()):
        start.small.start(i)
        start.small.finish(i)
    g.finish()
    start.vectors_here()


def gather(masters, vec, counts, sizes, units, events, cid=0):
    ext = extents(sizes)
    an = pl.BlockSpec(memory_space=pl.ANY)
    vm = pl.BlockSpec(memory_space=pltpu.VMEM)
    sm = pl.BlockSpec(memory_space=pltpu.SMEM)
    shapes = shard_shapes(masters)
    heads = (ext["n"], ext["h"], ext["l"], ext["w"], 2)
    res = pl.pallas_call(
        functools.partial(gather_kernel, sizes, units, events),
        out_shape=[jax.ShapeDtypeStruct(heads + s, jnp.bfloat16) for s in shapes]
        + [jax.ShapeDtypeStruct((sizes[2],) + vec.shape, vec.dtype), jax.ShapeDtypeStruct((8, 128), jnp.float32)],
        in_specs=[vm] * 12 + [sm],
        out_specs=[an] * 10 + [vm, vm],
        scratch_shapes=Start.scratch(sizes, shapes) + gather_sems(sizes, units),
        compiler_params=pltpu.CompilerParams(collective_id=cid, has_side_effects=True),
    )(*masters, vec, counts)
    return res[:10], res[10], res[11]


GATHER_UNITS = (
    (0, 0, 256, "lhwn"), (0, 256, 512, "nlhw"), (0, 512, 768, "nhlw"), (1, 0, 256, "nlhw"), (2, 0, 384, "nhlw"),
    (2, 384, 768, "nlhw"), (3, 0, 384, "nlhw"), (3, 384, 768, "nhlw"), (4, 0, 128, "nhlw"), (5, 0, 384, "hlwn"),
    (6, 0, 128, "lnhw"), (7, 0, 256, "nhlw"), (7, 256, 512, "nlhw"), (8, 0, 256, "nlhw"), (8, 256, 512, "nhlw"),
    (9, 0, 256, "hnlw"),
)
GATHER_ORDER = (
    (8, 0), (3, 0), (2, 0), (1, 0), (0, 0), (7, 0), (8, 1), (0, 1), (5, 0), (4, 0), (3, 1), (8, 2), (6, 0), (0,
    2), (2, 1), (15, 0), (3, 2), (1, 1), (10, 0), (8, 3), (2, 2), (15, 1), (12, 0), (7, 1), (1, 2), (10, 1), (9,
    0), (13, 0), (3, 3), (5, 1), (14, 0), (2, 3), (7, 2), (4, 1), (11, 0), (5, 2), (6, 1), (1, 3), (9, 1), (4, 2),
    (7, 3), (6, 2), (0, 3), (9, 2), (5, 3), (15, 2), (12, 1), (10, 2), (4, 3), (13, 1), (6, 3), (14, 1), (15, 3),
    (10, 3), (11, 1), (12, 2), (14, 2), (13, 2), (11, 2), (14, 3), (12, 3), (11, 3), (13, 3), (9, 3),
)


def gather_plan(ext, shapes):
    cols = [s[1] for s in shapes]
    if ext["w"] > 1:
        units = [(m, 0, c, "nlhw") for m, c in enumerate(cols)]
        return units, [[(u, p)] for u in range(len(units)) for p in range(5)]
    units = [(m, lo, min(hi, cols[m]), order) for m, lo, hi, order in GATHER_UNITS]
    return units, [list(GATHER_ORDER[i : i + 12]) for i in range(0, len(GATHER_ORDER), 12)]


REDUCE_UNITS = (
    (0, 0, 256, "lnhw"), (0, 256, 512, "lhwn"), (0, 512, 768, "hlwn"), (1, 0, 256, "lhwn"), (2, 0, 256, "hlwn"),
    (2, 256, 512, "nhlw"), (2, 512, 768, "lhwn"), (3, 0, 256, "hnlw"), (3, 256, 512, "lhwn"), (3, 512, 768,
    "lhwn"), (4, 0, 128, "lnhw"), (5, 0, 256, "lhwn"), (5, 256, 384, "hlwn"), (6, 0, 128, "hnlw"), (7, 0, 256,
    "hnlw"), (7, 256, 512, "lhwn"), (8, 0, 256, "hlwn"), (8, 256, 512, "hlwn"), (9, 0, 256, "hlwn"),
)
REDUCE_ORDER = (
    (13, 0), (10, 0), (14, 0), (15, 0), (13, 1), (10, 1), (14, 1), (15, 1), (13, 2), (10, 2), (13, 3), (2, 0),
    (10, 3), (14, 2), (2, 1), (0, 0), (15, 2), (14, 3), (0, 1), (5, 0), (13, 4), (15, 3), (5, 1), (8, 0), (2, 2),
    (8, 1), (10, 4), (2, 3), (0, 2), (12, 0), (13, 5), (12, 1), (0, 3), (14, 4), (5, 2), (4, 0), (15, 4), (13, 6),
    (4, 1), (8, 2), (10, 5), (5, 3), (12, 2), (3, 0), (8, 3), (12, 3), (3, 1), (16, 0), (9, 0), (4, 2), (16, 1),
    (9, 1), (2, 4), (14, 5), (4, 3), (7, 0), (3, 2), (0, 4), (15, 5), (7, 1), (10, 6), (16, 2), (3, 3), (18, 0),
    (16, 3), (12, 4), (9, 2), (18, 1), (17, 0), (17, 1), (9, 3), (7, 2), (11, 0), (8, 4), (18, 2), (11, 1), (7,
    3), (1, 0), (17, 2), (18, 3), (6, 0), (1, 1), (4, 4), (2, 5), (17, 3), (14, 6), (11, 2), (6, 1), (5, 4), (11,
    3), (1, 2), (16, 4), (1, 3), (6, 2), (6, 3), (8, 5), (3, 4), (0, 5), (12, 5), (15, 6), (2, 6), (7, 4), (9, 4),
    (8, 6), (12, 6), (4, 5), (18, 4), (11, 4), (17, 4), (5, 5), (7, 5), (16, 5), (3, 5), (4, 6), (0, 6), (16, 6),
    (1, 4), (9, 5), (3, 6), (11, 5), (9, 6), (1, 5), (6, 4), (11, 6), (18, 5), (17, 5), (1, 6), (5, 6), (6, 5),
    (7, 6), (18, 6), (17, 6), (6, 6),
)


def reduce_plan(ext, mats):
    if ext["w"] > 1:
        units = [(m, lo, min(lo + 256, x[1]), "wlhn") for m, x in enumerate(mats) for lo in range(0, x[1], 256)]
        return units, [[(u, p)] for u in range(len(units)) for p in range(8)]
    return list(REDUCE_UNITS), [list(REDUCE_ORDER)]


def sincos_table(rows, width):
    column = np.arange(width)
    freq = np.power(np.float32(10000.0), (-(2 * (column // 2)).astype(np.float32) / np.float32(width)).astype(np.float32))
    angle = (np.arange(rows, dtype=np.float32)[:, None] * freq[None, :]).astype(np.float32)
    return np.where(column % 2 == 0, np.sin(angle), np.cos(angle)).astype(np.float32)


def dot_nn(a, b):
    return lax.dot_general(a, b, (((1,), (0,)), ((), ())), preferred_element_type=jnp.float32)


def dot_nt(a, b):
    return lax.dot_general(a, b, (((1,), (1,)), ((), ())), preferred_element_type=jnp.float32)


def dot_tn(a, b):
    return lax.dot_general(a, b, (((0,), (0,)), ((), ())), preferred_element_type=jnp.float32)


def dot_exact(a, b):
    return lax.dot_general(a, b, (((1,), (0,)), ((), ())), precision=HIGH, preferred_element_type=jnp.float32)


class Side:
    def __init__(self, width, head, heads, rows, images, slabs):
        self.width, self.head, self.heads, self.rows = width, head, heads, rows
        self.slabs = slabs
        self.tokens = rows * images
        self.lane = head * heads
        self.packed = -(-3 * self.lane // 128) * 128

    def scratch(self, hidden):
        t, n, w = self.tokens, self.slabs, self.width
        bf, f = jnp.bfloat16, jnp.float32
        return {
            "x": ((t, w), f),
            "hat1": ((t, w), f), "hat2": ((t, w), f), "hat3": ((t, w), f),
            "inv": ((t, 128), f),
            "n1": ((t, w), bf), "n2": ((t, w), bf), "n3": ((t, w), bf),
            "qkv": ((n, t, self.packed), bf),
            "lse": ((t // self.rows, -(-n * self.heads // 8) * 8, self.rows), f),
            "att": ((n, t, -(-self.lane // 128) * 128), bf),
            "slope": ((n, t, hidden), f),
            "act": ((n, t, hidden), bf),
            "dn": ((t, w), f),
            "og1": ((t, w), bf),
            "og2": ((t, w), bf),
        }


LEFTS = ("e_n1", "chosen", "e_og1", "e_n2", "e_og2", "e_n3", "d_n1", "d_og1", "d_n2", "d_og2", "d_n3")
RIGHTS = ("e_qkv", "part0", "e_att", "e_dh", "e_act", "part4", "d_qkv", "d_att", "d_dh", "d_act", "part9")
SHIPPED = LEFTS + RIGHTS
BUFFER_OF = {"e_dh": "e_act", "d_dh": "d_act"}


def compute_kernel(sizes, merged, per, slabs, names, units, events, *refs):
    it = iter(refs)
    take = lambda k: [next(it) for _ in range(k)]
    f32, bf16 = jnp.float32, jnp.bfloat16
    count = 10
    sources = take(11 if merged else 10)
    vec_parts, weight_in = (take(1)[0], None) if merged else take(2)
    patches_all, vis_all, keep_all, table_e, table_d, counts_all = take(6)
    shipped = take(len(SHIPPED))
    vec_out, weight_out = take(2)
    store = take(count)
    load_sem, store_sem = take(2)
    if merged:
        vec_all = take(1)[0]
        shards = take(count)
        lands = take(len(SmallSum.scratch(sizes, (8, 128), False, True)))
        small_sems, sems = take(4), take(3)
    buf = dict(zip(names, it))

    all_images = counts_all.shape[0]
    first_image = lax.axis_index("narrow") * per
    start_image = jnp.minimum(first_image, all_images - per)
    patch_copies = []
    for i in range(per):
        c = pltpu.make_async_copy(patches_all.at[start_image + i], buf["raw"].at[i], load_sem.at[count + i])
        c.start()
        patch_copies.append(c)

    ticks = [0]
    if merged:
        begin = Start(sizes, sources, shards, vec_parts, counts_all, vec_all, weight_out, lands, small_sems)
        g = Gather(begin.place, units, events, shards, store, sems)
        g.tick(12)
        for i in range(begin.sum_hops()):
            begin.small.start(i)
            g.tick(12)
            begin.small.finish(i)
        begin.vectors_here()
        need = g.need
    else:
        vec_all = vec_parts
        weight_out[...] = weight_in[...]
        loads = []
        for m in range(count):
            c = pltpu.make_async_copy(sources[m], store[m], load_sem.at[m])
            c.start()
            loads.append(c)
        waited = set()

        def need(m):
            if m not in waited:
                waited.add(m)
                loads[m].wait()

    def tick():
        if merged:
            g.tick(TICK)

    class Weight:
        def __init__(self, ref):
            self.ref = ref
            self.shape = (slabs, math.prod(ref.shape[1:-1]), ref.shape[-1])

        def __getitem__(self, at):
            n, lo, hi = at if isinstance(at, tuple) else (at, 0, self.shape[2])
            v = self.ref[n] if (lo, hi) == (0, self.shape[2]) else self.ref.at[..., lo:hi][n]
            return v.reshape(self.shape[1], hi - lo)

    w_eq, w_out, w_up, w_down, w_bridge, w_dqkv, w_dout, w_dup, w_ddown, w_head = [Weight(r) for r in store]
    enc_w, dec_w = table_e.shape[1], table_d.shape[1]
    dec_rows, enc_rows = table_e.shape[0], -(-KEEP_MOST // 16) * 16
    patches, loss_w, vis_rows = buf["patches"], buf["loss_w"], []
    patches[...] = jnp.zeros_like(patches)
    loss_w[...] = jnp.zeros_like(loss_w)
    counts = []
    for i in range(per):
        patch_copies[i].wait()
        patches[i, 0:NP, :] = buf["raw"][i]
        vis_rows.append(vis_all[pl.ds(start_image + i, 1), :])
        counts.append(counts_all[start_image + i])
        live = jnp.where(start_image + i >= first_image, 1.0, 0.0)
        row = jnp.where(keep_all[pl.ds(start_image + i, 1), :] == 1, VISIBLE_WEIGHT, 1.0) * live
        loss_w[i, 0:NP, :] = jnp.broadcast_to(row, (8, NP)).T[:, 0:1]
    enc = Side(enc_w, DH, w_out.shape[2] // DH, enc_rows, per, slabs)
    dec = Side(dec_w, DHD, w_dout.shape[2] // DHD, dec_rows, per, slabs)
    for s, tag in ((enc, "e_"), (dec, "d_")):
        s.tag = tag
        s.b = {k[2:]: v for k, v in buf.items() if k.startswith(tag)}
    enc.w, dec.w = (w_eq, w_out, w_up, w_down), (w_dqkv, w_dout, w_dup, w_ddown)
    enc.ids, dec.ids = (0, 1, 2, 3), (5, 6, 7, 8)
    enc.base, dec.base = 0, 7
    vec_full = buf["vec_full"]
    enc_c, dec_c = enc_w // slabs, dec_w // slabs
    at = 0
    for k in range(13):
        width = enc_c if k < 6 else dec_c
        for n in range(slabs):
            vec_full[k : k + 1, n * width : (n + 1) * width] = vec_all[n, :, at : at + width]
        at += width
    vec_out[...] = jnp.zeros_like(vec_out)

    def vector(k, width):
        return vec_full[k : k + 1, 0:width]

    CH = 32

    def chunks(total, body):
        def step(i, carry):
            body(pl.ds(pl.multiple_of(i * CH, CH), CH))
            return carry
        lax.fori_loop(0, total // CH, step, 0)

    def norm_fwd(s, k, out, hat, inv):
        gain, bias = vector(s.base + k, s.width), vector(s.base + k + 1, s.width)
        x = s.b["x"]
        def body(r):
            v = x[r, :]
            mean = jnp.mean(v, axis=1, keepdims=True)
            d = v - mean
            i = lax.rsqrt(jnp.mean(d * d, axis=1, keepdims=True) + EPS_NORM)
            h = d * i
            s.b[hat][r, :] = h
            s.b["inv"][r, inv : inv + 1] = i
            s.b[out][r, :] = (h * gain + bias).astype(bf16)
        chunks(s.tokens, body)

    def norm_bwd(s, k, hat, inv, add):
        gain = vector(s.base + k, s.width)
        def body(r):
            dn = s.b["dn"][r, :]
            h = s.b[hat][r, :]
            vec_out[s.base + k : s.base + k + 1, 0 : s.width] += jnp.sum(dn * h, axis=0, keepdims=True)
            vec_out[s.base + k + 1 : s.base + k + 2, 0 : s.width] += jnp.sum(dn, axis=0, keepdims=True)
            g = dn * gain
            d = s.b["inv"][r, inv : inv + 1] * (
                g - jnp.mean(g, axis=1, keepdims=True) - h * jnp.mean(g * h, axis=1, keepdims=True)
            )
            s.b["x"][r, :] = s.b["x"][r, :] + d if add else d
        chunks(s.tokens, body)

    def slab_loop(body):
        def step(n, carry):
            body(n)
            return carry
        lax.fori_loop(0, slabs, step, 0)

    def head_mask(s, h):
        lane = lax.broadcasted_iota(jnp.int32, (1, s.lane), 1)
        return (lane >= h * s.head) & (lane < (h + 1) * s.head)

    def scores(s, q, k, mask, limit):
        v = dot_nt(k, jnp.where(mask, q, jnp.zeros_like(q))) * (s.head ** -0.5)
        key = lax.broadcasted_iota(jnp.int32, (s.rows, s.rows), 0)
        return jnp.where(key < limit, v, -1e30)

    def attention_loop(body, between=None):
        def step(i, carry):
            body(i // slabs, i % slabs)
            return carry
        if between is None or not merged:
            lax.fori_loop(0, per * slabs, step, 0)
            return
        for image in range(per):
            lax.fori_loop(image * slabs, (image + 1) * slabs, step, 0)
            between()

    def image_rows(s, image):
        return pl.ds(pl.multiple_of(image * s.rows, 16), s.rows)

    def block_fwd(s, limit):
        b = s.b
        if b["att"].shape[2] != s.lane:
            b["att"][...] = jnp.zeros_like(b["att"])
        qkv_w, out_w, up_w, down_w = s.w
        need(s.ids[0])
        norm_fwd(s, 0, "n1", "hat1", 1)
        tick()
        def qkv(n):
            b["qkv"][n] = dot_nn(b["n1"][...], qkv_w[n, 0, s.packed]).astype(bf16)
        slab_loop(qkv)
        tick()
        def attend(image, n):
            r = image_rows(s, image)
            q = b["qkv"][n, r, 0 : s.lane]
            k = b["qkv"][n, r, s.lane : 2 * s.lane]
            v = b["qkv"][n, r, 2 * s.lane : 3 * s.lane]
            v_t = v.T
            parts = []
            for h in range(s.heads):
                sc = scores(s, q, k, head_mask(s, h), limit(image))
                top = jnp.max(sc, axis=0, keepdims=True)
                e = jnp.exp(sc - top)
                z = jnp.sum(e, axis=0, keepdims=True)
                p = (e * (1.0 / z)).astype(bf16)
                parts.append(dot_nn(v_t[h * s.head : (h + 1) * s.head], p))
                b["lse"][image, pl.ds(n * s.heads + h, 1), :] = top + jnp.log(z)
            b["att"][n, r, 0 : s.lane] = jnp.concatenate(parts, axis=0).astype(bf16).T
        attention_loop(attend, tick)
        need(s.ids[1])
        ship(s.tag + "att")
        def project(n):
            b["x"][...] += dot_nt(b["att"][n, :, 0 : s.lane], out_w[n])
        slab_loop(project)
        norm_fwd(s, 2, "n2", "hat2", 2)
        need(s.ids[2])
        need(s.ids[3])
        hid = buf["hid"]
        c = up_w.shape[2]
        def mlp(n):
            hid[0 : s.tokens, 0:c] = dot_nn(b["n2"][...], up_w[n])
            def body(r):
                v = hid[r, 0:c]
                cdf = 0.5 * (1.0 + lax.erf(v * 0.7071067811865476))
                b["act"][n, r, :] = (v * cdf).astype(bf16)
                b["slope"][n, r, :] = cdf + v * (0.3989422804014327 * jnp.exp(-0.5 * v * v))
            chunks(s.tokens, body)
            b["x"][...] += dot_nt(b["act"][n], down_w[n])
        if merged and s is enc:
            for n in range(slabs):
                mlp(n)
                tick()
        else:
            slab_loop(mlp)
        ship(s.tag + "act")
        norm_fwd(s, 4, "n3", "hat3", 3)
        for name in ("n1", "n2", "n3"):
            ship(s.tag + name)

    on_way = {}

    def ship(name):
        at = SHIPPED.index(name)
        c = pltpu.make_async_copy(buf[BUFFER_OF.get(name, name)], shipped[at], store_sem.at[at])
        c.start()
        on_way[name] = c

    def arrived(name):
        on_way.pop(name).wait()

    def block_bwd(s, limit):
        b = s.b
        qkv_w, out_w, up_w, down_w = s.w
        b["og2"][...] = b["x"][...].astype(bf16)
        ship(s.tag + "og2")
        b["dn"][...] = jnp.zeros_like(b["dn"])
        arrived(s.tag + "act")
        def down(n):
            b["act"][n] = (dot_nn(b["og2"][...], down_w[n]) * b["slope"][n]).astype(bf16)
            b["dn"][...] += dot_nt(b["act"][n], up_w[n])
        slab_loop(down)
        ship(s.tag + "dh")
        norm_bwd(s, 2, "hat2", 2, True)
        b["og1"][...] = b["x"][...].astype(bf16)
        ship(s.tag + "og1")
        arrived(s.tag + "att")
        def proj(n):
            b["att"][n, :, 0 : s.lane] = dot_nn(b["og1"][...], out_w[n]).astype(bf16)
        slab_loop(proj)
        def attend(image, n):
            r = image_rows(s, image)
            q = b["qkv"][n, r, 0 : s.lane]
            k = b["qkv"][n, r, s.lane : 2 * s.lane]
            v = b["qkv"][n, r, 2 * s.lane : 3 * s.lane]
            g = b["att"][n, r, 0 : s.lane]
            k_t = k.T
            parts = []
            dk = jnp.zeros((s.rows, s.lane), f32)
            dv = dk
            for h in range(s.heads):
                mask = head_mask(s, h)
                p = jnp.exp(scores(s, q, k, mask, limit(image)) - b["lse"][image, pl.ds(n * s.heads + h, 1), :])
                dp = dot_nt(v, jnp.where(mask, g, jnp.zeros_like(g)))
                dv = jnp.where(mask, dot_nn(p.astype(bf16), g), dv)
                ds = (p * (dp - jnp.sum(dp * p, axis=0, keepdims=True))).astype(bf16)
                dk = jnp.where(mask, dot_nn(ds, q), dk)
                parts.append(dot_nn(k_t[h * s.head : (h + 1) * s.head], ds))
            dq = jnp.concatenate(parts, axis=0).T
            scale = s.head ** -0.5
            if s.packed != 3 * s.lane:
                b["qkv"][n, r, 2 * s.lane : s.packed] = jnp.zeros((s.rows, s.packed - 2 * s.lane), bf16)
            b["qkv"][n, r, 0 : s.lane] = (dq * scale).astype(bf16)
            b["qkv"][n, r, s.lane : 2 * s.lane] = (dk * scale).astype(bf16)
            b["qkv"][n, r, 2 * s.lane : 3 * s.lane] = dv.astype(bf16)
        attention_loop(attend)
        ship(s.tag + "qkv")
        b["dn"][...] = jnp.zeros_like(b["dn"])
        def qkv(n):
            b["dn"][...] += dot_nt(b["qkv"][n], qkv_w[n, 0, s.packed])
        slab_loop(qkv)
        norm_bwd(s, 0, "hat1", 1, True)

    chosen = buf["chosen"]
    slots = KEEP_MOST
    chosen[...] = jnp.zeros_like(chosen)
    enc.b["x"][...] = jnp.zeros_like(enc.b["x"])
    for i in range(per):
        r = pl.ds(i * enc_rows, slots)
        patch = lax.broadcasted_iota(jnp.int32, (dec_rows, slots), 0)
        one = (patch == vis_rows[i]).astype(f32).T
        chosen[r, :] = dot_nn(one.astype(bf16), patches[i]).astype(bf16)
        enc.b["x"][r, :] = dot_exact(one, table_e[...])
    need(0)
    for n in range(slabs):
        lead = w_eq.shape[2] - 256
        part = dot_nn(chosen[...], w_eq[n, lead, lead + 256])
        enc.b["x"][:, n * enc_c : (n + 1) * enc_c] += part[:, 256 - enc_c : 256]
    ship("chosen")
    block_fwd(enc, lambda image: counts_all[start_image + image])
    need(4)
    bridged = buf["hid"]
    for n in range(slabs):
        bridged[0 : enc.tokens, n * dec_c : (n + 1) * dec_c] = dot_nn(enc.b["n3"][...], w_bridge[n])

    def hits(i, turned_way):
        patch = lax.broadcasted_iota(jnp.int32, (dec_rows, slots), 0)
        slot = lax.broadcasted_iota(jnp.int32, (dec_rows, slots), 1)
        hit = ((patch == vis_rows[i]) & (slot < counts[i])).astype(f32)
        return hit if turned_way else hit.T

    for i in range(per):
        r = pl.ds(i * dec_rows, dec_rows)
        hit = hits(i, True)
        placed = dot_exact(hit, bridged[pl.ds(i * enc_rows, slots), 0:dec_w])
        seen = jnp.sum(hit, axis=1, keepdims=True) > 0
        dec.b["x"][r, :] = jnp.where(seen, placed, vector(6, dec_w)) + table_d[...]
    block_fwd(dec, lambda image: NP)
    need(9)
    pred = buf["hid"]
    pix_c = w_head.shape[2]
    pix = patches.shape[2]
    for n in range(slabs):
        pred[0 : dec.tokens, n * pix_c : (n + 1) * pix_c] = dot_nn(dec.b["n3"][...], w_head[n])

    pgrad = buf["pgrad"]
    divisor = weight_out[0:1, 0:1]
    loss = jnp.zeros((1, 1), f32)
    LC = 16
    for i in range(per):
        def lossy(j, total):
            r = pl.ds(pl.multiple_of(j * LC, LC), LC)
            px = patches[i, r, :].astype(f32)
            d = px - jnp.mean(px, axis=1, keepdims=True)
            target = d * lax.rsqrt(jnp.mean(d * d, axis=1, keepdims=True) + EPS_NORM)
            rr = pl.ds(pl.multiple_of(i * dec_rows + j * LC, LC), LC)
            error = pred[rr, 0:pix] - target
            weight = loss_w[i, r, :]
            pgrad[rr, :] = (2.0 * weight * error / divisor).astype(bf16)
            return total + jnp.sum(weight * error * error, keepdims=True)
        loss = lax.fori_loop(0, dec_rows // LC, lossy, loss)
    part9 = buf["part9"]
    part9[...] = jnp.zeros_like(part9)
    for n in range(slabs):
        part9[n, :, 0:pix_c] = pgrad[:, n * pix_c : (n + 1) * pix_c]
    dec.b["dn"][...] = jnp.zeros_like(dec.b["dn"])
    ship("part9")
    def head_bwd(n):
        dec.b["dn"][...] += dot_nt(part9[n, :, 0:pix_c], w_head[n])
    slab_loop(head_bwd)
    norm_bwd(dec, 4, "hat3", 3, False)
    block_bwd(dec, lambda image: NP)
    part4 = buf["part4"]
    part4[...] = jnp.zeros_like(part4)
    for i in range(per):
        r = pl.ds(i * dec_rows, dec_rows)
        seen = jnp.sum(hits(i, True), axis=1, keepdims=True) > 0
        grad = dec.b["x"][r, :]
        vec_out[6:7, 0:dec_w] += jnp.sum(jnp.where(seen, 0.0, grad), axis=0, keepdims=True)
        back = dot_exact(hits(i, False), grad).astype(bf16)
        for n in range(slabs):
            part4[n, pl.ds(i * enc_rows, slots), :] = back[:, n * dec_c : (n + 1) * dec_c]
    ship("part4")
    enc.b["dn"][...] = jnp.zeros_like(enc.b["dn"])
    def bridge_bwd(n):
        enc.b["dn"][...] += dot_nt(part4[n], w_bridge[n])
    slab_loop(bridge_bwd)
    norm_bwd(enc, 4, "hat3", 3, False)
    block_bwd(enc, lambda image: counts_all[start_image + image])

    part0 = buf["part0"]
    part0[...] = jnp.zeros_like(part0)
    for n in range(slabs):
        part0[n, :, 256 - enc_c : 256] = enc.b["x"][:, n * enc_c : (n + 1) * enc_c].astype(bf16)
    ship("part0")
    row = lax.broadcasted_iota(jnp.int32, (1, vec_out.shape[1]), 1)
    vec_out[13:14, :] = jnp.where(row >= 0, loss, 0.0)
    for name in list(on_way):
        arrived(name)
    if merged:
        g.finish()


TICK = 3
MERGED = True


def compute(sources, shapes, vec_parts, weight_sum, patches, vis_index, keep_mask, counts, sizes, units, events, merged):
    slabs = sizes[2]
    ext = extents(sizes)
    heads = (slabs, ext["h"], ext["l"], ext["w"], 2)
    owners = math.prod(heads[1:])
    weights = [jax.ShapeDtypeStruct((slabs, owners * a, c), jnp.bfloat16) for a, c in shapes]
    per, pix = -(-counts.shape[0] // slabs), patches.shape[2]
    dec_rows, enc_rows = -(-NP // 16) * 16, -(-KEEP_MOST // 16) * 16
    enc_w, dec_w = weights[0].shape[1], weights[5].shape[1]
    enc = Side(enc_w, DH, weights[1].shape[2] // DH, enc_rows, per, slabs)
    dec = Side(dec_w, DHD, weights[6].shape[2] // DHD, dec_rows, per, slabs)
    named = {}
    for s, tag, up in ((enc, "e_", weights[2]), (dec, "d_", weights[7])):
        for k, v in s.scratch(up.shape[2]).items():
            named[tag + k] = v
    f32, bf16 = jnp.float32, jnp.bfloat16
    top = max(enc.tokens, dec.tokens)
    named["hid"] = ((top, max(pix, weights[2].shape[2], weights[7].shape[2])), f32)
    named["vec_full"] = ((16, enc_w), f32)
    named["chosen"] = ((enc.tokens, pix), bf16)
    named["pgrad"] = ((dec.tokens, pix), bf16)
    up128 = lambda c: -(-c // 128) * 128
    named["part9"] = ((slabs, dec.tokens, up128(weights[9].shape[2])), bf16)
    named["part4"] = ((slabs, enc.tokens, weights[4].shape[2]), bf16)
    named["part0"] = ((slabs, enc.tokens, 256), bf16)
    named["raw"] = ((per, NP, pix), bf16)
    named["patches"] = ((per, dec_rows, pix), bf16)
    named["loss_w"] = ((per, dec_rows, 1), f32)
    ship_shapes = [jax.ShapeDtypeStruct(named[BUFFER_OF.get(k, k)][0], bf16) for k in SHIPPED]
    an = pl.BlockSpec(memory_space=pl.ANY)
    vm = pl.BlockSpec(memory_space=pltpu.VMEM)
    sm = pl.BlockSpec(memory_space=pltpu.SMEM)
    DMA = pltpu.SemaphoreType.DMA
    table_e = jnp.asarray(np.pad(sincos_table(NP, enc_w), ((0, dec_rows - NP), (0, 0))))
    table_d = jnp.asarray(np.pad(sincos_table(NP, dec_w), ((0, dec_rows - NP), (0, 0))))
    store = [pltpu.VMEM(heads + s if merged else w.shape, bf16) for s, w in zip(shapes, weights)]
    scratch = store + [DMA((10 + per,)), DMA((len(SHIPPED),))]
    small = [vec_parts] if merged else [vec_parts, weight_sum]
    if merged:
        scratch += [pltpu.VMEM((slabs,) + vec_parts.shape, f32)] + Start.scratch(sizes, shapes) + gather_sems(sizes, units)
    params = dict(vmem_limit_bytes=61 << 20)
    if merged:
        params.update(collective_id=0, has_side_effects=True)
    res = pl.pallas_call(
        functools.partial(compute_kernel, sizes, merged, per, slabs, list(named), units, events),
        out_shape=ship_shapes + [jax.ShapeDtypeStruct((16, enc_w), f32), jax.ShapeDtypeStruct((8, 128), f32)],
        in_specs=[vm if merged else an] * len(sources) + [vm] * len(small) + [an] + [vm] * 4 + [sm],
        out_specs=[an] * len(SHIPPED) + [vm, vm],
        scratch_shapes=scratch + [pltpu.VMEM(s, d) for s, d in named.values()],
        compiler_params=pltpu.CompilerParams(**params),
    )(*sources, *small, patches, vis_index, keep_mask, table_e, table_d, counts)
    return res[: len(SHIPPED)], res[len(SHIPPED)], res[len(SHIPPED) + 1]


def split_low(x):
    high = x.astype(jnp.bfloat16)
    return high, (x - high.astype(jnp.float32)).astype(jnp.bfloat16)


def dot_three(a, b, kind=dot_nn):
    (ah, al), (bh, bl) = a, b
    return kind(ah, bh) + (kind(ah, bl) + kind(al, bh))


def roots(mats):
    side = mats[0].shape[0]
    eye = lax.broadcasted_iota(jnp.int32, (side, side), 0) == lax.broadcasted_iota(jnp.int32, (side, side), 1)
    five = jnp.where(eye, 5.0, 0.0)
    size = [jnp.sqrt(jnp.sum(m * m, keepdims=True)) for m in mats]
    current = [m * (1.0 / s) for m, s in zip(mats, size)]
    result = None
    for step in range(NEWTON):
        factor = [split_low((five - c) * 0.25) for c in current]
        if result is None:
            result = [(five - c) * 0.25 for c in current]
        else:
            result = [dot_three(split_low(r), f) for r, f in zip(result, factor)]
        if step + 1 < NEWTON:
            square = [split_low(dot_three(f, f)) for f in factor]
            fourth = [split_low(dot_three(q, q)) for q in square]
            current = [dot_three(q, split_low(c)) for q, c in zip(fourth, current)]
    return [r * lax.rsqrt(jnp.sqrt(s)) for r, s in zip(result, size)]


GROUPS = (21, 14)


def optimizer_kernel(pieces, upright, sides, enc_cols, dec_cols, *refs):
    it = iter(refs)
    take = lambda k: [next(it) for _ in range(k)]
    n_mats = len(pieces)
    owned = take(max(p[0] for blocks in pieces for parts in blocks for p in parts) + 1)
    masters = take(n_mats)
    stats = take(4)
    squares, vec_sum, weight_sum, vectors, first, second, step_count = take(7)
    new = take(n_mats)
    new_stats = take(4)
    new_vectors, new_first, new_second, norms, loss_out, weight_out = take(6)
    g_enc, g_dec, u_enc, u_dec = take(4)
    old = take(4)
    fresh = take(4)
    in_sem, out_sem = take(2)
    f32 = jnp.float32
    loads = []
    for i in (2, 3, 0, 1):
        c = pltpu.make_async_copy(stats[i], old[i], in_sem.at[i])
        c.start()
        loads.append((i, c))
    loads = dict(loads)

    enc_vec, dec_vec = vec_sum[0:6, :], vec_sum[6:13, 0 : dec_cols * (vec_sum.shape[1] // enc_cols)]
    enc_sq = squares[0:1, 0:1] + jnp.sum(enc_vec * enc_vec, keepdims=True)
    dec_sq = squares[1:2, 0:1] + jnp.sum(dec_vec * dec_vec, keepdims=True)
    norms[0] = jnp.sqrt(enc_sq)[0, 0]
    norms[1] = jnp.sqrt(dec_sq)[0, 0]
    loss_out[0] = vec_sum[13:14, 0:1][0, 0]
    weight_out[0] = weight_sum[0:1, 0:1][0, 0]
    clip = jnp.minimum(1.0, CLIP_NORM / jnp.sqrt(enc_sq + dec_sq))

    sections = ((1, g_dec, u_dec, 2, LR_MATRIX), (0, g_enc, u_enc, 0, LR_MATRIX * LAYER_DECAY))
    for which, grad, update, base, rate in sections:
        at = 0
        for i in range(n_mats):
            if sides[i] != which:
                continue
            for parts in pieces[i]:
                col = 0
                for src, lo, width in parts:
                    grad[at, :, col : col + width] = owned[src][:, lo : lo + width] * clip
                    col += width
                at += 1
        total = at
        loads[base].wait()
        loads[base + 1].wait()
        group = min(GROUPS[which], total)
        def body(i, carry):
            start = jnp.minimum(i * group, total - group)
            g = [grad[start + j] for j in range(group)]
            low = [split_low(x) for x in g]
            turned = [split_low(x.T) for x in g]
            small = [STAT_DECAY * old[base][start + j] + (1.0 - STAT_DECAY) * dot_three(low[j], low[j], dot_nt) for j in range(group)]
            large = [STAT_DECAY * old[base + 1][start + j] + (1.0 - STAT_DECAY) * dot_three(turned[j], turned[j], dot_nt) for j in range(group)]
            for j in range(group):
                fresh[base][start + j] = small[j]
                fresh[base + 1][start + j] = large[j]
            left = roots(small)
            right = roots(large)
            for j in range(group):
                half = dot_three(split_low(left[j]), low[j])
                update[start + j] = rate * dot_three(split_low(half), split_low(right[j]))
            return carry
        lax.fori_loop(0, -(-total // group), body, 0)
        for k in (base, base + 1):
            pltpu.make_async_copy(fresh[k], new_stats[k], out_sem.at[k]).start()
        at = 0
        for i in range(n_mats):
            if sides[i] != which:
                continue
            for k in range(len(pieces[i])):
                lo = k * BLOCK
                if upright[i]:
                    new[i][:, lo : lo + BLOCK] = masters[i][:, lo : lo + BLOCK] - update[at]
                else:
                    new[i][lo : lo + BLOCK, :] = masters[i][lo : lo + BLOCK, :] - update[at].T
                at += 1

    na = lax.axis_index("narrow")
    steps = jnp.full((1, 128), step_count[0], jnp.int32).astype(f32)[0:1, 0:1]
    scale_one = 1.0 / (1.0 - jnp.exp(steps * math.log(BETA_FIRST)))
    scale_two = 1.0 / (1.0 - jnp.exp(steps * math.log(BETA_SECOND)))
    slabs = vec_sum.shape[1] // enc_cols
    at = 0
    for k in range(13):
        width = enc_cols if k < 6 else dec_cols
        rate = LR_VECTOR * LAYER_DECAY if k < 6 else LR_VECTOR
        g = vec_sum[k : k + 1, 0:width]
        for n in range(1, slabs):
            g = jnp.where(na == n, vec_sum[k : k + 1, n * width : (n + 1) * width], g)
        g = g * clip
        cols = slice(at, at + width)
        one = BETA_FIRST * first[:, cols] + (1.0 - BETA_FIRST) * g
        two = BETA_SECOND * second[:, cols] + (1.0 - BETA_SECOND) * g * g
        new_first[:, cols] = one
        new_second[:, cols] = two
        new_vectors[:, cols] = vectors[:, cols] - rate * (one * scale_one) / (jnp.sqrt(two * scale_two) + EPS_ADAM)
        at += width
    for k in range(4):
        pltpu.make_async_copy(fresh[k], new_stats[k], out_sem.at[k]).wait()


def optimizer(owned, masters, stats, squares, vec_sum, weight_sum, vectors, first, second, step_count, enc_cols, dec_cols):
    kinds = ENC_KINDS + DEC_KINDS
    sides = (0,) * len(ENC_KINDS) + (1,) * len(DEC_KINDS)
    width = [m.shape[1] if kind else m.shape[0] for m, kind in zip(masters, kinds)]
    def plain(src, first_col, cols):
        return [[(src, first_col + k * BLOCK, BLOCK)] for k in range(cols // BLOCK)]
    def by_head(src, cols, head):
        heads = cols // (3 * head)
        per = BLOCK // head
        order = [(t * heads + h) * head for h in range(heads) for t in range(3)]
        return [[(src, order[k * per + j], head) for j in range(per)] for k in range(cols // BLOCK)]
    pieces = [
        plain(0, width[1], width[0]), by_head(0, width[1], DH), plain(1, 0, width[2]), plain(2, 0, width[3]),
        plain(3, 0, width[4]), plain(4, 0, width[5]), by_head(5, width[6], DHD), plain(6, 0, width[7]),
        plain(7, 0, width[8]), plain(8, 0, width[9]), plain(9, 0, width[10]),
    ]
    flat = [s.reshape(s.shape[2:]) for s in stats]
    upright = [kind or i != 2 for i, kind in enumerate(kinds)]
    masters = [m if kind or not up else m.T for m, kind, up in zip(masters, kinds, upright)]
    f32 = jnp.float32
    like = lambda x: jax.ShapeDtypeStruct(x.shape, f32)
    an = pl.BlockSpec(memory_space=pl.ANY)
    vm = pl.BlockSpec(memory_space=pltpu.VMEM)
    sm = pl.BlockSpec(memory_space=pltpu.SMEM)
    block = [pltpu.VMEM((flat[i].shape[0], flat[i].shape[1], BLOCK), f32) for i in (0, 2)]
    whole = [pltpu.VMEM(s.shape, f32) for s in flat]
    DMA = pltpu.SemaphoreType.DMA
    n = len(masters)
    res = pl.pallas_call(
        functools.partial(optimizer_kernel, pieces, upright, sides, enc_cols, dec_cols),
        out_shape=[like(m) for m in masters] + [like(s) for s in flat]
        + [like(vectors)] * 3 + [jax.ShapeDtypeStruct((k,), f32) for k in (2, 1, 1)],
        in_specs=[vm] * (len(owned) + n) + [an] * 4 + [vm] * 6 + [sm],
        out_specs=[vm] * n + [an] * 4 + [vm] * 3 + [sm] * 3,
        scratch_shapes=block + block + whole + whole + [DMA((4,)), DMA((4,))],
        compiler_params=pltpu.CompilerParams(vmem_limit_bytes=56 << 20),
    )(*owned, *masters, *flat, squares, vec_sum, weight_sum, vectors, first, second, step_count)
    new_stats = [r.reshape(s.shape) for r, s in zip(res[n : n + 4], stats)]
    new = [r if kind or not up else r.T for r, kind, up in zip(res[:n], kinds, upright)]
    return new, new_stats, res[n + 4 : n + 7], res[n + 7], res[n + 8].reshape(()), res[n + 9].reshape(())


def per_device(
    sizes,
    patches, vis_index, keep_mask, counts, step_count,
    w_embed, enc_qkv, enc_out, enc_up, enc_down, w_bridge,
    dec_qkv, dec_out, dec_up, dec_down, w_head,
    vectors, first_moment, second_moment, enc_small, enc_big, dec_small, dec_big,
):
    n_dp, n_wide, n_nar = sizes
    ext = extents(sizes)
    masters = (w_embed, enc_qkv, enc_out, enc_up, enc_down, w_bridge, dec_qkv, dec_out, dec_up, dec_down, w_head)
    sources = [m if kind or i == 2 else m.T for i, (m, kind) in enumerate(zip(masters, ENC_KINDS + DEC_KINDS))]
    enc_cols, dec_cols = w_embed.shape[1], w_bridge.shape[1]
    shapes = shard_shapes(sources)
    units, events = gather_plan(ext, shapes)
    merged = MERGED and all(a % 16 == 0 for a, _ in shapes)
    if merged:
        weights, vec_all, weight_sum = sources, vectors, None
    else:
        gathered, vec_all, weight_sum = gather(sources, vectors, counts, sizes, units, events)
        weights = [g.reshape(n_nar, -1, g.shape[-1]) for g in gathered]
    shipped, vec_grad, weight_sum = compute(
        weights, shapes, vec_all, weight_sum, patches, vis_index, keep_mask, counts, sizes, units, events, merged
    )
    lefts, rights = shipped[: len(LEFTS)], shipped[len(LEFTS) :]
    pairs = ([(0, 0), (1, 1)], [(2, 2)], [(3, 3)], [(4, 4)], [(5, 5)], [(6, 6)], [(7, 7)], [(8, 8)], [(9, 9)], [(10, 10)])
    mats = []
    for terms, shape in zip(pairs, shapes):
        cols = -(-shape[1] // 128) * 128
        wide = [rights[g].shape[2] for _, g in terms]
        mats.append((shape[0], cols, [(x, g, 0 if i == 0 else cols - wide[i], wide[i]) for i, (x, g) in enumerate(terms)]))
    units, events = reduce_plan(ext, mats)
    owned, vec_sum, squares = reduce_scatter(
        lefts, rights, mats, vec_grad, sizes, units, events, [True] * 5 + [False] * 5
    )
    new, new_stats, new_vecs, norms, loss_total, weight_total = optimizer(
        owned, masters, (enc_small, enc_big, dec_small, dec_big), squares, vec_sum,
        weight_sum, vectors, first_moment, second_moment, step_count, enc_cols, dec_cols,
    )
    return (*new, *new_stats, *new_vecs, norms, loss_total, weight_total)


def solution(mesh):
    sizes = (mesh.shape["dp"], mesh.shape["wide"], mesh.shape["narrow"])
    rows = P(("dp", "wide"))
    matrix = P(("dp", "wide"), "narrow")
    turned = P("narrow", ("dp", "wide"))
    matrices = tuple(matrix if kind else turned for kind in ENC_KINDS + DEC_KINDS)
    stats = (P(("dp", "wide"), "narrow"),) * 4
    packed = (P("narrow"),) * 3
    in_specs = (rows, rows, rows, rows, P()) + matrices + packed + stats
    out_specs = matrices + stats + packed + (P(), P(), P())
    return jax.shard_map(
        functools.partial(per_device, sizes), mesh=mesh, in_specs=in_specs, out_specs=out_specs, check_vma=False
    )
```

```python
import functools
import math

import jax
import jax.numpy as jnp
import numpy as np
from jax import lax
from jax.experimental import pallas as pl
from jax.experimental.pallas import tpu as pltpu
from jax.sharding import PartitionSpec as P

D = 768
DH = 64
DD = 512
DHD = 32
PIX = 768
NP = 196
BLOCK = 64
NEWTON = 3
KEEP_MOST = 98

HIGH = lax.Precision.HIGHEST
EPS_NORM = 1e-06
VISIBLE_WEIGHT = 0.1
STAT_DECAY = 0.5
LR_MATRIX = 0.2
LR_VECTOR = 0.2
LAYER_DECAY = 0.75
BETA_FIRST = 0.9
BETA_SECOND = 0.999
EPS_ADAM = 1e-08
CLIP_NORM = 1.0
ENC_KINDS = (True, True, False, True, False, True)
DEC_KINDS = (True, False, True, False, True)


MESHT = pl.DeviceIdType.MESH
FULL_CODE = 32767.0
FLOOR = 1e-30


def xors(n):
    return list(range(1, n))


def extents(sizes):
    n_dp, n_wide, n_nar = sizes
    return {"n": n_nar, "h": n_dp // 2, "l": 2, "w": n_wide // 2}


def phases_of(order, ext):
    return [d for d in order if ext[d] > 1]


def messages(order, ext):
    out, left = [], 1
    for d in ext:
        left *= ext[d]
    for d in phases_of(order, ext):
        left //= ext[d]
        out.append((d, ext[d] - 1, left))
    return out


class Place:
    def __init__(self, sizes):
        self.sizes = sizes
        self.ext = extents(sizes)
        self.dp, self.wi, self.na = (lax.axis_index(x) for x in ("dp", "wide", "narrow"))
        self.own = {"n": self.na, "h": self.dp // 2, "l": self.dp % 2, "w": self.wi // 2}
        self.core = self.wi % 2

    def peer(self, dim, k):
        if dim == "n":
            return {"narrow": self.na ^ k}
        if dim == "h":
            return {"dp": self.dp ^ (2 * k)}
        if dim in "ld":
            return {"dp": self.dp ^ k}
        if dim == "w":
            return {"wide": self.wi ^ (2 * k)}
        if dim == "g":
            return {"dp": self.dp ^ (k // 2), "wide": self.wi ^ (k % 2)}
        return {"wide": self.wi ^ 1}

    def greet(self):
        ext = self.ext
        partners = [self.peer(d, k) for d in "nw" for k in xors(ext[d])]
        partners += [self.peer("g", k) for k in xors(2 * self.sizes[0])]
        barrier = pltpu.get_barrier_semaphore()
        for p in partners:
            pl.semaphore_signal(barrier, inc=1, device_id=p, device_id_type=MESHT)
        pl.semaphore_wait(barrier, len(partners))

    def hops(self, narrow, joint):
        out = [("c", 2, self.core), ("d", self.sizes[0], self.dp)]
        if joint:
            out = [("g", 2 * self.sizes[0], self.dp * 2 + self.core)]
        if self.ext["w"] > 1:
            out.append(("w", self.ext["w"], self.wi // 2))
        if narrow and self.ext["n"] > 1:
            out.append(("n", self.ext["n"], self.na))
        return out


def remote(src, dst, ss, rs, dev):
    return pltpu.make_async_remote_copy(
        src_ref=src, dst_ref=dst, send_sem=ss, recv_sem=rs, device_id=dev, device_id_type=MESHT
    )


class SmallSum:
    def __init__(self, place, value, lands, send, recv, narrow, joint):
        self.place, self.value, self.lands, self.send, self.recv = place, value, lands, send, recv
        self.axes = place.hops(narrow, joint)
        self.flight = None

    def start(self, i):
        d, members, at = self.axes[i]
        land = self.lands[i]
        land[at] = self.value[...]
        self.flight = []
        for k in xors(members):
            c = remote(self.value, land.at[at], self.send.at[i, k - 1], self.recv.at[i, k - 1], self.place.peer(d, k))
            c.start()
            self.flight.append(c)

    def finish(self, i):
        d, members, at = self.axes[i]
        for c in self.flight:
            c.wait()
        total = self.lands[i][0]
        for j in range(1, members):
            total = total + self.lands[i][j]
        self.value[...] = total

    @staticmethod
    def scratch(sizes, shape, narrow, joint):
        members = ([2 * sizes[0]] if joint else [2, sizes[0]]) + ([sizes[1] // 2] if sizes[1] > 2 else []) + ([sizes[2]] if narrow and sizes[2] > 1 else [])
        return [pltpu.VMEM((m,) + shape, jnp.float32) for m in members]

    @staticmethod
    def sems(sizes):
        return [pltpu.SemaphoreType.DMA((4, max(*sizes, 2 * sizes[0])))] * 2


def plan(units, events, mats, ext, tokens):
    flat = []
    for step in events:
        for u, p in step:
            if p <= len(phases_of(units[u][3], ext)) + 3:
                flat.append((u, p))
    at = {e: i for i, e in enumerate(flat)}
    blocks = ext["h"] * ext["l"] * ext["w"]
    wants = []
    big = max((mats[m][0] for m, *_ in units)), max(hi - lo for m, lo, hi, o in units)
    first_use, last_need = {}, {}
    for u, (m, lo, hi, order) in enumerate(units):
        a, c = mats[m][0], hi - lo
        for x, g, *_ in terms_of(mats, m, lo, hi):
            first_use[x] = min(first_use.get(x, (len(flat),)), (at[u, 0], at[u, 1], tokens[g], a))
            last_need[x] = max(last_need.get(x, 0), at[u, 3])
        last = at[u, len(phases_of(order, ext)) + 3]
        full = (ext["n"], blocks) + (big if a * c * 5 > 2 * big[0] * big[1] else (a, c))
        for j, (x, g, c_lo, c_hi, g_lo) in enumerate(terms_of(mats, m, lo, hi)):
            wants.append((at[u, 0], at[u, 3], ("g", u, j), (ext["n"], tokens[g], c_hi - c_lo), "b"))
        wants.append((at[u, 1], at[u, 3], ("out", u), full, "f"))
        wants.append((at[u, 2], at[u, 3], ("stage", u), full, "f"))
        wants.append((at[u, 3], at[u, 3], ("acc", u), full, "f"))
        wants.append((at[u, 3], last, ("kept", u), (messages(order, ext)[0][2], a, c), "f"))
        for p, (d, k, n) in enumerate(messages(order, ext)):
            wants.append((at[u, p + 3], last, ("q", u, p), (k, n, a, c), "q"))
    for x, (start, turn, rows, a) in first_use.items():
        turn = min(at[u, 1] for u, (m, lo, hi, o) in enumerate(units) if any(x == t[0] for t in terms_of(mats, m, lo, hi)))
        wants.append((start, turn, ("plain", x), (rows, 2 * blocks * a), "b"))
        wants.append((start, last_need[x], ("turned", x), (blocks, 2, a, rows), "b"))
    wants.sort(key=lambda w: w[0])
    bufs, where = [], {}
    for start, end, name, shape, kind in wants:
        for i, b in enumerate(bufs):
            if b[0] == (shape, kind) and b[1] < start:
                b[1] = end
                where[name] = i
                break
        else:
            bufs.append([(shape, kind), end])
            where[name] = len(bufs) - 1
    return [b[0] for b in bufs], where


def terms_of(mats, m, lo, hi):
    out = []
    for x, g, first, width in mats[m][2]:
        a, b = max(lo, first), min(hi, first + width)
        if a < b:
            out.append((x, g, a - lo, b - lo, a - first))
    out.sort(key=lambda t: t[2] - t[3])
    return out


def reduce_kernel(sizes, units, events, mats, n_left, n_right, planned, is_enc, *refs):
    place = Place(sizes)
    ext, own, core = place.ext, place.own, place.core
    count, nu = len(mats), len(units)
    blocks = ext["h"] * ext["l"] * ext["w"]
    f32 = jnp.float32
    it = iter(refs)
    take = lambda k: [next(it) for _ in range(k)]
    lefts, rights = take(n_left), take(n_right)
    vec = next(it)
    outs = take(count)
    vec_out, sq_out = take(2)
    land = take(nu)
    kinds, where = planned
    pool = [tuple(take(2)) if kind == "q" else take(1)[0] for _, kind in kinds]
    recv_q, recv_s = [], []
    for u in range(nu):
        k = len(messages(units[u][3], ext))
        recv_q.append(take(k))
        recv_s.append(take(k))
    plain = [pool[where["plain", x]] for x in range(n_left)]
    turned = [pool[where["turned", x]] for x in range(n_left)]
    n_axes, n_square = len(place.hops(False, False)), len(place.hops(True, True))
    vec_land, sq_land = take(n_axes), take(n_square)
    slab_land = next(it)
    (core_send, core_recv, stage_sem, g_sem, x_sem, q_send, q_recv, s_send, s_recv, v_send, v_recv, t_send, t_recv, n_send, n_recv) = take(15)
    left_copies = {}
    place.greet()
    small = SmallSum(place, vec_out, vec_land, v_send, v_recv, False, False)
    slab_flight = []
    for k in xors(ext["n"]):
        c = remote(vec.at[place.na ^ k], slab_land.at[place.na], n_send.at[k - 1], n_recv.at[k - 1], place.peer("n", k))
        c.start()
        slab_flight.append(c)
    slab_land[place.na] = vec[place.na]

    def slabs_here():
        for c in slab_flight:
            c.wait()
        total = slab_land[0]
        for j in range(1, ext["n"]):
            total = total + slab_land[j]
        vec_out[...] = total

    squares = SmallSum(place, sq_out, sq_land, t_send, t_recv, True, True)

    pending = []
    last_use = {}
    flight = {}
    sums = [jnp.zeros((1, 1), f32), jnp.zeros((1, 1), f32)]
    ready = set()

    def turn(k):
        if k in ready:
            return
        ready.add(k)
        left_copies[k].wait()
        t = plain[k][...].T
        a = turned[k].shape[2]
        if a % 16 == 0:
            turned[k][...] = t.reshape(turned[k].shape)
        else:
            for i in range(2 * blocks):
                turned[k][i // 2, i % 2] = t[i * a : (i + 1) * a]

    def product(u, n, which, ref_of):
        m, lo, hi, order = units[u]
        a, c = mats[m][0], hi - lo
        for j, (x, g, c_lo, c_hi, g_lo) in enumerate(terms_of(mats, m, lo, hi)):
            right = pool[where["g", u, j]][n]
            if a % 16 == 0:
                rows = turned[x][:, which].reshape(blocks * a, turned[x].shape[3])
                v = lax.dot_general(rows, right, (((1,), (0,)), ((), ())), preferred_element_type=f32)
                v = v.reshape(blocks, a, c_hi - c_lo)
                if j == 0:
                    ref_of[n] = v
                else:
                    ref_of[n, :, :, c_lo:c_hi] += v
            else:
                for b in range(blocks):
                    v = lax.dot_general(turned[x][b, which], right, (((1,), (0,)), ((), ())), preferred_element_type=f32)
                    if j == 0:
                        ref_of[n, b] = v
                    else:
                        ref_of[n, b, :, c_lo:c_hi] += v

    def whole(kind, u):
        m, lo, hi, order = units[u]
        ref = pool[where[kind, u]]
        a, c = mats[m][0], hi - lo
        return ref if ref.shape[2:] == (a, c) else ref.at[:, :, pl.ds(0, a), pl.ds(0, c)]

    def block_of(idx):
        return (idx["h"] * ext["l"] + idx["l"]) * ext["w"] + idx["w"]

    def slab(u, idx):
        at = 0
        for d in "nhlw":
            if d != phases_of(units[u][3], ext)[0]:
                at = at * ext[d] + idx[d]
        return pool[where["kept", u]].at[at]

    def split(s, dims):
        idx = {}
        for d in reversed(dims):
            if ext[d] == 1:
                idx[d] = 0
            else:
                idx[d] = s % ext[d]
                s = s // ext[d]
        return idx

    def loop(total, body):
        def step(s, carry):
            body(s)
            return carry
        lax.fori_loop(0, total, step, 0)

    def reuse(b):
        for c in last_use.pop(b, []):
            c.wait_send()

    def code_and_send(u, p):
        ph = phases_of(units[u][3], ext)
        d, peers, slabs = messages(units[u][3], ext)[p]
        gone = ph[:p]
        free = [x for x in "nhlw" if x != d and x not in gone]
        b = where["q", u, p]
        reuse(b)
        out_q, out_s = pool[b]
        sends = []
        for k in range(1, peers + 1):
            def body(s):
                idx = split(s, free)
                for x in gone:
                    idx[x] = own[x]
                idx[d] = own[d] ^ k
                x = (whole("acc", u).at[idx["n"], block_of(idx)] if p == 0 else slab(u, idx))[...]
                top = jnp.maximum(jnp.max(jnp.abs(x), axis=0, keepdims=True), FLOOR)
                out_q[k - 1, s] = jnp.round(x * (FULL_CODE / top)).astype(jnp.int32).astype(jnp.int16)
                out_s[k - 1, s] = top * (1.0 / FULL_CODE)
            loop(slabs, body)
            dev = place.peer(d, k)
            first = remote(out_q.at[k - 1], recv_q[u][p].at[k - 1], q_send.at[u, p, k - 1], q_recv.at[u, p, k - 1], dev)
            second = remote(out_s.at[k - 1], recv_s[u][p].at[k - 1], s_send.at[u, p, k - 1], s_recv.at[u, p, k - 1], dev)
            first.start()
            second.start()
            sends += [first, second]
        flight[u, p] = sends
        last_use[b] = sends

    def take_in(u, p):
        ph = phases_of(units[u][3], ext)
        d, peers, slabs = messages(units[u][3], ext)[p]
        gone = ph[: p + 1]
        free = [x for x in "nhlw" if x not in gone]
        for c in flight[u, p]:
            c.wait_recv()
        def body(s):
            idx = split(s, free)
            for x in gone:
                idx[x] = own[x]
            ref = slab(u, idx)
            v = ref[...]
            for k in range(peers):
                v = v + recv_q[u][p][k, s].astype(jnp.int32).astype(f32) * recv_s[u][p][k, s]
            ref[...] = v
        loop(slabs, body)

    def stage(u, p):
        m, lo, hi, order = units[u]
        n_ph = len(phases_of(order, ext))
        if p == 0:
            copies = []
            for j, (x, g, c_lo, c_hi, g_lo) in enumerate(terms_of(mats, m, lo, hi)):
                if x not in left_copies:
                    left_copies[x] = pltpu.make_async_copy(lefts[x], plain[x], x_sem.at[x])
                    left_copies[x].start()
                src = rights[g]
                if c_hi - c_lo != src.shape[2]:
                    src = src.at[:, :, slice(g_lo, g_lo + c_hi - c_lo)]
                c = pltpu.make_async_copy(src, pool[where["g", u, j]], g_sem.at[u, j])
                c.start()
                copies.append(c)
            flight[u, "g"] = copies
        elif p == 1:
            for c in flight[u, "g"]:
                c.wait()
            for x, *_ in terms_of(mats, m, lo, hi):
                turn(x)
            b = where["out", u]
            reuse(b)
            loop(ext["n"], lambda n: product(u, n, 1 - core, whole("out", u)))
            c = remote(whole("out", u), land[u], core_send.at[u], core_recv.at[u], place.peer("c", 1))
            c.start()
            flight[u, "core"] = c
            last_use[b] = [c]
        elif p == 2:
            flight[u, "core"].wait_recv()
            reuse(where["stage", u])
            c = pltpu.make_async_copy(land[u], whole("stage", u), stage_sem.at[u])
            c.start()
            flight[u, "stage"] = c
        elif p == 3:
            acc, more = whole("acc", u), whole("stage", u)
            reuse(where["acc", u])
            flight[u, "stage"].wait()
            def body(n):
                product(u, n, core, acc)
                acc[n] = acc[n] + more[n]
            loop(ext["n"], body)
            code_and_send(u, 0)
            d, peers, slabs = messages(order, ext)[0]
            def keep(i):
                idx = split(i, [x for x in "nhlw" if x != d])
                idx[d] = own[d]
                slab(u, idx)[...] = acc.at[idx["n"], block_of(idx)][...]
            loop(slabs, keep)
        else:
            take_in(u, p - 4)
            if p - 3 < n_ph:
                code_and_send(u, p - 3)
            else:
                x = slab(u, own)[...]
                outs[m][:, pl.ds(lo, hi - lo)] = x
                w = 0 if is_enc[m] else 1
                sums[w] = sums[w] + jnp.sum(x * x, keepdims=True)

    flat = [(u, p) for step in events for u, p in step if p <= len(phases_of(units[u][3], ext)) + 3]
    turns = [(i + 1) * len(flat) // (n_axes + 2) for i in range(n_axes + 1)]
    for i, (u, p) in enumerate(flat):
        stage(u, p)
        if i in turns:
            hop = turns.index(i)
            if hop:
                small.finish(hop - 1)
            else:
                slabs_here()
            if hop < n_axes:
                small.start(hop)
    row = lax.broadcasted_iota(jnp.int32, (8, 128), 0)
    share = 1.0 / (sizes[0] * sizes[1])
    enc_vec, dec_vec = vec_out[0:6, :], vec_out[6:13, :]
    sums[0] = sums[0] + share * jnp.sum(enc_vec * enc_vec, keepdims=True)
    sums[1] = sums[1] + share * jnp.sum(dec_vec * dec_vec, keepdims=True)
    loss = vec[0, 13:14, 0:1]
    sq_out[...] = jnp.where(row == 0, sums[0], jnp.where(row == 1, sums[1], jnp.where(row == 2, loss, 0.0)))
    for i in range(n_square):
        squares.start(i)
        squares.finish(i)
    for c in [c for cs in last_use.values() for c in cs]:
        c.wait_send()


def reduce_scatter(lefts, rights, mats, vec, sizes, units, events, is_enc, cid=1):
    ext = extents(sizes)
    blocks = ext["h"] * ext["l"] * ext["w"]
    f32, bf16 = jnp.float32, jnp.bfloat16
    tokens = [r.shape[1] for r in rights]
    planned = plan(units, events, mats, ext, tokens)
    coded = lambda k, n, a, c: [pltpu.VMEM((k, n, a, c), jnp.int16), pltpu.VMEM((k, n, 1, c), f32)]
    scratch = []
    for shape, kind in planned[0]:
        scratch += coded(*shape) if kind == "q" else [pltpu.VMEM(shape, f32 if kind == "f" else bf16)]
    for m, lo, hi, order in units:
        ms = [coded(k, n, mats[m][0], hi - lo) for d, k, n in messages(order, ext)]
        scratch += [x[0] for x in ms] + [x[1] for x in ms]
    scratch += SmallSum.scratch(sizes, vec.shape[1:], False, False) + SmallSum.scratch(sizes, (8, 128), True, True)
    scratch += [pltpu.VMEM(vec.shape, f32)]
    nu, kmax = len(units), max(ext.values())
    D_ = pltpu.SemaphoreType.DMA
    scratch += [D_((nu,))] * 3 + [D_((nu, 2)), D_((len(lefts),))] + [D_((nu, 4, kmax))] * 4 + SmallSum.sems(sizes) * 2 + [D_((kmax,))] * 2
    vm = pl.BlockSpec(memory_space=pltpu.VMEM)
    an = pl.BlockSpec(memory_space=pl.ANY)
    res = pl.pallas_call(
        functools.partial(reduce_kernel, sizes, units, events, mats, len(lefts), len(rights), planned, is_enc),
        out_shape=[jax.ShapeDtypeStruct(m[:2], f32) for m in mats]
        + [jax.ShapeDtypeStruct(vec.shape[1:], f32), jax.ShapeDtypeStruct((8, 128), f32)]
        + [jax.ShapeDtypeStruct((ext["n"], blocks, mats[m][0], hi - lo), f32) for m, lo, hi, o in units],
        in_specs=[an] * (len(lefts) + len(rights)) + [vm],
        out_specs=[vm] * (len(mats) + 2) + [an] * nu,
        scratch_shapes=scratch,
        compiler_params=pltpu.CompilerParams(collective_id=cid, has_side_effects=True, vmem_limit_bytes=60 << 20),
    )(*lefts, *rights, vec)
    return res[: len(mats)], res[len(mats)], res[len(mats) + 1]


class Gather:
    def __init__(self, place, units, events, shards, outs, sems):
        self.place, self.units, self.shards, self.outs = place, units, shards, outs
        self.send_sem, self.recv_sem, self.loc_sem = sems
        self.events = [(u, p) for step in events for u, p in step if p <= len(self.phases(u, units))]
        self.next = 0
        self.pending, self.from_sibling = [], []
        self.slots = [0] * len(units)
        self.flight, self.local = {}, {}
        self.complete = set()

    def phases(self, u, units=None):
        return [d for d in (units or self.units)[u][3] if self.place.ext[d] > 1]

    def region(self, u, full, at, which_core):
        m, lo, hi, order = self.units[u]
        own = self.place.own
        idx = [slice(None) if d in full else own[d] ^ at[1] if at and d == at[0] else own[d] for d in "nhlw"]
        if (lo, hi) == (0, self.shards[m].shape[1]):
            return self.outs[m].at[tuple(idx) + (which_core,)]
        return self.outs[m].at[tuple(idx) + (which_core, slice(None), slice(lo, hi))]

    def shard(self, u):
        m, lo, hi, order = self.units[u]
        return self.shards[m] if (lo, hi) == (0, self.shards[m].shape[1]) else self.shards[m].at[:, slice(lo, hi)]

    def send(self, u, src, dst, dev, landing):
        k = self.slots[u]
        self.slots[u] += 1
        c = remote(src, dst, self.send_sem.at[u, k], self.recv_sem.at[u, k], dev)
        c.start()
        self.pending.append(c)
        return remote(landing, landing, self.send_sem.at[u, k], self.recv_sem.at[u, k], dev)

    def stage(self, u, p):
        place, core = self.place, self.place.core
        m, ph = self.units[u][0], self.phases(u)
        sibling = place.peer("c", 1)
        came = self.flight.pop(u, [])
        if p == 0:
            c = pltpu.make_async_copy(self.shard(u), self.region(u, (), None, core), self.loc_sem.at[u])
            c.start()
            self.local[u] = c
            src = self.shard(u)
            self.from_sibling.append((m, self.send(u, src, self.region(u, (), None, core), sibling, self.region(u, (), None, 1 - core))))
        else:
            for k, w in came:
                w.wait_recv()
            if p == 1:
                self.local[u].wait()
            src = None
        if p < len(ph):
            mine = src if src is not None else self.region(u, ph[:p], None, core)
            self.flight[u] = [
                (k, self.send(u, mine, self.region(u, ph[:p], None, core), place.peer(ph[p], k), self.region(u, ph[:p], (ph[p], k), core)))
                for k in xors(place.ext[ph[p]])
            ]
        for k, _ in came:
            here = self.region(u, ph[: p - 1], (ph[p - 1], k), core)
            there = self.region(u, ph[: p - 1], (ph[p - 1], k), 1 - core)
            self.from_sibling.append((m, self.send(u, here, here, sibling, there)))

    def tick(self, steps):
        for u, p in self.events[self.next : self.next + steps]:
            self.stage(u, p)
        self.next += steps

    def need(self, m):
        if m in self.complete:
            return
        self.complete.add(m)
        last = max(i for i, (u, p) in enumerate(self.events) if self.units[u][0] == m)
        self.tick(max(0, last + 1 - self.next))
        for which, c in self.from_sibling:
            if which == m:
                c.wait_recv()

    def finish(self):
        for m in range(len(self.shards)):
            self.need(m)
        for c in self.pending:
            c.wait_send()


def cast_shards(masters, shards):
    embed, eqkv, eout, eup, edown, bridge, dqkv, dout, dup, ddown, head = masters
    low = jnp.bfloat16
    def by_kind(src, dst, size):
        heads = src.shape[1] // (3 * size)
        for t in range(3):
            for h in range(heads):
                to, at = (t * heads + h) * size, (h * 3 + t) * size
                dst[:, to : to + size] = src[:, at : at + size].astype(low)
    by_kind(eqkv, shards[0], DH)
    shards[0][:, eqkv.shape[1] :] = embed[...].astype(low)
    shards[1][...] = eout[...].T.astype(low)
    by_kind(dqkv, shards[5], DHD)
    for m, src in ((2, eup), (3, edown), (4, bridge), (6, dout), (7, dup), (8, ddown), (9, head)):
        shards[m][...] = src[...].astype(low)


def shard_shapes(masters):
    a, d = masters[0].shape[0], masters[6].shape[0]
    enc = (masters[0].shape[1] + masters[1].shape[1], masters[2].shape[0], *(m.shape[1] for m in masters[3:6]))
    return [(a, c) for c in enc] + [(d, m.shape[1]) for m in masters[6:]]


class Start:
    def __init__(self, sizes, masters, shards, vec, counts, vec_all, weight_sum, lands, sems):
        self.place = place = Place(sizes)
        vec_send, vec_recv, sum_send, sum_recv = sems
        cast_shards(masters, shards)
        total = jnp.float32(0.0)
        for i in range(counts.shape[0]):
            total = total + (NP - (1.0 - VISIBLE_WEIGHT) * counts[i].astype(jnp.float32))
        weight_sum[...] = jnp.zeros(weight_sum.shape, jnp.float32) + total
        place.greet()
        self.flight = []
        for k in xors(place.ext["n"]):
            c = remote(vec, vec_all.at[place.na], vec_send.at[k - 1], vec_recv.at[k - 1], place.peer("n", k))
            c.start()
            self.flight.append(c)
        vec_all[place.na] = vec[...]
        self.small = SmallSum(place, weight_sum, lands, sum_send, sum_recv, False, True)

    def sum_hops(self):
        return len(self.small.axes)

    def vectors_here(self):
        for c in self.flight:
            c.wait()

    @staticmethod
    def scratch(sizes, shapes):
        n = sizes[2]
        return (
            [pltpu.VMEM(s, jnp.bfloat16) for s in shapes]
            + SmallSum.scratch(sizes, (8, 128), False, True)
            + [pltpu.SemaphoreType.DMA((n,))] * 2
            + SmallSum.sems(sizes)
        )


def gather_sems(sizes, units):
    slots = 2 * sum(extents(sizes).values())
    DMA = pltpu.SemaphoreType.DMA
    return [DMA((len(units), slots)), DMA((len(units), slots)), DMA((len(units),))]


def gather_kernel(sizes, units, events, *refs):
    it = iter(refs)
    take = lambda k: [next(it) for _ in range(k)]
    masters = take(11)
    vec, counts = take(2)
    outs = take(10)
    vec_all, weight_sum = take(2)
    shards = take(10)
    lands = take(len(SmallSum.scratch(sizes, (8, 128), False, True)))
    small_sems, sems = take(4), take(3)
    start = Start(sizes, masters, shards, vec, counts, vec_all, weight_sum, lands, small_sems)
    g = Gather(start.place, units, events, shards, outs, sems)
    for i in range(start.sum_hops()):
        start.small.start(i)
        start.small.finish(i)
    g.finish()
    start.vectors_here()


def gather(masters, vec, counts, sizes, units, events, cid=0):
    ext = extents(sizes)
    an = pl.BlockSpec(memory_space=pl.ANY)
    vm = pl.BlockSpec(memory_space=pltpu.VMEM)
    sm = pl.BlockSpec(memory_space=pltpu.SMEM)
    shapes = shard_shapes(masters)
    heads = (ext["n"], ext["h"], ext["l"], ext["w"], 2)
    res = pl.pallas_call(
        functools.partial(gather_kernel, sizes, units, events),
        out_shape=[jax.ShapeDtypeStruct(heads + s, jnp.bfloat16) for s in shapes]
        + [jax.ShapeDtypeStruct((sizes[2],) + vec.shape, vec.dtype), jax.ShapeDtypeStruct((8, 128), jnp.float32)],
        in_specs=[vm] * 12 + [sm],
        out_specs=[an] * 10 + [vm, vm],
        scratch_shapes=Start.scratch(sizes, shapes) + gather_sems(sizes, units),
        compiler_params=pltpu.CompilerParams(collective_id=cid, has_side_effects=True),
    )(*masters, vec, counts)
    return res[:10], res[10], res[11]


GATHER_UNITS = (
    (0, 0, 256, "lhwn"), (0, 256, 512, "nlhw"), (0, 512, 768, "nhlw"), (1, 0, 256, "nlhw"), (2, 0, 384, "nhlw"),
    (2, 384, 768, "nlhw"), (3, 0, 384, "nlhw"), (3, 384, 768, "nhlw"), (4, 0, 128, "nhlw"), (5, 0, 384, "hlwn"),
    (6, 0, 128, "lnhw"), (7, 0, 256, "nhlw"), (7, 256, 512, "nlhw"), (8, 0, 256, "nlhw"), (8, 256, 512, "nhlw"),
    (9, 0, 256, "hnlw"),
)
GATHER_ORDER = (
    (8, 0), (3, 0), (2, 0), (1, 0), (0, 0), (7, 0), (8, 1), (0, 1), (5, 0), (4, 0), (3, 1), (8, 2), (6, 0), (0,
    2), (2, 1), (15, 0), (3, 2), (1, 1), (10, 0), (8, 3), (2, 2), (15, 1), (12, 0), (7, 1), (1, 2), (10, 1), (9,
    0), (13, 0), (3, 3), (5, 1), (14, 0), (2, 3), (7, 2), (4, 1), (11, 0), (5, 2), (6, 1), (1, 3), (9, 1), (4, 2),
    (7, 3), (6, 2), (0, 3), (9, 2), (5, 3), (15, 2), (12, 1), (10, 2), (4, 3), (13, 1), (6, 3), (14, 1), (15, 3),
    (10, 3), (11, 1), (12, 2), (14, 2), (13, 2), (11, 2), (14, 3), (12, 3), (11, 3), (13, 3), (9, 3),
)


def gather_plan(ext, shapes):
    cols = [s[1] for s in shapes]
    if ext["w"] > 1:
        units = [(m, 0, c, "nlhw") for m, c in enumerate(cols)]
        return units, [[(u, p)] for u in range(len(units)) for p in range(5)]
    units = [(m, lo, min(hi, cols[m]), order) for m, lo, hi, order in GATHER_UNITS]
    return units, [list(GATHER_ORDER[i : i + 12]) for i in range(0, len(GATHER_ORDER), 12)]


REDUCE_UNITS = (
    (0, 0, 256, "lnhw"), (0, 256, 512, "lhwn"), (0, 512, 768, "hlwn"), (1, 0, 256, "lhwn"), (2, 0, 256, "hlwn"),
    (2, 256, 512, "nhlw"), (2, 512, 768, "lhwn"), (3, 0, 256, "hnlw"), (3, 256, 512, "lhwn"), (3, 512, 768,
    "lhwn"), (4, 0, 128, "lnhw"), (5, 0, 256, "lhwn"), (5, 256, 384, "hlwn"), (6, 0, 128, "hnlw"), (7, 0, 256,
    "hnlw"), (7, 256, 512, "lhwn"), (8, 0, 256, "hlwn"), (8, 256, 512, "hlwn"), (9, 0, 256, "hlwn"),
)
REDUCE_ORDER = (
    (13, 0), (10, 0), (14, 0), (15, 0), (13, 1), (10, 1), (14, 1), (15, 1), (13, 2), (10, 2), (13, 3), (2, 0),
    (10, 3), (14, 2), (2, 1), (0, 0), (15, 2), (14, 3), (0, 1), (5, 0), (13, 4), (15, 3), (5, 1), (8, 0), (2, 2),
    (8, 1), (10, 4), (2, 3), (0, 2), (12, 0), (13, 5), (12, 1), (0, 3), (14, 4), (5, 2), (4, 0), (15, 4), (13, 6),
    (4, 1), (8, 2), (10, 5), (5, 3), (12, 2), (3, 0), (8, 3), (12, 3), (3, 1), (16, 0), (9, 0), (4, 2), (16, 1),
    (9, 1), (2, 4), (14, 5), (4, 3), (7, 0), (3, 2), (0, 4), (15, 5), (7, 1), (10, 6), (16, 2), (3, 3), (18, 0),
    (16, 3), (12, 4), (9, 2), (18, 1), (17, 0), (17, 1), (9, 3), (7, 2), (11, 0), (8, 4), (18, 2), (11, 1), (7,
    3), (1, 0), (17, 2), (18, 3), (6, 0), (1, 1), (4, 4), (2, 5), (17, 3), (14, 6), (11, 2), (6, 1), (5, 4), (11,
    3), (1, 2), (16, 4), (1, 3), (6, 2), (6, 3), (8, 5), (3, 4), (0, 5), (12, 5), (15, 6), (2, 6), (7, 4), (9, 4),
    (8, 6), (12, 6), (4, 5), (18, 4), (11, 4), (17, 4), (5, 5), (7, 5), (16, 5), (3, 5), (4, 6), (0, 6), (16, 6),
    (1, 4), (9, 5), (3, 6), (11, 5), (9, 6), (1, 5), (6, 4), (11, 6), (18, 5), (17, 5), (1, 6), (5, 6), (6, 5),
    (7, 6), (18, 6), (17, 6), (6, 6),
)


def reduce_plan(ext, mats):
    if ext["w"] > 1:
        units = [(m, lo, min(lo + 256, x[1]), "wlhn") for m, x in enumerate(mats) for lo in range(0, x[1], 256)]
        return units, [[(u, p)] for u in range(len(units)) for p in range(8)]
    return list(REDUCE_UNITS), [list(REDUCE_ORDER)]


def sincos_table(rows, width):
    column = np.arange(width)
    freq = np.power(np.float32(10000.0), (-(2 * (column // 2)).astype(np.float32) / np.float32(width)).astype(np.float32))
    angle = (np.arange(rows, dtype=np.float32)[:, None] * freq[None, :]).astype(np.float32)
    return np.where(column % 2 == 0, np.sin(angle), np.cos(angle)).astype(np.float32)


def dot_nn(a, b):
    return lax.dot_general(a, b, (((1,), (0,)), ((), ())), preferred_element_type=jnp.float32)


def dot_nt(a, b):
    return lax.dot_general(a, b, (((1,), (1,)), ((), ())), preferred_element_type=jnp.float32)


def dot_tn(a, b):
    return lax.dot_general(a, b, (((0,), (0,)), ((), ())), preferred_element_type=jnp.float32)


def dot_exact(a, b):
    return lax.dot_general(a, b, (((1,), (0,)), ((), ())), precision=HIGH, preferred_element_type=jnp.float32)


class Side:
    def __init__(self, width, head, heads, rows, images, slabs):
        self.width, self.head, self.heads, self.rows = width, head, heads, rows
        self.slabs = slabs
        self.tokens = rows * images
        self.lane = head * heads
        self.packed = -(-3 * self.lane // 128) * 128

    def scratch(self, hidden):
        t, n, w = self.tokens, self.slabs, self.width
        bf, f = jnp.bfloat16, jnp.float32
        return {
            "x": ((t, w), f),
            "hat1": ((t, w), f), "hat2": ((t, w), f), "hat3": ((t, w), f),
            "inv": ((t, 128), f),
            "n1": ((t, w), bf), "n2": ((t, w), bf), "n3": ((t, w), bf),
            "qkv": ((n, t, self.packed), bf),
            "lse": ((t // self.rows, -(-n * self.heads // 8) * 8, self.rows), f),
            "att": ((n, t, -(-self.lane // 128) * 128), bf),
            "slope": ((n, t, hidden), f),
            "act": ((n, t, hidden), bf),
            "dn": ((t, w), f),
            "og1": ((t, w), bf),
            "og2": ((t, w), bf),
        }


LEFTS = ("e_n1", "chosen", "e_og1", "e_n2", "e_og2", "e_n3", "d_n1", "d_og1", "d_n2", "d_og2", "d_n3")
RIGHTS = ("e_qkv", "part0", "e_att", "e_dh", "e_act", "part4", "d_qkv", "d_att", "d_dh", "d_act", "part9")
SHIPPED = LEFTS + RIGHTS
BUFFER_OF = {"e_dh": "e_act", "d_dh": "d_act"}


def compute_kernel(sizes, merged, per, slabs, names, units, events, *refs):
    it = iter(refs)
    take = lambda k: [next(it) for _ in range(k)]
    f32, bf16 = jnp.float32, jnp.bfloat16
    count = 10
    sources = take(11 if merged else 10)
    vec_parts, weight_in = (take(1)[0], None) if merged else take(2)
    patches_all, vis_all, keep_all, table_e, table_d, counts_all = take(6)
    shipped = take(len(SHIPPED))
    vec_out, weight_out = take(2)
    store = take(count)
    load_sem, store_sem = take(2)
    if merged:
        vec_all = take(1)[0]
        shards = take(count)
        lands = take(len(SmallSum.scratch(sizes, (8, 128), False, True)))
        small_sems, sems = take(4), take(3)
    buf = dict(zip(names, it))

    all_images = counts_all.shape[0]
    first_image = lax.axis_index("narrow") * per
    start_image = jnp.minimum(first_image, all_images - per)
    patch_copies = []
    for i in range(per):
        c = pltpu.make_async_copy(patches_all.at[start_image + i], buf["raw"].at[i], load_sem.at[count + i])
        c.start()
        patch_copies.append(c)

    ticks = [0]
    if merged:
        begin = Start(sizes, sources, shards, vec_parts, counts_all, vec_all, weight_out, lands, small_sems)
        g = Gather(begin.place, units, events, shards, store, sems)
        g.tick(12)
        for i in range(begin.sum_hops()):
            begin.small.start(i)
            g.tick(12)
            begin.small.finish(i)
        begin.vectors_here()
        need = g.need
    else:
        vec_all = vec_parts
        weight_out[...] = weight_in[...]
        loads = []
        for m in range(count):
            c = pltpu.make_async_copy(sources[m], store[m], load_sem.at[m])
            c.start()
            loads.append(c)
        waited = set()

        def need(m):
            if m not in waited:
                waited.add(m)
                loads[m].wait()

    def tick():
        if merged:
            g.tick(TICK)

    class Weight:
        def __init__(self, ref):
            self.ref = ref
            self.shape = (slabs, math.prod(ref.shape[1:-1]), ref.shape[-1])

        def __getitem__(self, at):
            n, lo, hi = at if isinstance(at, tuple) else (at, 0, self.shape[2])
            v = self.ref[n] if (lo, hi) == (0, self.shape[2]) else self.ref.at[..., lo:hi][n]
            return v.reshape(self.shape[1], hi - lo)

    w_eq, w_out, w_up, w_down, w_bridge, w_dqkv, w_dout, w_dup, w_ddown, w_head = [Weight(r) for r in store]
    enc_w, dec_w = table_e.shape[1], table_d.shape[1]
    dec_rows, enc_rows = table_e.shape[0], -(-KEEP_MOST // 16) * 16
    patches, loss_w, vis_rows = buf["patches"], buf["loss_w"], []
    patches[...] = jnp.zeros_like(patches)
    loss_w[...] = jnp.zeros_like(loss_w)
    counts = []
    for i in range(per):
        patch_copies[i].wait()
        patches[i, 0:NP, :] = buf["raw"][i]
        vis_rows.append(vis_all[pl.ds(start_image + i, 1), :])
        counts.append(counts_all[start_image + i])
        live = jnp.where(start_image + i >= first_image, 1.0, 0.0)
        row = jnp.where(keep_all[pl.ds(start_image + i, 1), :] == 1, VISIBLE_WEIGHT, 1.0) * live
        loss_w[i, 0:NP, :] = jnp.broadcast_to(row, (8, NP)).T[:, 0:1]
    enc = Side(enc_w, DH, w_out.shape[2] // DH, enc_rows, per, slabs)
    dec = Side(dec_w, DHD, w_dout.shape[2] // DHD, dec_rows, per, slabs)
    for s, tag in ((enc, "e_"), (dec, "d_")):
        s.tag = tag
        s.b = {k[2:]: v for k, v in buf.items() if k.startswith(tag)}
    enc.w, dec.w = (w_eq, w_out, w_up, w_down), (w_dqkv, w_dout, w_dup, w_ddown)
    enc.ids, dec.ids = (0, 1, 2, 3), (5, 6, 7, 8)
    enc.base, dec.base = 0, 7
    vec_full = buf["vec_full"]
    enc_c, dec_c = enc_w // slabs, dec_w // slabs
    at = 0
    for k in range(13):
        width = enc_c if k < 6 else dec_c
        for n in range(slabs):
            vec_full[k : k + 1, n * width : (n + 1) * width] = vec_all[n, :, at : at + width]
        at += width
    vec_grad = buf["vec_grad"]
    vec_grad[...] = jnp.zeros_like(vec_grad)

    def vector(k, width):
        return vec_full[k : k + 1, 0:width]

    CH = 32

    def chunks(total, body):
        def step(i, carry):
            body(pl.ds(pl.multiple_of(i * CH, CH), CH))
            return carry
        lax.fori_loop(0, total // CH, step, 0)

    def norm_fwd(s, k, out, hat, inv):
        gain, bias = vector(s.base + k, s.width), vector(s.base + k + 1, s.width)
        x = s.b["x"]
        def body(r):
            v = x[r, :]
            mean = jnp.mean(v, axis=1, keepdims=True)
            d = v - mean
            i = lax.rsqrt(jnp.mean(d * d, axis=1, keepdims=True) + EPS_NORM)
            h = d * i
            s.b[hat][r, :] = h
            s.b["inv"][r, inv : inv + 1] = i
            s.b[out][r, :] = (h * gain + bias).astype(bf16)
        chunks(s.tokens, body)

    def norm_bwd(s, k, hat, inv, add):
        gain = vector(s.base + k, s.width)
        def body(r):
            dn = s.b["dn"][r, :]
            h = s.b[hat][r, :]
            vec_grad[s.base + k : s.base + k + 1, 0 : s.width] += jnp.sum(dn * h, axis=0, keepdims=True)
            vec_grad[s.base + k + 1 : s.base + k + 2, 0 : s.width] += jnp.sum(dn, axis=0, keepdims=True)
            g = dn * gain
            d = s.b["inv"][r, inv : inv + 1] * (
                g - jnp.mean(g, axis=1, keepdims=True) - h * jnp.mean(g * h, axis=1, keepdims=True)
            )
            s.b["x"][r, :] = s.b["x"][r, :] + d if add else d
        chunks(s.tokens, body)

    def slab_loop(body):
        def step(n, carry):
            body(n)
            return carry
        lax.fori_loop(0, slabs, step, 0)

    def head_mask(s, h):
        lane = lax.broadcasted_iota(jnp.int32, (1, s.lane), 1)
        return (lane >= h * s.head) & (lane < (h + 1) * s.head)

    def scores(s, q, k, mask, limit):
        v = dot_nt(k, jnp.where(mask, q, jnp.zeros_like(q))) * (s.head ** -0.5)
        key = lax.broadcasted_iota(jnp.int32, (s.rows, s.rows), 0)
        return jnp.where(key < limit, v, -1e30)

    def attention_loop(body, between=None):
        def step(i, carry):
            body(i // slabs, i % slabs)
            return carry
        if between is None or not merged:
            lax.fori_loop(0, per * slabs, step, 0)
            return
        for image in range(per):
            lax.fori_loop(image * slabs, (image + 1) * slabs, step, 0)
            between()

    def image_rows(s, image):
        return pl.ds(pl.multiple_of(image * s.rows, 16), s.rows)

    def block_fwd(s, limit):
        b = s.b
        if b["att"].shape[2] != s.lane:
            b["att"][...] = jnp.zeros_like(b["att"])
        qkv_w, out_w, up_w, down_w = s.w
        need(s.ids[0])
        norm_fwd(s, 0, "n1", "hat1", 1)
        tick()
        def qkv(n):
            b["qkv"][n] = dot_nn(b["n1"][...], qkv_w[n, 0, s.packed]).astype(bf16)
        slab_loop(qkv)
        tick()
        def attend(image, n):
            r = image_rows(s, image)
            q = b["qkv"][n, r, 0 : s.lane]
            k = b["qkv"][n, r, s.lane : 2 * s.lane]
            v = b["qkv"][n, r, 2 * s.lane : 3 * s.lane]
            v_t = v.T
            parts = []
            for h in range(s.heads):
                sc = scores(s, q, k, head_mask(s, h), limit(image))
                top = jnp.max(sc, axis=0, keepdims=True)
                e = jnp.exp(sc - top)
                z = jnp.sum(e, axis=0, keepdims=True)
                p = (e * (1.0 / z)).astype(bf16)
                parts.append(dot_nn(v_t[h * s.head : (h + 1) * s.head], p))
                b["lse"][image, pl.ds(n * s.heads + h, 1), :] = top + jnp.log(z)
            b["att"][n, r, 0 : s.lane] = jnp.concatenate(parts, axis=0).astype(bf16).T
        attention_loop(attend, tick)
        need(s.ids[1])
        ship(s.tag + "att")
        def project(n):
            b["x"][...] += dot_nt(b["att"][n, :, 0 : s.lane], out_w[n])
        slab_loop(project)
        norm_fwd(s, 2, "n2", "hat2", 2)
        need(s.ids[2])
        need(s.ids[3])
        hid = buf["hid"]
        c = up_w.shape[2]
        def mlp(n):
            hid[0 : s.tokens, 0:c] = dot_nn(b["n2"][...], up_w[n])
            def body(r):
                v = hid[r, 0:c]
                cdf = 0.5 * (1.0 + lax.erf(v * 0.7071067811865476))
                b["act"][n, r, :] = (v * cdf).astype(bf16)
                b["slope"][n, r, :] = cdf + v * (0.3989422804014327 * jnp.exp(-0.5 * v * v))
            chunks(s.tokens, body)
            b["x"][...] += dot_nt(b["act"][n], down_w[n])
        if merged and s is enc:
            for n in range(slabs):
                mlp(n)
                tick()
        else:
            slab_loop(mlp)
        ship(s.tag + "act")
        norm_fwd(s, 4, "n3", "hat3", 3)
        for name in ("n1", "n2", "n3"):
            ship(s.tag + name)

    on_way = {}

    def ship(name):
        at = SHIPPED.index(name)
        c = pltpu.make_async_copy(buf[BUFFER_OF.get(name, name)], shipped[at], store_sem.at[at])
        c.start()
        on_way[name] = c

    def arrived(name):
        on_way.pop(name).wait()

    def block_bwd(s, limit):
        b = s.b
        qkv_w, out_w, up_w, down_w = s.w
        b["og2"][...] = b["x"][...].astype(bf16)
        ship(s.tag + "og2")
        b["dn"][...] = jnp.zeros_like(b["dn"])
        arrived(s.tag + "act")
        def down(n):
            b["act"][n] = (dot_nn(b["og2"][...], down_w[n]) * b["slope"][n]).astype(bf16)
            b["dn"][...] += dot_nt(b["act"][n], up_w[n])
        slab_loop(down)
        ship(s.tag + "dh")
        norm_bwd(s, 2, "hat2", 2, True)
        b["og1"][...] = b["x"][...].astype(bf16)
        ship(s.tag + "og1")
        arrived(s.tag + "att")
        def proj(n):
            b["att"][n, :, 0 : s.lane] = dot_nn(b["og1"][...], out_w[n]).astype(bf16)
        slab_loop(proj)
        def attend(image, n):
            r = image_rows(s, image)
            q = b["qkv"][n, r, 0 : s.lane]
            k = b["qkv"][n, r, s.lane : 2 * s.lane]
            v = b["qkv"][n, r, 2 * s.lane : 3 * s.lane]
            g = b["att"][n, r, 0 : s.lane]
            k_t = k.T
            parts = []
            dk = jnp.zeros((s.rows, s.lane), f32)
            dv = dk
            for h in range(s.heads):
                mask = head_mask(s, h)
                p = jnp.exp(scores(s, q, k, mask, limit(image)) - b["lse"][image, pl.ds(n * s.heads + h, 1), :])
                dp = dot_nt(v, jnp.where(mask, g, jnp.zeros_like(g)))
                dv = jnp.where(mask, dot_nn(p.astype(bf16), g), dv)
                ds = (p * (dp - jnp.sum(dp * p, axis=0, keepdims=True))).astype(bf16)
                dk = jnp.where(mask, dot_nn(ds, q), dk)
                parts.append(dot_nn(k_t[h * s.head : (h + 1) * s.head], ds))
            dq = jnp.concatenate(parts, axis=0).T
            scale = s.head ** -0.5
            if s.packed != 3 * s.lane:
                b["qkv"][n, r, 2 * s.lane : s.packed] = jnp.zeros((s.rows, s.packed - 2 * s.lane), bf16)
            b["qkv"][n, r, 0 : s.lane] = (dq * scale).astype(bf16)
            b["qkv"][n, r, s.lane : 2 * s.lane] = (dk * scale).astype(bf16)
            b["qkv"][n, r, 2 * s.lane : 3 * s.lane] = dv.astype(bf16)
        attention_loop(attend)
        ship(s.tag + "qkv")
        b["dn"][...] = jnp.zeros_like(b["dn"])
        def qkv(n):
            b["dn"][...] += dot_nt(b["qkv"][n], qkv_w[n, 0, s.packed])
        slab_loop(qkv)
        norm_bwd(s, 0, "hat1", 1, True)

    chosen = buf["chosen"]
    slots = KEEP_MOST
    chosen[...] = jnp.zeros_like(chosen)
    enc.b["x"][...] = jnp.zeros_like(enc.b["x"])
    for i in range(per):
        r = pl.ds(i * enc_rows, slots)
        patch = lax.broadcasted_iota(jnp.int32, (dec_rows, slots), 0)
        one = (patch == vis_rows[i]).astype(f32).T
        chosen[r, :] = dot_nn(one.astype(bf16), patches[i]).astype(bf16)
        enc.b["x"][r, :] = dot_exact(one, table_e[...])
    need(0)
    for n in range(slabs):
        lead = w_eq.shape[2] - 256
        part = dot_nn(chosen[...], w_eq[n, lead, lead + 256])
        enc.b["x"][:, n * enc_c : (n + 1) * enc_c] += part[:, 256 - enc_c : 256]
    ship("chosen")
    block_fwd(enc, lambda image: counts_all[start_image + image])
    need(4)
    bridged = buf["hid"]
    for n in range(slabs):
        bridged[0 : enc.tokens, n * dec_c : (n + 1) * dec_c] = dot_nn(enc.b["n3"][...], w_bridge[n])

    def hits(i, turned_way):
        patch = lax.broadcasted_iota(jnp.int32, (dec_rows, slots), 0)
        slot = lax.broadcasted_iota(jnp.int32, (dec_rows, slots), 1)
        hit = ((patch == vis_rows[i]) & (slot < counts[i])).astype(f32)
        return hit if turned_way else hit.T

    for i in range(per):
        r = pl.ds(i * dec_rows, dec_rows)
        hit = hits(i, True)
        placed = dot_exact(hit, bridged[pl.ds(i * enc_rows, slots), 0:dec_w])
        seen = jnp.sum(hit, axis=1, keepdims=True) > 0
        dec.b["x"][r, :] = jnp.where(seen, placed, vector(6, dec_w)) + table_d[...]
    block_fwd(dec, lambda image: NP)
    need(9)
    pred = buf["hid"]
    pix_c = w_head.shape[2]
    pix = patches.shape[2]
    for n in range(slabs):
        pred[0 : dec.tokens, n * pix_c : (n + 1) * pix_c] = dot_nn(dec.b["n3"][...], w_head[n])

    pgrad = buf["pgrad"]
    divisor = weight_out[0:1, 0:1]
    loss = jnp.zeros((1, 1), f32)
    LC = 16
    for i in range(per):
        def lossy(j, total):
            r = pl.ds(pl.multiple_of(j * LC, LC), LC)
            px = patches[i, r, :].astype(f32)
            d = px - jnp.mean(px, axis=1, keepdims=True)
            target = d * lax.rsqrt(jnp.mean(d * d, axis=1, keepdims=True) + EPS_NORM)
            rr = pl.ds(pl.multiple_of(i * dec_rows + j * LC, LC), LC)
            error = pred[rr, 0:pix] - target
            weight = loss_w[i, r, :]
            pgrad[rr, :] = (2.0 * weight * error / divisor).astype(bf16)
            return total + jnp.sum(weight * error * error, keepdims=True)
        loss = lax.fori_loop(0, dec_rows // LC, lossy, loss)
    part9 = buf["part9"]
    part9[...] = jnp.zeros_like(part9)
    for n in range(slabs):
        part9[n, :, 0:pix_c] = pgrad[:, n * pix_c : (n + 1) * pix_c]
    dec.b["dn"][...] = jnp.zeros_like(dec.b["dn"])
    ship("part9")
    def head_bwd(n):
        dec.b["dn"][...] += dot_nt(part9[n, :, 0:pix_c], w_head[n])
    slab_loop(head_bwd)
    norm_bwd(dec, 4, "hat3", 3, False)
    block_bwd(dec, lambda image: NP)
    part4 = buf["part4"]
    part4[...] = jnp.zeros_like(part4)
    for i in range(per):
        r = pl.ds(i * dec_rows, dec_rows)
        seen = jnp.sum(hits(i, True), axis=1, keepdims=True) > 0
        grad = dec.b["x"][r, :]
        vec_grad[6:7, 0:dec_w] += jnp.sum(jnp.where(seen, 0.0, grad), axis=0, keepdims=True)
        back = dot_exact(hits(i, False), grad).astype(bf16)
        for n in range(slabs):
            part4[n, pl.ds(i * enc_rows, slots), :] = back[:, n * dec_c : (n + 1) * dec_c]
    ship("part4")
    enc.b["dn"][...] = jnp.zeros_like(enc.b["dn"])
    def bridge_bwd(n):
        enc.b["dn"][...] += dot_nt(part4[n], w_bridge[n])
    slab_loop(bridge_bwd)
    norm_bwd(enc, 4, "hat3", 3, False)
    block_bwd(enc, lambda image: counts_all[start_image + image])

    part0 = buf["part0"]
    part0[...] = jnp.zeros_like(part0)
    for n in range(slabs):
        part0[n, :, 256 - enc_c : 256] = enc.b["x"][:, n * enc_c : (n + 1) * enc_c].astype(bf16)
    ship("part0")
    vec_out[...] = jnp.zeros_like(vec_out)
    for n in range(slabs):
        vec_out[n, 0:6, :] = vec_grad[0:6, n * enc_c : (n + 1) * enc_c]
        vec_out[n, 6:13, 0:dec_c] = vec_grad[6:13, n * dec_c : (n + 1) * dec_c]
        vec_out[n, 13:14, :] = jnp.zeros((1, enc_c), f32) + loss
    for name in list(on_way):
        arrived(name)
    if merged:
        g.finish()


TICK = 3
MERGED = True


def compute(sources, shapes, vec_parts, weight_sum, patches, vis_index, keep_mask, counts, sizes, units, events, merged):
    slabs = sizes[2]
    ext = extents(sizes)
    heads = (slabs, ext["h"], ext["l"], ext["w"], 2)
    owners = math.prod(heads[1:])
    weights = [jax.ShapeDtypeStruct((slabs, owners * a, c), jnp.bfloat16) for a, c in shapes]
    per, pix = -(-counts.shape[0] // slabs), patches.shape[2]
    dec_rows, enc_rows = -(-NP // 16) * 16, -(-KEEP_MOST // 16) * 16
    enc_w, dec_w = weights[0].shape[1], weights[5].shape[1]
    enc = Side(enc_w, DH, weights[1].shape[2] // DH, enc_rows, per, slabs)
    dec = Side(dec_w, DHD, weights[6].shape[2] // DHD, dec_rows, per, slabs)
    named = {}
    for s, tag, up in ((enc, "e_", weights[2]), (dec, "d_", weights[7])):
        for k, v in s.scratch(up.shape[2]).items():
            named[tag + k] = v
    f32, bf16 = jnp.float32, jnp.bfloat16
    top = max(enc.tokens, dec.tokens)
    named["hid"] = ((top, max(pix, weights[2].shape[2], weights[7].shape[2])), f32)
    named["vec_full"] = ((16, enc_w), f32)
    named["chosen"] = ((enc.tokens, pix), bf16)
    named["pgrad"] = ((dec.tokens, pix), bf16)
    up128 = lambda c: -(-c // 128) * 128
    named["part9"] = ((slabs, dec.tokens, up128(weights[9].shape[2])), bf16)
    named["part4"] = ((slabs, enc.tokens, weights[4].shape[2]), bf16)
    named["part0"] = ((slabs, enc.tokens, 256), bf16)
    named["vec_grad"] = ((16, enc_w), f32)
    named["raw"] = ((per, NP, pix), bf16)
    named["patches"] = ((per, dec_rows, pix), bf16)
    named["loss_w"] = ((per, dec_rows, 1), f32)
    ship_shapes = [jax.ShapeDtypeStruct(named[BUFFER_OF.get(k, k)][0], bf16) for k in SHIPPED]
    an = pl.BlockSpec(memory_space=pl.ANY)
    vm = pl.BlockSpec(memory_space=pltpu.VMEM)
    sm = pl.BlockSpec(memory_space=pltpu.SMEM)
    DMA = pltpu.SemaphoreType.DMA
    table_e = jnp.asarray(np.pad(sincos_table(NP, enc_w), ((0, dec_rows - NP), (0, 0))))
    table_d = jnp.asarray(np.pad(sincos_table(NP, dec_w), ((0, dec_rows - NP), (0, 0))))
    store = [pltpu.VMEM(heads + s if merged else w.shape, bf16) for s, w in zip(shapes, weights)]
    scratch = store + [DMA((10 + per,)), DMA((len(SHIPPED),))]
    small = [vec_parts] if merged else [vec_parts, weight_sum]
    if merged:
        scratch += [pltpu.VMEM((slabs,) + vec_parts.shape, f32)] + Start.scratch(sizes, shapes) + gather_sems(sizes, units)
    params = dict(vmem_limit_bytes=61 << 20)
    if merged:
        params.update(collective_id=0, has_side_effects=True)
    res = pl.pallas_call(
        functools.partial(compute_kernel, sizes, merged, per, slabs, list(named), units, events),
        out_shape=ship_shapes + [jax.ShapeDtypeStruct((slabs, 16, enc_w // slabs), f32), jax.ShapeDtypeStruct((8, 128), f32)],
        in_specs=[vm if merged else an] * len(sources) + [vm] * len(small) + [an] + [vm] * 4 + [sm],
        out_specs=[an] * len(SHIPPED) + [vm, vm],
        scratch_shapes=scratch + [pltpu.VMEM(s, d) for s, d in named.values()],
        compiler_params=pltpu.CompilerParams(**params),
    )(*sources, *small, patches, vis_index, keep_mask, table_e, table_d, counts)
    return res[: len(SHIPPED)], res[len(SHIPPED)], res[len(SHIPPED) + 1]


def split_low(x):
    high = x.astype(jnp.bfloat16)
    return high, (x - high.astype(jnp.float32)).astype(jnp.bfloat16)


def dot_three(a, b, kind=dot_nn):
    (ah, al), (bh, bl) = a, b
    return kind(ah, bh) + (kind(ah, bl) + kind(al, bh))


def roots(mats):
    side = mats[0].shape[0]
    eye = lax.broadcasted_iota(jnp.int32, (side, side), 0) == lax.broadcasted_iota(jnp.int32, (side, side), 1)
    five = jnp.where(eye, 5.0, 0.0)
    size = [jnp.sqrt(jnp.sum(m * m, keepdims=True)) for m in mats]
    current = [m * (1.0 / s) for m, s in zip(mats, size)]
    result = None
    for step in range(NEWTON):
        factor = [split_low((five - c) * 0.25) for c in current]
        if result is None:
            result = [(five - c) * 0.25 for c in current]
        else:
            result = [dot_three(split_low(r), f) for r, f in zip(result, factor)]
        if step + 1 < NEWTON:
            square = [split_low(dot_three(f, f)) for f in factor]
            fourth = [split_low(dot_three(q, q)) for q in square]
            current = [dot_three(q, split_low(c)) for q, c in zip(fourth, current)]
    return [r * lax.rsqrt(jnp.sqrt(s)) for r, s in zip(result, size)]


GROUPS = (41, 27)


def optimizer_kernel(pieces, upright, sides, enc_cols, dec_cols, *refs):
    it = iter(refs)
    take = lambda k: [next(it) for _ in range(k)]
    n_mats = len(pieces)
    owned = take(max(p[0] for blocks in pieces for parts in blocks for p in parts) + 1)
    masters = take(n_mats)
    stats = take(4)
    squares, vec_sum, weight_sum, vectors, first, second, step_count = take(7)
    new = take(n_mats)
    new_stats = take(4)
    new_vectors, new_first, new_second, norms, loss_out, weight_out = take(6)
    g_enc, g_dec, u_enc, u_dec = take(4)
    old = take(4)
    fresh = take(4)
    in_sem, out_sem = take(2)
    f32 = jnp.float32
    loads = []
    for i in (2, 3, 0, 1):
        c = pltpu.make_async_copy(stats[i], old[i], in_sem.at[i])
        c.start()
        loads.append((i, c))
    loads = dict(loads)

    enc_sq, dec_sq = squares[0:1, 0:1], squares[1:2, 0:1]
    norms[0] = jnp.sqrt(enc_sq)[0, 0]
    norms[1] = jnp.sqrt(dec_sq)[0, 0]
    loss_out[0] = squares[2:3, 0:1][0, 0]
    weight_out[0] = weight_sum[0:1, 0:1][0, 0]
    clip = jnp.minimum(1.0, CLIP_NORM / jnp.sqrt(enc_sq + dec_sq))

    sections = ((1, g_dec, u_dec, 2, LR_MATRIX), (0, g_enc, u_enc, 0, LR_MATRIX * LAYER_DECAY))
    for which, grad, update, base, rate in sections:
        at = 0
        for i in range(n_mats):
            if sides[i] != which:
                continue
            for parts in pieces[i]:
                col = 0
                for src, lo, width in parts:
                    grad[at, :, col : col + width] = owned[src][:, lo : lo + width] * clip
                    col += width
                at += 1
        total = at
        loads[base].wait()
        loads[base + 1].wait()
        group = min(GROUPS[which], total)
        def body(i, carry):
            start = jnp.minimum(i * group, total - group)
            g = [grad[start + j] for j in range(group)]
            low = [split_low(x) for x in g]
            turned = [split_low(x.T) for x in g]
            small = [STAT_DECAY * old[base][start + j] + (1.0 - STAT_DECAY) * dot_three(low[j], low[j], dot_nt) for j in range(group)]
            large = [STAT_DECAY * old[base + 1][start + j] + (1.0 - STAT_DECAY) * dot_three(turned[j], turned[j], dot_nt) for j in range(group)]
            for j in range(group):
                fresh[base][start + j] = small[j]
                fresh[base + 1][start + j] = large[j]
            left = roots(small)
            right = roots(large)
            for j in range(group):
                half = dot_three(split_low(left[j]), low[j])
                update[start + j] = rate * dot_three(split_low(half), split_low(right[j]))
            return carry
        lax.fori_loop(0, -(-total // group), body, 0)
        for k in (base, base + 1):
            pltpu.make_async_copy(fresh[k], new_stats[k], out_sem.at[k]).start()
        at = 0
        for i in range(n_mats):
            if sides[i] != which:
                continue
            for k in range(len(pieces[i])):
                lo = k * BLOCK
                if upright[i]:
                    new[i][:, lo : lo + BLOCK] = masters[i][:, lo : lo + BLOCK] - update[at]
                else:
                    new[i][lo : lo + BLOCK, :] = masters[i][lo : lo + BLOCK, :] - update[at].T
                at += 1

    steps = jnp.full((1, 128), step_count[0], jnp.int32).astype(f32)[0:1, 0:1]
    scale_one = 1.0 / (1.0 - jnp.exp(steps * math.log(BETA_FIRST)))
    scale_two = 1.0 / (1.0 - jnp.exp(steps * math.log(BETA_SECOND)))
    at = 0
    for k in range(13):
        width = enc_cols if k < 6 else dec_cols
        rate = LR_VECTOR * LAYER_DECAY if k < 6 else LR_VECTOR
        g = vec_sum[k : k + 1, 0:width] * clip
        cols = slice(at, at + width)
        one = BETA_FIRST * first[:, cols] + (1.0 - BETA_FIRST) * g
        two = BETA_SECOND * second[:, cols] + (1.0 - BETA_SECOND) * g * g
        new_first[:, cols] = one
        new_second[:, cols] = two
        new_vectors[:, cols] = vectors[:, cols] - rate * (one * scale_one) / (jnp.sqrt(two * scale_two) + EPS_ADAM)
        at += width
    for k in range(4):
        pltpu.make_async_copy(fresh[k], new_stats[k], out_sem.at[k]).wait()


def optimizer(owned, masters, stats, squares, vec_sum, weight_sum, vectors, first, second, step_count, enc_cols, dec_cols):
    kinds = ENC_KINDS + DEC_KINDS
    sides = (0,) * len(ENC_KINDS) + (1,) * len(DEC_KINDS)
    width = [m.shape[1] if kind else m.shape[0] for m, kind in zip(masters, kinds)]
    def plain(src, first_col, cols):
        return [[(src, first_col + k * BLOCK, BLOCK)] for k in range(cols // BLOCK)]
    def by_head(src, cols, head):
        heads = cols // (3 * head)
        per = BLOCK // head
        order = [(t * heads + h) * head for h in range(heads) for t in range(3)]
        return [[(src, order[k * per + j], head) for j in range(per)] for k in range(cols // BLOCK)]
    pieces = [
        plain(0, width[1], width[0]), by_head(0, width[1], DH), plain(1, 0, width[2]), plain(2, 0, width[3]),
        plain(3, 0, width[4]), plain(4, 0, width[5]), by_head(5, width[6], DHD), plain(6, 0, width[7]),
        plain(7, 0, width[8]), plain(8, 0, width[9]), plain(9, 0, width[10]),
    ]
    flat = [s.reshape(s.shape[2:]) for s in stats]
    upright = [kind or i != 2 for i, kind in enumerate(kinds)]
    masters = [m if kind or not up else m.T for m, kind, up in zip(masters, kinds, upright)]
    f32 = jnp.float32
    like = lambda x: jax.ShapeDtypeStruct(x.shape, f32)
    an = pl.BlockSpec(memory_space=pl.ANY)
    vm = pl.BlockSpec(memory_space=pltpu.VMEM)
    sm = pl.BlockSpec(memory_space=pltpu.SMEM)
    block = [pltpu.VMEM((flat[i].shape[0], flat[i].shape[1], BLOCK), f32) for i in (0, 2)]
    whole = [pltpu.VMEM(s.shape, f32) for s in flat]
    DMA = pltpu.SemaphoreType.DMA
    n = len(masters)
    res = pl.pallas_call(
        functools.partial(optimizer_kernel, pieces, upright, sides, enc_cols, dec_cols),
        out_shape=[like(m) for m in masters] + [like(s) for s in flat]
        + [like(vectors)] * 3 + [jax.ShapeDtypeStruct((k,), f32) for k in (2, 1, 1)],
        in_specs=[vm] * (len(owned) + n) + [an] * 4 + [vm] * 6 + [sm],
        out_specs=[vm] * n + [an] * 4 + [vm] * 3 + [sm] * 3,
        scratch_shapes=block + block + whole + whole + [DMA((4,)), DMA((4,))],
        compiler_params=pltpu.CompilerParams(vmem_limit_bytes=56 << 20),
    )(*owned, *masters, *flat, squares, vec_sum, weight_sum, vectors, first, second, step_count)
    new_stats = [r.reshape(s.shape) for r, s in zip(res[n : n + 4], stats)]
    new = [r if kind or not up else r.T for r, kind, up in zip(res[:n], kinds, upright)]
    return new, new_stats, res[n + 4 : n + 7], res[n + 7], res[n + 8].reshape(()), res[n + 9].reshape(())


def per_device(
    sizes,
    patches, vis_index, keep_mask, counts, step_count,
    w_embed, enc_qkv, enc_out, enc_up, enc_down, w_bridge,
    dec_qkv, dec_out, dec_up, dec_down, w_head,
    vectors, first_moment, second_moment, enc_small, enc_big, dec_small, dec_big,
):
    n_dp, n_wide, n_nar = sizes
    ext = extents(sizes)
    masters = (w_embed, enc_qkv, enc_out, enc_up, enc_down, w_bridge, dec_qkv, dec_out, dec_up, dec_down, w_head)
    sources = [m if kind or i == 2 else m.T for i, (m, kind) in enumerate(zip(masters, ENC_KINDS + DEC_KINDS))]
    enc_cols, dec_cols = w_embed.shape[1], w_bridge.shape[1]
    shapes = shard_shapes(sources)
    units, events = gather_plan(ext, shapes)
    merged = MERGED and all(a % 16 == 0 for a, _ in shapes)
    if merged:
        weights, vec_all, weight_sum = sources, vectors, None
    else:
        gathered, vec_all, weight_sum = gather(sources, vectors, counts, sizes, units, events)
        weights = [g.reshape(n_nar, -1, g.shape[-1]) for g in gathered]
    shipped, vec_grad, weight_sum = compute(
        weights, shapes, vec_all, weight_sum, patches, vis_index, keep_mask, counts, sizes, units, events, merged
    )
    lefts, rights = shipped[: len(LEFTS)], shipped[len(LEFTS) :]
    pairs = ([(0, 0), (1, 1)], [(2, 2)], [(3, 3)], [(4, 4)], [(5, 5)], [(6, 6)], [(7, 7)], [(8, 8)], [(9, 9)], [(10, 10)])
    mats = []
    for terms, shape in zip(pairs, shapes):
        cols = -(-shape[1] // 128) * 128
        wide = [rights[g].shape[2] for _, g in terms]
        mats.append((shape[0], cols, [(x, g, 0 if i == 0 else cols - wide[i], wide[i]) for i, (x, g) in enumerate(terms)]))
    units, events = reduce_plan(ext, mats)
    owned, vec_sum, squares = reduce_scatter(
        lefts, rights, mats, vec_grad, sizes, units, events, [True] * 5 + [False] * 5
    )
    new, new_stats, new_vecs, norms, loss_total, weight_total = optimizer(
        owned, masters, (enc_small, enc_big, dec_small, dec_big), squares, vec_sum,
        weight_sum, vectors, first_moment, second_moment, step_count, enc_cols, dec_cols,
    )
    return (*new, *new_stats, *new_vecs, norms, loss_total, weight_total)


def solution(mesh):
    sizes = (mesh.shape["dp"], mesh.shape["wide"], mesh.shape["narrow"])
    rows = P(("dp", "wide"))
    matrix = P(("dp", "wide"), "narrow")
    turned = P("narrow", ("dp", "wide"))
    matrices = tuple(matrix if kind else turned for kind in ENC_KINDS + DEC_KINDS)
    stats = (P(("dp", "wide"), "narrow"),) * 4
    packed = (P("narrow"),) * 3
    in_specs = (rows, rows, rows, rows, P()) + matrices + packed + stats
    out_specs = matrices + stats + packed + (P(), P(), P())
    return jax.shard_map(
        functools.partial(per_device, sizes), mesh=mesh, in_specs=in_specs, out_specs=out_specs, check_vma=False
    )
```

```python
import functools
import math

import jax
import jax.numpy as jnp
import numpy as np
from jax import lax
from jax.experimental import pallas as pl
from jax.experimental.pallas import tpu as pltpu
from jax.sharding import PartitionSpec as P

D = 768
DH = 64
DD = 512
DHD = 32
PIX = 768
NP = 196
BLOCK = 64
NEWTON = 3
KEEP_MOST = 98

HIGH = lax.Precision.HIGHEST
EPS_NORM = 1e-06
VISIBLE_WEIGHT = 0.1
STAT_DECAY = 0.5
LR_MATRIX = 0.2
LR_VECTOR = 0.2
LAYER_DECAY = 0.75
BETA_FIRST = 0.9
BETA_SECOND = 0.999
EPS_ADAM = 1e-08
CLIP_NORM = 1.0
ENC_KINDS = (True, True, False, True, False, True)
DEC_KINDS = (True, False, True, False, True)


MESHT = pl.DeviceIdType.MESH
FULL_CODE = 32767.0
FLOOR = 1e-30


def xors(n):
    return list(range(1, n))


def extents(sizes):
    n_dp, n_wide, n_nar = sizes
    return {"n": n_nar, "h": n_dp // 2, "l": 2, "w": n_wide // 2}


def phases_of(order, ext):
    return [d for d in order if ext[d] > 1]


def messages(order, ext):
    out, left = [], 1
    for d in ext:
        left *= ext[d]
    for d in phases_of(order, ext):
        left //= ext[d]
        out.append((d, ext[d] - 1, left))
    return out


class Place:
    def __init__(self, sizes):
        self.sizes = sizes
        self.ext = extents(sizes)
        self.dp, self.wi, self.na = (lax.axis_index(x) for x in ("dp", "wide", "narrow"))
        self.own = {"n": self.na, "h": self.dp // 2, "l": self.dp % 2, "w": self.wi // 2}
        self.core = self.wi % 2

    def peer(self, dim, k):
        if dim == "n":
            return {"narrow": self.na ^ k}
        if dim == "h":
            return {"dp": self.dp ^ (2 * k)}
        if dim in "ld":
            return {"dp": self.dp ^ k}
        if dim == "w":
            return {"wide": self.wi ^ (2 * k)}
        if dim == "g":
            return {"dp": self.dp ^ (k // 2), "wide": self.wi ^ (k % 2)}
        return {"wide": self.wi ^ 1}

    def greet(self):
        ext = self.ext
        partners = [self.peer(d, k) for d in "nw" for k in xors(ext[d])]
        partners += [self.peer("g", k) for k in xors(2 * self.sizes[0])]
        barrier = pltpu.get_barrier_semaphore()
        for p in partners:
            pl.semaphore_signal(barrier, inc=1, device_id=p, device_id_type=MESHT)
        pl.semaphore_wait(barrier, len(partners))

    def hops(self, narrow, joint):
        out = [("c", 2, self.core), ("d", self.sizes[0], self.dp)]
        if joint:
            out = [("g", 2 * self.sizes[0], self.dp * 2 + self.core)]
        if self.ext["w"] > 1:
            out.append(("w", self.ext["w"], self.wi // 2))
        if narrow and self.ext["n"] > 1:
            out.append(("n", self.ext["n"], self.na))
        return out


def remote(src, dst, ss, rs, dev):
    return pltpu.make_async_remote_copy(
        src_ref=src, dst_ref=dst, send_sem=ss, recv_sem=rs, device_id=dev, device_id_type=MESHT
    )


class SmallSum:
    def __init__(self, place, value, lands, send, recv, narrow, joint):
        self.place, self.value, self.lands, self.send, self.recv = place, value, lands, send, recv
        self.axes = place.hops(narrow, joint)
        self.flight = None

    def start(self, i):
        d, members, at = self.axes[i]
        land = self.lands[i]
        land[at] = self.value[...]
        self.flight = []
        for k in xors(members):
            c = remote(self.value, land.at[at], self.send.at[i, k - 1], self.recv.at[i, k - 1], self.place.peer(d, k))
            c.start()
            self.flight.append(c)

    def finish(self, i):
        d, members, at = self.axes[i]
        for c in self.flight:
            c.wait()
        total = self.lands[i][0]
        for j in range(1, members):
            total = total + self.lands[i][j]
        self.value[...] = total

    @staticmethod
    def scratch(sizes, shape, narrow, joint):
        members = ([2 * sizes[0]] if joint else [2, sizes[0]]) + ([sizes[1] // 2] if sizes[1] > 2 else []) + ([sizes[2]] if narrow and sizes[2] > 1 else [])
        return [pltpu.VMEM((m,) + shape, jnp.float32) for m in members]

    @staticmethod
    def sems(sizes):
        return [pltpu.SemaphoreType.DMA((4, max(*sizes, 2 * sizes[0])))] * 2


def plan(units, events, mats, ext, tokens):
    flat = []
    for step in events:
        for u, p in step:
            if p <= len(phases_of(units[u][3], ext)) + 3:
                flat.append((u, p))
    at = {e: i for i, e in enumerate(flat)}
    blocks = ext["h"] * ext["l"] * ext["w"]
    wants = []
    big = max((mats[m][0] for m, *_ in units)), max(hi - lo for m, lo, hi, o in units)
    first_use, last_need = {}, {}
    for u, (m, lo, hi, order) in enumerate(units):
        a, c = mats[m][0], hi - lo
        for x, g, *_ in terms_of(mats, m, lo, hi):
            first_use[x] = min(first_use.get(x, (len(flat),)), (at[u, 0], at[u, 1], tokens[g], a))
            last_need[x] = max(last_need.get(x, 0), at[u, 3])
        last = at[u, len(phases_of(order, ext)) + 3]
        full = (ext["n"], blocks) + (big if a * c * 5 > 2 * big[0] * big[1] else (a, c))
        for j, (x, g, c_lo, c_hi, g_lo) in enumerate(terms_of(mats, m, lo, hi)):
            wants.append((at[u, 0], at[u, 3], ("g", u, j), (ext["n"], tokens[g], c_hi - c_lo), "b"))
        wants.append((at[u, 1], at[u, 3], ("out", u), full, "f"))
        wants.append((at[u, 2], at[u, 3], ("stage", u), full, "f"))
        wants.append((at[u, 3], at[u, 3], ("acc", u), full, "f"))
        wants.append((at[u, 3], last, ("kept", u), (messages(order, ext)[0][2], a, c), "f"))
        for p, (d, k, n) in enumerate(messages(order, ext)):
            wants.append((at[u, p + 3], last, ("q", u, p), (k, n, a, c), "q"))
    for x, (start, turn, rows, a) in first_use.items():
        turn = min(at[u, 1] for u, (m, lo, hi, o) in enumerate(units) if any(x == t[0] for t in terms_of(mats, m, lo, hi)))
        wants.append((start, turn, ("plain", x), (rows, 2 * blocks * a), "b"))
        wants.append((start, last_need[x], ("turned", x), (blocks, 2, a, rows), "b"))
    wants.sort(key=lambda w: w[0])
    bufs, where = [], {}
    for start, end, name, shape, kind in wants:
        for i, b in enumerate(bufs):
            if b[0] == (shape, kind) and b[1] < start:
                b[1] = end
                where[name] = i
                break
        else:
            bufs.append([(shape, kind), end])
            where[name] = len(bufs) - 1
    return [b[0] for b in bufs], where


def terms_of(mats, m, lo, hi):
    out = []
    for x, g, first, width in mats[m][2]:
        a, b = max(lo, first), min(hi, first + width)
        if a < b:
            out.append((x, g, a - lo, b - lo, a - first))
    out.sort(key=lambda t: t[2] - t[3])
    return out


def reduce_kernel(sizes, units, events, mats, n_left, n_right, planned, is_enc, *refs):
    place = Place(sizes)
    ext, own, core = place.ext, place.own, place.core
    count, nu = len(mats), len(units)
    blocks = ext["h"] * ext["l"] * ext["w"]
    f32 = jnp.float32
    it = iter(refs)
    take = lambda k: [next(it) for _ in range(k)]
    lefts, rights = take(n_left), take(n_right)
    vec = next(it)
    outs = take(count)
    vec_out, sq_out = take(2)
    land = take(nu)
    kinds, where = planned
    pool = [tuple(take(2)) if kind == "q" else take(1)[0] for _, kind in kinds]
    recv_q, recv_s = [], []
    for u in range(nu):
        k = len(messages(units[u][3], ext))
        recv_q.append(take(k))
        recv_s.append(take(k))
    plain = [pool[where["plain", x]] for x in range(n_left)]
    turned = [pool[where["turned", x]] for x in range(n_left)]
    n_axes, n_square = len(place.hops(False, False)), len(place.hops(True, True))
    vec_land, sq_land = take(n_axes), take(n_square)
    slab_land = next(it)
    (core_send, core_recv, stage_sem, g_sem, x_sem, q_send, q_recv, s_send, s_recv, v_send, v_recv, t_send, t_recv, n_send, n_recv) = take(15)
    left_copies = {}
    place.greet()
    small = SmallSum(place, vec_out, vec_land, v_send, v_recv, False, False)
    slab_flight = []
    for k in xors(ext["n"]):
        c = remote(vec.at[place.na ^ k], slab_land.at[place.na], n_send.at[k - 1], n_recv.at[k - 1], place.peer("n", k))
        c.start()
        slab_flight.append(c)
    slab_land[place.na] = vec[place.na]

    def slabs_here():
        for c in slab_flight:
            c.wait()
        total = slab_land[0]
        for j in range(1, ext["n"]):
            total = total + slab_land[j]
        vec_out[...] = total

    squares = SmallSum(place, sq_out, sq_land, t_send, t_recv, True, True)

    pending = []
    last_use = {}
    flight = {}
    sums = [jnp.zeros((1, 1), f32), jnp.zeros((1, 1), f32)]
    ready = set()

    def turn(k):
        if k in ready:
            return
        ready.add(k)
        left_copies[k].wait()
        t = plain[k][...].T
        a = turned[k].shape[2]
        if a % 16 == 0:
            turned[k][...] = t.reshape(turned[k].shape)
        else:
            for i in range(2 * blocks):
                turned[k][i // 2, i % 2] = t[i * a : (i + 1) * a]

    def product(u, n, which, ref_of):
        m, lo, hi, order = units[u]
        a, c = mats[m][0], hi - lo
        for j, (x, g, c_lo, c_hi, g_lo) in enumerate(terms_of(mats, m, lo, hi)):
            right = pool[where["g", u, j]][n]
            if a % 16 == 0:
                rows = turned[x][:, which].reshape(blocks * a, turned[x].shape[3])
                v = lax.dot_general(rows, right, (((1,), (0,)), ((), ())), preferred_element_type=f32)
                v = v.reshape(blocks, a, c_hi - c_lo)
                if j == 0:
                    ref_of[n] = v
                else:
                    ref_of[n, :, :, c_lo:c_hi] += v
            else:
                for b in range(blocks):
                    v = lax.dot_general(turned[x][b, which], right, (((1,), (0,)), ((), ())), preferred_element_type=f32)
                    if j == 0:
                        ref_of[n, b] = v
                    else:
                        ref_of[n, b, :, c_lo:c_hi] += v

    def whole(kind, u):
        m, lo, hi, order = units[u]
        ref = pool[where[kind, u]]
        a, c = mats[m][0], hi - lo
        return ref if ref.shape[2:] == (a, c) else ref.at[:, :, pl.ds(0, a), pl.ds(0, c)]

    def block_of(idx):
        return (idx["h"] * ext["l"] + idx["l"]) * ext["w"] + idx["w"]

    def slab(u, idx):
        at = 0
        for d in "nhlw":
            if d != phases_of(units[u][3], ext)[0]:
                at = at * ext[d] + idx[d]
        return pool[where["kept", u]].at[at]

    def split(s, dims):
        idx = {}
        for d in reversed(dims):
            if ext[d] == 1:
                idx[d] = 0
            else:
                idx[d] = s % ext[d]
                s = s // ext[d]
        return idx

    def loop(total, body):
        def step(s, carry):
            body(s)
            return carry
        lax.fori_loop(0, total, step, 0)

    def reuse(b):
        for c in last_use.pop(b, []):
            c.wait_send()

    def code_and_send(u, p):
        ph = phases_of(units[u][3], ext)
        d, peers, slabs = messages(units[u][3], ext)[p]
        gone = ph[:p]
        free = [x for x in "nhlw" if x != d and x not in gone]
        b = where["q", u, p]
        reuse(b)
        out_q, out_s = pool[b]
        sends = []
        for k in range(1, peers + 1):
            def body(s):
                idx = split(s, free)
                for x in gone:
                    idx[x] = own[x]
                idx[d] = own[d] ^ k
                x = (whole("acc", u).at[idx["n"], block_of(idx)] if p == 0 else slab(u, idx))[...]
                top = jnp.maximum(jnp.max(jnp.abs(x), axis=0, keepdims=True), FLOOR)
                out_q[k - 1, s] = jnp.round(x * (FULL_CODE / top)).astype(jnp.int32).astype(jnp.int16)
                out_s[k - 1, s] = top * (1.0 / FULL_CODE)
            loop(slabs, body)
            dev = place.peer(d, k)
            first = remote(out_q.at[k - 1], recv_q[u][p].at[k - 1], q_send.at[u, p, k - 1], q_recv.at[u, p, k - 1], dev)
            second = remote(out_s.at[k - 1], recv_s[u][p].at[k - 1], s_send.at[u, p, k - 1], s_recv.at[u, p, k - 1], dev)
            first.start()
            second.start()
            sends += [first, second]
        flight[u, p] = sends
        last_use[b] = sends

    def take_in(u, p):
        ph = phases_of(units[u][3], ext)
        d, peers, slabs = messages(units[u][3], ext)[p]
        gone = ph[: p + 1]
        free = [x for x in "nhlw" if x not in gone]
        for c in flight[u, p]:
            c.wait_recv()
        def body(s):
            idx = split(s, free)
            for x in gone:
                idx[x] = own[x]
            ref = slab(u, idx)
            v = ref[...]
            for k in range(peers):
                v = v + recv_q[u][p][k, s].astype(jnp.int32).astype(f32) * recv_s[u][p][k, s]
            ref[...] = v
        loop(slabs, body)

    def stage(u, p):
        m, lo, hi, order = units[u]
        n_ph = len(phases_of(order, ext))
        if p == 0:
            copies = []
            for j, (x, g, c_lo, c_hi, g_lo) in enumerate(terms_of(mats, m, lo, hi)):
                if x not in left_copies:
                    left_copies[x] = pltpu.make_async_copy(lefts[x], plain[x], x_sem.at[x])
                    left_copies[x].start()
                src = rights[g]
                if c_hi - c_lo != src.shape[2]:
                    src = src.at[:, :, slice(g_lo, g_lo + c_hi - c_lo)]
                c = pltpu.make_async_copy(src, pool[where["g", u, j]], g_sem.at[u, j])
                c.start()
                copies.append(c)
            flight[u, "g"] = copies
        elif p == 1:
            for c in flight[u, "g"]:
                c.wait()
            for x, *_ in terms_of(mats, m, lo, hi):
                turn(x)
            b = where["out", u]
            reuse(b)
            loop(ext["n"], lambda n: product(u, n, 1 - core, whole("out", u)))
            c = remote(whole("out", u), land[u], core_send.at[u], core_recv.at[u], place.peer("c", 1))
            c.start()
            flight[u, "core"] = c
            last_use[b] = [c]
        elif p == 2:
            flight[u, "core"].wait_recv()
            reuse(where["stage", u])
            c = pltpu.make_async_copy(land[u], whole("stage", u), stage_sem.at[u])
            c.start()
            flight[u, "stage"] = c
        elif p == 3:
            acc, more = whole("acc", u), whole("stage", u)
            reuse(where["acc", u])
            flight[u, "stage"].wait()
            def body(n):
                product(u, n, core, acc)
                acc[n] = acc[n] + more[n]
            loop(ext["n"], body)
            code_and_send(u, 0)
            d, peers, slabs = messages(order, ext)[0]
            def keep(i):
                idx = split(i, [x for x in "nhlw" if x != d])
                idx[d] = own[d]
                slab(u, idx)[...] = acc.at[idx["n"], block_of(idx)][...]
            loop(slabs, keep)
        else:
            take_in(u, p - 4)
            if p - 3 < n_ph:
                code_and_send(u, p - 3)
            else:
                x = slab(u, own)[...]
                outs[m][:, pl.ds(lo, hi - lo)] = x
                w = 0 if is_enc[m] else 1
                sums[w] = sums[w] + jnp.sum(x * x, keepdims=True)

    flat = [(u, p) for step in events for u, p in step if p <= len(phases_of(units[u][3], ext)) + 3]
    turns = [(i + 1) * len(flat) // (n_axes + 2) for i in range(n_axes + 1)]
    for i, (u, p) in enumerate(flat):
        stage(u, p)
        if i in turns:
            hop = turns.index(i)
            if hop:
                small.finish(hop - 1)
            else:
                slabs_here()
            if hop < n_axes:
                small.start(hop)
    row = lax.broadcasted_iota(jnp.int32, (8, 128), 0)
    share = 1.0 / (sizes[0] * sizes[1])
    enc_vec, dec_vec = vec_out[0:6, :], vec_out[6:13, :]
    sums[0] = sums[0] + share * jnp.sum(enc_vec * enc_vec, keepdims=True)
    sums[1] = sums[1] + share * jnp.sum(dec_vec * dec_vec, keepdims=True)
    loss = vec[0, 13:14, 0:1]
    sq_out[...] = jnp.where(row == 0, sums[0], jnp.where(row == 1, sums[1], jnp.where(row == 2, loss, 0.0)))
    for i in range(n_square):
        squares.start(i)
        squares.finish(i)
    for c in [c for cs in last_use.values() for c in cs]:
        c.wait_send()


def reduce_scatter(lefts, rights, mats, vec, sizes, units, events, is_enc, cid=1):
    ext = extents(sizes)
    blocks = ext["h"] * ext["l"] * ext["w"]
    f32, bf16 = jnp.float32, jnp.bfloat16
    tokens = [r.shape[1] for r in rights]
    planned = plan(units, events, mats, ext, tokens)
    coded = lambda k, n, a, c: [pltpu.VMEM((k, n, a, c), jnp.int16), pltpu.VMEM((k, n, 1, c), f32)]
    scratch = []
    for shape, kind in planned[0]:
        scratch += coded(*shape) if kind == "q" else [pltpu.VMEM(shape, f32 if kind == "f" else bf16)]
    for m, lo, hi, order in units:
        ms = [coded(k, n, mats[m][0], hi - lo) for d, k, n in messages(order, ext)]
        scratch += [x[0] for x in ms] + [x[1] for x in ms]
    scratch += SmallSum.scratch(sizes, vec.shape[1:], False, False) + SmallSum.scratch(sizes, (8, 128), True, True)
    scratch += [pltpu.VMEM(vec.shape, f32)]
    nu, kmax = len(units), max(ext.values())
    D_ = pltpu.SemaphoreType.DMA
    scratch += [D_((nu,))] * 3 + [D_((nu, 2)), D_((len(lefts),))] + [D_((nu, 4, kmax))] * 4 + SmallSum.sems(sizes) * 2 + [D_((kmax,))] * 2
    vm = pl.BlockSpec(memory_space=pltpu.VMEM)
    an = pl.BlockSpec(memory_space=pl.ANY)
    res = pl.pallas_call(
        functools.partial(reduce_kernel, sizes, units, events, mats, len(lefts), len(rights), planned, is_enc),
        out_shape=[jax.ShapeDtypeStruct(m[:2], f32) for m in mats]
        + [jax.ShapeDtypeStruct(vec.shape[1:], f32), jax.ShapeDtypeStruct((8, 128), f32)]
        + [jax.ShapeDtypeStruct((ext["n"], blocks, mats[m][0], hi - lo), f32) for m, lo, hi, o in units],
        in_specs=[an] * (len(lefts) + len(rights)) + [vm],
        out_specs=[vm] * (len(mats) + 2) + [an] * nu,
        scratch_shapes=scratch,
        compiler_params=pltpu.CompilerParams(collective_id=cid, has_side_effects=True, vmem_limit_bytes=60 << 20),
    )(*lefts, *rights, vec)
    return res[: len(mats)], res[len(mats)], res[len(mats) + 1]


class Gather:
    def __init__(self, place, units, events, shards, outs, sems):
        self.place, self.units, self.shards, self.outs = place, units, shards, outs
        self.send_sem, self.recv_sem, self.loc_sem = sems
        self.events = [(u, p) for step in events for u, p in step if p <= len(self.phases(u, units))]
        self.next = 0
        self.pending, self.from_sibling = [], []
        self.slots = [0] * len(units)
        self.flight, self.local = {}, {}
        self.complete = set()

    def phases(self, u, units=None):
        return [d for d in (units or self.units)[u][3] if self.place.ext[d] > 1]

    def region(self, u, full, at, which_core):
        m, lo, hi, order = self.units[u]
        own = self.place.own
        idx = [slice(None) if d in full else own[d] ^ at[1] if at and d == at[0] else own[d] for d in "nhlw"]
        if (lo, hi) == (0, self.shards[m].shape[1]):
            return self.outs[m].at[tuple(idx) + (which_core,)]
        return self.outs[m].at[tuple(idx) + (which_core, slice(None), slice(lo, hi))]

    def shard(self, u):
        m, lo, hi, order = self.units[u]
        return self.shards[m] if (lo, hi) == (0, self.shards[m].shape[1]) else self.shards[m].at[:, slice(lo, hi)]

    def send(self, u, src, dst, dev, landing):
        k = self.slots[u]
        self.slots[u] += 1
        c = remote(src, dst, self.send_sem.at[u, k], self.recv_sem.at[u, k], dev)
        c.start()
        self.pending.append(c)
        return remote(landing, landing, self.send_sem.at[u, k], self.recv_sem.at[u, k], dev)

    def stage(self, u, p):
        place, core = self.place, self.place.core
        m, ph = self.units[u][0], self.phases(u)
        sibling = place.peer("c", 1)
        came = self.flight.pop(u, [])
        if p == 0:
            c = pltpu.make_async_copy(self.shard(u), self.region(u, (), None, core), self.loc_sem.at[u])
            c.start()
            self.local[u] = c
            src = self.shard(u)
            self.from_sibling.append((m, self.send(u, src, self.region(u, (), None, core), sibling, self.region(u, (), None, 1 - core))))
        else:
            for k, w in came:
                w.wait_recv()
            if p == 1:
                self.local[u].wait()
            src = None
        if p < len(ph):
            mine = src if src is not None else self.region(u, ph[:p], None, core)
            self.flight[u] = [
                (k, self.send(u, mine, self.region(u, ph[:p], None, core), place.peer(ph[p], k), self.region(u, ph[:p], (ph[p], k), core)))
                for k in xors(place.ext[ph[p]])
            ]
        for k, _ in came:
            here = self.region(u, ph[: p - 1], (ph[p - 1], k), core)
            there = self.region(u, ph[: p - 1], (ph[p - 1], k), 1 - core)
            self.from_sibling.append((m, self.send(u, here, here, sibling, there)))

    def tick(self, steps):
        for u, p in self.events[self.next : self.next + steps]:
            self.stage(u, p)
        self.next += steps

    def need(self, m):
        if m in self.complete:
            return
        self.complete.add(m)
        last = max(i for i, (u, p) in enumerate(self.events) if self.units[u][0] == m)
        self.tick(max(0, last + 1 - self.next))
        for which, c in self.from_sibling:
            if which == m:
                c.wait_recv()

    def finish(self):
        for m in range(len(self.shards)):
            self.need(m)
        for c in self.pending:
            c.wait_send()


def cast_shards(masters, shards):
    embed, eqkv, eout, eup, edown, bridge, dqkv, dout, dup, ddown, head = masters
    low = jnp.bfloat16
    def by_kind(src, dst, size):
        heads = src.shape[1] // (3 * size)
        for t in range(3):
            for h in range(heads):
                to, at = (t * heads + h) * size, (h * 3 + t) * size
                dst[:, to : to + size] = src[:, at : at + size].astype(low)
    by_kind(eqkv, shards[0], DH)
    shards[0][:, eqkv.shape[1] :] = embed[...].astype(low)
    shards[1][...] = eout[...].T.astype(low)
    by_kind(dqkv, shards[5], DHD)
    for m, src in ((2, eup), (3, edown), (4, bridge), (6, dout), (7, dup), (8, ddown), (9, head)):
        shards[m][...] = src[...].astype(low)


def shard_shapes(masters):
    a, d = masters[0].shape[0], masters[6].shape[0]
    enc = (masters[0].shape[1] + masters[1].shape[1], masters[2].shape[0], *(m.shape[1] for m in masters[3:6]))
    return [(a, c) for c in enc] + [(d, m.shape[1]) for m in masters[6:]]


class Start:
    def __init__(self, sizes, masters, shards, vec, counts, vec_all, weight_sum, lands, sems):
        self.place = place = Place(sizes)
        vec_send, vec_recv, sum_send, sum_recv = sems
        cast_shards(masters, shards)
        total = jnp.float32(0.0)
        for i in range(counts.shape[0]):
            total = total + (NP - (1.0 - VISIBLE_WEIGHT) * counts[i].astype(jnp.float32))
        weight_sum[...] = jnp.zeros(weight_sum.shape, jnp.float32) + total
        place.greet()
        self.flight = []
        for k in xors(place.ext["n"]):
            c = remote(vec, vec_all.at[place.na], vec_send.at[k - 1], vec_recv.at[k - 1], place.peer("n", k))
            c.start()
            self.flight.append(c)
        vec_all[place.na] = vec[...]
        self.small = SmallSum(place, weight_sum, lands, sum_send, sum_recv, False, True)

    def sum_hops(self):
        return len(self.small.axes)

    def vectors_here(self):
        for c in self.flight:
            c.wait()

    @staticmethod
    def scratch(sizes, shapes):
        n = sizes[2]
        return (
            [pltpu.VMEM(s, jnp.bfloat16) for s in shapes]
            + SmallSum.scratch(sizes, (8, 128), False, True)
            + [pltpu.SemaphoreType.DMA((n,))] * 2
            + SmallSum.sems(sizes)
        )


def gather_sems(sizes, units):
    slots = 2 * sum(extents(sizes).values())
    DMA = pltpu.SemaphoreType.DMA
    return [DMA((len(units), slots)), DMA((len(units), slots)), DMA((len(units),))]


def gather_kernel(sizes, units, events, *refs):
    it = iter(refs)
    take = lambda k: [next(it) for _ in range(k)]
    masters = take(11)
    vec, counts = take(2)
    outs = take(10)
    vec_all, weight_sum = take(2)
    shards = take(10)
    lands = take(len(SmallSum.scratch(sizes, (8, 128), False, True)))
    small_sems, sems = take(4), take(3)
    start = Start(sizes, masters, shards, vec, counts, vec_all, weight_sum, lands, small_sems)
    g = Gather(start.place, units, events, shards, outs, sems)
    for i in range(start.sum_hops()):
        start.small.start(i)
        start.small.finish(i)
    g.finish()
    start.vectors_here()


def gather(masters, vec, counts, sizes, units, events, cid=0):
    ext = extents(sizes)
    an = pl.BlockSpec(memory_space=pl.ANY)
    vm = pl.BlockSpec(memory_space=pltpu.VMEM)
    sm = pl.BlockSpec(memory_space=pltpu.SMEM)
    shapes = shard_shapes(masters)
    heads = (ext["n"], ext["h"], ext["l"], ext["w"], 2)
    res = pl.pallas_call(
        functools.partial(gather_kernel, sizes, units, events),
        out_shape=[jax.ShapeDtypeStruct(heads + s, jnp.bfloat16) for s in shapes]
        + [jax.ShapeDtypeStruct((sizes[2],) + vec.shape, vec.dtype), jax.ShapeDtypeStruct((8, 128), jnp.float32)],
        in_specs=[vm] * 12 + [sm],
        out_specs=[an] * 10 + [vm, vm],
        scratch_shapes=Start.scratch(sizes, shapes) + gather_sems(sizes, units),
        compiler_params=pltpu.CompilerParams(collective_id=cid, has_side_effects=True),
    )(*masters, vec, counts)
    return res[:10], res[10], res[11]


GATHER_UNITS = (
    (0, 0, 256, "lhwn"), (0, 256, 512, "nlhw"), (0, 512, 768, "nhlw"), (1, 0, 256, "nlhw"), (2, 0, 384, "nhlw"),
    (2, 384, 768, "nlhw"), (3, 0, 384, "nlhw"), (3, 384, 768, "nhlw"), (4, 0, 128, "nhlw"), (5, 0, 384, "hlwn"),
    (6, 0, 128, "lnhw"), (7, 0, 256, "nhlw"), (7, 256, 512, "nlhw"), (8, 0, 256, "nlhw"), (8, 256, 512, "nhlw"),
    (9, 0, 256, "hnlw"),
)
GATHER_ORDER = (
    (8, 0), (3, 0), (2, 0), (1, 0), (0, 0), (7, 0), (8, 1), (0, 1), (5, 0), (4, 0), (3, 1), (8, 2), (6, 0), (0,
    2), (2, 1), (15, 0), (3, 2), (1, 1), (10, 0), (8, 3), (2, 2), (15, 1), (12, 0), (7, 1), (1, 2), (10, 1), (9,
    0), (13, 0), (3, 3), (5, 1), (14, 0), (2, 3), (7, 2), (4, 1), (11, 0), (5, 2), (6, 1), (1, 3), (9, 1), (4, 2),
    (7, 3), (6, 2), (0, 3), (9, 2), (5, 3), (15, 2), (12, 1), (10, 2), (4, 3), (13, 1), (6, 3), (14, 1), (15, 3),
    (10, 3), (11, 1), (12, 2), (14, 2), (13, 2), (11, 2), (14, 3), (12, 3), (11, 3), (13, 3), (9, 3),
)


def gather_plan(ext, shapes):
    cols = [s[1] for s in shapes]
    if ext["w"] > 1:
        units = [(m, 0, c, "nlhw") for m, c in enumerate(cols)]
        return units, [[(u, p)] for u in range(len(units)) for p in range(5)]
    units = [(m, lo, min(hi, cols[m]), order) for m, lo, hi, order in GATHER_UNITS]
    return units, [list(GATHER_ORDER[i : i + 12]) for i in range(0, len(GATHER_ORDER), 12)]


REDUCE_UNITS = (
    (0, 0, 256, "lnhw"), (0, 256, 512, "lhwn"), (0, 512, 768, "hlwn"), (1, 0, 256, "lhwn"), (2, 0, 256, "hlwn"),
    (2, 256, 512, "nhlw"), (2, 512, 768, "lhwn"), (3, 0, 256, "hnlw"), (3, 256, 512, "lhwn"), (3, 512, 768,
    "lhwn"), (4, 0, 128, "lnhw"), (5, 0, 256, "lhwn"), (5, 256, 384, "hlwn"), (6, 0, 128, "hnlw"), (7, 0, 256,
    "hnlw"), (7, 256, 512, "lhwn"), (8, 0, 256, "hlwn"), (8, 256, 512, "hlwn"), (9, 0, 256, "hlwn"),
)
REDUCE_ORDER = (
    (13, 0), (10, 0), (14, 0), (15, 0), (13, 1), (10, 1), (14, 1), (15, 1), (13, 2), (10, 2), (13, 3), (2, 0),
    (10, 3), (14, 2), (2, 1), (0, 0), (15, 2), (14, 3), (0, 1), (5, 0), (13, 4), (15, 3), (5, 1), (8, 0), (2, 2),
    (8, 1), (10, 4), (2, 3), (0, 2), (12, 0), (13, 5), (12, 1), (0, 3), (14, 4), (5, 2), (4, 0), (15, 4), (13, 6),
    (4, 1), (8, 2), (10, 5), (5, 3), (12, 2), (3, 0), (8, 3), (12, 3), (3, 1), (16, 0), (9, 0), (4, 2), (16, 1),
    (9, 1), (2, 4), (14, 5), (4, 3), (7, 0), (3, 2), (0, 4), (15, 5), (7, 1), (10, 6), (16, 2), (3, 3), (18, 0),
    (16, 3), (12, 4), (9, 2), (18, 1), (17, 0), (17, 1), (9, 3), (7, 2), (11, 0), (8, 4), (18, 2), (11, 1), (7,
    3), (1, 0), (17, 2), (18, 3), (6, 0), (1, 1), (4, 4), (2, 5), (17, 3), (14, 6), (11, 2), (6, 1), (5, 4), (11,
    3), (1, 2), (16, 4), (1, 3), (6, 2), (6, 3), (8, 5), (3, 4), (0, 5), (12, 5), (15, 6), (2, 6), (7, 4), (9, 4),
    (8, 6), (12, 6), (4, 5), (18, 4), (11, 4), (17, 4), (5, 5), (7, 5), (16, 5), (3, 5), (4, 6), (0, 6), (16, 6),
    (1, 4), (9, 5), (3, 6), (11, 5), (9, 6), (1, 5), (6, 4), (11, 6), (18, 5), (17, 5), (1, 6), (5, 6), (6, 5),
    (7, 6), (18, 6), (17, 6), (6, 6),
)


def reduce_plan(ext, mats):
    if ext["w"] > 1:
        units = [(m, lo, min(lo + 256, x[1]), "wlhn") for m, x in enumerate(mats) for lo in range(0, x[1], 256)]
        return units, [[(u, p)] for u in range(len(units)) for p in range(8)]
    return list(REDUCE_UNITS), [list(REDUCE_ORDER)]


def sincos_table(rows, width):
    column = np.arange(width)
    freq = np.power(np.float32(10000.0), (-(2 * (column // 2)).astype(np.float32) / np.float32(width)).astype(np.float32))
    angle = (np.arange(rows, dtype=np.float32)[:, None] * freq[None, :]).astype(np.float32)
    return np.where(column % 2 == 0, np.sin(angle), np.cos(angle)).astype(np.float32)


def dot_nn(a, b):
    return lax.dot_general(a, b, (((1,), (0,)), ((), ())), preferred_element_type=jnp.float32)


def dot_nt(a, b):
    return lax.dot_general(a, b, (((1,), (1,)), ((), ())), preferred_element_type=jnp.float32)


def dot_tn(a, b):
    return lax.dot_general(a, b, (((0,), (0,)), ((), ())), preferred_element_type=jnp.float32)


def dot_exact(a, b):
    return lax.dot_general(a, b, (((1,), (0,)), ((), ())), precision=HIGH, preferred_element_type=jnp.float32)


class Side:
    def __init__(self, width, head, heads, rows, images, slabs):
        self.width, self.head, self.heads, self.rows = width, head, heads, rows
        self.slabs = slabs
        self.tokens = rows * images
        self.lane = head * heads
        self.packed = -(-3 * self.lane // 128) * 128

    def scratch(self, hidden):
        t, n, w = self.tokens, self.slabs, self.width
        bf, f = jnp.bfloat16, jnp.float32
        return {
            "x": ((t, w), f),
            "hat1": ((t, w), f), "hat2": ((t, w), f), "hat3": ((t, w), f),
            "inv": ((t, 128), f),
            "n1": ((t, w), bf), "n2": ((t, w), bf), "n3": ((t, w), bf),
            "qkv": ((n, t, self.packed), bf),
            "lse": ((t // self.rows, -(-n * self.heads // 8) * 8, self.rows), f),
            "att": ((n, t, -(-self.lane // 128) * 128), bf),
            "slope": ((n, t, hidden), f),
            "act": ((n, t, hidden), bf),
            "dn": ((t, w), f),
            "og1": ((t, w), bf),
            "og2": ((t, w), bf),
        }


LEFTS = ("e_n1", "chosen", "e_og1", "e_n2", "e_og2", "e_n3", "d_n1", "d_og1", "d_n2", "d_og2", "d_n3")
RIGHTS = ("e_qkv", "part0", "e_att", "e_dh", "e_act", "part4", "d_qkv", "d_att", "d_dh", "d_act", "part9")
SHIPPED = LEFTS + RIGHTS
BUFFER_OF = {"e_dh": "e_act", "d_dh": "d_act"}


def compute_kernel(sizes, merged, per, slabs, names, units, events, *refs):
    it = iter(refs)
    take = lambda k: [next(it) for _ in range(k)]
    f32, bf16 = jnp.float32, jnp.bfloat16
    count = 10
    sources = take(11 if merged else 10)
    vec_parts, weight_in = (take(1)[0], None) if merged else take(2)
    patches_all, vis_all, keep_all, table_e, table_d, counts_all = take(6)
    shipped = take(len(SHIPPED))
    vec_out, weight_out = take(2)
    store = take(count)
    load_sem, store_sem = take(2)
    if merged:
        vec_all = take(1)[0]
        shards = take(count)
        lands = take(len(SmallSum.scratch(sizes, (8, 128), False, True)))
        small_sems, sems = take(4), take(3)
    buf = dict(zip(names, it))

    all_images = counts_all.shape[0]
    first_image = lax.axis_index("narrow") * per
    start_image = jnp.minimum(first_image, all_images - per)
    patch_copies = []
    for i in range(per):
        c = pltpu.make_async_copy(patches_all.at[start_image + i], buf["raw"].at[i], load_sem.at[count + i])
        c.start()
        patch_copies.append(c)

    ticks = [0]
    if merged:
        begin = Start(sizes, sources, shards, vec_parts, counts_all, vec_all, weight_out, lands, small_sems)
        g = Gather(begin.place, units, events, shards, store, sems)
        g.tick(12)
        for i in range(begin.sum_hops()):
            begin.small.start(i)
            g.tick(12)
            begin.small.finish(i)
        begin.vectors_here()
        need = g.need
    else:
        vec_all = vec_parts
        weight_out[...] = weight_in[...]
        loads = []
        for m in range(count):
            c = pltpu.make_async_copy(sources[m], store[m], load_sem.at[m])
            c.start()
            loads.append(c)
        waited = set()

        def need(m):
            if m not in waited:
                waited.add(m)
                loads[m].wait()

    def tick():
        if merged:
            g.tick(TICK)

    class Weight:
        def __init__(self, ref):
            self.ref = ref
            self.shape = (slabs, math.prod(ref.shape[1:-1]), ref.shape[-1])

        def __getitem__(self, at):
            n, lo, hi = at if isinstance(at, tuple) else (at, 0, self.shape[2])
            v = self.ref[n] if (lo, hi) == (0, self.shape[2]) else self.ref.at[..., lo:hi][n]
            return v.reshape(self.shape[1], hi - lo)

    w_eq, w_out, w_up, w_down, w_bridge, w_dqkv, w_dout, w_dup, w_ddown, w_head = [Weight(r) for r in store]
    enc_w, dec_w = table_e.shape[1], table_d.shape[1]
    dec_rows, enc_rows = table_e.shape[0], -(-KEEP_MOST // 16) * 16
    patches, loss_w, vis_rows = buf["patches"], buf["loss_w"], []
    patches[...] = jnp.zeros_like(patches)
    loss_w[...] = jnp.zeros_like(loss_w)
    counts = []
    for i in range(per):
        patch_copies[i].wait()
        patches[i, 0:NP, :] = buf["raw"][i]
        vis_rows.append(vis_all[pl.ds(start_image + i, 1), :])
        counts.append(counts_all[start_image + i])
        live = jnp.where(start_image + i >= first_image, 1.0, 0.0)
        row = jnp.where(keep_all[pl.ds(start_image + i, 1), :] == 1, VISIBLE_WEIGHT, 1.0) * live
        loss_w[i, 0:NP, :] = jnp.broadcast_to(row, (8, NP)).T[:, 0:1]
    enc = Side(enc_w, DH, w_out.shape[2] // DH, enc_rows, per, slabs)
    dec = Side(dec_w, DHD, w_dout.shape[2] // DHD, dec_rows, per, slabs)
    for s, tag in ((enc, "e_"), (dec, "d_")):
        s.tag = tag
        s.b = {k[2:]: v for k, v in buf.items() if k.startswith(tag)}
    enc.w, dec.w = (w_eq, w_out, w_up, w_down), (w_dqkv, w_dout, w_dup, w_ddown)
    enc.ids, dec.ids = (0, 1, 2, 3), (5, 6, 7, 8)
    enc.base, dec.base = 0, 7
    vec_full = buf["vec_full"]
    enc_c, dec_c = enc_w // slabs, dec_w // slabs
    at = 0
    for k in range(13):
        width = enc_c if k < 6 else dec_c
        for n in range(slabs):
            vec_full[k : k + 1, n * width : (n + 1) * width] = vec_all[n, :, at : at + width]
        at += width
    vec_grad = buf["vec_grad"]
    vec_grad[...] = jnp.zeros_like(vec_grad)

    def vector(k, width):
        return vec_full[k : k + 1, 0:width]

    CH = 32

    def chunks(total, body):
        def step(i, carry):
            body(pl.ds(pl.multiple_of(i * CH, CH), CH))
            return carry
        lax.fori_loop(0, total // CH, step, 0, unroll=True)

    def norm_fwd(s, k, out, hat, inv):
        gain, bias = vector(s.base + k, s.width), vector(s.base + k + 1, s.width)
        x = s.b["x"]
        def body(r):
            v = x[r, :]
            mean = jnp.mean(v, axis=1, keepdims=True)
            d = v - mean
            i = lax.rsqrt(jnp.mean(d * d, axis=1, keepdims=True) + EPS_NORM)
            h = d * i
            s.b[hat][r, :] = h
            s.b["inv"][r, inv : inv + 1] = i
            s.b[out][r, :] = (h * gain + bias).astype(bf16)
        chunks(s.tokens, body)

    def norm_bwd(s, k, hat, inv, add):
        gain = vector(s.base + k, s.width)
        def body(r):
            dn = s.b["dn"][r, :]
            h = s.b[hat][r, :]
            vec_grad[s.base + k : s.base + k + 1, 0 : s.width] += jnp.sum(dn * h, axis=0, keepdims=True)
            vec_grad[s.base + k + 1 : s.base + k + 2, 0 : s.width] += jnp.sum(dn, axis=0, keepdims=True)
            g = dn * gain
            d = s.b["inv"][r, inv : inv + 1] * (
                g - jnp.mean(g, axis=1, keepdims=True) - h * jnp.mean(g * h, axis=1, keepdims=True)
            )
            s.b["x"][r, :] = s.b["x"][r, :] + d if add else d
        chunks(s.tokens, body)

    def slab_loop(body):
        def step(n, carry):
            body(n)
            return carry
        lax.fori_loop(0, slabs, step, 0)

    def head_mask(s, h):
        lane = lax.broadcasted_iota(jnp.int32, (1, s.lane), 1)
        return (lane >= h * s.head) & (lane < (h + 1) * s.head)

    def scores(s, q, k, mask, limit):
        v = dot_nt(k, jnp.where(mask, q, jnp.zeros_like(q))) * (s.head ** -0.5)
        key = lax.broadcasted_iota(jnp.int32, (s.rows, s.rows), 0)
        return jnp.where(key < limit, v, -1e30)

    def attention_loop(body, between=None):
        def step(i, carry):
            body(i // slabs, i % slabs)
            return carry
        if between is None or not merged:
            lax.fori_loop(0, per * slabs, step, 0)
            return
        for image in range(per):
            lax.fori_loop(image * slabs, (image + 1) * slabs, step, 0)
            between()

    def image_rows(s, image):
        return pl.ds(pl.multiple_of(image * s.rows, 16), s.rows)

    def block_fwd(s, limit):
        b = s.b
        if b["att"].shape[2] != s.lane:
            b["att"][...] = jnp.zeros_like(b["att"])
        qkv_w, out_w, up_w, down_w = s.w
        need(s.ids[0])
        norm_fwd(s, 0, "n1", "hat1", 1)
        tick()
        def qkv(n):
            b["qkv"][n] = dot_nn(b["n1"][...], qkv_w[n, 0, s.packed]).astype(bf16)
        slab_loop(qkv)
        tick()
        def attend(image, n):
            r = image_rows(s, image)
            q = b["qkv"][n, r, 0 : s.lane]
            k = b["qkv"][n, r, s.lane : 2 * s.lane]
            v = b["qkv"][n, r, 2 * s.lane : 3 * s.lane]
            v_t = v.T
            parts = []
            for h in range(s.heads):
                sc = scores(s, q, k, head_mask(s, h), limit(image))
                top = jnp.max(sc, axis=0, keepdims=True)
                e = jnp.exp(sc - top)
                z = jnp.sum(e, axis=0, keepdims=True)
                p = (e * (1.0 / z)).astype(bf16)
                parts.append(dot_nn(v_t[h * s.head : (h + 1) * s.head], p))
                b["lse"][image, pl.ds(n * s.heads + h, 1), :] = top + jnp.log(z)
            b["att"][n, r, 0 : s.lane] = jnp.concatenate(parts, axis=0).astype(bf16).T
        attention_loop(attend, tick)
        need(s.ids[1])
        ship(s.tag + "att")
        def project(n):
            b["x"][...] += dot_nt(b["att"][n, :, 0 : s.lane], out_w[n])
        slab_loop(project)
        norm_fwd(s, 2, "n2", "hat2", 2)
        need(s.ids[2])
        need(s.ids[3])
        hid = buf["hid"]
        c = up_w.shape[2]
        def mlp(n):
            hid[0 : s.tokens, 0:c] = dot_nn(b["n2"][...], up_w[n])
            def body(r):
                v = hid[r, 0:c]
                cdf = 0.5 * (1.0 + lax.erf(v * 0.7071067811865476))
                b["act"][n, r, :] = (v * cdf).astype(bf16)
                b["slope"][n, r, :] = cdf + v * (0.3989422804014327 * jnp.exp(-0.5 * v * v))
            chunks(s.tokens, body)
            b["x"][...] += dot_nt(b["act"][n], down_w[n])
        if merged and s is enc:
            for n in range(slabs):
                mlp(n)
                tick()
        else:
            slab_loop(mlp)
        ship(s.tag + "act")
        norm_fwd(s, 4, "n3", "hat3", 3)
        for name in ("n1", "n2", "n3"):
            ship(s.tag + name)

    on_way = {}

    def ship(name):
        at = SHIPPED.index(name)
        c = pltpu.make_async_copy(buf[BUFFER_OF.get(name, name)], shipped[at], store_sem.at[at])
        c.start()
        on_way[name] = c

    def arrived(name):
        on_way.pop(name).wait()

    def block_bwd(s, limit):
        b = s.b
        qkv_w, out_w, up_w, down_w = s.w
        b["og2"][...] = b["x"][...].astype(bf16)
        ship(s.tag + "og2")
        b["dn"][...] = jnp.zeros_like(b["dn"])
        arrived(s.tag + "act")
        def down(n):
            b["act"][n] = (dot_nn(b["og2"][...], down_w[n]) * b["slope"][n]).astype(bf16)
            b["dn"][...] += dot_nt(b["act"][n], up_w[n])
        slab_loop(down)
        ship(s.tag + "dh")
        norm_bwd(s, 2, "hat2", 2, True)
        b["og1"][...] = b["x"][...].astype(bf16)
        ship(s.tag + "og1")
        arrived(s.tag + "att")
        def proj(n):
            b["att"][n, :, 0 : s.lane] = dot_nn(b["og1"][...], out_w[n]).astype(bf16)
        slab_loop(proj)
        def attend(image, n):
            r = image_rows(s, image)
            q = b["qkv"][n, r, 0 : s.lane]
            k = b["qkv"][n, r, s.lane : 2 * s.lane]
            v = b["qkv"][n, r, 2 * s.lane : 3 * s.lane]
            g = b["att"][n, r, 0 : s.lane]
            k_t = k.T
            parts = []
            dk = jnp.zeros((s.rows, s.lane), f32)
            dv = dk
            for h in range(s.heads):
                mask = head_mask(s, h)
                p = jnp.exp(scores(s, q, k, mask, limit(image)) - b["lse"][image, pl.ds(n * s.heads + h, 1), :])
                dp = dot_nt(v, jnp.where(mask, g, jnp.zeros_like(g)))
                dv = jnp.where(mask, dot_nn(p.astype(bf16), g), dv)
                ds = (p * (dp - jnp.sum(dp * p, axis=0, keepdims=True))).astype(bf16)
                dk = jnp.where(mask, dot_nn(ds, q), dk)
                parts.append(dot_nn(k_t[h * s.head : (h + 1) * s.head], ds))
            dq = jnp.concatenate(parts, axis=0).T
            scale = s.head ** -0.5
            if s.packed != 3 * s.lane:
                b["qkv"][n, r, 2 * s.lane : s.packed] = jnp.zeros((s.rows, s.packed - 2 * s.lane), bf16)
            b["qkv"][n, r, 0 : s.lane] = (dq * scale).astype(bf16)
            b["qkv"][n, r, s.lane : 2 * s.lane] = (dk * scale).astype(bf16)
            b["qkv"][n, r, 2 * s.lane : 3 * s.lane] = dv.astype(bf16)
        attention_loop(attend)
        ship(s.tag + "qkv")
        b["dn"][...] = jnp.zeros_like(b["dn"])
        def qkv(n):
            b["dn"][...] += dot_nt(b["qkv"][n], qkv_w[n, 0, s.packed])
        slab_loop(qkv)
        norm_bwd(s, 0, "hat1", 1, True)

    chosen = buf["chosen"]
    slots = KEEP_MOST
    chosen[...] = jnp.zeros_like(chosen)
    enc.b["x"][...] = jnp.zeros_like(enc.b["x"])
    for i in range(per):
        r = pl.ds(i * enc_rows, slots)
        patch = lax.broadcasted_iota(jnp.int32, (dec_rows, slots), 0)
        one = (patch == vis_rows[i]).astype(f32).T
        chosen[r, :] = dot_nn(one.astype(bf16), patches[i]).astype(bf16)
        enc.b["x"][r, :] = dot_exact(one, table_e[...])
    need(0)
    for n in range(slabs):
        lead = w_eq.shape[2] - 256
        part = dot_nn(chosen[...], w_eq[n, lead, lead + 256])
        enc.b["x"][:, n * enc_c : (n + 1) * enc_c] += part[:, 256 - enc_c : 256]
    ship("chosen")
    block_fwd(enc, lambda image: counts_all[start_image + image])
    need(4)
    bridged = buf["hid"]
    for n in range(slabs):
        bridged[0 : enc.tokens, n * dec_c : (n + 1) * dec_c] = dot_nn(enc.b["n3"][...], w_bridge[n])

    def hits(i, turned_way):
        patch = lax.broadcasted_iota(jnp.int32, (dec_rows, slots), 0)
        slot = lax.broadcasted_iota(jnp.int32, (dec_rows, slots), 1)
        hit = ((patch == vis_rows[i]) & (slot < counts[i])).astype(f32)
        return hit if turned_way else hit.T

    for i in range(per):
        r = pl.ds(i * dec_rows, dec_rows)
        hit = hits(i, True)
        placed = dot_exact(hit, bridged[pl.ds(i * enc_rows, slots), 0:dec_w])
        seen = jnp.sum(hit, axis=1, keepdims=True) > 0
        dec.b["x"][r, :] = jnp.where(seen, placed, vector(6, dec_w)) + table_d[...]
    block_fwd(dec, lambda image: NP)
    need(9)
    pred = buf["hid"]
    pix_c = w_head.shape[2]
    pix = patches.shape[2]
    for n in range(slabs):
        pred[0 : dec.tokens, n * pix_c : (n + 1) * pix_c] = dot_nn(dec.b["n3"][...], w_head[n])

    pgrad = buf["pgrad"]
    divisor = weight_out[0:1, 0:1]
    loss = jnp.zeros((1, 1), f32)
    LC = 16
    for i in range(per):
        def lossy(j, total):
            r = pl.ds(pl.multiple_of(j * LC, LC), LC)
            px = patches[i, r, :].astype(f32)
            d = px - jnp.mean(px, axis=1, keepdims=True)
            target = d * lax.rsqrt(jnp.mean(d * d, axis=1, keepdims=True) + EPS_NORM)
            rr = pl.ds(pl.multiple_of(i * dec_rows + j * LC, LC), LC)
            error = pred[rr, 0:pix] - target
            weight = loss_w[i, r, :]
            pgrad[rr, :] = (2.0 * weight * error / divisor).astype(bf16)
            return total + jnp.sum(weight * error * error, keepdims=True)
        loss = lax.fori_loop(0, dec_rows // LC, lossy, loss, unroll=True)
    part9 = buf["part9"]
    part9[...] = jnp.zeros_like(part9)
    for n in range(slabs):
        part9[n, :, 0:pix_c] = pgrad[:, n * pix_c : (n + 1) * pix_c]
    dec.b["dn"][...] = jnp.zeros_like(dec.b["dn"])
    ship("part9")
    def head_bwd(n):
        dec.b["dn"][...] += dot_nt(part9[n, :, 0:pix_c], w_head[n])
    slab_loop(head_bwd)
    norm_bwd(dec, 4, "hat3", 3, False)
    block_bwd(dec, lambda image: NP)
    part4 = buf["part4"]
    part4[...] = jnp.zeros_like(part4)
    for i in range(per):
        r = pl.ds(i * dec_rows, dec_rows)
        seen = jnp.sum(hits(i, True), axis=1, keepdims=True) > 0
        grad = dec.b["x"][r, :]
        vec_grad[6:7, 0:dec_w] += jnp.sum(jnp.where(seen, 0.0, grad), axis=0, keepdims=True)
        back = dot_exact(hits(i, False), grad).astype(bf16)
        for n in range(slabs):
            part4[n, pl.ds(i * enc_rows, slots), :] = back[:, n * dec_c : (n + 1) * dec_c]
    ship("part4")
    enc.b["dn"][...] = jnp.zeros_like(enc.b["dn"])
    def bridge_bwd(n):
        enc.b["dn"][...] += dot_nt(part4[n], w_bridge[n])
    slab_loop(bridge_bwd)
    norm_bwd(enc, 4, "hat3", 3, False)
    block_bwd(enc, lambda image: counts_all[start_image + image])

    part0 = buf["part0"]
    part0[...] = jnp.zeros_like(part0)
    for n in range(slabs):
        part0[n, :, 256 - enc_c : 256] = enc.b["x"][:, n * enc_c : (n + 1) * enc_c].astype(bf16)
    ship("part0")
    vec_out[...] = jnp.zeros_like(vec_out)
    for n in range(slabs):
        vec_out[n, 0:6, :] = vec_grad[0:6, n * enc_c : (n + 1) * enc_c]
        vec_out[n, 6:13, 0:dec_c] = vec_grad[6:13, n * dec_c : (n + 1) * dec_c]
        vec_out[n, 13:14, :] = jnp.zeros((1, enc_c), f32) + loss
    for name in list(on_way):
        arrived(name)
    if merged:
        g.finish()


TICK = 3
MERGED = True


def compute(sources, shapes, vec_parts, weight_sum, patches, vis_index, keep_mask, counts, sizes, units, events, merged):
    slabs = sizes[2]
    ext = extents(sizes)
    heads = (slabs, ext["h"], ext["l"], ext["w"], 2)
    owners = math.prod(heads[1:])
    weights = [jax.ShapeDtypeStruct((slabs, owners * a, c), jnp.bfloat16) for a, c in shapes]
    per, pix = -(-counts.shape[0] // slabs), patches.shape[2]
    dec_rows, enc_rows = -(-NP // 16) * 16, -(-KEEP_MOST // 16) * 16
    enc_w, dec_w = weights[0].shape[1], weights[5].shape[1]
    enc = Side(enc_w, DH, weights[1].shape[2] // DH, enc_rows, per, slabs)
    dec = Side(dec_w, DHD, weights[6].shape[2] // DHD, dec_rows, per, slabs)
    named = {}
    for s, tag, up in ((enc, "e_", weights[2]), (dec, "d_", weights[7])):
        for k, v in s.scratch(up.shape[2]).items():
            named[tag + k] = v
    f32, bf16 = jnp.float32, jnp.bfloat16
    top = max(enc.tokens, dec.tokens)
    named["hid"] = ((top, max(pix, weights[2].shape[2], weights[7].shape[2])), f32)
    named["vec_full"] = ((16, enc_w), f32)
    named["chosen"] = ((enc.tokens, pix), bf16)
    named["pgrad"] = ((dec.tokens, pix), bf16)
    up128 = lambda c: -(-c // 128) * 128
    named["part9"] = ((slabs, dec.tokens, up128(weights[9].shape[2])), bf16)
    named["part4"] = ((slabs, enc.tokens, weights[4].shape[2]), bf16)
    named["part0"] = ((slabs, enc.tokens, 256), bf16)
    named["vec_grad"] = ((16, enc_w), f32)
    named["raw"] = ((per, NP, pix), bf16)
    named["patches"] = ((per, dec_rows, pix), bf16)
    named["loss_w"] = ((per, dec_rows, 1), f32)
    ship_shapes = [jax.ShapeDtypeStruct(named[BUFFER_OF.get(k, k)][0], bf16) for k in SHIPPED]
    an = pl.BlockSpec(memory_space=pl.ANY)
    vm = pl.BlockSpec(memory_space=pltpu.VMEM)
    sm = pl.BlockSpec(memory_space=pltpu.SMEM)
    DMA = pltpu.SemaphoreType.DMA
    table_e = jnp.asarray(np.pad(sincos_table(NP, enc_w), ((0, dec_rows - NP), (0, 0))))
    table_d = jnp.asarray(np.pad(sincos_table(NP, dec_w), ((0, dec_rows - NP), (0, 0))))
    store = [pltpu.VMEM(heads + s if merged else w.shape, bf16) for s, w in zip(shapes, weights)]
    scratch = store + [DMA((10 + per,)), DMA((len(SHIPPED),))]
    small = [vec_parts] if merged else [vec_parts, weight_sum]
    if merged:
        scratch += [pltpu.VMEM((slabs,) + vec_parts.shape, f32)] + Start.scratch(sizes, shapes) + gather_sems(sizes, units)
    params = dict(vmem_limit_bytes=61 << 20)
    if merged:
        params.update(collective_id=0, has_side_effects=True)
    res = pl.pallas_call(
        functools.partial(compute_kernel, sizes, merged, per, slabs, list(named), units, events),
        out_shape=ship_shapes + [jax.ShapeDtypeStruct((slabs, 16, enc_w // slabs), f32), jax.ShapeDtypeStruct((8, 128), f32)],
        in_specs=[vm if merged else an] * len(sources) + [vm] * len(small) + [an] + [vm] * 4 + [sm],
        out_specs=[an] * len(SHIPPED) + [vm, vm],
        scratch_shapes=scratch + [pltpu.VMEM(s, d) for s, d in named.values()],
        compiler_params=pltpu.CompilerParams(**params),
    )(*sources, *small, patches, vis_index, keep_mask, table_e, table_d, counts)
    return res[: len(SHIPPED)], res[len(SHIPPED)], res[len(SHIPPED) + 1]


def split_low(x):
    high = x.astype(jnp.bfloat16)
    return high, (x - high.astype(jnp.float32)).astype(jnp.bfloat16)


def dot_three(a, b, kind=dot_nn):
    (ah, al), (bh, bl) = a, b
    return kind(ah, bh) + (kind(ah, bl) + kind(al, bh))


def roots(mats):
    side = mats[0].shape[0]
    eye = lax.broadcasted_iota(jnp.int32, (side, side), 0) == lax.broadcasted_iota(jnp.int32, (side, side), 1)
    five = jnp.where(eye, 5.0, 0.0)
    size = [jnp.sqrt(jnp.sum(m * m, keepdims=True)) for m in mats]
    current = [m * (1.0 / s) for m, s in zip(mats, size)]
    result = None
    for step in range(NEWTON):
        factor = [split_low((five - c) * 0.25) for c in current]
        if result is None:
            result = [(five - c) * 0.25 for c in current]
        else:
            result = [dot_three(split_low(r), f) for r, f in zip(result, factor)]
        if step + 1 < NEWTON:
            square = [split_low(dot_three(f, f)) for f in factor]
            fourth = [split_low(dot_three(q, q)) for q in square]
            current = [dot_three(q, split_low(c)) for q, c in zip(fourth, current)]
    return [r * lax.rsqrt(jnp.sqrt(s)) for r, s in zip(result, size)]


GROUPS = (41, 27)


def optimizer_kernel(pieces, upright, sides, enc_cols, dec_cols, *refs):
    it = iter(refs)
    take = lambda k: [next(it) for _ in range(k)]
    n_mats = len(pieces)
    owned = take(max(p[0] for blocks in pieces for parts in blocks for p in parts) + 1)
    masters = take(n_mats)
    stats = take(4)
    squares, vec_sum, weight_sum, vectors, first, second, step_count = take(7)
    new = take(n_mats)
    new_stats = take(4)
    new_vectors, new_first, new_second, norms, loss_out, weight_out = take(6)
    g_enc, g_dec, u_enc, u_dec = take(4)
    old = take(4)
    fresh = take(4)
    in_sem, out_sem = take(2)
    f32 = jnp.float32
    loads = []
    for i in (2, 3, 0, 1):
        c = pltpu.make_async_copy(stats[i], old[i], in_sem.at[i])
        c.start()
        loads.append((i, c))
    loads = dict(loads)

    enc_sq, dec_sq = squares[0:1, 0:1], squares[1:2, 0:1]
    norms[0] = jnp.sqrt(enc_sq)[0, 0]
    norms[1] = jnp.sqrt(dec_sq)[0, 0]
    loss_out[0] = squares[2:3, 0:1][0, 0]
    weight_out[0] = weight_sum[0:1, 0:1][0, 0]
    clip = jnp.minimum(1.0, CLIP_NORM / jnp.sqrt(enc_sq + dec_sq))

    sections = ((1, g_dec, u_dec, 2, LR_MATRIX), (0, g_enc, u_enc, 0, LR_MATRIX * LAYER_DECAY))
    for which, grad, update, base, rate in sections:
        at = 0
        for i in range(n_mats):
            if sides[i] != which:
                continue
            for parts in pieces[i]:
                col = 0
                for src, lo, width in parts:
                    grad[at, :, col : col + width] = owned[src][:, lo : lo + width] * clip
                    col += width
                at += 1
        total = at
        loads[base].wait()
        loads[base + 1].wait()
        group = min(GROUPS[which], total)
        def body(i, carry):
            start = jnp.minimum(i * group, total - group)
            g = [grad[start + j] for j in range(group)]
            low = [split_low(x) for x in g]
            turned = [split_low(x.T) for x in g]
            small = [STAT_DECAY * old[base][start + j] + (1.0 - STAT_DECAY) * dot_three(low[j], low[j], dot_nt) for j in range(group)]
            large = [STAT_DECAY * old[base + 1][start + j] + (1.0 - STAT_DECAY) * dot_three(turned[j], turned[j], dot_nt) for j in range(group)]
            for j in range(group):
                fresh[base][start + j] = small[j]
                fresh[base + 1][start + j] = large[j]
            left = roots(small)
            right = roots(large)
            for j in range(group):
                half = dot_three(split_low(left[j]), low[j])
                update[start + j] = rate * dot_three(split_low(half), split_low(right[j]))
            return carry
        lax.fori_loop(0, -(-total // group), body, 0)
        for k in (base, base + 1):
            pltpu.make_async_copy(fresh[k], new_stats[k], out_sem.at[k]).start()
        at = 0
        for i in range(n_mats):
            if sides[i] != which:
                continue
            for k in range(len(pieces[i])):
                lo = k * BLOCK
                if upright[i]:
                    new[i][:, lo : lo + BLOCK] = masters[i][:, lo : lo + BLOCK] - update[at]
                else:
                    new[i][lo : lo + BLOCK, :] = masters[i][lo : lo + BLOCK, :] - update[at].T
                at += 1

    steps = jnp.full((1, 128), step_count[0], jnp.int32).astype(f32)[0:1, 0:1]
    scale_one = 1.0 / (1.0 - jnp.exp(steps * math.log(BETA_FIRST)))
    scale_two = 1.0 / (1.0 - jnp.exp(steps * math.log(BETA_SECOND)))
    at = 0
    for k in range(13):
        width = enc_cols if k < 6 else dec_cols
        rate = LR_VECTOR * LAYER_DECAY if k < 6 else LR_VECTOR
        g = vec_sum[k : k + 1, 0:width] * clip
        cols = slice(at, at + width)
        one = BETA_FIRST * first[:, cols] + (1.0 - BETA_FIRST) * g
        two = BETA_SECOND * second[:, cols] + (1.0 - BETA_SECOND) * g * g
        new_first[:, cols] = one
        new_second[:, cols] = two
        new_vectors[:, cols] = vectors[:, cols] - rate * (one * scale_one) / (jnp.sqrt(two * scale_two) + EPS_ADAM)
        at += width
    for k in range(4):
        pltpu.make_async_copy(fresh[k], new_stats[k], out_sem.at[k]).wait()


def optimizer(owned, masters, stats, squares, vec_sum, weight_sum, vectors, first, second, step_count, enc_cols, dec_cols):
    kinds = ENC_KINDS + DEC_KINDS
    sides = (0,) * len(ENC_KINDS) + (1,) * len(DEC_KINDS)
    width = [m.shape[1] if kind else m.shape[0] for m, kind in zip(masters, kinds)]
    def plain(src, first_col, cols):
        return [[(src, first_col + k * BLOCK, BLOCK)] for k in range(cols // BLOCK)]
    def by_head(src, cols, head):
        heads = cols // (3 * head)
        per = BLOCK // head
        order = [(t * heads + h) * head for h in range(heads) for t in range(3)]
        return [[(src, order[k * per + j], head) for j in range(per)] for k in range(cols // BLOCK)]
    pieces = [
        plain(0, width[1], width[0]), by_head(0, width[1], DH), plain(1, 0, width[2]), plain(2, 0, width[3]),
        plain(3, 0, width[4]), plain(4, 0, width[5]), by_head(5, width[6], DHD), plain(6, 0, width[7]),
        plain(7, 0, width[8]), plain(8, 0, width[9]), plain(9, 0, width[10]),
    ]
    flat = [s.reshape(s.shape[2:]) for s in stats]
    upright = [kind or i != 2 for i, kind in enumerate(kinds)]
    masters = [m if kind or not up else m.T for m, kind, up in zip(masters, kinds, upright)]
    f32 = jnp.float32
    like = lambda x: jax.ShapeDtypeStruct(x.shape, f32)
    an = pl.BlockSpec(memory_space=pl.ANY)
    vm = pl.BlockSpec(memory_space=pltpu.VMEM)
    sm = pl.BlockSpec(memory_space=pltpu.SMEM)
    block = [pltpu.VMEM((flat[i].shape[0], flat[i].shape[1], BLOCK), f32) for i in (0, 2)]
    whole = [pltpu.VMEM(s.shape, f32) for s in flat]
    DMA = pltpu.SemaphoreType.DMA
    n = len(masters)
    res = pl.pallas_call(
        functools.partial(optimizer_kernel, pieces, upright, sides, enc_cols, dec_cols),
        out_shape=[like(m) for m in masters] + [like(s) for s in flat]
        + [like(vectors)] * 3 + [jax.ShapeDtypeStruct((k,), f32) for k in (2, 1, 1)],
        in_specs=[vm] * (len(owned) + n) + [an] * 4 + [vm] * 6 + [sm],
        out_specs=[vm] * n + [an] * 4 + [vm] * 3 + [sm] * 3,
        scratch_shapes=block + block + whole + whole + [DMA((4,)), DMA((4,))],
        compiler_params=pltpu.CompilerParams(vmem_limit_bytes=56 << 20),
    )(*owned, *masters, *flat, squares, vec_sum, weight_sum, vectors, first, second, step_count)
    new_stats = [r.reshape(s.shape) for r, s in zip(res[n : n + 4], stats)]
    new = [r if kind or not up else r.T for r, kind, up in zip(res[:n], kinds, upright)]
    return new, new_stats, res[n + 4 : n + 7], res[n + 7], res[n + 8].reshape(()), res[n + 9].reshape(())


def per_device(
    sizes,
    patches, vis_index, keep_mask, counts, step_count,
    w_embed, enc_qkv, enc_out, enc_up, enc_down, w_bridge,
    dec_qkv, dec_out, dec_up, dec_down, w_head,
    vectors, first_moment, second_moment, enc_small, enc_big, dec_small, dec_big,
):
    n_dp, n_wide, n_nar = sizes
    ext = extents(sizes)
    masters = (w_embed, enc_qkv, enc_out, enc_up, enc_down, w_bridge, dec_qkv, dec_out, dec_up, dec_down, w_head)
    sources = [m if kind or i == 2 else m.T for i, (m, kind) in enumerate(zip(masters, ENC_KINDS + DEC_KINDS))]
    enc_cols, dec_cols = w_embed.shape[1], w_bridge.shape[1]
    shapes = shard_shapes(sources)
    units, events = gather_plan(ext, shapes)
    merged = MERGED and all(a % 16 == 0 for a, _ in shapes)
    if merged:
        weights, vec_all, weight_sum = sources, vectors, None
    else:
        gathered, vec_all, weight_sum = gather(sources, vectors, counts, sizes, units, events)
        weights = [g.reshape(n_nar, -1, g.shape[-1]) for g in gathered]
    shipped, vec_grad, weight_sum = compute(
        weights, shapes, vec_all, weight_sum, patches, vis_index, keep_mask, counts, sizes, units, events, merged
    )
    lefts, rights = shipped[: len(LEFTS)], shipped[len(LEFTS) :]
    pairs = ([(0, 0), (1, 1)], [(2, 2)], [(3, 3)], [(4, 4)], [(5, 5)], [(6, 6)], [(7, 7)], [(8, 8)], [(9, 9)], [(10, 10)])
    mats = []
    for terms, shape in zip(pairs, shapes):
        cols = -(-shape[1] // 128) * 128
        wide = [rights[g].shape[2] for _, g in terms]
        mats.append((shape[0], cols, [(x, g, 0 if i == 0 else cols - wide[i], wide[i]) for i, (x, g) in enumerate(terms)]))
    units, events = reduce_plan(ext, mats)
    owned, vec_sum, squares = reduce_scatter(
        lefts, rights, mats, vec_grad, sizes, units, events, [True] * 5 + [False] * 5
    )
    new, new_stats, new_vecs, norms, loss_total, weight_total = optimizer(
        owned, masters, (enc_small, enc_big, dec_small, dec_big), squares, vec_sum,
        weight_sum, vectors, first_moment, second_moment, step_count, enc_cols, dec_cols,
    )
    return (*new, *new_stats, *new_vecs, norms, loss_total, weight_total)


def solution(mesh):
    sizes = (mesh.shape["dp"], mesh.shape["wide"], mesh.shape["narrow"])
    rows = P(("dp", "wide"))
    matrix = P(("dp", "wide"), "narrow")
    turned = P("narrow", ("dp", "wide"))
    matrices = tuple(matrix if kind else turned for kind in ENC_KINDS + DEC_KINDS)
    stats = (P(("dp", "wide"), "narrow"),) * 4
    packed = (P("narrow"),) * 3
    in_specs = (rows, rows, rows, rows, P()) + matrices + packed + stats
    out_specs = matrices + stats + packed + (P(), P(), P())
    return jax.shard_map(
        functools.partial(per_device, sizes), mesh=mesh, in_specs=in_specs, out_specs=out_specs, check_vma=False
    )
```
